32 devices in a mesh: dp: 2 (over y), row: 4 (over z), col: 4 (over x, core).
Axes of the slice: x: 2, y: 2, z: 4, core: 2. Of those that a mesh axis runs over, the one named last changes fastest.
Arguments:
- inputs: bfloat16 [18464, 1024], P(('dp', 'row'), 'col'), may hold values from -30 to 30
- query_weight: bfloat16 [1024, 1024], P('row', 'col'), may hold values from -7 to 7
- key_weight: bfloat16 [1024, 1024], P('row', 'col'), may hold values from -7 to 7
- value_weight: bfloat16 [1024, 1024], P('row', 'col'), may hold values from -0.1875 to 0.1875
- query_bias: float32 [1024], P('col'), may hold values from -3 to 3
- value_bias: float32 [1024], P('col'), may hold values from -0.3 to 0.3
- out_weight: bfloat16 [1024, 1024], P('col', 'row'), may hold values from -1.5 to 1.5
- out_bias: float32 [1024], P('col'), may hold values from -3 to 3
- up_weight: bfloat16 [1024, 4096], P('row', 'col'), may hold values from -0.1875 to 0.1875
- up_bias: float32 [4096], P('col'), may hold values from -3 to 3
- down_weight: bfloat16 [4096, 1024], P('col', 'row'), may hold values from -0.09375 to 0.09375
- down_bias: float32 [1024], P('col'), may hold values from -3 to 3
- first_gain: float32 [1024], P('col'), may hold values from 0.1 to 1.9
- first_shift: float32 [1024], P('col'), may hold values from -2 to 2
- second_gain: float32 [1024], P('col'), may hold values from 0.1 to 1.9
- second_shift: float32 [1024], P('col'), may hold values from -2 to 2
- cotangent: bfloat16 [18464, 1024], P(('dp', 'row'), 'col'), may hold values from -6 to 6
Outputs:
- outputs: bfloat16 [18464, 1024], P(('dp', 'row'), 'col')
- input_grad: float32 [18464, 1024], P(('dp', 'row'), 'col')
- query_weight_grad: float32 [1024, 1024], P('row', 'col')
- key_weight_grad: float32 [1024, 1024], P('row', 'col')
- value_weight_grad: float32 [1024, 1024], P('row', 'col')
- query_bias_grad: float32 [1024], P('col')
- value_bias_grad: float32 [1024], P('col')
- out_weight_grad: float32 [1024, 1024], P('col', 'row')
- out_bias_grad: float32 [1024], P('col')
- up_weight_grad: float32 [1024, 4096], P('row', 'col')
- up_bias_grad: float32 [4096], P('col')
- down_weight_grad: float32 [4096, 1024], P('col', 'row')
- down_bias_grad: float32 [1024], P('col')
- first_gain_grad: float32 [1024], P('col')
- first_shift_grad: float32 [1024], P('col')
- second_gain_grad: float32 [1024], P('col')
- second_shift_grad: float32 [1024], P('col')
The draws below stay inside these ranges and needn't reach their ends.
All inputs are finite; a program needn't handle non-finite values.
Results may differ from the reference program's by a relative error of at most 0.012.
The reference program's roundings to bfloat16 on the way count: a program that leaves them out, or rounds other values in their place, can miss the bound.
Values may be sent and summed in bfloat16 or wider, within the bound.
No kernel may reach another device: no remote copies, remote signals or barrier semaphores. Data moves between devices by JAX's collectives and lax.ppermute only.
A program may use at most 192 MiB of HBM per device.

```python
import math
import jax
import jax.numpy as jnp
from jax import lax

D = 1024
HEADS = 16
HD = 64
FF = 4096
SEQ = 577
IMG_DEV = 4
IMAGES = 32
TOKENS = 18464


def draw_inputs(key, part):
    key_base = jax.random.fold_in(key, 1)
    key_rough = jax.random.fold_in(key, 2)
    key_rows = jax.random.fold_in(key, 3)
    key_offset = jax.random.fold_in(key, 4)
    base_draw = jnp.clip(jax.random.normal(key_base, (TOKENS, D), jnp.float32), -6.0, 6.0)
    offset = 0.5 * jax.random.normal(key_offset, (TOKENS, 1), jnp.float32)
    feature_rise = 0.55 * jnp.exp(math.log(3.0) * jnp.arange(D, dtype=jnp.float32) / D)
    roughness = jnp.exp(jax.random.uniform(key_rough, (D,), jnp.float32, -0.35, 0.35))
    row_scale = jnp.exp(jax.random.uniform(key_rows, (TOKENS, 1), jnp.float32, math.log(0.3), math.log(3.0)))
    return jnp.clip((base_draw * feature_rise * roughness + offset) * row_scale, -30.0, 30.0).astype(jnp.bfloat16)


def base_weight(key, salt):
    base_draw = jax.random.normal(jax.random.fold_in(key, salt), (D, D), jnp.float32)
    return jnp.clip(base_draw, -6.0, 6.0) * D ** (-0.5)


def draw_query_weight(key, part):
    matrix = base_weight(key, 21)
    return matrix.astype(jnp.bfloat16)


def draw_key_weight(key, part):
    matrix = base_weight(key, 22)
    return matrix.astype(jnp.bfloat16)


def block_levels(stream_key, dims, pieces, least, high):
    def one(dim, parts):
        steps = jax.random.uniform(jax.random.fold_in(jax.random.fold_in(stream_key, 6), dim), (parts,), jnp.float32, least / len(pieces), high / len(pieces))
        return jnp.repeat(jnp.exp(steps), dims[dim] // parts).reshape((-1,) + (1,) * (len(dims) - dim - 1))

    level = one(*pieces[0])
    for cut in pieces[1:]:
        level = level * one(*cut)
    return level


def normal_values(rng, extent, deviation, bound, shards=(), kind=jnp.bfloat16):
    values = deviation * jax.random.normal(rng, extent, jnp.float32)
    if shards:
        values = values * block_levels(rng, extent, shards, -0.22, 0.18)
    return jnp.clip(values, -bound, bound).astype(kind)


def setup_inputs(seed: int = 0) -> dict:
    key_of = jax.random.split(jax.random.key(seed), 18)
    inputs = draw_inputs(jax.random.fold_in(key_of[17], 71), 0)
    query_weight = draw_query_weight(jax.random.fold_in(key_of[17], 71), 0)
    key_weight = draw_key_weight(jax.random.fold_in(key_of[17], 71), 0)
    value_weight = normal_values(key_of[3], (D, D), D ** -0.5, 0.1875, ((0, 4), (1, 4)))
    query_bias = normal_values(key_of[4], (D,), 0.5, 3.0, ((0, 4),), jnp.float32)
    value_bias = normal_values(key_of[5], (D,), 0.05, 0.3, ((0, 4),), jnp.float32)
    out_weight = normal_values(key_of[6], (D, D), (max(D // 64, 2)) ** -0.5, 1.5, ((0, 4), (1, 4)))
    out_bias = normal_values(key_of[7], (D,), 0.5, 3.0, ((0, 4),), jnp.float32)
    up_weight = normal_values(key_of[8], (D, FF), D ** -0.5, 0.1875, ((0, 4), (1, 4)))
    up_bias = normal_values(key_of[9], (FF,), 0.5, 3.0, ((0, 4),), jnp.float32)
    down_weight = normal_values(key_of[10], (FF, D), FF ** -0.5, 0.09375, ((0, 4), (1, 4)))
    down_bias = normal_values(key_of[11], (D,), 0.5, 3.0, ((0, 4),), jnp.float32)
    first_gain = jnp.clip(1.0 + 0.18 * jax.random.normal(key_of[12], (D,), jnp.float32), 0.1, 1.9)
    first_shift = normal_values(key_of[13], (D,), 0.3, 2.0, ((0, 4),), jnp.float32)
    second_gain = jnp.clip(1.0 + 0.18 * jax.random.normal(key_of[14], (D,), jnp.float32), 0.1, 1.9)
    second_shift = normal_values(key_of[15], (D,), 0.3, 2.0, ((0, 4),), jnp.float32)
    cotangent = normal_values(key_of[16], (TOKENS, D), 1.0, 6.0, ((0, 8), (1, 4)))
    return dict(inputs=inputs, query_weight=query_weight, key_weight=key_weight, value_weight=value_weight, query_bias=query_bias, value_bias=value_bias, out_weight=out_weight, out_bias=out_bias, up_weight=up_weight, up_bias=up_bias, down_weight=down_weight, down_bias=down_bias, first_gain=first_gain, first_shift=first_shift, second_gain=second_gain, second_shift=second_shift, cotangent=cotangent)


@jax.custom_vjp
def low(v):
    return lax.optimization_barrier(v.astype(jnp.bfloat16)).astype(jnp.float32)

@jax.custom_vjp
def low_back(v):
    return v

def low_keep(v):
    return (low(v), None)

def low_pass(kept, grad):
    return (grad,)

def back_keep(v):
    return (v, None)

def back_low(kept, grad):
    return (low(grad),)
low.defvjp(low_keep, low_pass)
low_back.defvjp(back_keep, back_low)
EPSILON = 1e-06

def product(left_side, right_side):
    return jnp.dot(left_side, right_side, precision=lax.Precision.HIGHEST, preferred_element_type=jnp.float32)

def norm_rows(values, gain_vector, shift_vector):
    middle = lax.optimization_barrier(jnp.sum(values, axis=-1, keepdims=True)) / D
    spread = lax.optimization_barrier(jnp.sum(values * values, axis=-1, keepdims=True)) / D - middle * middle
    return (values - middle) * lax.rsqrt(spread + EPSILON) * gain_vector + shift_vector

def attend_image(operands):
    query_rows, key_rows, value_rows = operands
    scores = jnp.einsum('qhd,khd->hqk', query_rows, key_rows, precision=lax.Precision.HIGHEST) * 0.125
    scores = low_back(scores)
    row_peak = lax.optimization_barrier(jnp.max(scores, axis=-1, keepdims=True))
    exponent = jnp.exp(scores - row_peak)
    soft_weights = low(exponent / lax.optimization_barrier(jnp.sum(exponent, axis=-1, keepdims=True)))
    return jnp.einsum('hqk,khd->qhd', soft_weights, value_rows, precision=lax.Precision.HIGHEST)

def layer_forward(params, inputs_rows):
    query_weight, key_weight, value_weight, query_bias, value_bias, out_weight, out_bias, up_weight, up_bias, down_weight, down_bias, first_gain, first_shift, second_gain, second_shift = params
    normed_one = low(norm_rows(inputs_rows, first_gain, first_shift))
    queries = low_back(low(product(normed_one, query_weight) + query_bias))
    key_rows = low_back(low(product(normed_one, key_weight)))
    values = low_back(low(product(normed_one, value_weight) + value_bias))
    head_shape = (IMG_DEV, SEQ, HEADS, HD)
    attended = lax.map(jax.checkpoint(attend_image), (queries.reshape(head_shape), key_rows.reshape(head_shape), values.reshape(head_shape)))
    attended = low_back(low(attended.reshape(IMG_DEV * SEQ, D)))
    middle_sum = inputs_rows + low_back(product(attended, out_weight) + out_bias)
    normed_two = low(norm_rows(middle_sum, second_gain, second_shift))
    up_values = low_back(product(normed_two, up_weight) + up_bias)
    hidden = low(jax.nn.gelu(up_values, approximate=False))
    return middle_sum + low_back(product(hidden, down_weight) + down_bias)

def reference(inputs, query_weight, key_weight, value_weight, query_bias, value_bias, out_weight, out_bias, up_weight, up_bias, down_weight, down_bias, first_gain, first_shift, second_gain, second_shift, cotangent):
    params = tuple((item.astype(jnp.float32) for item in (query_weight, key_weight, value_weight, query_bias, value_bias, out_weight, out_bias, up_weight, up_bias, down_weight, down_bias, first_gain, first_shift, second_gain, second_shift)))
    groups = IMAGES // IMG_DEV
    rows_in = inputs.astype(jnp.float32).reshape(groups, IMG_DEV * SEQ, D)
    grads_in = cotangent.astype(jnp.float32).reshape(groups, IMG_DEV * SEQ, D)

    def one_group(carry, operands):
        group_in, group_cot = operands
        group_out, pullback = jax.vjp(layer_forward, params, group_in)
        param_grads, input_grads = pullback(group_cot)
        carry = jax.tree.map(jnp.add, carry, param_grads)
        return (carry, (group_out, input_grads))
    zeros_start = jax.tree.map(jnp.zeros_like, params)
    totals, (group_outputs, group_grads) = lax.scan(one_group, zeros_start, (rows_in, grads_in))
    outputs = group_outputs.reshape(TOKENS, D).astype(jnp.bfloat16)
    input_grad = group_grads.reshape(TOKENS, D)
    return (outputs, input_grad, totals[0], totals[1], totals[2], totals[3], totals[4], totals[5], totals[6], totals[7], totals[8], totals[9], totals[10], totals[11], totals[12], totals[13], totals[14])
```

```python
import functools

import jax
import jax.numpy as jnp
from jax import lax
from jax.sharding import Mesh, PartitionSpec as P

D = 1024
HD = 64
SEQ = 577
PAD = 592
EPS = 1e-06
F32 = jnp.float32
BF16 = jnp.bfloat16


def mm(left_side, right_side):
    return jnp.dot(left_side, right_side, preferred_element_type=F32)


def mm_tn(left_side, right_side):
    return lax.dot_general(
        left_side, right_side, (((0,), (0,)), ((), ())), preferred_element_type=F32
    )


def mm_nt(left_side, right_side):
    return lax.dot_general(
        left_side, right_side, (((1,), (1,)), ((), ())), preferred_element_type=F32
    )


def swap(value, axis, size):
    return lax.ppermute(value, axis, [(place, place ^ 1) for place in range(size)])


def row_mean(values):
    return jnp.sum(values, axis=1, keepdims=True) / D


def norm_forward(rows, gain, shift):
    middle = row_mean(rows)
    spread = row_mean(rows * rows) - middle * middle
    scaled = lax.rsqrt(spread + EPS)
    centred = (rows - middle) * scaled
    return centred * gain + shift, centred, scaled


def norm_backward(upstream, gain, centred, scaled):
    lifted = upstream * gain
    return scaled * (lifted - row_mean(lifted) - centred * row_mean(lifted * centred))


def attend_image(operands):
    query_rows, key_rows, value_rows = operands
    scores = jnp.einsum("qhd,khd->hqk", query_rows, key_rows, preferred_element_type=F32) * 0.125
    live = lax.broadcasted_iota(jnp.int32, (1, 1, PAD), 2) < SEQ
    scores = jnp.where(live, scores, -1e30)
    row_peak = jnp.max(scores, axis=-1, keepdims=True)
    exponent = jnp.exp(scores - row_peak)
    row_total = jnp.sum(exponent, axis=-1, keepdims=True)
    soft_weights = (exponent / row_total).astype(BF16)
    mixed_rows = jnp.einsum("hqk,khd->qhd", soft_weights, value_rows, preferred_element_type=F32)
    return (mixed_rows.astype(BF16), row_peak + jnp.log(row_total))


def attend_back(operands):
    query_rows, key_rows, value_rows, grad_rows, logsum = operands
    scores = jnp.einsum("qhd,khd->hqk", query_rows, key_rows, preferred_element_type=F32) * 0.125
    live = lax.broadcasted_iota(jnp.int32, (1, 1, PAD), 2) < SEQ
    soft_weights = jnp.where(live, jnp.exp(scores - logsum), 0.0)
    dprobs = jnp.einsum("qhd,khd->hqk", grad_rows, value_rows, preferred_element_type=F32)
    dvalues = jnp.einsum(
        "hqk,qhd->khd", soft_weights.astype(BF16), grad_rows, preferred_element_type=F32
    )
    row_dot = jnp.sum(soft_weights * dprobs, axis=-1, keepdims=True)
    dscores = (soft_weights * (dprobs - row_dot)).astype(BF16)
    dqueries = jnp.einsum("hqk,khd->qhd", dscores, key_rows, preferred_element_type=F32) * 0.125
    key_grads = jnp.einsum("hqk,qhd->khd", dscores, query_rows, preferred_element_type=F32) * 0.125
    return dqueries.astype(BF16), key_grads.astype(BF16), dvalues.astype(BF16)


def gelu_exact(values):
    return jax.nn.gelu(values, approximate=False)


def local(
    sizes,
    inputs,
    query_weight,
    key_weight,
    value_weight,
    query_bias,
    value_bias,
    out_weight,
    out_bias,
    up_weight,
    up_bias,
    down_weight,
    down_bias,
    first_gain,
    first_shift,
    second_gain,
    second_shift,
    cotangent,
):
    n_dp, n_row, n_xa, n_core = sizes
    my_x = lax.axis_index("xa")
    my_core = lax.axis_index("core")
    tokens_here, width = inputs.shape
    images = tokens_here // SEQ
    held = images // n_xa
    rows = held * PAD
    hidden = up_weight.shape[1]

    def across(value):
        return swap(value, "xa", n_xa)

    def beside(value):
        return swap(value, "core", n_core)

    def image_halves(value):
        padded = jnp.pad(value.reshape(images, SEQ, -1), ((0, 0), (0, PAD - SEQ), (0, 0)))
        halves = padded.reshape(n_xa, rows, -1)
        mine = lax.dynamic_index_in_dim(halves, my_x, 0, keepdims=False)
        theirs = lax.dynamic_index_in_dim(halves, my_x ^ 1, 0, keepdims=False)
        return mine, theirs

    def in_order(mine, other, place):
        first = jnp.where(place == 0, mine, other)
        second = jnp.where(place == 0, other, mine)
        return first, second

    def wide_tokens(value):
        mine, theirs = image_halves(value)
        got = across(theirs)
        pair = jnp.stack(in_order(mine, got, my_x))
        other = beside(pair)
        left, right = in_order(pair, other, my_core)
        return jnp.concatenate([left[0], right[0], left[1], right[1]], axis=1)

    small = jnp.concatenate(
        [
            out_bias,
            down_bias,
            first_gain,
            first_shift,
            second_gain,
            second_shift,
            query_bias,
            value_bias,
            up_bias,
        ]
    )
    small_far = across(small)
    small_pair = jnp.stack(in_order(small, small_far, my_x))
    small_other = beside(small_pair)
    small_left, small_right = in_order(small_pair, small_other, my_core)

    def whole_vector(place):
        cut = slice(width * place, width * (place + 1))
        return jnp.concatenate(
            [small_left[0, cut], small_right[0, cut], small_left[1, cut], small_right[1, cut]]
        )

    out_bias_all, down_bias_all, gain_one, shift_one, gain_two, shift_two = (
        whole_vector(place) for place in range(6)
    )
    query_bias_far = small_far[6 * width : 7 * width]
    value_bias_far = small_far[7 * width : 8 * width]
    up_bias_far = small_far[8 * width :]

    def gather_rows(value):
        return lax.all_gather(value, "row", axis=0, tiled=True)

    qkv_near = gather_rows(jnp.concatenate([query_weight, key_weight, value_weight], axis=1))
    qkv_far = across(qkv_near)
    out_near = gather_rows(out_weight.T)
    out_far = across(out_near)
    up_near = gather_rows(up_weight)
    up_far = across(up_near)
    down_near = gather_rows(down_weight.T)
    down_far = across(down_near)

    wide_input = wide_tokens(inputs)
    wide_grad = wide_tokens(cotangent)
    residual = wide_input.astype(F32)

    normed_one, centred_one, scaled_one = norm_forward(residual, gain_one, shift_one)
    wide_one = normed_one.astype(BF16)

    zeros = jnp.zeros_like(query_bias)
    bias_near = jnp.concatenate([query_bias, zeros, value_bias])
    bias_far = jnp.concatenate([query_bias_far, zeros, value_bias_far])
    near = (mm(wide_one, qkv_near) + bias_near).astype(BF16)
    far = (mm(wide_one, qkv_far) + bias_far).astype(BF16)
    heads_here = 2 * width // HD
    head_shape = (held, PAD, heads_here, HD)

    def heads(place):
        cut = slice(width * place, width * (place + 1))
        return jnp.concatenate([near[:, cut], far[:, cut]], axis=1).reshape(head_shape)

    query_heads, key_heads, value_heads = heads(0), heads(1), heads(2)
    attended, logsums = lax.map(attend_image, (query_heads, key_heads, value_heads))
    attended = attended.reshape(rows, 2 * width)
    mixed = mm_nt(attended[:, :width], out_near) + mm_nt(attended[:, width:], out_far)
    mixed = mixed.astype(BF16)
    middle_sum = residual + (mixed.astype(F32) + beside(mixed).astype(F32)) + out_bias_all

    normed_two, centred_two, scaled_two = norm_forward(middle_sum, gain_two, shift_two)
    wide_two = normed_two.astype(BF16)

    def mlp(up_block, up_bias_block, down_block):
        up_values = mm(wide_two, up_block) + up_bias_block
        gelu_value, gelu_back = jax.vjp(gelu_exact, up_values)
        gate = gelu_value.astype(BF16)
        pre_grad = gelu_back(mm(wide_grad, down_block))[0].astype(BF16)
        return gate, pre_grad

    gate_near, pre_near = mlp(up_near, up_bias, down_near)
    gate_far, pre_far = mlp(up_far, up_bias_far, down_far)

    def feature_split(value):
        blocks = value.reshape(rows, n_xa, 2, width)
        mine = lax.dynamic_index_in_dim(blocks, my_core, 2, keepdims=False)
        theirs = lax.dynamic_index_in_dim(blocks, my_core ^ 1, 2, keepdims=False)
        return mine.reshape(rows, -1), theirs.reshape(rows, -1)

    def to_feature_blocks(value):
        blocks = value.reshape(rows, n_xa, width)
        mine = lax.dynamic_index_in_dim(blocks, my_x, 1, keepdims=False)
        theirs = lax.dynamic_index_in_dim(blocks, my_x ^ 1, 1, keepdims=False)
        got = across(theirs)
        first, second = in_order(mine, got, my_x)
        both = jnp.concatenate([first, second]).reshape(images, PAD, width)
        return both[:, :SEQ].reshape(tokens_here, width)

    lowered = mm_nt(gate_near, down_near) + mm_nt(gate_far, down_far)
    lowered_mine, lowered_theirs = feature_split(lowered)
    middle_mine, _ = feature_split(middle_sum)
    down_bias_mine, _ = feature_split(jnp.broadcast_to(down_bias_all, (rows, D)))
    branch = lowered_mine + beside(lowered_theirs.astype(BF16)).astype(F32)
    outputs = to_feature_blocks((middle_mine + branch + down_bias_mine).astype(BF16))

    def reduce_grad(near_grad, far_grad):
        total = (near_grad + across(far_grad.astype(BF16)).astype(F32)).astype(BF16)
        piece = lax.psum_scatter(total, "row", scatter_dimension=0, tiled=True)
        return piece.astype(F32) + swap(piece, "dp", n_dp).astype(F32) if n_dp == 2 else (
            lax.psum(piece.astype(F32), "dp")
        )

    down_grad = reduce_grad(mm_tn(wide_grad, gate_near), mm_tn(wide_grad, gate_far)).T
    up_grad = reduce_grad(mm_tn(wide_two, pre_near), mm_tn(wide_two, pre_far))
    lifted_two = (mm_nt(pre_near, up_near) + mm_nt(pre_far, up_far)).astype(BF16)
    normed_grad_two = lifted_two.astype(F32) + beside(lifted_two).astype(F32)
    grad_top = wide_grad.astype(F32)
    middle_grad = grad_top + norm_backward(normed_grad_two, gain_two, centred_two, scaled_two)
    attn_grad = middle_grad.astype(BF16)
    out_grad = reduce_grad(
        mm_tn(attn_grad, attended[:, :width]), mm_tn(attn_grad, attended[:, width:])
    ).T
    head_grad = jnp.concatenate([mm(attn_grad, out_near), mm(attn_grad, out_far)], axis=1)
    head_grad = head_grad.astype(BF16).reshape(head_shape)
    dqueries, key_grads, dvalues = lax.map(
        attend_back, (query_heads, key_heads, value_heads, head_grad, logsums)
    )
    dqueries, key_grads, dvalues = (
        item.reshape(rows, 2 * width) for item in (dqueries, key_grads, dvalues)
    )
    grads_near = jnp.concatenate([item[:, :width] for item in (dqueries, key_grads, dvalues)], axis=1)
    grads_far = jnp.concatenate([item[:, width:] for item in (dqueries, key_grads, dvalues)], axis=1)
    qkv_grad = reduce_grad(mm_tn(wide_one, grads_near), mm_tn(wide_one, grads_far))
    lifted_one = (mm_nt(grads_near, qkv_near) + mm_nt(grads_far, qkv_far)).astype(BF16)
    normed_grad_one = lifted_one.astype(F32) + beside(lifted_one).astype(F32)
    input_wide = middle_grad + norm_backward(normed_grad_one, gain_one, centred_one, scaled_one)
    input_mine, _ = feature_split(input_wide)
    input_grad = to_feature_blocks(input_mine.astype(BF16)).astype(F32)

    def column_sum(value):
        return jnp.sum(value.astype(F32), axis=0)

    def own_features(value):
        blocks = value.reshape(n_xa, 2, width)
        return lax.dynamic_index_in_dim(blocks, my_core, 1, keepdims=False)

    def by_x(near_sum, far_sum):
        return jnp.stack(in_order(near_sum, far_sum, my_x))

    near_sums, far_sums = column_sum(grads_near), column_sum(grads_far)
    vectors = jnp.concatenate(
        [
            by_x(near_sums[:width], far_sums[:width]),
            by_x(near_sums[2 * width :], far_sums[2 * width :]),
            own_features(column_sum(attn_grad)),
            own_features(column_sum(grad_top)),
            own_features(column_sum(normed_grad_one * centred_one)),
            own_features(column_sum(normed_grad_one)),
            own_features(column_sum(normed_grad_two * centred_two)),
            own_features(column_sum(normed_grad_two)),
            by_x(column_sum(pre_near), column_sum(pre_far)),
        ],
        axis=1,
    )
    vector_sums = lax.dynamic_index_in_dim(
        lax.psum(vectors, ("dp", "row", "xa")), my_x, 0, keepdims=False
    )
    pieces = [vector_sums[width * place : width * (place + 1)] for place in range(8)]
    up_bias_sum = vector_sums[8 * width :]
    return (
        outputs,
        input_grad,
        qkv_grad[:, :width],
        qkv_grad[:, width : 2 * width],
        qkv_grad[:, 2 * width :],
        pieces[0],
        pieces[1],
        out_grad,
        pieces[2],
        up_grad,
        up_bias_sum,
        down_grad,
        pieces[3],
        pieces[4],
        pieces[5],
        pieces[6],
        pieces[7],
    )


def solution(mesh):
    n_dp, n_row, n_col = (mesh.shape[name] for name in ("dp", "row", "col"))
    sizes = (n_dp, n_row, n_col // 2, 2)
    split = Mesh(mesh.devices.reshape(sizes), ("dp", "row", "xa", "core"))
    col = ("xa", "core")
    tokens, rows, cols, vec = P(("dp", "row"), col), P("row", col), P(col, "row"), P(col)
    in_specs = (
        tokens, rows, rows, rows, vec, vec, cols, vec, rows, vec, cols, vec, vec, vec, vec, vec, tokens,
    )
    out_specs = (
        tokens, tokens, rows, rows, rows, vec, vec, cols, vec, rows, vec, cols, vec, vec, vec, vec, vec,
    )
    return jax.shard_map(
        functools.partial(local, sizes),
        mesh=split,
        in_specs=in_specs,
        out_specs=out_specs,
        check_vma=False,
    )
```

```python
import functools
import math
import jax
import jax.numpy as jnp
from jax import lax
from jax.sharding import Mesh, PartitionSpec as P
from jax.experimental import pallas as pl
from jax.experimental.pallas import tpu as pltpu

D = 1024
HD = 64
SEQ = 577
PAD = 592
EPS = 1e-06
F32 = jnp.float32
BF16 = jnp.bfloat16
VM = 60 * 1024 * 1024


def mm(a, b):
    return lax.dot_general(a, b, (((1,), (0,)), ((), ())), preferred_element_type=F32)

def mm_nt(a, b):
    return lax.dot_general(a, b, (((1,), (1,)), ((), ())), preferred_element_type=F32)

def mm_tn(a, b):
    return lax.dot_general(a, b, (((0,), (0,)), ((), ())), preferred_element_type=F32)

def row_mean(v):
    return jnp.sum(v, axis=1, keepdims=True) * (1.0 / D)

def stats(rows):
    middle = row_mean(rows)
    spread = row_mean(rows * rows) - middle * middle
    return middle, lax.rsqrt(spread + EPS)

def params(n, **kw):
    return pltpu.CompilerParams(dimension_semantics=("arbitrary",) * n, vmem_limit_bytes=VM, **kw)

def qkv_kernel(x_ref, gain_ref, shift_ref, wn_ref, wf_ref, bn_ref, bf_ref, n_ref, o_ref):
    x = x_ref[...].astype(F32)
    middle, scaled = stats(x)
    n = (((x - middle) * scaled) * gain_ref[...] + shift_ref[...]).astype(BF16)
    n_ref[...] = n
    w = bn_ref.shape[1]
    o_ref[:, :w] = (mm(n, wn_ref[...]) + bn_ref[...]).astype(BF16)
    o_ref[:, w:] = (mm(n, wf_ref[...]) + bf_ref[...]).astype(BF16)

def norm_qkv(x, gain, shift, wn, wf, bn, bf, tm=296):
    rows = x.shape[0]; w = bn.shape[1]
    row = lambda c: pl.BlockSpec((tm, c), lambda i: (i, 0))
    vec = lambda c: pl.BlockSpec((1, c), lambda i: (0, 0))
    whole = lambda s: pl.BlockSpec((D, w), lambda i: (0, 0), pipeline_mode=pl.Buffered(1))
    return pl.pallas_call(qkv_kernel, grid=(rows // tm,), name="norm_qkv",
        in_specs=[row(D), vec(D), vec(D), whole(wn.shape), whole(wf.shape), vec(w), vec(w)],
        out_specs=[row(D), row(2 * w)],
        out_shape=[jax.ShapeDtypeStruct((rows, D), BF16), jax.ShapeDtypeStruct((rows, 2 * w), BF16)],
        compiler_params=params(1))(x, gain, shift, wn, wf, bn, bf)

def attend_kernel(q_ref, k_ref, v_ref, o_ref, p_ref):
    live = lax.broadcasted_iota(jnp.int32, (1, PAD), 1) < SEQ
    for h in range(2):
        cut = slice(HD * h, HD * (h + 1))
        s = mm_nt(q_ref[:, cut] * jnp.asarray(0.125, BF16), k_ref[:, cut])
        s = jnp.where(live, s, -1e30)
        peak = jnp.max(s, axis=1, keepdims=True)
        e = jnp.exp(s - peak)
        total = jnp.sum(e, axis=1, keepdims=True)
        p = (e * (1.0 / total)).astype(BF16)
        p_ref[h] = p
        o_ref[:, cut] = mm(p, v_ref[:, cut]).astype(BF16)

def head_spec(which, pairs):
    return pl.BlockSpec((PAD, 2 * HD), lambda i, p: (i, (p // pairs) * 3 * pairs + which * pairs + p % pairs))

def attend(qkv):
    rows, w3 = qkv.shape
    pairs = w3 // (6 * 2 * HD)
    held = rows // PAD
    return pl.pallas_call(attend_kernel, grid=(held, 2 * pairs), name="attend",
        in_specs=[head_spec(0, pairs), head_spec(1, pairs), head_spec(2, pairs)],
        out_specs=[pl.BlockSpec((PAD, 2 * HD), lambda i, p: (i, p)),
                   pl.BlockSpec((None, 2, PAD, PAD), lambda i, p: (i, p, 0, 0))],
        out_shape=[jax.ShapeDtypeStruct((rows, w3 // 3), BF16),
                   jax.ShapeDtypeStruct((held, 4 * pairs, PAD, PAD), BF16)],
        compiler_params=params(2))(qkv, qkv, qkv)

def attend_back_kernel(q_ref, k_ref, v_ref, p_ref, g_ref, dq_ref, dk_ref, dv_ref):
    for h in range(2):
        cut = slice(HD * h, HD * (h + 1))
        g = g_ref[:, cut]
        pb = p_ref[h]
        p = pb.astype(F32)
        dp = mm_nt(g, v_ref[:, cut])
        z = jnp.sum(p * dp, axis=1, keepdims=True)
        ds = (p * (dp - z)).astype(BF16)
        dq_ref[:, cut] = (mm(ds, k_ref[:, cut]) * 0.125).astype(BF16)
        dk_ref[:, cut] = (mm_tn(ds, q_ref[:, cut]) * 0.125).astype(BF16)
        dv_ref[:, cut] = mm_tn(pb, g).astype(BF16)

def attend_back(qkv, probs, grads):
    rows, w3 = qkv.shape
    pairs = w3 // (6 * 2 * HD)
    held = rows // PAD
    pair = pl.BlockSpec((PAD, 2 * HD), lambda i, p: (i, p))
    out = jax.ShapeDtypeStruct((rows, w3 // 3), BF16)
    return pl.pallas_call(attend_back_kernel, grid=(held, 2 * pairs), name="attend_back",
        in_specs=[head_spec(0, pairs), head_spec(1, pairs), head_spec(2, pairs),
                  pl.BlockSpec((None, 2, PAD, PAD), lambda i, p: (i, p, 0, 0)), pair],
        out_specs=[pair, pair, pair], out_shape=[out, out, out],
        compiler_params=params(2))(qkv, qkv, qkv, probs, grads)

def middle_kernel(x_ref, a_ref, b_ref, bias_ref, gain_ref, shift_ref, h_ref, n_ref):
    h = x_ref[...].astype(F32) + (a_ref[...].astype(F32) + b_ref[...].astype(F32)) + bias_ref[...]
    h_ref[...] = h
    middle, scaled = stats(h)
    n_ref[...] = (((h - middle) * scaled) * gain_ref[...] + shift_ref[...]).astype(BF16)

def middle(x, a, b, bias, gain, shift, tm=296):
    rows = x.shape[0]
    row = pl.BlockSpec((tm, D), lambda i: (i, 0))
    vec = pl.BlockSpec((1, D), lambda i: (0, 0))
    return pl.pallas_call(middle_kernel, grid=(rows // tm,), name="middle",
        in_specs=[row, row, row, vec, vec, vec], out_specs=[row, row],
        out_shape=[jax.ShapeDtypeStruct((rows, D), F32), jax.ShapeDtypeStruct((rows, D), BF16)],
        compiler_params=params(1))(x, a, b, bias, gain, shift)

ROOT_HALF = math.sqrt(0.5)
DENSITY = 1.0 / math.sqrt(2.0 * math.pi)

def mlp_kernel(tiles, n_ref, dy_ref, *refs):
    ups, downs, biases = refs[0:4], refs[4:8], refs[8:12]
    g_ref, du_ref, low_ref, lift_ref, bsum_ref, low_acc, lift_acc = refs[12:]
    j = pl.program_id(0)

    @pl.when(j == 0)
    def _():
        low_acc[...] = jnp.zeros_like(low_acc)
        lift_acc[...] = jnp.zeros_like(lift_acc)

    def step(up_ref, down_ref, bias_ref):
        u = mm(n_ref[...], up_ref[...]) + bias_ref[...]
        cdf = 0.5 * (1.0 + lax.erf(u * ROOT_HALF))
        g = (u * cdf).astype(BF16)
        slope = cdf + u * (jnp.exp(-0.5 * u * u) * DENSITY)
        g_ref[...] = g
        du = (mm(dy_ref[...], down_ref[...]) * slope).astype(BF16)
        du_ref[...] = du
        bsum_ref[...] = jnp.sum(du.astype(F32), axis=0, keepdims=True)
        low_acc[...] += mm_nt(g, down_ref[...])
        lift_acc[...] += mm_nt(du, up_ref[...])

    for block in range(4):

        @pl.when((j >= block * tiles) & (j < (block + 1) * tiles))
        def _(block=block):
            step(ups[block], downs[block], biases[block])

    @pl.when(j == 4 * tiles - 1)
    def _():
        low_ref[...] = low_acc[...].astype(BF16)
        lift_ref[...] = lift_acc[...].astype(BF16)


def mlp(n2, dy, packs, biases, tn=256):
    rows = n2.shape[0]
    half = packs[0].shape[1] // 2
    tiles = half // tn
    hid = 4 * half
    whole = pl.BlockSpec((rows, D), lambda j: (0, 0), pipeline_mode=pl.Buffered(1))

    def part(height, block, skip):
        return pl.BlockSpec(
            (height, tn), lambda j: (0, jnp.clip(j - block * tiles, 0, tiles - 1) + skip)
        )

    tile = pl.BlockSpec((rows, tn), lambda j: (0, j))
    return pl.pallas_call(
        functools.partial(mlp_kernel, tiles),
        grid=(4 * tiles,),
        name="mlp",
        in_specs=[whole, whole]
        + [part(D, block, 0) for block in range(4)]
        + [part(D, block, tiles) for block in range(4)]
        + [part(1, block, 0) for block in range(4)],
        out_specs=[tile, tile, whole, whole, pl.BlockSpec((1, tn), lambda j: (0, j))],
        out_shape=[
            jax.ShapeDtypeStruct((rows, hid), BF16),
            jax.ShapeDtypeStruct((rows, hid), BF16),
            jax.ShapeDtypeStruct((rows, D), BF16),
            jax.ShapeDtypeStruct((rows, D), BF16),
            jax.ShapeDtypeStruct((1, hid), F32),
        ],
        scratch_shapes=[pltpu.VMEM((rows, D), F32), pltpu.VMEM((rows, D), F32)],
        compiler_params=params(1),
    )(n2, dy, *packs, *packs, *biases)


def turn_kernel(h_ref, dy_ref, a_ref, b_ref, gain_ref, wn_ref, wf_ref, dh_ref, da_ref, do_ref, sums_ref):
    i = pl.program_id(0)
    h = h_ref[...]
    middle, scaled = stats(h)
    c = (h - middle) * scaled
    dn = a_ref[...].astype(F32) + b_ref[...].astype(F32)
    dy = dy_ref[...].astype(F32)
    e = dn * gain_ref[...]
    dh = dy + scaled * (e - row_mean(e) - c * row_mean(e * c))
    dh_ref[...] = dh
    da = dh.astype(BF16)
    da_ref[...] = da
    w = wn_ref.shape[1]
    do_ref[:, :w] = mm(da, wn_ref[...]).astype(BF16)
    do_ref[:, w:] = mm(da, wf_ref[...]).astype(BF16)
    col = lambda v: jnp.sum(v, axis=0, keepdims=True)
    part = jnp.concatenate([col(dn * c), col(dn), col(da.astype(F32)), col(dy)], axis=0)
    @pl.when(i == 0)
    def _(): sums_ref[...] = part
    @pl.when(i > 0)
    def _(): sums_ref[...] += part

def turn(h, dy, a, b, gain, wn, wf, tm=296):
    rows = h.shape[0]; w = wn.shape[1] // 4
    row = lambda c: pl.BlockSpec((tm, c), lambda i: (i, 0))
    vec = pl.BlockSpec((1, D), lambda i: (0, 0))
    whole = pl.BlockSpec((D, w), lambda i: (0, 3), pipeline_mode=pl.Buffered(1))
    return pl.pallas_call(turn_kernel, grid=(rows // tm,), name="turn",
        in_specs=[row(D), row(D), row(D), row(D), vec, whole, whole],
        out_specs=[row(D), row(D), row(2 * w), pl.BlockSpec((4, D), lambda i: (0, 0))],
        out_shape=[jax.ShapeDtypeStruct((rows, D), F32), jax.ShapeDtypeStruct((rows, D), BF16),
                   jax.ShapeDtypeStruct((rows, 2 * w), BF16), jax.ShapeDtypeStruct((4, D), F32)],
        compiler_params=params(1))(h, dy, a, b, gain, wn, wf)

def last_kernel(x_ref, dh_ref, a_ref, b_ref, gain_ref, o_ref, sums_ref):
    i = pl.program_id(0)
    x = x_ref[...].astype(F32)
    middle, scaled = stats(x)
    c = (x - middle) * scaled
    dn = a_ref[...].astype(F32) + b_ref[...].astype(F32)
    e = dn * gain_ref[...]
    o_ref[...] = (dh_ref[...] + scaled * (e - row_mean(e) - c * row_mean(e * c))).astype(BF16)
    part = jnp.concatenate([jnp.sum(dn * c, axis=0, keepdims=True), jnp.sum(dn, axis=0, keepdims=True)], axis=0)
    @pl.when(i == 0)
    def _(): sums_ref[...] = part
    @pl.when(i > 0)
    def _(): sums_ref[...] += part

def last(x, dh, a, b, gain, tm=296):
    rows = x.shape[0]
    row = pl.BlockSpec((tm, D), lambda i: (i, 0))
    vec = pl.BlockSpec((1, D), lambda i: (0, 0))
    return pl.pallas_call(last_kernel, grid=(rows // tm,), name="last",
        in_specs=[row, row, row, row, vec], out_specs=[row, pl.BlockSpec((2, D), lambda i: (0, 0))],
        out_shape=[jax.ShapeDtypeStruct((rows, D), BF16), jax.ShapeDtypeStruct((2, D), F32)],
        compiler_params=params(1))(x, dh, a, b, gain)


def local(
    sizes,
    inputs,
    query_weight,
    key_weight,
    value_weight,
    query_bias,
    value_bias,
    out_weight,
    out_bias,
    up_weight,
    up_bias,
    down_weight,
    down_bias,
    first_gain,
    first_shift,
    second_gain,
    second_shift,
    cotangent,
):
    n_dp, n_row, n_xa, n_core = sizes
    my_x = lax.axis_index("xa")
    my_core = lax.axis_index("core")
    my_row = lax.axis_index("row")
    my_half = lax.axis_index("dp") % 2
    tokens_here, width = inputs.shape
    images = tokens_here // SEQ
    held = images // n_xa
    rows = held * PAD
    hidden = up_weight.shape[1]
    half = hidden // 2

    def swap(value, axis, size, bit=1):
        return lax.ppermute(value, axis, [(place, place ^ bit) for place in range(size)])

    def across(value):
        return swap(value, "xa", n_xa)

    def beside(value):
        return swap(value, "core", n_core)

    def over(value):
        return swap(value, "dp", n_dp)

    def pick(value, place, axis):
        return lax.dynamic_index_in_dim(value, place, axis, keepdims=False)

    def in_order(mine, other, place):
        return jnp.where(place == 0, mine, other), jnp.where(place == 0, other, mine)

    def wide_tokens(value):
        padded = jnp.pad(value.reshape(images, SEQ, -1), ((0, 0), (0, PAD - SEQ), (0, 0)))
        halves = padded.reshape(n_xa, rows, -1)
        mine, theirs = pick(halves, my_x, 0), pick(halves, my_x ^ 1, 0)
        got = across(theirs)
        pair = jnp.concatenate([mine, got], axis=1)
        other = beside(pair)
        left, right = in_order(pair, other, my_core)
        first_left, second_left = in_order(left[:, :width], left[:, width:], my_x)
        first_right, second_right = in_order(right[:, :width], right[:, width:], my_x)
        return jnp.concatenate([first_left, first_right, second_left, second_right], axis=1)

    small = jnp.concatenate(
        [
            out_bias,
            down_bias,
            first_gain,
            first_shift,
            second_gain,
            second_shift,
            query_bias,
            value_bias,
            up_bias,
        ]
    )
    small_far = across(small)
    small_pair = jnp.stack(in_order(small, small_far, my_x))
    small_left, small_right = in_order(small_pair, beside(small_pair), my_core)

    def whole_vector(place):
        cut = slice(width * place, width * (place + 1))
        return jnp.concatenate(
            [small_left[0, cut], small_right[0, cut], small_left[1, cut], small_right[1, cut]]
        )[None]

    out_bias_all, down_bias_all, gain_one, shift_one, gain_two, shift_two = (
        whole_vector(place) for place in range(6)
    )
    query_bias_far = small_far[6 * width : 7 * width]
    value_bias_far = small_far[7 * width : 8 * width]
    up_bias_far = small_far[8 * width :]

    shard = jnp.concatenate([query_weight, key_weight, value_weight, out_weight.T], axis=1)
    near = jnp.zeros((D, 4 * width), BF16)
    far = jnp.zeros((D, 4 * width), BF16)
    for shift in range(n_row):
        piece = shard
        if shift:
            piece = lax.ppermute(
                shard, "row", [(place, (place + shift) % n_row) for place in range(n_row)]
            )
        start = (my_row - shift) % n_row * (D // n_row)
        near = lax.dynamic_update_slice(near, piece, (start, 0))
        far = lax.dynamic_update_slice(far, across(piece), (start, 0))

    def halves(value, axis):
        shape = value.shape[:axis] + (2, half) + value.shape[axis + 1 :]
        both = value.reshape(shape)
        return pick(both, my_half, axis), pick(both, my_half ^ 1, axis)

    up_own, _ = halves(up_weight, 1)
    down_own, _ = halves(down_weight, 0)
    own_shard = jnp.concatenate([up_own, down_own.T], axis=1)
    near_own = lax.all_gather(own_shard, "row", axis=0, tiled=True)
    near_oth = over(near_own)
    far_own = across(near_own)
    far_oth = across(near_oth)
    bias_near_own, bias_near_oth = halves(up_bias[None], 1)
    bias_far_own, bias_far_oth = halves(up_bias_far[None], 1)

    wide_input = wide_tokens(inputs)
    wide_grad = wide_tokens(cotangent)

    zeros = jnp.zeros_like(query_bias)
    bias_near = jnp.concatenate([query_bias, zeros, value_bias])[None]
    bias_far = jnp.concatenate([query_bias_far, zeros, value_bias_far])[None]
    wide_one, qkv = norm_qkv(wide_input, gain_one, shift_one, near, far, bias_near, bias_far)
    attended, probs = attend(qkv)
    mixed = mm_nt(attended[:, :width], near[:, 3 * width :])
    mixed = (mixed + mm_nt(attended[:, width:], far[:, 3 * width :])).astype(BF16)
    middle_sum, wide_two = middle(
        wide_input, mixed, beside(mixed), out_bias_all, gain_two, shift_two
    )
    gate, pre, lowered, lifted_two, up_sums = mlp(
        wide_two,
        wide_grad,
        (near_own, near_oth, far_own, far_oth),
        (bias_near_own, bias_near_oth, bias_far_own, bias_far_oth),
    )

    def block(value, place):
        return value[:, half * place : half * (place + 1)]

    def to_wire(value):
        return value.astype(BF16)

    def wide_add(mine, got):
        return (mine.astype(F32) + got.astype(F32)).astype(BF16)

    lifted_other = beside(lifted_two)
    down_far = to_wire(mm_tn(wide_grad, gate[:, 2 * half :]))
    down_near = wide_add(mm_tn(wide_grad, gate[:, : 2 * half]), across(down_far))
    down_sum = wide_add(block(down_near, 0), over(block(down_near, 1)))
    up_oth = jnp.concatenate(
        [to_wire(mm_tn(wide_two, block(pre, 1))), to_wire(mm_tn(wide_two, block(pre, 3)))], axis=1
    )
    up_got = over(up_oth)
    up_far = wide_add(mm_tn(wide_two, block(pre, 2)), block(up_got, 1))
    up_near = wide_add(mm_tn(wide_two, block(pre, 0)), block(up_got, 0))
    up_sum = wide_add(up_near, across(up_far))
    mlp_piece = lax.psum_scatter(
        jnp.concatenate([up_sum, down_sum], axis=1), "row", scatter_dimension=0, tiled=True
    )
    if n_dp > 2:
        pairs = [[place + bit for place in range(0, n_dp, 2)] for bit in range(2)]
        mlp_piece = lax.psum(mlp_piece.astype(F32), "dp", axis_index_groups=pairs).astype(BF16)
    mlp_other = over(mlp_piece)
    up_first, up_second = in_order(mlp_piece[:, :half], mlp_other[:, :half], my_half)
    down_first, down_second = in_order(mlp_piece[:, half:], mlp_other[:, half:], my_half)
    up_grad = jnp.concatenate([up_first, up_second], axis=1).astype(F32)
    down_grad = jnp.concatenate([down_first, down_second], axis=1).astype(F32).T

    def to_feature_blocks(pair):
        mine, theirs = pick(pair, my_x, 1), pick(pair, my_x ^ 1, 1)
        got = across(theirs)
        first, second = in_order(mine, got, my_x)
        both = jnp.concatenate([first, second]).reshape(images, PAD, width)
        return both[:, :SEQ].reshape(tokens_here, width)

    def feature_split(value):
        return value.reshape(value.shape[0], n_xa, 2, width)

    low_parts = feature_split(lowered)
    branch = pick(low_parts, my_core, 2).astype(F32) + beside(
        pick(low_parts, my_core ^ 1, 2)
    ).astype(F32)
    total = pick(feature_split(middle_sum), my_core, 2) + branch
    total = total + pick(feature_split(down_bias_all), my_core, 2)
    outputs = to_feature_blocks(total.astype(BF16))

    middle_grad, attn_grad, head_grad, turn_sums = turn(
        middle_sum, wide_grad, lifted_two, lifted_other, gain_two, near, far
    )
    dqueries, key_grads, dvalues = attend_back(qkv, probs, head_grad)

    def column_block(value, place):
        return value[:, width * place : width * (place + 1)]

    def four(place):
        out_part = to_wire(mm_tn(attn_grad, column_block(attended, place)))
        return jnp.concatenate(
            [
                to_wire(mm_tn(wide_one, column_block(item, place)))
                for item in (dqueries, key_grads, dvalues)
            ]
            + [out_part],
            axis=1,
        )

    attn_far = four(1)
    attn_sum = wide_add(four(0), across(attn_far))
    attn_piece = lax.psum_scatter(attn_sum, "row", scatter_dimension=0, tiled=True)
    if n_dp > 2:
        attn_weights = lax.psum(attn_piece.astype(F32), "dp")
    else:
        attn_weights = attn_piece.astype(F32) + over(attn_piece).astype(F32)

    lifted_one = mm_nt(dqueries[:, :width], near[:, :width])
    for place, (item, part) in enumerate(
        (item, part) for item in (dqueries, key_grads, dvalues) for part in range(2)
    ):
        if place:
            side = (near, far)[part]
            lifted_one = lifted_one + mm_nt(
                column_block(item, part), column_block(side, place // 2)
            )
    lifted_one = to_wire(lifted_one)
    input_wide, last_sums = last(wide_input, middle_grad, lifted_one, beside(lifted_one), gain_one)
    input_grad = to_feature_blocks(pick(feature_split(input_wide), my_core, 2)).astype(F32)

    def own_features(value):
        return pick(value.reshape(-1, n_xa, 2, width), my_core, 2)

    def column_sum(value):
        return jnp.sum(value.astype(F32), axis=0)

    def by_x(near_sum, far_sum):
        return jnp.stack(in_order(near_sum, far_sum, my_x))

    def everywhere(value):
        value = value + across(value)
        bit = 1
        while bit < n_row:
            value = value + swap(value, "row", n_row, bit)
            bit *= 2
        bit = 1
        while bit < n_dp:
            value = value + swap(value, "dp", n_dp, bit)
            bit *= 2
        return pick(value, my_x, 0)

    query_sums, value_sums = column_sum(dqueries), column_sum(dvalues)
    turn_own = own_features(turn_sums)
    up_sums = up_sums[0].reshape(2, 2, half)
    up_ordered = jnp.concatenate(
        in_order(up_sums[:, 0], up_sums[:, 1], my_half), axis=1
    )
    early = everywhere(
        jnp.concatenate(
            [
                by_x(query_sums[:width], query_sums[width:]),
                by_x(value_sums[:width], value_sums[width:]),
                turn_own[2],
                turn_own[3],
                turn_own[0],
                turn_own[1],
                by_x(up_ordered[0], up_ordered[1]),
            ],
            axis=1,
        )
    )
    last_own = own_features(last_sums)
    late = everywhere(jnp.concatenate([last_own[0], last_own[1]], axis=1))

    def piece_of(value, place):
        return value[width * place : width * (place + 1)]

    return (
        outputs,
        input_grad,
        column_block(attn_weights, 0),
        column_block(attn_weights, 1),
        column_block(attn_weights, 2),
        piece_of(early, 0),
        piece_of(early, 1),
        column_block(attn_weights, 3).T,
        piece_of(early, 2),
        up_grad,
        early[6 * width :],
        down_grad,
        piece_of(early, 3),
        piece_of(late, 0),
        piece_of(late, 1),
        piece_of(early, 4),
        piece_of(early, 5),
    )


def solution(mesh):
    n_dp, n_row, n_col = (mesh.shape[name] for name in ("dp", "row", "col"))
    sizes = (n_dp, n_row, n_col // 2, 2)
    split = Mesh(mesh.devices.reshape(sizes), ("dp", "row", "xa", "core"))
    col = ("xa", "core")
    tokens, rows, cols, vec = P(("dp", "row"), col), P("row", col), P(col, "row"), P(col)
    in_specs = (
        (tokens, rows, rows, rows, vec, vec, cols, vec, rows, vec, cols)
        + (vec,) * 5
        + (tokens,)
    )
    out_specs = (
        (tokens, tokens, rows, rows, rows, vec, vec, cols, vec, rows, vec, cols) + (vec,) * 5
    )
    return jax.shard_map(
        functools.partial(local, sizes),
        mesh=split,
        in_specs=in_specs,
        out_specs=out_specs,
        check_vma=False,
    )
```

```python
import functools
import math

import jax
import jax.numpy as jnp
from jax import lax
from jax.experimental import pallas as pl
from jax.experimental.pallas import tpu as pltpu
from jax.sharding import Mesh, PartitionSpec as P

D = 1024
HD = 64
SEQ = 577
PAD = 592
TM = 296
EPS = 1e-06
F32 = jnp.float32
BF16 = jnp.bfloat16
VMEM_LIMIT = 60 * 1024 * 1024
ROOT_HALF = math.sqrt(0.5)
DENSITY = 1.0 / math.sqrt(2.0 * math.pi)


def mm(a, b):
    return lax.dot_general(a, b, (((1,), (0,)), ((), ())), preferred_element_type=F32)


def mm_nt(a, b):
    return lax.dot_general(a, b, (((1,), (1,)), ((), ())), preferred_element_type=F32)


def mm_tn(a, b):
    return lax.dot_general(a, b, (((0,), (0,)), ((), ())), preferred_element_type=F32)


def row_mean(v):
    return jnp.sum(v, axis=1, keepdims=True) * (1.0 / D)


def col_sum(v):
    return jnp.sum(v, axis=0, keepdims=True)


def stats(rows):
    middle = row_mean(rows)
    spread = row_mean(rows * rows) - middle * middle
    return middle, lax.rsqrt(spread + EPS)


def params(n):
    return pltpu.CompilerParams(
        dimension_semantics=("arbitrary",) * n, vmem_limit_bytes=VMEM_LIMIT
    )


def cost(flops, moved, exps=0):
    return pl.CostEstimate(flops=int(flops), bytes_accessed=int(moved), transcendentals=int(exps))


def like(shape, dtype):
    return jax.ShapeDtypeStruct(shape, dtype)


def row_spec(cols):
    return pl.BlockSpec((TM, cols), lambda i, *_: (i, 0))


def fixed(shape):
    return pl.BlockSpec(shape, lambda *_: (0,) * len(shape))


def held_once(shape):
    return pl.BlockSpec(shape, lambda *_: (0,) * len(shape), pipeline_mode=pl.Buffered(1))


def add_up(ref, first, part):
    @pl.when(first)
    def _():
        ref[...] = part

    @pl.when(jnp.logical_not(first))
    def _():
        ref[...] += part


def norm_qkv_kernel(x_ref, gain_ref, shift_ref, bias_ref, a_ref, b_ref, c_ref, d_ref, n_ref, o_ref, w_ref):
    wide = a_ref.shape[1]
    three = wide // 4 * 3

    @pl.when(pl.program_id(0) == 0)
    def _():
        for place, ref in enumerate((a_ref, b_ref, c_ref, d_ref)):
            w_ref[:, three * place : three * (place + 1)] = ref[:, :three]
            low = 4 * three + (wide - three) * place
            w_ref[:, low : low + wide - three] = ref[:, three:]

    x = x_ref[...].astype(F32)
    middle, scaled = stats(x)
    n = (((x - middle) * scaled) * gain_ref[...] + shift_ref[...]).astype(BF16)
    n_ref[...] = n
    o_ref[...] = (mm(n, w_ref[:, : 4 * three]) + bias_ref[...]).astype(BF16)


def norm_qkv(x, gain, shift, bias, blocks):
    rows = x.shape[0]
    wide = blocks[0].shape[1]
    out = 3 * wide
    return pl.pallas_call(
        norm_qkv_kernel,
        grid=(rows // TM,),
        name="norm_qkv",
        in_specs=[row_spec(D), fixed((1, D)), fixed((1, D)), fixed((1, out))]
        + [held_once((D, wide))] * 4,
        out_specs=[row_spec(D), row_spec(out), held_once((D, 4 * wide))],
        out_shape=[like((rows, D), BF16), like((rows, out), BF16), like((D, 4 * wide), BF16)],
        compiler_params=params(1),
        cost_estimate=cost(2 * rows * D * out, 16 * rows * D),
    )(x, gain, shift, bias, *blocks)


def attend_kernel(qkv_ref, o_ref, p_ref):
    live = lax.broadcasted_iota(jnp.int32, (1, PAD), 1) < SEQ
    step = 2 * HD
    for h in range(2):
        q, k, v = (qkv_ref[:, step * w + HD * h : step * w + HD * (h + 1)] for w in range(3))
        s = mm_nt(q * jnp.asarray(0.125, BF16), k)
        s = jnp.where(live, s, -1e30)
        e = jnp.exp(s - jnp.max(s, axis=1, keepdims=True))
        p = (e * (1.0 / jnp.sum(e, axis=1, keepdims=True))).astype(BF16)
        p_ref[h] = p
        o_ref[:, HD * h : HD * (h + 1)] = mm(p, v).astype(BF16)


def attend(qkv):
    rows, cols = qkv.shape
    pairs = cols // (6 * HD)
    held = rows // PAD
    return pl.pallas_call(
        attend_kernel,
        grid=(pairs, held),
        name="attend",
        in_specs=[pl.BlockSpec((PAD, 6 * HD), lambda p, i: (i, p))],
        out_specs=[
            pl.BlockSpec((PAD, 2 * HD), lambda p, i: (i, p)),
            pl.BlockSpec((None, 2, PAD, PAD), lambda p, i: (i, p, 0, 0)),
        ],
        out_shape=[like((rows, cols // 3), BF16), like((held, 2 * pairs, PAD, PAD), BF16)],
        compiler_params=params(2),
        cost_estimate=cost(16 * rows * PAD * cols, 40 * rows * D, 4 * rows * PAD * pairs),
    )(qkv)


def attend_back_kernel(qkv_ref, p_ref, g_ref, d_ref, sum_ref):
    step = 2 * HD
    for h in range(2):
        q, k, v = (qkv_ref[:, step * w + HD * h : step * w + HD * (h + 1)] for w in range(3))
        g = g_ref[:, HD * h : HD * (h + 1)]
        pb = p_ref[h]
        p = pb.astype(F32)
        dp = mm_nt(g, v)
        z = jnp.sum(p * dp, axis=1, keepdims=True)
        ds = (p * (dp - z)).astype(BF16)
        parts = (mm(ds, k) * 0.125, mm_tn(ds, q) * 0.125, mm_tn(pb, g))
        for w, part in enumerate(parts):
            d_ref[:, step * w + HD * h : step * w + HD * (h + 1)] = part.astype(BF16)
    add_up(sum_ref, pl.program_id(1) == 0, col_sum(d_ref[...].astype(F32)))


def attend_back(qkv, probs, grads):
    rows, cols = qkv.shape
    pairs = cols // (6 * HD)
    held = rows // PAD
    three = pl.BlockSpec((PAD, 6 * HD), lambda p, i: (i, p))
    return pl.pallas_call(
        attend_back_kernel,
        grid=(pairs, held),
        name="attend_back",
        in_specs=[
            three,
            pl.BlockSpec((None, 2, PAD, PAD), lambda p, i: (i, p, 0, 0)),
            pl.BlockSpec((PAD, 2 * HD), lambda p, i: (i, p)),
        ],
        out_specs=[three, pl.BlockSpec((1, 6 * HD), lambda p, i: (0, p))],
        out_shape=[like((rows, cols), BF16), like((1, cols), F32)],
        compiler_params=params(2),
        cost_estimate=cost(20 * rows * PAD * cols, 50 * rows * D),
    )(qkv, probs, grads)


def middle_kernel(x_ref, a_ref, b_ref, bias_ref, gain_ref, shift_ref, h_ref, n_ref):
    h = x_ref[...].astype(F32) + (a_ref[...].astype(F32) + b_ref[...].astype(F32)) + bias_ref[...]
    h_ref[...] = h
    middle, scaled = stats(h)
    n_ref[...] = (((h - middle) * scaled) * gain_ref[...] + shift_ref[...]).astype(BF16)


def middle(x, a, b, bias, gain, shift):
    rows = x.shape[0]
    vec = fixed((1, D))
    return pl.pallas_call(
        middle_kernel,
        grid=(rows // TM,),
        name="middle",
        in_specs=[row_spec(D)] * 3 + [vec] * 3,
        out_specs=[row_spec(D)] * 2,
        out_shape=[like((rows, D), F32), like((rows, D), BF16)],
        compiler_params=params(1),
        cost_estimate=cost(20 * rows * D, 12 * rows * D),
    )(x, a, b, bias, gain, shift)


def mlp_kernel(tiles, place_ref, n_ref, dy_ref, *refs):
    ups, downs, biases = refs[0:4], refs[4:8], refs[8:12]
    g_ref, du_ref, mine_ref, theirs_ref, lift_ref, bsum_ref, low_acc, lift_acc = refs[12:]
    j = pl.program_id(0)

    @pl.when(j == 0)
    def _():
        low_acc[...] = jnp.zeros_like(low_acc)
        lift_acc[...] = jnp.zeros_like(lift_acc)

    def step(up_ref, down_ref, bias_ref):
        u = mm(n_ref[...], up_ref[...]) + bias_ref[...]
        cdf = 0.5 * (1.0 + lax.erf(u * ROOT_HALF))
        g = (u * cdf).astype(BF16)
        slope = cdf + u * (jnp.exp(-0.5 * u * u) * DENSITY)
        g_ref[...] = g
        du = (mm(dy_ref[...], down_ref[...]) * slope).astype(BF16)
        du_ref[...] = du
        bsum_ref[...] = col_sum(du.astype(F32))
        low_acc[...] += mm_nt(g, down_ref[...])
        lift_acc[...] += mm_nt(du, up_ref[...])

    for block in range(4):

        @pl.when((j >= block * tiles) & (j < (block + 1) * tiles))
        def _(block=block):
            step(ups[block], downs[block], biases[block])

    @pl.when(j == 4 * tiles - 1)
    def _():
        lift_ref[...] = lift_acc[...].astype(BF16)
        width = D // 4
        core = place_ref[0]
        for far in range(2):
            low = pl.multiple_of((2 * far + core) * width, width)
            other = pl.multiple_of((2 * far + 1 - core) * width, width)
            mine_ref[:, far * width : (far + 1) * width] = low_acc[:, pl.ds(low, width)]
            theirs_ref[:, far * width : (far + 1) * width] = low_acc[:, pl.ds(other, width)].astype(
                BF16
            )


def mlp(place, n2, dy, ups, downs, biases, half, tn=256):
    rows = n2.shape[0]
    tiles = half // tn
    hid = 4 * half
    whole = held_once((rows, D))

    def part(height, block, start):
        return pl.BlockSpec(
            (height, tn), lambda j, *_: (0, jnp.clip(j - block * tiles, 0, tiles - 1) + start // tn)
        )

    tile = pl.BlockSpec((rows, tn), lambda j, *_: (0, j))
    return pl.pallas_call(
        functools.partial(mlp_kernel, tiles),
        name="mlp",
        grid_spec=pltpu.PrefetchScalarGridSpec(
            num_scalar_prefetch=1,
            grid=(4 * tiles,),
            in_specs=[whole, whole]
            + [part(D, block, item[1]) for block, item in enumerate(ups)]
            + [part(D, block, item[1]) for block, item in enumerate(downs)]
            + [part(1, block, 0) for block in range(4)],
            out_specs=[
                tile,
                tile,
                held_once((rows, D // 2)),
                held_once((rows, D // 2)),
                whole,
                pl.BlockSpec((1, tn), lambda j, *_: (0, j)),
            ],
            scratch_shapes=[pltpu.VMEM((rows, D), F32), pltpu.VMEM((rows, D), F32)],
        ),
        out_shape=[
            like((rows, hid), BF16),
            like((rows, hid), BF16),
            like((rows, D // 2), F32),
            like((rows, D // 2), BF16),
            like((rows, D), BF16),
            like((1, hid), F32),
        ],
        compiler_params=params(1),
        cost_estimate=cost(8 * rows * D * hid, 24 * rows * D, 2 * rows * hid),
    )(place, n2, dy, *[item[0] for item in ups], *[item[0] for item in downs], *biases)


def finish_kernel(place_ref, h_ref, a_ref, b_ref, bias_ref, mine_ref, theirs_ref):
    value = h_ref[...] + (a_ref[...] + b_ref[...].astype(F32)) + bias_ref[...]
    value = value.astype(BF16)

    @pl.when(pl.program_id(0) == 0)
    def _():
        theirs_ref[...] = value

    @pl.when(pl.program_id(0) == 1)
    def _():
        mine_ref[...] = value


def finish(place, h, a, b, bias):
    rows = h.shape[0]
    width = D // 4
    n = rows // TM

    def block(k, s):
        return jnp.where(k == 0, 1 - s[1], s[1])

    return pl.pallas_call(
        finish_kernel,
        name="finish",
        grid_spec=pltpu.PrefetchScalarGridSpec(
            num_scalar_prefetch=1,
            grid=(2, n),
            in_specs=[
                pl.BlockSpec((TM, width), lambda k, i, s: (i, 2 * block(k, s) + s[0])),
                pl.BlockSpec((TM, width), lambda k, i, s: (i, block(k, s))),
                pl.BlockSpec((TM, width), lambda k, i, s: (i, block(k, s))),
                pl.BlockSpec((1, width), lambda k, i, s: (0, 2 * block(k, s) + s[0])),
            ],
            out_specs=[
                pl.BlockSpec((TM, width), lambda k, i, s: (jnp.where(k == 0, 0, i), 0)),
                pl.BlockSpec((TM, width), lambda k, i, s: (jnp.where(k == 0, i, n - 1), 0)),
            ],
        ),
        out_shape=[like((rows, width), BF16), like((rows, width), BF16)],
        compiler_params=params(2),
        cost_estimate=cost(2 * rows * D, 6 * rows * D),
    )(place, h, a, b, bias)


def turn_kernel(h_ref, dy_ref, a_ref, b_ref, gain_ref, w_ref, dh_ref, da_ref, do_ref, sums_ref):
    h = h_ref[...]
    middle, scaled = stats(h)
    c = (h - middle) * scaled
    dn = a_ref[...].astype(F32) + b_ref[...].astype(F32)
    dy = dy_ref[...].astype(F32)
    e = dn * gain_ref[...]
    dh = dy + scaled * (e - row_mean(e) - c * row_mean(e * c))
    dh_ref[...] = dh
    da = dh.astype(BF16)
    da_ref[...] = da
    do_ref[...] = mm(da, w_ref[...]).astype(BF16)
    part = jnp.concatenate(
        [col_sum(dn * c), col_sum(dn), col_sum(da.astype(F32)), col_sum(dy)], axis=0
    )
    add_up(sums_ref, pl.program_id(0) == 0, part)


def turn(h, dy, a, b, gain, weights):
    rows = h.shape[0]
    wide = weights.shape[1] // 4
    return pl.pallas_call(
        turn_kernel,
        grid=(rows // TM,),
        name="turn",
        in_specs=[row_spec(D)] * 4
        + [fixed((1, D)), pl.BlockSpec((D, wide), lambda i: (0, 3), pipeline_mode=pl.Buffered(1))],
        out_specs=[row_spec(D), row_spec(D), row_spec(wide), fixed((4, D))],
        out_shape=[
            like((rows, D), F32),
            like((rows, D), BF16),
            like((rows, wide), BF16),
            like((4, D), F32),
        ],
        compiler_params=params(1),
        cost_estimate=cost(2 * rows * D * wide, 18 * rows * D),
    )(h, dy, a, b, gain, weights)


def last_kernel(place_ref, x_ref, dh_ref, a_ref, b_ref, gain_ref, mine_ref, theirs_ref, sums_ref, held):
    x = x_ref[...].astype(F32)
    middle, scaled = stats(x)
    c = (x - middle) * scaled
    dn = a_ref[...].astype(F32) + b_ref[...].astype(F32)
    e = dn * gain_ref[...]
    held[...] = dh_ref[...] + scaled * (e - row_mean(e) - c * row_mean(e * c))
    width = D // 4
    core, side = place_ref[0], place_ref[1]
    mine_ref[...] = held[:, pl.ds(pl.multiple_of((2 * side + core) * width, width), width)]
    theirs_ref[...] = held[
        :, pl.ds(pl.multiple_of((2 * (1 - side) + core) * width, width), width)
    ].astype(BF16)
    add_up(
        sums_ref,
        pl.program_id(0) == 0,
        jnp.concatenate([col_sum(dn * c), col_sum(dn)], axis=0),
    )


def last(place, x, dh, a, b, gain):
    rows = x.shape[0]
    width = D // 4
    return pl.pallas_call(
        last_kernel,
        name="last",
        grid_spec=pltpu.PrefetchScalarGridSpec(
            num_scalar_prefetch=1,
            grid=(rows // TM,),
            in_specs=[row_spec(D)] * 4 + [fixed((1, D))],
            out_specs=[row_spec(width), row_spec(width), fixed((2, D))],
            scratch_shapes=[pltpu.VMEM((TM, D), F32)],
        ),
        out_shape=[like((rows, width), F32), like((rows, width), BF16), like((2, D), F32)],
        compiler_params=params(1),
        cost_estimate=cost(20 * rows * D, 12 * rows * D),
    )(place, x, dh, a, b, gain)


def local(
    sizes,
    inputs,
    query_weight,
    key_weight,
    value_weight,
    query_bias,
    value_bias,
    out_weight,
    out_bias,
    up_weight,
    up_bias,
    down_weight,
    down_bias,
    first_gain,
    first_shift,
    second_gain,
    second_shift,
    cotangent,
):
    n_dp, n_row, n_xa, n_core = sizes
    my_x = lax.axis_index("xa")
    my_core = lax.axis_index("core")
    my_row = lax.axis_index("row")
    my_half = lax.axis_index("dp") % 2
    place = jnp.stack([my_core, my_x]).astype(jnp.int32)
    tokens_here, width = inputs.shape
    images = tokens_here // SEQ
    held = images // n_xa
    rows = held * PAD
    hidden = up_weight.shape[1]
    half = hidden // 2
    heads_half = width // 2
    three = 3 * heads_half

    def swap(value, axis, size, bit=1):
        return lax.ppermute(value, axis, [(at, at ^ bit) for at in range(size)])

    def across(value):
        return swap(value, "xa", n_xa)

    def beside(value):
        return swap(value, "core", n_core)

    def over(value):
        return swap(value, "dp", n_dp)

    def pick(value, at, axis):
        return lax.dynamic_index_in_dim(value, at, axis, keepdims=False)

    def in_order(mine, other, at):
        return jnp.where(at == 0, mine, other), jnp.where(at == 0, other, mine)

    def after(value, *others):
        return lax.optimization_barrier((value, *others))[0]

    def halves(value, axis):
        cut = value.shape[axis] // 2
        both = value.reshape(value.shape[:axis] + (2, cut) + value.shape[axis + 1 :])
        return pick(both, my_half, axis), pick(both, my_half ^ 1, axis)

    attn_shard = jnp.concatenate(
        [halves(item, 1)[0] for item in (query_weight, key_weight, value_weight)]
        + [halves(out_weight, 0)[0].T],
        axis=1,
    )
    pieces = [attn_shard] + [
        lax.ppermute(attn_shard, "row", [(at, (at + shift) % n_row) for at in range(n_row)])
        for shift in range(1, n_row)
    ]

    count = held * SEQ

    def send_tokens(value):
        theirs = lax.dynamic_slice_in_dim(value, (my_x ^ 1) * count, count, 0)
        return across(theirs)

    def wide_tokens(value, got):
        mine = lax.dynamic_slice_in_dim(value, my_x * count, count, 0)
        pair = jnp.concatenate([mine, got], axis=1)
        other = beside(pair)
        left, right = in_order(pair, other, my_core)
        first_left, second_left = in_order(left[:, :width], left[:, width:], my_x)
        first_right, second_right = in_order(right[:, :width], right[:, width:], my_x)
        whole = jnp.concatenate([first_left, first_right, second_left, second_right], axis=1)
        whole = jnp.pad(whole.reshape(held, SEQ, D), ((0, 0), (0, PAD - SEQ), (0, 0)))
        return whole.reshape(rows, D)

    wide_input = wide_tokens(inputs, send_tokens(inputs))

    small = jnp.concatenate(
        [
            out_bias,
            down_bias,
            first_gain,
            first_shift,
            second_gain,
            second_shift,
            query_bias,
            value_bias,
            up_bias,
        ]
    )
    small_far = across(small)
    small_pair = jnp.stack(in_order(small, small_far, my_x))
    small_left, small_right = in_order(small_pair, beside(small_pair), my_core)

    def whole_vector(at):
        cut = slice(width * at, width * (at + 1))
        return jnp.concatenate(
            [small_left[0, cut], small_right[0, cut], small_left[1, cut], small_right[1, cut]]
        )[None]

    out_bias_all, down_bias_all, gain_one, shift_one, gain_two, shift_two = (
        whole_vector(at) for at in range(6)
    )

    attn_own = jnp.zeros((D, 4 * heads_half), BF16)
    for shift, piece in enumerate(pieces):
        start = (my_row - shift) % n_row * (D // n_row)
        attn_own = lax.dynamic_update_slice(attn_own, piece, (start, 0))
    attn_oth, attn_far = over(attn_own), across(attn_own)
    cut = 2 * heads_half
    attn_far_oth = jnp.concatenate([over(attn_far[:, :cut]), across(attn_oth[:, cut:])], axis=1)

    down_own = halves(down_weight, 0)[0].T
    mlp_shard = jnp.concatenate([halves(up_weight, 1)[0], down_own], axis=1)
    mlp_shard = after(mlp_shard, attn_own)
    mlp_own = lax.all_gather(mlp_shard, "row", axis=0, tiled=True)
    mlp_oth, mlp_far = over(mlp_own), across(mlp_own)
    up_far_oth, down_far_oth = over(mlp_far[:, :half]), across(mlp_oth[:, half:])
    grad_here = after(cotangent, attn_far_oth)
    wide_grad = wide_tokens(grad_here, send_tokens(grad_here))

    def four(near_vector, far_vector):
        near_own, near_oth = halves(near_vector, 0)
        far_own, far_oth = halves(far_vector, 0)
        return near_own, far_own, near_oth, far_oth

    zeros = jnp.zeros((heads_half,), F32)
    query_parts = four(query_bias, small_far[6 * width : 7 * width])
    value_parts = four(value_bias, small_far[7 * width : 8 * width])
    qkv_bias = jnp.concatenate(
        [item for q, v in zip(query_parts, value_parts) for item in (q, zeros, v)]
    )[None]
    up_biases = [item[None] for item in four(up_bias, small_far[8 * width :])]

    wide_one, qkv, attn_weights = norm_qkv(
        wide_input, gain_one, shift_one, qkv_bias, (attn_own, attn_far, attn_oth, attn_far_oth)
    )
    attended, probs = attend(qkv)
    mixed = mm_nt(attended, attn_weights[:, 4 * three :]).astype(BF16)
    middle_sum, wide_two = middle(
        wide_input, mixed, beside(mixed), out_bias_all, gain_two, shift_two
    )
    gate, pre, low_mine, low_theirs, lifted_two, up_sums = mlp(
        place,
        wide_two,
        wide_grad,
        ((mlp_own, 0), (mlp_far, 0), (mlp_oth, 0), (up_far_oth, 0)),
        ((mlp_own, half), (mlp_far, half), (mlp_oth, half), (down_far_oth, 0)),
        up_biases,
        half,
    )

    def wide_add(mine, got):
        return (mine.astype(F32) + got.astype(F32)).astype(BF16)

    def same_half(value):
        if n_dp == 2:
            return value
        groups = [[at + bit for at in range(0, n_dp, 2)] for bit in range(2)]
        return lax.psum(value.astype(F32), "dp", axis_index_groups=groups).astype(BF16)

    def scatter(value):
        return lax.psum_scatter(value, "row", scatter_dimension=0, tiled=True)

    lifted_other = beside(lifted_two)
    down_all = mm_tn(wide_grad, gate).astype(BF16)
    down_piece = scatter(down_all)
    up_oth_got = over(mm_tn(wide_two, pre[:, 2 * half :]).astype(BF16))

    middle_grad, attn_grad, head_grad, turn_sums = turn(
        middle_sum, wide_grad, lifted_two, lifted_other, gain_two, attn_weights
    )
    dqkv, qkv_sums = attend_back(qkv, probs, head_grad)

    def feature_split(value):
        return value.reshape(value.shape[0], n_xa, 2, width)

    def to_feature_blocks(mine, got, dtype):
        first, second = in_order(mine.astype(dtype), got.astype(dtype), my_x)
        both = jnp.concatenate([first, second]).reshape(images, PAD, width)
        return both[:, :SEQ].reshape(tokens_here, width)

    out_mine, out_theirs = finish(place, middle_sum, low_mine, beside(low_theirs), down_bias_all)
    outputs = to_feature_blocks(out_mine, across(out_theirs), BF16)

    far_oth_got = over(mm_tn(wide_one, dqkv[:, 3 * three :]).astype(BF16))
    near_oth_got = over(mm_tn(wide_one, dqkv[:, 2 * three : 3 * three]).astype(BF16))
    lifted_one = mm_nt(dqkv, attn_weights[:, : 4 * three]).astype(BF16)
    lifted_one_other = beside(lifted_one)
    far_own = wide_add(mm_tn(wide_one, dqkv[:, three : 2 * three]), far_oth_got)
    far_own_got = across(far_own)
    near_own = wide_add(mm_tn(wide_one, dqkv[:, :three]), near_oth_got)
    qkv_piece = same_half(scatter(wide_add(near_own, far_own_got)))
    qkv_other = over(qkv_piece)

    input_mine, input_theirs, last_sums = last(
        place, wide_input, middle_grad, lifted_one, lifted_one_other, gain_one
    )
    input_grad = to_feature_blocks(input_mine, across(input_theirs), F32)

    out_all = mm_tn(attn_grad, attended).astype(BF16)
    out_got = over(out_all[:, 2 * heads_half :])
    out_own = wide_add(out_all[:, : 2 * heads_half], out_got)
    up_own = wide_add(mm_tn(wide_two, pre[:, : 2 * half]), up_oth_got)
    far_part = jnp.concatenate([up_own[:, half:], out_own[:, heads_half:]], axis=1)
    near_part = jnp.concatenate([up_own[:, :half], out_own[:, :heads_half]], axis=1)
    up_piece = same_half(scatter(wide_add(near_part, across(far_part))))
    up_other = over(up_piece)

    down_x = wide_add(
        jnp.concatenate([down_piece[:, :half], down_piece[:, 2 * half : 3 * half]], axis=1),
        across(
            jnp.concatenate([down_piece[:, half : 2 * half], down_piece[:, 3 * half :]], axis=1)
        ),
    )
    down_got = over(down_x)
    down_total = down_x.astype(F32) + jnp.concatenate(
        [down_got[:, half:], down_got[:, :half]], axis=1
    ).astype(F32)
    if n_dp > 2:
        groups = [[at + bit for at in range(0, n_dp, 2)] for bit in range(2)]
        down_total = lax.psum(down_total, "dp", axis_index_groups=groups)
    down_first, down_second = in_order(down_total[:, :half], down_total[:, half:], my_half)
    down_grad = jnp.concatenate([down_first, down_second], axis=1).T

    def both_halves(mine, other, low, high):
        first, second = in_order(mine[:, low:high], other[:, low:high], my_half)
        return jnp.concatenate([first, second], axis=1).astype(F32)

    up_grad = both_halves(up_piece, up_other, 0, half)
    out_grad = both_halves(up_piece, up_other, half, half + heads_half).T
    query_grad, key_grad, value_grad = (
        both_halves(qkv_piece, qkv_other, heads_half * at, heads_half * (at + 1))
        for at in range(3)
    )

    def own_features(value):
        return pick(value.reshape(-1, n_xa, 2, width), my_core, 2)

    def by_x(parts):
        near_own, far_own, near_oth, far_oth = parts
        near = jnp.concatenate(in_order(near_own, near_oth, my_half))
        far = jnp.concatenate(in_order(far_own, far_oth, my_half))
        return jnp.stack(in_order(near, far, my_x))

    def everywhere(value):
        value = value + across(value)
        bit = 1
        while bit < n_row:
            value = value + swap(value, "row", n_row, bit)
            bit *= 2
        bit = 1
        while bit < n_dp:
            value = value + swap(value, "dp", n_dp, bit)
            bit *= 2
        return pick(value, my_x, 0)

    turn_own = own_features(turn_sums)
    qkv_parts = qkv_sums.reshape(4, 3, heads_half)
    early = everywhere(
        jnp.concatenate(
            [
                by_x(qkv_parts[:, 0]),
                by_x(qkv_parts[:, 2]),
                turn_own[2],
                turn_own[3],
                turn_own[0],
                turn_own[1],
                by_x(up_sums.reshape(4, half)),
            ],
            axis=1,
        )
    )
    last_own = own_features(last_sums)
    late = everywhere(jnp.concatenate([last_own[0], last_own[1]], axis=1))

    def piece_of(value, at):
        return value[width * at : width * (at + 1)]

    return (
        outputs,
        input_grad,
        query_grad,
        key_grad,
        value_grad,
        piece_of(early, 0),
        piece_of(early, 1),
        out_grad,
        piece_of(early, 2),
        up_grad,
        early[6 * width :],
        down_grad,
        piece_of(early, 3),
        piece_of(late, 0),
        piece_of(late, 1),
        piece_of(early, 4),
        piece_of(early, 5),
    )


def solution(mesh):
    n_dp, n_row, n_col = (mesh.shape[name] for name in ("dp", "row", "col"))
    sizes = (n_dp, n_row, n_col // 2, 2)
    split = Mesh(mesh.devices.reshape(sizes), ("dp", "row", "xa", "core"))
    col = ("xa", "core")
    tokens, rows, cols, vec = P(("dp", "row"), col), P("row", col), P(col, "row"), P(col)
    in_specs = (
        (tokens, rows, rows, rows, vec, vec, cols, vec, rows, vec, cols)
        + (vec,) * 5
        + (tokens,)
    )
    out_specs = (
        (tokens, tokens, rows, rows, rows, vec, vec, cols, vec, rows, vec, cols) + (vec,) * 5
    )
    return jax.shard_map(
        functools.partial(local, sizes),
        mesh=split,
        in_specs=in_specs,
        out_specs=out_specs,
        check_vma=False,
    )
```

```python
import functools
import math

import jax
import jax.numpy as jnp
from jax import lax
from jax.experimental import pallas as pl
from jax.experimental.pallas import tpu as pltpu
from jax.sharding import Mesh, PartitionSpec as P

D = 1024
HD = 64
SEQ = 577
PAD = 592
TM = 296
EPS = 1e-06
F32 = jnp.float32
BF16 = jnp.bfloat16
VMEM_LIMIT = 60 * 1024 * 1024
ROOT_HALF = math.sqrt(0.5)
DENSITY = 1.0 / math.sqrt(2.0 * math.pi)


def mm(a, b):
    return lax.dot_general(a, b, (((1,), (0,)), ((), ())), preferred_element_type=F32)


def mm_nt(a, b):
    return lax.dot_general(a, b, (((1,), (1,)), ((), ())), preferred_element_type=F32)


def mm_tn(a, b):
    return lax.dot_general(a, b, (((0,), (0,)), ((), ())), preferred_element_type=F32)


def row_mean(v):
    return jnp.sum(v, axis=1, keepdims=True) * (1.0 / D)


def col_sum(v):
    return jnp.sum(v, axis=0, keepdims=True)


def stats(rows):
    middle = row_mean(rows)
    spread = row_mean(rows * rows) - middle * middle
    return middle, lax.rsqrt(spread + EPS)


def params(n):
    return pltpu.CompilerParams(
        dimension_semantics=("arbitrary",) * n, vmem_limit_bytes=VMEM_LIMIT
    )


def cost(flops, moved, exps=0):
    return pl.CostEstimate(flops=int(flops), bytes_accessed=int(moved), transcendentals=int(exps))


def like(shape, dtype):
    return jax.ShapeDtypeStruct(shape, dtype)


def row_spec(cols):
    return pl.BlockSpec((TM, cols), lambda i, *_: (i, 0))


def fixed(shape):
    return pl.BlockSpec(shape, lambda *_: (0,) * len(shape))


def held_once(shape):
    return pl.BlockSpec(shape, lambda *_: (0,) * len(shape), pipeline_mode=pl.Buffered(1))


def add_up(ref, first, part):
    @pl.when(first)
    def _():
        ref[...] = part

    @pl.when(jnp.logical_not(first))
    def _():
        ref[...] += part


def norm_qkv_kernel(x_ref, gain_ref, shift_ref, bias_ref, a_ref, b_ref, c_ref, d_ref, n_ref, o_ref, w_ref):
    wide = a_ref.shape[1]
    three = wide // 4 * 3

    @pl.when(pl.program_id(0) == 0)
    def _():
        for place, ref in enumerate((a_ref, b_ref, c_ref, d_ref)):
            w_ref[:, three * place : three * (place + 1)] = ref[:, :three]
            low = 4 * three + (wide - three) * place
            w_ref[:, low : low + wide - three] = ref[:, three:]

    x = x_ref[...].astype(F32)
    middle, scaled = stats(x)
    n = (((x - middle) * scaled) * gain_ref[...] + shift_ref[...]).astype(BF16)
    n_ref[...] = n
    o_ref[...] = (mm(n, w_ref[:, : 4 * three]) + bias_ref[...]).astype(BF16)


def norm_qkv(x, gain, shift, bias, blocks):
    rows = x.shape[0]
    wide = blocks[0].shape[1]
    out = 3 * wide
    return pl.pallas_call(
        norm_qkv_kernel,
        grid=(rows // TM,),
        name="norm_qkv",
        in_specs=[row_spec(D), fixed((1, D)), fixed((1, D)), fixed((1, out))]
        + [held_once((D, wide))] * 4,
        out_specs=[row_spec(D), row_spec(out), held_once((D, 4 * wide))],
        out_shape=[like((rows, D), BF16), like((rows, out), BF16), like((D, 4 * wide), BF16)],
        compiler_params=params(1),
        cost_estimate=cost(2 * rows * D * out, 16 * rows * D),
    )(x, gain, shift, bias, *blocks)


def attend_kernel(qkv_ref, o_ref, p_ref):
    live = lax.broadcasted_iota(jnp.int32, (1, PAD), 1) < SEQ
    step = 2 * HD
    for h in range(2):
        q, k, v = (qkv_ref[:, step * w + HD * h : step * w + HD * (h + 1)] for w in range(3))
        s = mm_nt(q * jnp.asarray(0.125, BF16), k)
        s = jnp.where(live, s, -1e30)
        e = jnp.exp(s - jnp.max(s, axis=1, keepdims=True))
        p = (e * (1.0 / jnp.sum(e, axis=1, keepdims=True))).astype(BF16)
        p_ref[h] = p
        o_ref[:, HD * h : HD * (h + 1)] = mm(p, v).astype(BF16)


def attend(qkv):
    rows, cols = qkv.shape
    pairs = cols // (6 * HD)
    held = rows // PAD
    return pl.pallas_call(
        attend_kernel,
        grid=(pairs, held),
        name="attend",
        in_specs=[pl.BlockSpec((PAD, 6 * HD), lambda p, i: (i, p))],
        out_specs=[
            pl.BlockSpec((PAD, 2 * HD), lambda p, i: (i, p)),
            pl.BlockSpec((None, 2, PAD, PAD), lambda p, i: (i, p, 0, 0)),
        ],
        out_shape=[like((rows, cols // 3), BF16), like((held, 2 * pairs, PAD, PAD), BF16)],
        compiler_params=params(2),
        cost_estimate=cost(16 * rows * PAD * cols, 40 * rows * D, 4 * rows * PAD * pairs),
    )(qkv)


def attend_back_kernel(qkv_ref, p_ref, g_ref, d_ref, sum_ref):
    step = 2 * HD
    for h in range(2):
        q, k, v = (qkv_ref[:, step * w + HD * h : step * w + HD * (h + 1)] for w in range(3))
        g = g_ref[:, HD * h : HD * (h + 1)]
        pb = p_ref[h]
        p = pb.astype(F32)
        dp = mm_nt(g, v)
        z = jnp.sum(p * dp, axis=1, keepdims=True)
        ds = (p * (dp - z)).astype(BF16)
        parts = (mm(ds, k) * 0.125, mm_tn(ds, q) * 0.125, mm_tn(pb, g))
        for w, part in enumerate(parts):
            d_ref[:, step * w + HD * h : step * w + HD * (h + 1)] = part.astype(BF16)
    add_up(sum_ref, pl.program_id(1) == 0, col_sum(d_ref[...].astype(F32)))


def attend_back(qkv, probs, grads):
    rows, cols = qkv.shape
    pairs = cols // (6 * HD)
    held = rows // PAD
    three = pl.BlockSpec((PAD, 6 * HD), lambda p, i: (i, p))
    return pl.pallas_call(
        attend_back_kernel,
        grid=(pairs, held),
        name="attend_back",
        in_specs=[
            three,
            pl.BlockSpec((None, 2, PAD, PAD), lambda p, i: (i, p, 0, 0)),
            pl.BlockSpec((PAD, 2 * HD), lambda p, i: (i, p)),
        ],
        out_specs=[three, pl.BlockSpec((1, 6 * HD), lambda p, i: (0, p))],
        out_shape=[like((rows, cols), BF16), like((1, cols), F32)],
        compiler_params=params(2),
        cost_estimate=cost(20 * rows * PAD * cols, 50 * rows * D),
    )(qkv, probs, grads)


def middle_kernel(x_ref, a_ref, b_ref, bias_ref, gain_ref, shift_ref, h_ref, n_ref):
    h = x_ref[...].astype(F32) + (a_ref[...].astype(F32) + b_ref[...].astype(F32)) + bias_ref[...]
    h_ref[...] = h
    middle, scaled = stats(h)
    n_ref[...] = (((h - middle) * scaled) * gain_ref[...] + shift_ref[...]).astype(BF16)


def middle(x, a, b, bias, gain, shift):
    rows = x.shape[0]
    vec = fixed((1, D))
    return pl.pallas_call(
        middle_kernel,
        grid=(rows // TM,),
        name="middle",
        in_specs=[row_spec(D)] * 3 + [vec] * 3,
        out_specs=[row_spec(D)] * 2,
        out_shape=[like((rows, D), F32), like((rows, D), BF16)],
        compiler_params=params(1),
        cost_estimate=cost(20 * rows * D, 12 * rows * D),
    )(x, a, b, bias, gain, shift)


def mlp_kernel(plan, place_ref, n_ref, dy_ref, bias_ref, *refs):
    n_arrays = 1 + max(index for index, _ in plan)
    ups, downs = refs[:n_arrays], refs[n_arrays : 2 * n_arrays]
    g_ref, du_ref, mine_ref, theirs_ref, lift_ref, bsum_ref = refs[2 * n_arrays : 2 * n_arrays + 6]
    low_acc, lift_acc, up_buf, down_buf, sems = refs[2 * n_arrays + 6 :]
    j = pl.program_id(0)
    tn = up_buf.shape[2]
    slot = lax.rem(j, 2)

    def copies(tile, at):
        index, start = plan[tile]
        cut = (slice(None), pl.ds(start, tn))
        return (
            pltpu.make_async_copy(ups[index].at[cut], up_buf.at[at], sems.at[0, at]),
            pltpu.make_async_copy(downs[index].at[cut], down_buf.at[at], sems.at[1, at]),
        )

    @pl.when(j == 0)
    def _():
        for copy in copies(0, 0):
            copy.start()
        low_acc[...] = jnp.zeros_like(low_acc)
        lift_acc[...] = jnp.zeros_like(lift_acc)

    for tile in range(1, len(plan)):

        @pl.when(j == tile - 1)
        def _(tile=tile):
            for copy in copies(tile, tile % 2):
                copy.start()

    for copy in copies(0, slot):
        copy.wait()
    u = mm(n_ref[...], up_buf[slot]) + bias_ref[...]
    cdf = 0.5 * (1.0 + lax.erf(u * ROOT_HALF))
    g = (u * cdf).astype(BF16)
    slope = cdf + u * (jnp.exp(-0.5 * u * u) * DENSITY)
    g_ref[...] = g
    du = (mm(dy_ref[...], down_buf[slot]) * slope).astype(BF16)
    du_ref[...] = du
    bsum_ref[...] = col_sum(du.astype(F32))
    low_acc[...] += mm_nt(g, down_buf[slot])
    lift_acc[...] += mm_nt(du, up_buf[slot])

    @pl.when(j == len(plan) - 1)
    def _():
        lift_ref[...] = lift_acc[...].astype(BF16)
        width = D // 4
        core = place_ref[0]
        for far in range(2):
            low = pl.multiple_of((2 * far + core) * width, width)
            other = pl.multiple_of((2 * far + 1 - core) * width, width)
            mine_ref[:, far * width : (far + 1) * width] = low_acc[:, pl.ds(low, width)]
            theirs_ref[:, far * width : (far + 1) * width] = low_acc[:, pl.ds(other, width)].astype(
                BF16
            )


def mlp(place, n2, dy, bias, ups, downs, plan):
    rows = n2.shape[0]
    hid = bias.shape[1]
    tn = hid // len(plan)
    whole = held_once((rows, D))
    tile = pl.BlockSpec((rows, tn), lambda j, *_: (0, j))
    thin = pl.BlockSpec((1, tn), lambda j, *_: (0, j))
    return pl.pallas_call(
        functools.partial(mlp_kernel, plan),
        name="mlp",
        grid_spec=pltpu.PrefetchScalarGridSpec(
            num_scalar_prefetch=1,
            grid=(len(plan),),
            in_specs=[whole, whole, thin]
            + [pl.BlockSpec(memory_space=pl.ANY)] * (len(ups) + len(downs)),
            out_specs=[
                tile,
                tile,
                held_once((rows, D // 2)),
                held_once((rows, D // 2)),
                whole,
                thin,
            ],
            scratch_shapes=[
                pltpu.VMEM((rows, D), F32),
                pltpu.VMEM((rows, D), F32),
                pltpu.VMEM((2, D, tn), BF16),
                pltpu.VMEM((2, D, tn), BF16),
                pltpu.SemaphoreType.DMA((2, 2)),
            ],
        ),
        out_shape=[
            like((rows, hid), BF16),
            like((rows, hid), BF16),
            like((rows, D // 2), F32),
            like((rows, D // 2), BF16),
            like((rows, D), BF16),
            like((1, hid), F32),
        ],
        compiler_params=params(1),
        cost_estimate=cost(8 * rows * D * hid, 24 * rows * D, 2 * rows * hid),
    )(place, n2, dy, bias, *ups, *downs)


def finish_kernel(place_ref, h_ref, a_ref, b_ref, bias_ref, mine_ref, theirs_ref):
    value = h_ref[...] + (a_ref[...] + b_ref[...].astype(F32)) + bias_ref[...]
    value = value.astype(BF16)

    @pl.when(pl.program_id(0) == 0)
    def _():
        theirs_ref[...] = value

    @pl.when(pl.program_id(0) == 1)
    def _():
        mine_ref[...] = value


def finish(place, h, a, b, bias):
    rows = h.shape[0]
    width = D // 4
    n = rows // TM

    def block(k, s):
        return jnp.where(k == 0, 1 - s[1], s[1])

    return pl.pallas_call(
        finish_kernel,
        name="finish",
        grid_spec=pltpu.PrefetchScalarGridSpec(
            num_scalar_prefetch=1,
            grid=(2, n),
            in_specs=[
                pl.BlockSpec((TM, width), lambda k, i, s: (i, 2 * block(k, s) + s[0])),
                pl.BlockSpec((TM, width), lambda k, i, s: (i, block(k, s))),
                pl.BlockSpec((TM, width), lambda k, i, s: (i, block(k, s))),
                pl.BlockSpec((1, width), lambda k, i, s: (0, 2 * block(k, s) + s[0])),
            ],
            out_specs=[
                pl.BlockSpec((TM, width), lambda k, i, s: (jnp.where(k == 0, 0, i), 0)),
                pl.BlockSpec((TM, width), lambda k, i, s: (jnp.where(k == 0, i, n - 1), 0)),
            ],
        ),
        out_shape=[like((rows, width), BF16), like((rows, width), BF16)],
        compiler_params=params(2),
        cost_estimate=cost(2 * rows * D, 6 * rows * D),
    )(place, h, a, b, bias)


def turn_kernel(h_ref, dy_ref, a_ref, b_ref, gain_ref, w_ref, dh_ref, da_ref, do_ref, sums_ref):
    h = h_ref[...]
    middle, scaled = stats(h)
    c = (h - middle) * scaled
    dn = a_ref[...].astype(F32) + b_ref[...].astype(F32)
    dy = dy_ref[...].astype(F32)
    e = dn * gain_ref[...]
    dh = dy + scaled * (e - row_mean(e) - c * row_mean(e * c))
    dh_ref[...] = dh
    da = dh.astype(BF16)
    da_ref[...] = da
    do_ref[...] = mm(da, w_ref[...]).astype(BF16)
    part = jnp.concatenate(
        [col_sum(dn * c), col_sum(dn), col_sum(da.astype(F32)), col_sum(dy)], axis=0
    )
    add_up(sums_ref, pl.program_id(0) == 0, part)


def turn(h, dy, a, b, gain, weights):
    rows = h.shape[0]
    wide = weights.shape[1] // 4
    return pl.pallas_call(
        turn_kernel,
        grid=(rows // TM,),
        name="turn",
        in_specs=[row_spec(D)] * 4
        + [fixed((1, D)), pl.BlockSpec((D, wide), lambda i: (0, 3), pipeline_mode=pl.Buffered(1))],
        out_specs=[row_spec(D), row_spec(D), row_spec(wide), fixed((4, D))],
        out_shape=[
            like((rows, D), F32),
            like((rows, D), BF16),
            like((rows, wide), BF16),
            like((4, D), F32),
        ],
        compiler_params=params(1),
        cost_estimate=cost(2 * rows * D * wide, 18 * rows * D),
    )(h, dy, a, b, gain, weights)


def last_kernel(place_ref, x_ref, dh_ref, a_ref, b_ref, gain_ref, mine_ref, theirs_ref, sums_ref, held):
    x = x_ref[...].astype(F32)
    middle, scaled = stats(x)
    c = (x - middle) * scaled
    dn = a_ref[...].astype(F32) + b_ref[...].astype(F32)
    e = dn * gain_ref[...]
    held[...] = dh_ref[...] + scaled * (e - row_mean(e) - c * row_mean(e * c))
    width = D // 4
    core, side = place_ref[0], place_ref[1]
    mine_ref[...] = held[:, pl.ds(pl.multiple_of((2 * side + core) * width, width), width)]
    theirs_ref[...] = held[
        :, pl.ds(pl.multiple_of((2 * (1 - side) + core) * width, width), width)
    ].astype(BF16)
    add_up(
        sums_ref,
        pl.program_id(0) == 0,
        jnp.concatenate([col_sum(dn * c), col_sum(dn)], axis=0),
    )


def last(place, x, dh, a, b, gain):
    rows = x.shape[0]
    width = D // 4
    return pl.pallas_call(
        last_kernel,
        name="last",
        grid_spec=pltpu.PrefetchScalarGridSpec(
            num_scalar_prefetch=1,
            grid=(rows // TM,),
            in_specs=[row_spec(D)] * 4 + [fixed((1, D))],
            out_specs=[row_spec(width), row_spec(width), fixed((2, D))],
            scratch_shapes=[pltpu.VMEM((TM, D), F32)],
        ),
        out_shape=[like((rows, width), F32), like((rows, width), BF16), like((2, D), F32)],
        compiler_params=params(1),
        cost_estimate=cost(20 * rows * D, 12 * rows * D),
    )(place, x, dh, a, b, gain)


def local(
    sizes,
    inputs,
    query_weight,
    key_weight,
    value_weight,
    query_bias,
    value_bias,
    out_weight,
    out_bias,
    up_weight,
    up_bias,
    down_weight,
    down_bias,
    first_gain,
    first_shift,
    second_gain,
    second_shift,
    cotangent,
):
    n_dp, n_row, n_xa, n_core = sizes
    my_x = lax.axis_index("xa")
    my_core = lax.axis_index("core")
    my_row = lax.axis_index("row")
    my_half = lax.axis_index("dp") % 2
    place = jnp.stack([my_core, my_x]).astype(jnp.int32)
    tokens_here, width = inputs.shape
    images = tokens_here // SEQ
    held = images // n_xa
    rows = held * PAD
    hidden = up_weight.shape[1]
    half = hidden // 2
    heads_half = width // 2
    three = 3 * heads_half

    def swap(value, axis, size, bit=1):
        return lax.ppermute(value, axis, [(at, at ^ bit) for at in range(size)])

    def across(value):
        return swap(value, "xa", n_xa)

    def beside(value):
        return swap(value, "core", n_core)

    def over(value):
        return swap(value, "dp", n_dp)

    def pick(value, at, axis):
        return lax.dynamic_index_in_dim(value, at, axis, keepdims=False)

    def in_order(mine, other, at):
        return jnp.where(at == 0, mine, other), jnp.where(at == 0, other, mine)

    def after(value, *others):
        return lax.optimization_barrier((value, *others))[0]

    def halves(value, axis):
        cut = value.shape[axis] // 2
        both = value.reshape(value.shape[:axis] + (2, cut) + value.shape[axis + 1 :])
        return pick(both, my_half, axis), pick(both, my_half ^ 1, axis)

    attn_shard = jnp.concatenate(
        [halves(item, 1)[0] for item in (query_weight, key_weight, value_weight)]
        + [halves(out_weight, 0)[0].T],
        axis=1,
    )
    pieces = [attn_shard] + [
        lax.ppermute(attn_shard, "row", [(at, (at + shift) % n_row) for at in range(n_row)])
        for shift in range(1, n_row)
    ]

    count = held * SEQ

    def send_tokens(value):
        theirs = lax.dynamic_slice_in_dim(value, (my_x ^ 1) * count, count, 0)
        return across(theirs)

    def wide_tokens(value, got):
        mine = lax.dynamic_slice_in_dim(value, my_x * count, count, 0)
        pair = jnp.concatenate([mine, got], axis=1)
        other = beside(pair)
        left, right = in_order(pair, other, my_core)
        first_left, second_left = in_order(left[:, :width], left[:, width:], my_x)
        first_right, second_right = in_order(right[:, :width], right[:, width:], my_x)
        whole = jnp.concatenate([first_left, first_right, second_left, second_right], axis=1)
        whole = jnp.pad(whole.reshape(held, SEQ, D), ((0, 0), (0, PAD - SEQ), (0, 0)))
        return whole.reshape(rows, D)

    wide_input = wide_tokens(inputs, send_tokens(inputs))

    small = jnp.concatenate(
        [
            out_bias,
            down_bias,
            first_gain,
            first_shift,
            second_gain,
            second_shift,
            query_bias,
            value_bias,
            up_bias,
        ]
    )
    small_far = across(small)
    small_pair = jnp.stack(in_order(small, small_far, my_x))
    small_left, small_right = in_order(small_pair, beside(small_pair), my_core)

    def whole_vector(at):
        cut = slice(width * at, width * (at + 1))
        return jnp.concatenate(
            [small_left[0, cut], small_right[0, cut], small_left[1, cut], small_right[1, cut]]
        )[None]

    out_bias_all, down_bias_all, gain_one, shift_one, gain_two, shift_two = (
        whole_vector(at) for at in range(6)
    )

    attn_own = jnp.zeros((D, 4 * heads_half), BF16)
    for shift, piece in enumerate(pieces):
        start = (my_row - shift) % n_row * (D // n_row)
        attn_own = lax.dynamic_update_slice(attn_own, piece, (start, 0))
    attn_oth, attn_far = over(attn_own), across(attn_own)
    cut = 2 * heads_half
    attn_far_oth = jnp.concatenate(
        [over(after(attn_far, wide_input)[:, :cut]), across(attn_oth[:, cut:])], axis=1
    )

    def spread(shard):
        own = lax.all_gather(shard, "row", axis=0, tiled=True)
        oth, far = over(own), across(own)
        cut = half // 2
        return own, far, oth, over(far[:, :cut]), across(oth[:, cut:])

    up_shard = after(halves(up_weight, 1)[0], attn_own)
    ups = spread(up_shard)
    down_shard = after(halves(down_weight, 0)[0].T, attn_own)
    downs = spread(down_shard)
    grad_here = after(cotangent, attn_far_oth)
    wide_grad = wide_tokens(grad_here, send_tokens(grad_here))

    def four(near_vector, far_vector):
        near_own, near_oth = halves(near_vector, 0)
        far_own, far_oth = halves(far_vector, 0)
        return near_own, far_own, near_oth, far_oth

    zeros = jnp.zeros((heads_half,), F32)
    query_parts = four(query_bias, small_far[6 * width : 7 * width])
    value_parts = four(value_bias, small_far[7 * width : 8 * width])
    qkv_bias = jnp.concatenate(
        [item for q, v in zip(query_parts, value_parts) for item in (q, zeros, v)]
    )[None]
    near_own, far_own, near_oth, far_oth = (
        item.reshape(2, half // 2) for item in four(up_bias, small_far[8 * width :])
    )
    tile_bias = jnp.concatenate(
        [near_own[0], far_own[0], near_oth[0], far_oth[0]]
        + [near_own[1], near_oth[1], far_own[1], far_oth[1]]
    )[None]
    quarter = half // 2
    plan = ((0, 0), (1, 0), (2, 0), (3, 0), (0, quarter), (2, quarter), (1, quarter), (4, 0))

    wide_one, qkv, attn_weights = norm_qkv(
        wide_input, gain_one, shift_one, qkv_bias, (attn_own, attn_far, attn_oth, attn_far_oth)
    )
    attended, probs = attend(qkv)
    mixed = mm_nt(attended, attn_weights[:, 4 * three :]).astype(BF16)
    middle_sum, wide_two = middle(
        wide_input, mixed, beside(mixed), out_bias_all, gain_two, shift_two
    )
    gate, pre, low_mine, low_theirs, lifted_two, up_sums = mlp(
        place,
        wide_two,
        wide_grad,
        tile_bias,
        ups,
        downs,
        plan,
    )

    def wide_add(mine, got):
        return (mine.astype(F32) + got.astype(F32)).astype(BF16)

    def same_half(value):
        if n_dp == 2:
            return value
        groups = [[at + bit for at in range(0, n_dp, 2)] for bit in range(2)]
        return lax.psum(value.astype(F32), "dp", axis_index_groups=groups).astype(BF16)

    def scatter(value):
        return lax.psum_scatter(value, "row", scatter_dimension=0, tiled=True)

    def tiles(value, first, last):
        return value[:, quarter * first : quarter * last]

    lifted_other = beside(lifted_two)
    down_all = mm_tn(wide_grad, gate).astype(BF16)
    down_piece = scatter(down_all)
    up_over = mm_tn(wide_two, tiles(pre, 2, 4)).astype(BF16)
    up_across = mm_tn(wide_two, tiles(pre, 6, 8)).astype(BF16)
    up_over_got, up_across_got = over(up_over), across(up_across)

    middle_grad, attn_grad, head_grad, turn_sums = turn(
        middle_sum,
        wide_grad,
        lifted_two,
        after(lifted_other, down_all, up_over, up_across),
        gain_two,
        attn_weights,
    )
    dqkv, qkv_sums = attend_back(qkv, probs, head_grad)

    def to_feature_blocks(mine, got, dtype):
        first, second = in_order(mine.astype(dtype), got.astype(dtype), my_x)
        both = jnp.concatenate([first, second]).reshape(images, PAD, width)
        return both[:, :SEQ].reshape(tokens_here, width)

    far_oth = mm_tn(wide_one, dqkv[:, 3 * three :]).astype(BF16)
    near_oth = mm_tn(wide_one, dqkv[:, 2 * three : 3 * three]).astype(BF16)
    far_oth_got, near_oth_got = over(far_oth), over(near_oth)
    lifted_one = mm_nt(
        after(dqkv, far_oth, near_oth), attn_weights[:, : 4 * three]
    ).astype(BF16)
    lifted_one_other = beside(lifted_one)

    up_over_got, up_across_got, _ = lax.optimization_barrier(
        (up_over_got, up_across_got, lifted_one)
    )
    up_a = wide_add(mm_tn(wide_two, tiles(pre, 0, 2)), up_over_got)
    up_b = wide_add(mm_tn(wide_two, tiles(pre, 4, 6)), up_across_got)
    up_a_got, up_b_got = across(up_a[:, quarter:]), over(up_b[:, quarter:])

    input_mine, input_theirs, last_sums = last(
        place, wide_input, middle_grad, lifted_one, after(lifted_one_other, up_a, up_b), gain_one
    )
    far_oth_got = after(far_oth_got, input_mine)
    far_own = wide_add(mm_tn(wide_one, dqkv[:, three : 2 * three]), far_oth_got)
    far_own_got = across(far_own)
    near_own = wide_add(mm_tn(wide_one, dqkv[:, :three]), near_oth_got)

    out_all = mm_tn(after(attn_grad, far_own), attended).astype(BF16)
    out_got = over(out_all[:, 2 * heads_half :])
    out_mine, out_theirs = finish(
        place, middle_sum, after(low_mine, far_own), beside(low_theirs), down_bias_all
    )
    outputs = to_feature_blocks(out_mine, across(out_theirs), BF16)
    out_own = wide_add(out_all[:, : 2 * heads_half], out_got)
    out_far_got = across(out_own[:, heads_half:])

    near_sum = wide_add(near_own, after(far_own_got, out_mine))
    strip = D // n_row

    def rows_of(value, shift):
        return lax.dynamic_slice_in_dim(value, (my_row + shift) % n_row * strip, strip, 0)

    qkv_total = rows_of(near_sum, 0).astype(F32)
    for shift in range(1, n_row):
        got = lax.ppermute(
            rows_of(near_sum, shift), "row", [(at, (at + shift) % n_row) for at in range(n_row)]
        )
        qkv_total = qkv_total + got.astype(F32)
    qkv_piece = same_half(qkv_total.astype(BF16))
    qkv_other = over(qkv_piece)

    input_theirs = after(input_theirs, far_own_got)
    input_grad = to_feature_blocks(input_mine, across(input_theirs), F32)

    up_piece = same_half(
        scatter(
            jnp.concatenate(
                [
                    wide_add(up_a[:, :quarter], up_a_got),
                    wide_add(up_b[:, :quarter], up_b_got),
                    wide_add(out_own[:, :heads_half], out_far_got),
                ],
                axis=1,
            )
        )
    )
    up_other = over(up_piece)

    def some(value, *which):
        return jnp.concatenate([tiles(value, at, at + 1) for at in which], axis=1)

    down_x = wide_add(some(down_piece, 0, 4, 2, 5), across(some(down_piece, 1, 6, 3, 7)))
    down_got = over(down_x)
    down_total = down_x.astype(F32) + jnp.concatenate(
        [down_got[:, half:], down_got[:, :half]], axis=1
    ).astype(F32)
    if n_dp > 2:
        groups = [[at + bit for at in range(0, n_dp, 2)] for bit in range(2)]
        down_total = lax.psum(down_total, "dp", axis_index_groups=groups)
    down_first, down_second = in_order(down_total[:, :half], down_total[:, half:], my_half)
    down_grad = jnp.concatenate([down_first, down_second], axis=1).T

    def both_halves(mine, other, low, high):
        first, second = in_order(mine[:, low:high], other[:, low:high], my_half)
        return jnp.concatenate([first, second], axis=1).astype(F32)

    up_grad = both_halves(up_piece, up_other, 0, half)
    out_grad = both_halves(up_piece, up_other, half, half + heads_half).T
    query_grad, key_grad, value_grad = (
        both_halves(qkv_piece, qkv_other, heads_half * at, heads_half * (at + 1))
        for at in range(3)
    )

    def own_features(value):
        return pick(value.reshape(-1, n_xa, 2, width), my_core, 2)

    def by_x(parts):
        near_own, far_own, near_oth, far_oth = parts
        near = jnp.concatenate(in_order(near_own, near_oth, my_half))
        far = jnp.concatenate(in_order(far_own, far_oth, my_half))
        return jnp.stack(in_order(near, far, my_x))

    def everywhere(value):
        value = value + across(value)
        bit = 1
        while bit < n_row:
            value = value + swap(value, "row", n_row, bit)
            bit *= 2
        bit = 1
        while bit < n_dp:
            value = value + swap(value, "dp", n_dp, bit)
            bit *= 2
        return pick(value, my_x, 0)

    turn_own = own_features(turn_sums)
    qkv_parts = qkv_sums.reshape(4, 3, heads_half)
    up_tiles = up_sums.reshape(8, quarter)
    up_parts = [
        jnp.concatenate([up_tiles[first], up_tiles[second]])
        for first, second in ((0, 4), (1, 6), (2, 5), (3, 7))
    ]
    early = everywhere(
        jnp.concatenate(
            [
                by_x(qkv_parts[:, 0]),
                by_x(qkv_parts[:, 2]),
                turn_own[2],
                turn_own[3],
                turn_own[0],
                turn_own[1],
                by_x(up_parts),
            ],
            axis=1,
        )
    )
    last_own = own_features(last_sums)
    late = everywhere(jnp.concatenate([last_own[0], last_own[1]], axis=1))

    def piece_of(value, at):
        return value[width * at : width * (at + 1)]

    return (
        outputs,
        input_grad,
        query_grad,
        key_grad,
        value_grad,
        piece_of(early, 0),
        piece_of(early, 1),
        out_grad,
        piece_of(early, 2),
        up_grad,
        early[6 * width :],
        down_grad,
        piece_of(early, 3),
        piece_of(late, 0),
        piece_of(late, 1),
        piece_of(early, 4),
        piece_of(early, 5),
    )


def solution(mesh):
    n_dp, n_row, n_col = (mesh.shape[name] for name in ("dp", "row", "col"))
    sizes = (n_dp, n_row, n_col // 2, 2)
    split = Mesh(mesh.devices.reshape(sizes), ("dp", "row", "xa", "core"))
    col = ("xa", "core")
    tokens, rows, cols, vec = P(("dp", "row"), col), P("row", col), P(col, "row"), P(col)
    in_specs = (
        (tokens, rows, rows, rows, vec, vec, cols, vec, rows, vec, cols)
        + (vec,) * 5
        + (tokens,)
    )
    out_specs = (
        (tokens, tokens, rows, rows, rows, vec, vec, cols, vec, rows, vec, cols) + (vec,) * 5
    )
    return jax.shard_map(
        functools.partial(local, sizes),
        mesh=split,
        in_specs=in_specs,
        out_specs=out_specs,
        check_vma=False,
    )
```

```python
import functools
import math

import jax
import jax.numpy as jnp
from jax import lax
from jax.experimental import pallas as pl
from jax.experimental.pallas import tpu as pltpu
from jax.sharding import Mesh, PartitionSpec as P

D = 1024
HD = 64
SEQ = 577
PAD = 592
TM = 296
EPS = 1e-06
F32 = jnp.float32
BF16 = jnp.bfloat16
VMEM_LIMIT = 60 * 1024 * 1024
ROOT_HALF = math.sqrt(0.5)
DENSITY = 1.0 / math.sqrt(2.0 * math.pi)


def mm(a, b):
    return lax.dot_general(a, b, (((1,), (0,)), ((), ())), preferred_element_type=F32)


def mm_nt(a, b):
    return lax.dot_general(a, b, (((1,), (1,)), ((), ())), preferred_element_type=F32)


def mm_tn(a, b):
    return lax.dot_general(a, b, (((0,), (0,)), ((), ())), preferred_element_type=F32)


def row_mean(v):
    return jnp.sum(v, axis=1, keepdims=True) * (1.0 / D)


def col_sum(v):
    return jnp.sum(v, axis=0, keepdims=True)


def stats(rows):
    middle = row_mean(rows)
    spread = row_mean(rows * rows) - middle * middle
    return middle, lax.rsqrt(spread + EPS)


def params(n):
    return pltpu.CompilerParams(
        dimension_semantics=("arbitrary",) * n, vmem_limit_bytes=VMEM_LIMIT
    )


def cost(flops, moved, exps=0):
    return pl.CostEstimate(flops=int(flops), bytes_accessed=int(moved), transcendentals=int(exps))


def like(shape, dtype):
    return jax.ShapeDtypeStruct(shape, dtype)


def row_spec(cols):
    return pl.BlockSpec((TM, cols), lambda i, *_: (i, 0))


def fixed(shape):
    return pl.BlockSpec(shape, lambda *_: (0,) * len(shape))


def held_once(shape):
    return pl.BlockSpec(shape, lambda *_: (0,) * len(shape), pipeline_mode=pl.Buffered(1))


def add_up(ref, first, part):
    @pl.when(first)
    def _():
        ref[...] = part

    @pl.when(jnp.logical_not(first))
    def _():
        ref[...] += part


def norm_qkv_kernel(x_ref, gain_ref, shift_ref, bias_ref, *refs):
    blocks, (n_ref, o_ref, w_ref) = refs[:8], refs[8:]
    one = blocks[1].shape[1] // 2

    @pl.when(pl.program_id(0) == 0)
    def _():
        for place in range(4):
            first, second = blocks[2 * place], blocks[2 * place + 1]
            start = 3 * one * place
            w_ref[:, start : start + 2 * one] = first[...]
            w_ref[:, start + 2 * one : start + 3 * one] = second[:, :one]
            w_ref[:, (12 + place) * one : (13 + place) * one] = second[:, one:]

    x = x_ref[...].astype(F32)
    middle, scaled = stats(x)
    n = (((x - middle) * scaled) * gain_ref[...] + shift_ref[...]).astype(BF16)
    n_ref[...] = n
    o_ref[...] = (mm(n, w_ref[:, : 12 * one]) + bias_ref[...]).astype(BF16)


def norm_qkv(x, gain, shift, bias, blocks):
    rows = x.shape[0]
    wide = blocks[0].shape[1]
    out = 6 * wide
    return pl.pallas_call(
        norm_qkv_kernel,
        grid=(rows // TM,),
        name="norm_qkv",
        in_specs=[row_spec(D), gain[1], shift[1], fixed((1, out))] + [held_once((D, wide))] * 8,
        out_specs=[row_spec(D), row_spec(out), held_once((D, 8 * wide))],
        out_shape=[like((rows, D), BF16), like((rows, out), BF16), like((D, 8 * wide), BF16)],
        compiler_params=params(1),
        cost_estimate=cost(2 * rows * D * out, 16 * rows * D),
    )(x, gain[0], shift[0], bias, *blocks)


def attend_kernel(qkv_ref, o_ref, p_ref):
    live = lax.broadcasted_iota(jnp.int32, (1, PAD), 1) < SEQ
    step = 2 * HD
    for h in range(2):
        q, k, v = (qkv_ref[:, step * w + HD * h : step * w + HD * (h + 1)] for w in range(3))
        s = mm_nt(q * jnp.asarray(0.125, BF16), k)
        s = jnp.where(live, s, -1e30)
        e = jnp.exp(s - jnp.max(s, axis=1, keepdims=True))
        p = (e * (1.0 / jnp.sum(e, axis=1, keepdims=True))).astype(BF16)
        p_ref[h] = p
        o_ref[:, HD * h : HD * (h + 1)] = mm(p, v).astype(BF16)


def attend(qkv):
    rows, cols = qkv.shape
    pairs = cols // (6 * HD)
    held = rows // PAD
    return pl.pallas_call(
        attend_kernel,
        grid=(pairs, held),
        name="attend",
        in_specs=[pl.BlockSpec((PAD, 6 * HD), lambda p, i: (i, p))],
        out_specs=[
            pl.BlockSpec((PAD, 2 * HD), lambda p, i: (i, p)),
            pl.BlockSpec((None, 2, PAD, PAD), lambda p, i: (i, p, 0, 0)),
        ],
        out_shape=[like((rows, cols // 3), BF16), like((held, 2 * pairs, PAD, PAD), BF16)],
        compiler_params=params(2),
        cost_estimate=cost(16 * rows * PAD * cols, 40 * rows * D, 4 * rows * PAD * pairs),
    )(qkv)


def attend_back_kernel(qkv_ref, p_ref, g_ref, d_ref, sum_ref):
    step = 2 * HD
    for h in range(2):
        q, k, v = (qkv_ref[:, step * w + HD * h : step * w + HD * (h + 1)] for w in range(3))
        g = g_ref[:, HD * h : HD * (h + 1)]
        pb = p_ref[h]
        p = pb.astype(F32)
        dp = mm_nt(g, v)
        z = jnp.sum(p * dp, axis=1, keepdims=True)
        ds = (p * (dp - z)).astype(BF16)
        parts = (mm(ds, k) * 0.125, mm_tn(ds, q) * 0.125, mm_tn(pb, g))
        for w, part in enumerate(parts):
            d_ref[:, step * w + HD * h : step * w + HD * (h + 1)] = part.astype(BF16)
    add_up(sum_ref, pl.program_id(1) == 0, col_sum(d_ref[...].astype(F32)))


def attend_back(qkv, probs, grads):
    rows, cols = qkv.shape
    pairs = cols // (6 * HD)
    held = rows // PAD
    three = pl.BlockSpec((PAD, 6 * HD), lambda p, i: (i, p))
    return pl.pallas_call(
        attend_back_kernel,
        grid=(pairs, held),
        name="attend_back",
        in_specs=[
            three,
            pl.BlockSpec((None, 2, PAD, PAD), lambda p, i: (i, p, 0, 0)),
            pl.BlockSpec((PAD, 2 * HD), lambda p, i: (i, p)),
        ],
        out_specs=[three, pl.BlockSpec((1, 6 * HD), lambda p, i: (0, p))],
        out_shape=[like((rows, cols), BF16), like((1, cols), F32)],
        compiler_params=params(2),
        cost_estimate=cost(20 * rows * PAD * cols, 50 * rows * D),
    )(qkv, probs, grads)


def middle_kernel(x_ref, a_ref, b_ref, bias_ref, gain_ref, shift_ref, h_ref, n_ref):
    h = x_ref[...].astype(F32) + (a_ref[...].astype(F32) + b_ref[...].astype(F32)) + bias_ref[...]
    h_ref[...] = h
    middle, scaled = stats(h)
    n_ref[...] = (((h - middle) * scaled) * gain_ref[...] + shift_ref[...]).astype(BF16)


def middle(x, a, b, bias, gain, shift):
    rows = x.shape[0]
    return pl.pallas_call(
        middle_kernel,
        grid=(rows // TM,),
        name="middle",
        in_specs=[row_spec(D)] * 3 + [bias[1], gain[1], shift[1]],
        out_specs=[row_spec(D)] * 2,
        out_shape=[like((rows, D), F32), like((rows, D), BF16)],
        compiler_params=params(1),
        cost_estimate=cost(20 * rows * D, 12 * rows * D),
    )(x, a, b, bias[0], gain[0], shift[0])


def mlp_kernel(plan, place_ref, n_ref, dy_ref, bias_ref, *refs):
    packs = refs[: len(plan)]
    g_ref, du_ref, mine_ref, theirs_ref, lift_ref, bsum_ref = refs[len(plan) : len(plan) + 6]
    low_acc, lift_acc, buf, sems = refs[len(plan) + 6 :]
    j = pl.program_id(0)
    tn = g_ref.shape[1]
    slot = lax.rem(j, 2)

    def load(tile, at):
        return pltpu.make_async_copy(packs[plan[tile]], buf.at[at], sems.at[at])

    @pl.when(j == 0)
    def _():
        load(0, 0).start()
        low_acc[...] = jnp.zeros_like(low_acc)
        lift_acc[...] = jnp.zeros_like(lift_acc)

    for tile in range(1, len(plan)):

        @pl.when(j == tile - 1)
        def _(tile=tile):
            load(tile, tile % 2).start()

    load(0, slot).wait()
    up, down = buf[slot, :, :tn], buf[slot, :, tn:]
    u = mm(n_ref[...], up) + bias_ref[...]
    cdf = 0.5 * (1.0 + lax.erf(u * ROOT_HALF))
    g = (u * cdf).astype(BF16)
    slope = cdf + u * (jnp.exp(-0.5 * u * u) * DENSITY)
    g_ref[...] = g
    du = (mm(dy_ref[...], down) * slope).astype(BF16)
    du_ref[...] = du
    bsum_ref[...] = col_sum(du.astype(F32))
    low_acc[...] += mm_nt(g, down)
    lift_acc[...] += mm_nt(du, up)

    @pl.when(j == len(plan) - 1)
    def _():
        lift_ref[...] = lift_acc[...].astype(BF16)
        width = D // 4
        core = place_ref[0]
        for far in range(2):
            low = pl.multiple_of((2 * far + core) * width, width)
            other = pl.multiple_of((2 * far + 1 - core) * width, width)
            mine_ref[:, far * width : (far + 1) * width] = low_acc[:, pl.ds(low, width)]
            theirs_ref[:, far * width : (far + 1) * width] = low_acc[:, pl.ds(other, width)].astype(
                BF16
            )


def mlp(place, n2, dy, bias, packs, plan):
    rows = n2.shape[0]
    hid = bias.shape[1]
    tn = hid // len(plan)
    whole = held_once((rows, D))
    tile = pl.BlockSpec((rows, tn), lambda j, *_: (0, j))
    thin = pl.BlockSpec((1, tn), lambda j, *_: (0, j))
    return pl.pallas_call(
        functools.partial(mlp_kernel, plan),
        name="mlp",
        grid_spec=pltpu.PrefetchScalarGridSpec(
            num_scalar_prefetch=1,
            grid=(len(plan),),
            in_specs=[whole, whole, thin]
            + [pl.BlockSpec(memory_space=pl.ANY)] * len(packs),
            out_specs=[
                tile,
                tile,
                held_once((rows, D // 2)),
                held_once((rows, D // 2)),
                whole,
                thin,
            ],
            scratch_shapes=[
                pltpu.VMEM((rows, D), F32),
                pltpu.VMEM((rows, D), F32),
                pltpu.VMEM((2, D, 2 * tn), BF16),
                pltpu.SemaphoreType.DMA((2,)),
            ],
        ),
        out_shape=[
            like((rows, hid), BF16),
            like((rows, hid), BF16),
            like((rows, D // 2), F32),
            like((rows, D // 2), BF16),
            like((rows, D), BF16),
            like((1, hid), F32),
        ],
        compiler_params=params(1),
        cost_estimate=cost(8 * rows * D * hid, 24 * rows * D, 2 * rows * hid),
    )(place, n2, dy, bias, *packs)


def turn_kernel(
    place_ref, h_ref, dy_ref, a_ref, b_ref, low_ref, other_ref, gain_ref, bias_ref, w_ref,
    dh_ref, da_ref, do_ref, sums_ref, mine_ref, theirs_ref, held,
):
    h = h_ref[...]
    held[...] = h + bias_ref[...]
    core, side = place_ref[0], place_ref[1]
    width = D // 4
    low = low_ref[...] + other_ref[...].astype(F32)
    for far in range(2):
        at = pl.ds(pl.multiple_of((2 * far + core) * width, width), width)
        out = (held[:, at] + low[:, far * width : (far + 1) * width]).astype(BF16)

        @pl.when(side == far)
        def _(out=out):
            mine_ref[...] = out

        @pl.when(side != far)
        def _(out=out):
            theirs_ref[...] = out

    middle, scaled = stats(h)
    c = (h - middle) * scaled
    dn = a_ref[...].astype(F32) + b_ref[...].astype(F32)
    dy = dy_ref[...].astype(F32)
    e = dn * gain_ref[...]
    dh = dy + scaled * (e - row_mean(e) - c * row_mean(e * c))
    dh_ref[...] = dh
    da = dh.astype(BF16)
    da_ref[...] = da
    do_ref[...] = mm(da, w_ref[...]).astype(BF16)
    part = jnp.concatenate(
        [col_sum(da.astype(F32)), col_sum(dy), col_sum(dn * c), col_sum(dn)], axis=0
    )
    add_up(sums_ref, pl.program_id(0) == 0, part)


def turn(place, h, dy, a, b, low_mine, low_other, gain, bias, weights):
    rows = h.shape[0]
    wide = weights.shape[1] // 4
    width = D // 4
    return pl.pallas_call(
        turn_kernel,
        name="turn",
        grid_spec=pltpu.PrefetchScalarGridSpec(
            num_scalar_prefetch=1,
            grid=(rows // TM,),
            in_specs=[row_spec(D)] * 4
            + [row_spec(D // 2)] * 2
            + [gain[1], bias[1]]
            + [pl.BlockSpec((D, wide), lambda i, *_: (0, 3), pipeline_mode=pl.Buffered(1))],
            out_specs=[
                row_spec(D),
                row_spec(D),
                row_spec(wide),
                fixed((4, D)),
                row_spec(width),
                row_spec(width),
            ],
            scratch_shapes=[pltpu.VMEM((TM, D), F32)],
        ),
        out_shape=[
            like((rows, D), F32),
            like((rows, D), BF16),
            like((rows, wide), BF16),
            like((4, D), F32),
            like((rows, width), BF16),
            like((rows, width), BF16),
        ],
        compiler_params=params(1),
        cost_estimate=cost(2 * rows * D * wide, 20 * rows * D),
    )(place, h, dy, a, b, low_mine, low_other, gain[0], bias[0], weights)


def last_kernel(
    place_ref, x_ref, dh_ref, a_ref, b_ref, gain_ref, mine_ref, theirs_ref, sum_mine, sum_theirs, held, sums
):
    x = x_ref[...].astype(F32)
    middle, scaled = stats(x)
    c = (x - middle) * scaled
    dn = a_ref[...].astype(F32) + b_ref[...].astype(F32)
    e = dn * gain_ref[...]
    held[...] = dh_ref[...] + scaled * (e - row_mean(e) - c * row_mean(e * c))
    width = D // 4
    core, side = place_ref[0], place_ref[1]
    here = pl.ds(pl.multiple_of((2 * side + core) * width, width), width)
    there = pl.ds(pl.multiple_of((2 * (1 - side) + core) * width, width), width)
    mine_ref[...] = held[:, here]
    theirs_ref[...] = held[:, there].astype(BF16)
    i = pl.program_id(0)
    add_up(sums, i == 0, jnp.concatenate([col_sum(dn * c), col_sum(dn)], axis=0))

    @pl.when(i == pl.num_programs(0) - 1)
    def _():
        sum_mine[...] = sums[:, here]
        sum_theirs[...] = sums[:, there]


def last(place, x, dh, a, b, gain):
    rows = x.shape[0]
    width = D // 4
    return pl.pallas_call(
        last_kernel,
        name="last",
        grid_spec=pltpu.PrefetchScalarGridSpec(
            num_scalar_prefetch=1,
            grid=(rows // TM,),
            in_specs=[row_spec(D)] * 4 + [gain[1]],
            out_specs=[row_spec(width), row_spec(width), fixed((2, width)), fixed((2, width))],
            scratch_shapes=[pltpu.VMEM((TM, D), F32), pltpu.VMEM((2, D), F32)],
        ),
        out_shape=[
            like((rows, width), F32),
            like((rows, width), BF16),
            like((2, width), F32),
            like((2, width), F32),
        ],
        compiler_params=params(1),
        cost_estimate=cost(20 * rows * D, 12 * rows * D),
    )(place, x, dh, a, b, gain[0])


def pack_kernel(*refs):
    out_ref = refs[-1]
    width = refs[0].shape[0]
    for at, ref in enumerate(refs[:-2]):
        out_ref[at, :] = ref[...]
    for at in range(4):
        out_ref[len(refs) - 2 + at, :] = refs[-2][width * at : width * (at + 1)]


def pack(vectors, long_vector):
    width = vectors[0].shape[0]
    return pl.pallas_call(
        pack_kernel,
        name="pack",
        out_shape=like((len(vectors) + 4, width), F32),
    )(*vectors, long_vector)


def unpack_kernel(place_ref, own, far, own_other, far_other, vec_ref, qkv_ref, tile_ref):
    core, side, half = place_ref[0], place_ref[1], place_ref[2]
    width = own.shape[1]
    one = width // 2

    def put(ref, at_side, at_core):
        at = pl.multiple_of((2 * at_side + at_core) * width, width)
        for k in range(6):
            vec_ref[k, :, pl.ds(at, width)] = ref[k : k + 1, :]

    put(own, side, core)
    put(far, 1 - side, core)
    put(own_other, side, 1 - core)
    put(far_other, 1 - side, 1 - core)
    qkv_ref[...] = jnp.zeros_like(qkv_ref)
    blocks = ((own, half), (far, half), (own, 1 - half), (far, 1 - half))
    for at, (ref, which) in enumerate(blocks):
        cut = pl.ds(pl.multiple_of(which * one, one), one)
        qkv_ref[:, 3 * one * at : 3 * one * at + one] = ref[6:7, cut]
        qkv_ref[:, 3 * one * at + 2 * one : 3 * one * (at + 1)] = ref[7:8, cut]
    order = (0, 1, 2, 3), (0, 2, 1, 3)
    for part in range(2):
        for at, index in enumerate(order[part]):
            ref, which = blocks[index]
            start = width * (4 * part + at)
            tile_ref[:, start : start + width] = ref[pl.ds(8 + 2 * which + part, 1), :]


def unpack(place, own, far, own_other, far_other):
    width = own.shape[1]
    return pl.pallas_call(
        unpack_kernel,
        name="unpack",
        in_specs=[pl.BlockSpec(memory_space=pltpu.SMEM)]
        + [pl.BlockSpec(memory_space=pltpu.VMEM)] * 4,
        out_shape=[like((6, 1, D), F32), like((1, 6 * width), F32), like((1, 8 * width), F32)],
    )(place, own, far, own_other, far_other)


def collect_kernel(place_ref, turn_ref, qkv_ref, up_ref, mine_ref, theirs_ref):
    core, side, half = place_ref[0], place_ref[1], place_ref[2]
    width = mine_ref.shape[1]
    one = width // 2
    for ref, at_side in ((mine_ref, side), (theirs_ref, 1 - side)):
        at = pl.ds(pl.multiple_of((2 * at_side + core) * width, width), width)
        ref[2:6, :] = turn_ref[:, at]
    for at in range(4):
        ref = (mine_ref, theirs_ref)[at % 2]
        which = half if at < 2 else 1 - half
        cut = pl.ds(pl.multiple_of(which * one, one), one)
        ref[0:1, cut] = qkv_ref[:, 3 * one * at : 3 * one * at + one]
        ref[1:2, cut] = qkv_ref[:, 3 * one * at + 2 * one : 3 * one * (at + 1)]
    order = (0, 1, 2, 3), (0, 2, 1, 3)
    for part in range(2):
        for at, index in enumerate(order[part]):
            ref = (mine_ref, theirs_ref)[index % 2]
            which = half if index < 2 else 1 - half
            start = width * (4 * part + at)
            ref[pl.ds(6 + 2 * which + part, 1), :] = up_ref[:, start : start + width]


def collect(place, turn_sums, qkv_sums, up_sums):
    width = D // 4
    return pl.pallas_call(
        collect_kernel,
        name="collect",
        in_specs=[pl.BlockSpec(memory_space=pltpu.SMEM)]
        + [pl.BlockSpec(memory_space=pltpu.VMEM)] * 3,
        out_shape=[like((10, width), F32)] * 2,
    )(place, turn_sums, qkv_sums, up_sums)


def hand_out_kernel(a_ref, b_ref, c_ref, d_ref, *outs):
    early = a_ref[...] + b_ref[...]
    late = c_ref[...] + d_ref[...]
    width = a_ref.shape[1]
    for at in range(6):
        outs[at][...] = early[at, :]
    for at in range(4):
        outs[6][width * at : width * (at + 1)] = early[6 + at, :]
    for at in range(2):
        outs[7 + at][...] = late[at, :]


def hand_out(early, early_got, late, late_got):
    width = early.shape[1]
    one = like((width,), F32)
    return pl.pallas_call(
        hand_out_kernel,
        name="hand_out",
        out_shape=[one] * 6 + [like((4 * width,), F32)] + [one] * 2,
    )(early, early_got, late, late_got)


def local(
    sizes,
    inputs,
    query_weight,
    key_weight,
    value_weight,
    query_bias,
    value_bias,
    out_weight,
    out_bias,
    up_weight,
    up_bias,
    down_weight,
    down_bias,
    first_gain,
    first_shift,
    second_gain,
    second_shift,
    cotangent,
):
    n_dp, n_row, n_xa, n_core = sizes
    my_x = lax.axis_index("xa")
    my_core = lax.axis_index("core")
    my_row = lax.axis_index("row")
    my_half = lax.axis_index("dp") % 2
    place = jnp.stack([my_core, my_x, my_half]).astype(jnp.int32)
    tokens_here, width = inputs.shape
    images = tokens_here // SEQ
    held = images // n_xa
    rows = held * PAD
    half = up_weight.shape[1] // 2
    quarter = half // 2
    heads_half = width // 2
    three = 3 * heads_half

    def swap(value, axis, size, bit=1):
        return lax.ppermute(value, axis, [(at, at ^ bit) for at in range(size)])

    def across(value):
        return swap(value, "xa", n_xa)

    def beside(value):
        return swap(value, "core", n_core)

    def over(value):
        return swap(value, "dp", n_dp)

    def pick(value, at, axis):
        return lax.dynamic_index_in_dim(value, at, axis, keepdims=False)

    def in_order(mine, other, at):
        return jnp.where(at == 0, mine, other), jnp.where(at == 0, other, mine)

    def after(value, *others):
        return lax.optimization_barrier((value, *others))[0]

    def halves(value, axis):
        cut = value.shape[axis] // 2
        both = value.reshape(value.shape[:axis] + (2, cut) + value.shape[axis + 1 :])
        return pick(both, my_half, axis), pick(both, my_half ^ 1, axis)

    count = held * SEQ

    def send_tokens(value):
        return lax.dynamic_slice_in_dim(value, (my_x ^ 1) * count, count, 0)

    def wide_tokens(value, got):
        mine = lax.dynamic_slice_in_dim(value, my_x * count, count, 0)
        pair = jnp.concatenate([mine, got], axis=1).reshape(held, SEQ, 2 * width)
        pair = jnp.pad(pair, ((0, 0), (0, PAD - SEQ), (0, 0))).reshape(rows, 2 * width)
        other = beside(pair)
        left, right = in_order(pair, other, my_core)
        first_left, second_left = in_order(left[:, :width], left[:, width:], my_x)
        first_right, second_right = in_order(right[:, :width], right[:, width:], my_x)
        return jnp.concatenate([first_left, first_right, second_left, second_right], axis=1)

    attn_shard = jnp.concatenate(
        [halves(item, 1)[0] for item in (query_weight, key_weight, value_weight)]
        + [halves(out_weight, 0)[0].T],
        axis=1,
    )
    input_leaves = send_tokens(inputs)
    attn_shard = after(attn_shard, input_leaves)
    input_got = across(input_leaves)
    pieces = [attn_shard] + [
        lax.ppermute(attn_shard, "row", [(at, (at + shift) % n_row) for at in range(n_row)])
        for shift in range(1, n_row)
    ]
    cut = 2 * heads_half
    first_own = jnp.zeros((D, cut), BF16)
    second_own = jnp.zeros((D, cut), BF16)
    for shift, piece in enumerate(pieces):
        start = (my_row - shift) % n_row * (D // n_row)
        first_own = lax.dynamic_update_slice(first_own, piece[:, :cut], (start, 0))
        second_own = lax.dynamic_update_slice(second_own, piece[:, cut:], (start, 0))
    first_far, second_oth = across(first_own), over(second_own)
    first_oth, second_far = over(first_own), across(second_own)

    small = pack(
        (
            out_bias,
            down_bias,
            first_gain,
            first_shift,
            second_gain,
            second_shift,
            query_bias,
            value_bias,
        ),
        up_bias,
    )
    small_far = across(small)
    vectors, qkv_bias, tile_bias = unpack(
        place, small, small_far, beside(small), beside(small_far)
    )
    out_bias_all, down_bias_all, gain_one, shift_one, gain_two, shift_two = (
        (vectors, pl.BlockSpec((None, 1, D), lambda i, *_, at=at: (at, 0, 0))) for at in range(6)
    )
    wide_input = wide_tokens(inputs, input_got)
    first_far_oth = over(after(first_far, wide_input, qkv_bias))
    second_far_oth = across(after(second_oth, wide_input, qkv_bias))

    def gather(part):
        up_part = halves(up_weight, 1)[0][:, quarter * part : quarter * (part + 1)]
        down_part = halves(down_weight, 0)[0][quarter * part : quarter * (part + 1)].T
        shard = after(jnp.concatenate([up_part, down_part], axis=1), first_own, second_own)
        return lax.all_gather(shard, "row", axis=0, tiled=True)

    own_a, own_b = gather(0), gather(1)
    grad_leaves = after(send_tokens(cotangent), first_far_oth)
    wide_grad = wide_tokens(cotangent, across(grad_leaves))

    wide_one, qkv, attn_weights = norm_qkv(
        wide_input,
        gain_one,
        shift_one,
        qkv_bias,
        (
            first_own,
            second_own,
            first_far,
            second_far,
            first_oth,
            second_oth,
            first_far_oth,
            second_far_oth,
        ),
    )
    oth_a, far_a = over(own_a), across(own_a)
    oth_b, far_b = over(own_b), across(own_b)
    attended, probs = attend(qkv)
    mixed = mm_nt(attended, attn_weights[:, 4 * three :]).astype(BF16)
    far_oth_a = over(after(far_a, mixed))
    middle_sum, wide_two = middle(
        wide_input, mixed, beside(mixed), out_bias_all, gain_two, shift_two
    )
    far_oth_b = across(after(oth_b, wide_two))
    plan = (0, 1, 2, 3, 4, 6, 5, 7)
    gate, pre, low_mine, low_theirs, lifted_two, up_sums = mlp(
        place,
        wide_two,
        wide_grad,
        tile_bias,
        (own_a, far_a, oth_a, far_oth_a, own_b, far_b, oth_b, far_oth_b),
        plan,
    )

    def wide_add(mine, got):
        return (mine.astype(F32) + got.astype(F32)).astype(BF16)

    def same_half(value):
        if n_dp == 2:
            return value
        groups = [[at + bit for at in range(0, n_dp, 2)] for bit in range(2)]
        return lax.psum(value.astype(F32), "dp", axis_index_groups=groups).astype(BF16)

    def scatter(value):
        return lax.psum_scatter(value, "row", scatter_dimension=0, tiled=True)

    def tiles(value, first, end):
        return value[:, quarter * first : quarter * end]

    lifted_other = beside(lifted_two)
    low_other = beside(low_theirs)
    down_all = mm_tn(wide_grad, gate).astype(BF16)
    down_piece = scatter(down_all)
    up_over = mm_tn(after(wide_two, down_all), tiles(pre, 2, 4)).astype(BF16)
    up_across = mm_tn(after(wide_two, down_all), tiles(pre, 6, 8)).astype(BF16)
    up_over_got, up_across_got = over(up_over), across(up_across)

    middle_grad, attn_grad, head_grad, turn_sums, out_mine, out_theirs = turn(
        place,
        middle_sum,
        wide_grad,
        lifted_two,
        after(lifted_other, down_all, up_over, up_across),
        low_mine,
        low_other,
        gain_two,
        down_bias_all,
        attn_weights,
    )
    up_over_got, up_across_got, _ = lax.optimization_barrier(
        (up_over_got, up_across_got, attn_grad)
    )
    up_a = wide_add(mm_tn(wide_two, tiles(pre, 0, 2)), up_over_got)
    up_b = wide_add(mm_tn(wide_two, tiles(pre, 4, 6)), up_across_got)
    up_a_got, up_b_got = across(up_a[:, quarter:]), over(up_b[:, quarter:])
    out_got = across(after(out_theirs, up_a))
    dqkv, qkv_sums = attend_back(qkv, probs, after(head_grad, up_a, up_b))

    def to_feature_blocks(mine, got, dtype):
        first, second = in_order(mine.astype(dtype), got.astype(dtype), my_x)
        both = jnp.concatenate([first, second]).reshape(images, PAD, width)
        return both[:, :SEQ].reshape(tokens_here, width)

    far_oth = mm_tn(wide_one, dqkv[:, 3 * three :]).astype(BF16)
    near_oth = mm_tn(wide_one, dqkv[:, 2 * three : 3 * three]).astype(BF16)
    far_oth_got, near_oth_got = over(far_oth), over(near_oth)
    lifted_one = mm_nt(
        after(dqkv, far_oth, near_oth), attn_weights[:, : 4 * three]
    ).astype(BF16)
    lifted_one_other = beside(lifted_one)

    out_all = mm_tn(after(attn_grad, lifted_one), attended).astype(BF16)
    out_over_got = over(out_all[:, 2 * heads_half :])
    mine_early, theirs_early = collect(place, turn_sums, qkv_sums, up_sums)
    early = mine_early + across(theirs_early)

    far_oth_got = after(far_oth_got, out_all)
    far_own = wide_add(mm_tn(wide_one, dqkv[:, three : 2 * three]), far_oth_got)
    far_own_got = across(far_own)
    near_own = wide_add(mm_tn(wide_one, dqkv[:, :three]), near_oth_got)
    out_own = wide_add(out_all[:, : 2 * heads_half], after(out_over_got, near_own))
    out_far_got = across(out_own[:, heads_half:])
    input_mine, input_theirs, late_mine, late_theirs = last(
        place, wide_input, middle_grad, lifted_one, after(lifted_one_other, out_own), gain_one
    )
    outputs = to_feature_blocks(out_mine, after(out_got, input_mine), BF16)

    near_sum = wide_add(near_own, after(far_own_got, input_mine))
    strip = D // n_row

    def rows_of(value, shift):
        return lax.dynamic_slice_in_dim(value, (my_row + shift) % n_row * strip, strip, 0)

    qkv_total = rows_of(near_sum, 0).astype(F32)
    for shift in range(1, n_row):
        got = lax.ppermute(
            rows_of(near_sum, shift), "row", [(at, (at + shift) % n_row) for at in range(n_row)]
        )
        qkv_total = qkv_total + got.astype(F32)
    qkv_piece = same_half(qkv_total.astype(BF16))
    qkv_other = over(qkv_piece)

    input_theirs = after(input_theirs, far_own_got)
    input_grad = to_feature_blocks(input_mine, across(input_theirs), F32)

    up_piece = same_half(
        scatter(
            jnp.concatenate(
                [
                    wide_add(up_a[:, :quarter], up_a_got),
                    wide_add(up_b[:, :quarter], up_b_got),
                    wide_add(out_own[:, :heads_half], out_far_got),
                ],
                axis=1,
            )
        )
    )
    up_other = over(up_piece)

    def some(value, *which):
        return jnp.concatenate([tiles(value, at, at + 1) for at in which], axis=1)

    down_x = wide_add(some(down_piece, 0, 4, 2, 5), across(some(down_piece, 1, 6, 3, 7)))
    down_got = over(down_x)
    down_total = down_x.astype(F32) + jnp.concatenate(
        [down_got[:, half:], down_got[:, :half]], axis=1
    ).astype(F32)
    if n_dp > 2:
        groups = [[at + bit for at in range(0, n_dp, 2)] for bit in range(2)]
        down_total = lax.psum(down_total, "dp", axis_index_groups=groups)
    down_first, down_second = in_order(down_total[:, :half], down_total[:, half:], my_half)
    down_grad = jnp.concatenate([down_first, down_second], axis=1).T

    def both_halves(mine, other, low, high):
        first, second = in_order(mine[:, low:high], other[:, low:high], my_half)
        return jnp.concatenate([first, second], axis=1).astype(F32)

    up_grad = both_halves(up_piece, up_other, 0, half)
    out_grad = both_halves(up_piece, up_other, half, half + heads_half).T
    query_grad, key_grad, value_grad = (
        both_halves(qkv_piece, qkv_other, heads_half * at, heads_half * (at + 1))
        for at in range(3)
    )

    late = late_mine + across(late_theirs)
    steps = [("row", n_row, 1 << bit) for bit in range(n_row.bit_length() - 1)]
    steps += [("dp", n_dp, 1 << bit) for bit in range(n_dp.bit_length() - 1)]
    for step in steps[:-1]:
        early, late = early + swap(early, *step), late + swap(late, *step)
    sums = hand_out(early, swap(early, *steps[-1]), late, swap(late, *steps[-1]))

    return (
        outputs,
        input_grad,
        query_grad,
        key_grad,
        value_grad,
        sums[0],
        sums[1],
        out_grad,
        sums[2],
        up_grad,
        sums[6],
        down_grad,
        sums[3],
        sums[7],
        sums[8],
        sums[4],
        sums[5],
    )


def solution(mesh):
    n_dp, n_row, n_col = (mesh.shape[name] for name in ("dp", "row", "col"))
    sizes = (n_dp, n_row, n_col // 2, 2)
    split = Mesh(mesh.devices.reshape(sizes), ("dp", "row", "xa", "core"))
    col = ("xa", "core")
    tokens, rows, cols, vec = P(("dp", "row"), col), P("row", col), P(col, "row"), P(col)
    in_specs = (
        (tokens, rows, rows, rows, vec, vec, cols, vec, rows, vec, cols)
        + (vec,) * 5
        + (tokens,)
    )
    out_specs = (
        (tokens, tokens, rows, rows, rows, vec, vec, cols, vec, rows, vec, cols) + (vec,) * 5
    )
    return jax.shard_map(
        functools.partial(local, sizes),
        mesh=split,
        in_specs=in_specs,
        out_specs=out_specs,
        check_vma=False,
    )
```

```python
import functools
import math

import jax
import jax.numpy as jnp
from jax import lax
from jax.experimental import pallas as pl
from jax.experimental.pallas import tpu as pltpu
from jax.sharding import Mesh, PartitionSpec as P


D = 1024
HD = 64
SEQ = 577
PAD = 592
TM = 296
EPS = 1e-06
F32 = jnp.float32
BF16 = jnp.bfloat16
VMEM_LIMIT = 60 * 1024 * 1024
ROOT_HALF = math.sqrt(0.5)
DENSITY = 1.0 / math.sqrt(2.0 * math.pi)


def mm(a, b):
    return lax.dot_general(a, b, (((1,), (0,)), ((), ())), preferred_element_type=F32)


def mm_nt(a, b):
    return lax.dot_general(a, b, (((1,), (1,)), ((), ())), preferred_element_type=F32)


def mm_tn(a, b):
    return lax.dot_general(a, b, (((0,), (0,)), ((), ())), preferred_element_type=F32)


def row_mean(v):
    return jnp.sum(v, axis=1, keepdims=True) * (1.0 / D)


def col_sum(v):
    return jnp.sum(v, axis=0, keepdims=True)


def stats(rows):
    middle = row_mean(rows)
    spread = row_mean(rows * rows) - middle * middle
    return middle, lax.rsqrt(spread + EPS)


def params(n):
    return pltpu.CompilerParams(
        dimension_semantics=("arbitrary",) * n, vmem_limit_bytes=VMEM_LIMIT
    )


def cost(flops, moved, exps=0):
    return pl.CostEstimate(flops=int(flops), bytes_accessed=int(moved), transcendentals=int(exps))


def like(shape, dtype):
    return jax.ShapeDtypeStruct(shape, dtype)


def row_spec(cols):
    return pl.BlockSpec((TM, cols), lambda i, *_: (i, 0))


def fixed(shape):
    return pl.BlockSpec(shape, lambda *_: (0,) * len(shape))


def held_once(shape):
    return pl.BlockSpec(shape, lambda *_: (0,) * len(shape), pipeline_mode=pl.Buffered(1))


def add_up(ref, first, part):
    @pl.when(first)
    def _():
        ref[...] = part

    @pl.when(jnp.logical_not(first))
    def _():
        ref[...] += part


def norm_qkv_kernel(x_ref, gain_ref, shift_ref, bias_ref, *refs):
    blocks, (n_ref, o_ref, w_ref) = refs[:8], refs[8:]
    one = blocks[1].shape[1] // 2

    @pl.when(pl.program_id(0) == 0)
    def _():
        for place in range(4):
            first, second = blocks[2 * place], blocks[2 * place + 1]
            start = 3 * one * place
            w_ref[:, start : start + 2 * one] = first[...]
            w_ref[:, start + 2 * one : start + 3 * one] = second[:, :one]
            w_ref[:, (12 + place) * one : (13 + place) * one] = second[:, one:]

    x = x_ref[...].astype(F32)
    middle, scaled = stats(x)
    n = (((x - middle) * scaled) * gain_ref[...] + shift_ref[...]).astype(BF16)
    n_ref[...] = n
    o_ref[...] = (mm(n, w_ref[:, : 12 * one]) + bias_ref[...]).astype(BF16)


def norm_qkv(x, gain, shift, bias, blocks):
    rows = x.shape[0]
    wide = blocks[0].shape[1]
    out = 6 * wide
    return pl.pallas_call(
        norm_qkv_kernel,
        grid=(rows // TM,),
        name="norm_qkv",
        in_specs=[row_spec(D), gain[1], shift[1], fixed((1, out))] + [held_once((D, wide))] * 8,
        out_specs=[row_spec(D), row_spec(out), held_once((D, 8 * wide))],
        out_shape=[like((rows, D), BF16), like((rows, out), BF16), like((D, 8 * wide), BF16)],
        compiler_params=params(1),
        cost_estimate=cost(2 * rows * D * out, 16 * rows * D),
    )(x, gain[0], shift[0], bias, *blocks)


def attend_kernel(qkv_ref, o_ref, p_ref):
    live = lax.broadcasted_iota(jnp.int32, (1, PAD), 1) < SEQ
    step = 2 * HD
    for h in range(2):
        q, k, v = (qkv_ref[:, step * w + HD * h : step * w + HD * (h + 1)] for w in range(3))
        s = mm_nt(q * jnp.asarray(0.125, BF16), k)
        s = jnp.where(live, s, -1e30)
        e = jnp.exp(s - jnp.max(s, axis=1, keepdims=True))
        p = (e * (1.0 / jnp.sum(e, axis=1, keepdims=True))).astype(BF16)
        p_ref[h] = p
        o_ref[:, HD * h : HD * (h + 1)] = mm(p, v).astype(BF16)


def attend(qkv):
    rows, cols = qkv.shape
    pairs = cols // (6 * HD)
    held = rows // PAD
    return pl.pallas_call(
        attend_kernel,
        grid=(pairs, held),
        name="attend",
        in_specs=[pl.BlockSpec((PAD, 6 * HD), lambda p, i: (i, p))],
        out_specs=[
            pl.BlockSpec((PAD, 2 * HD), lambda p, i: (i, p)),
            pl.BlockSpec((None, 2, PAD, PAD), lambda p, i: (i, p, 0, 0)),
        ],
        out_shape=[like((rows, cols // 3), BF16), like((held, 2 * pairs, PAD, PAD), BF16)],
        compiler_params=params(2),
        cost_estimate=cost(16 * rows * PAD * cols, 40 * rows * D, 4 * rows * PAD * pairs),
    )(qkv)


def attend_back_kernel(qkv_ref, p_ref, g_ref, d_ref, sum_ref):
    step = 2 * HD
    for h in range(2):
        q, k, v = (qkv_ref[:, step * w + HD * h : step * w + HD * (h + 1)] for w in range(3))
        g = g_ref[:, HD * h : HD * (h + 1)]
        pb = p_ref[h]
        p = pb.astype(F32)
        dp = mm_nt(g, v)
        z = jnp.sum(p * dp, axis=1, keepdims=True)
        ds = (p * (dp - z)).astype(BF16)
        parts = (mm(ds, k) * 0.125, mm_tn(ds, q) * 0.125, mm_tn(pb, g))
        for w, part in enumerate(parts):
            d_ref[:, step * w + HD * h : step * w + HD * (h + 1)] = part.astype(BF16)
    add_up(sum_ref, pl.program_id(1) == 0, col_sum(d_ref[...].astype(F32)))


def attend_back(qkv, probs, grads):
    rows, cols = qkv.shape
    pairs = cols // (6 * HD)
    held = rows // PAD
    three = pl.BlockSpec((PAD, 6 * HD), lambda p, i: (i, p))
    return pl.pallas_call(
        attend_back_kernel,
        grid=(pairs, held),
        name="attend_back",
        in_specs=[
            three,
            pl.BlockSpec((None, 2, PAD, PAD), lambda p, i: (i, p, 0, 0)),
            pl.BlockSpec((PAD, 2 * HD), lambda p, i: (i, p)),
        ],
        out_specs=[three, pl.BlockSpec((1, 6 * HD), lambda p, i: (0, p))],
        out_shape=[like((rows, cols), BF16), like((1, cols), F32)],
        compiler_params=params(2),
        cost_estimate=cost(20 * rows * PAD * cols, 50 * rows * D),
    )(qkv, probs, grads)


def middle_kernel(x_ref, a_ref, b_ref, bias_ref, gain_ref, shift_ref, h_ref, n_ref):
    h = x_ref[...].astype(F32) + (a_ref[...].astype(F32) + b_ref[...].astype(F32)) + bias_ref[...]
    h_ref[...] = h
    middle, scaled = stats(h)
    n_ref[...] = (((h - middle) * scaled) * gain_ref[...] + shift_ref[...]).astype(BF16)


def middle(x, a, b, bias, gain, shift):
    rows = x.shape[0]
    return pl.pallas_call(
        middle_kernel,
        grid=(rows // TM,),
        name="middle",
        in_specs=[row_spec(D)] * 3 + [bias[1], gain[1], shift[1]],
        out_specs=[row_spec(D)] * 2,
        out_shape=[like((rows, D), F32), like((rows, D), BF16)],
        compiler_params=params(1),
        cost_estimate=cost(20 * rows * D, 12 * rows * D),
    )(x, a, b, bias[0], gain[0], shift[0])


def mlp_kernel(plan, place_ref, n_ref, dy_ref, bias_ref, *refs):
    packs = refs[: len(plan)]
    g_ref, du_ref, mine_ref, theirs_ref, lift_ref, bsum_ref = refs[len(plan) : len(plan) + 6]
    low_acc, lift_acc, buf, sems = refs[len(plan) + 6 :]
    j = pl.program_id(0)
    tn = g_ref.shape[1]
    slot = lax.rem(j, 2)

    def load(tile, at):
        return pltpu.make_async_copy(packs[plan[tile]], buf.at[at], sems.at[at])

    @pl.when(j == 0)
    def _():
        load(0, 0).start()
        low_acc[...] = jnp.zeros_like(low_acc)
        lift_acc[...] = jnp.zeros_like(lift_acc)

    for tile in range(1, len(plan)):

        @pl.when(j == tile - 1)
        def _(tile=tile):
            load(tile, tile % 2).start()

    load(0, slot).wait()
    up, down = buf[slot, :, :tn], buf[slot, :, tn:]
    u = mm(n_ref[...], up) + bias_ref[...]
    cdf = 0.5 * (1.0 + lax.erf(u * ROOT_HALF))
    g = (u * cdf).astype(BF16)
    slope = cdf + u * (jnp.exp(-0.5 * u * u) * DENSITY)
    g_ref[...] = g
    du = (mm(dy_ref[...], down) * slope).astype(BF16)
    du_ref[...] = du
    bsum_ref[...] = col_sum(du.astype(F32))
    low_acc[...] += mm_nt(g, down)
    lift_acc[...] += mm_nt(du, up)

    @pl.when(j == len(plan) - 1)
    def _():
        lift_ref[...] = lift_acc[...].astype(BF16)
        width = D // 4
        core = place_ref[0]
        for far in range(2):
            low = pl.multiple_of((2 * far + core) * width, width)
            other = pl.multiple_of((2 * far + 1 - core) * width, width)
            mine_ref[:, far * width : (far + 1) * width] = low_acc[:, pl.ds(low, width)]
            theirs_ref[:, far * width : (far + 1) * width] = low_acc[:, pl.ds(other, width)].astype(
                BF16
            )


def mlp(place, n2, dy, bias, packs, plan):
    rows = n2.shape[0]
    hid = bias.shape[1]
    tn = hid // len(plan)
    whole = held_once((rows, D))
    tile = pl.BlockSpec((rows, tn), lambda j, *_: (0, j))
    thin = pl.BlockSpec((1, tn), lambda j, *_: (0, j))
    return pl.pallas_call(
        functools.partial(mlp_kernel, plan),
        name="mlp",
        grid_spec=pltpu.PrefetchScalarGridSpec(
            num_scalar_prefetch=1,
            grid=(len(plan),),
            in_specs=[whole, whole, thin]
            + [pl.BlockSpec(memory_space=pl.ANY)] * len(packs),
            out_specs=[
                tile,
                tile,
                held_once((rows, D // 2)),
                held_once((rows, D // 2)),
                whole,
                thin,
            ],
            scratch_shapes=[
                pltpu.VMEM((rows, D), F32),
                pltpu.VMEM((rows, D), F32),
                pltpu.VMEM((2, D, 2 * tn), BF16),
                pltpu.SemaphoreType.DMA((2,)),
            ],
        ),
        out_shape=[
            like((rows, hid), BF16),
            like((rows, hid), BF16),
            like((rows, D // 2), F32),
            like((rows, D // 2), BF16),
            like((rows, D), BF16),
            like((1, hid), F32),
        ],
        compiler_params=params(1),
        cost_estimate=cost(8 * rows * D * hid, 24 * rows * D, 2 * rows * hid),
    )(place, n2, dy, bias, *packs)


def turn_kernel(
    place_ref, h_ref, dy_ref, a_ref, b_ref, low_ref, other_ref, gain_ref, bias_ref, w_ref,
    dh_ref, da_ref, do_ref, sums_ref, mine_ref, theirs_ref, held,
):
    h = h_ref[...]
    held[...] = h + bias_ref[...]
    core, side = place_ref[0], place_ref[1]
    width = D // 4
    low = low_ref[...] + other_ref[...].astype(F32)
    for far in range(2):
        at = pl.ds(pl.multiple_of((2 * far + core) * width, width), width)
        out = (held[:, at] + low[:, far * width : (far + 1) * width]).astype(BF16)

        @pl.when(side == far)
        def _(out=out):
            mine_ref[...] = out

        @pl.when(side != far)
        def _(out=out):
            theirs_ref[...] = out

    middle, scaled = stats(h)
    c = (h - middle) * scaled
    dn = a_ref[...].astype(F32) + b_ref[...].astype(F32)
    dy = dy_ref[...].astype(F32)
    e = dn * gain_ref[...]
    dh = dy + scaled * (e - row_mean(e) - c * row_mean(e * c))
    dh_ref[...] = dh
    da = dh.astype(BF16)
    da_ref[...] = da
    do_ref[...] = mm(da, w_ref[...]).astype(BF16)
    part = jnp.concatenate(
        [col_sum(da.astype(F32)), col_sum(dy), col_sum(dn * c), col_sum(dn)], axis=0
    )
    add_up(sums_ref, pl.program_id(0) == 0, part)


def turn(place, h, dy, a, b, low_mine, low_other, gain, bias, weights):
    rows = h.shape[0]
    wide = weights.shape[1] // 4
    width = D // 4
    return pl.pallas_call(
        turn_kernel,
        name="turn",
        grid_spec=pltpu.PrefetchScalarGridSpec(
            num_scalar_prefetch=1,
            grid=(rows // TM,),
            in_specs=[row_spec(D)] * 4
            + [row_spec(D // 2)] * 2
            + [gain[1], bias[1]]
            + [pl.BlockSpec((D, wide), lambda i, *_: (0, 3), pipeline_mode=pl.Buffered(1))],
            out_specs=[
                row_spec(D),
                row_spec(D),
                row_spec(wide),
                fixed((4, D)),
                row_spec(width),
                row_spec(width),
            ],
            scratch_shapes=[pltpu.VMEM((TM, D), F32)],
        ),
        out_shape=[
            like((rows, D), F32),
            like((rows, D), BF16),
            like((rows, wide), BF16),
            like((4, D), F32),
            like((rows, width), BF16),
            like((rows, width), BF16),
        ],
        compiler_params=params(1),
        cost_estimate=cost(2 * rows * D * wide, 20 * rows * D),
    )(place, h, dy, a, b, low_mine, low_other, gain[0], bias[0], weights)


def last_kernel(
    place_ref, x_ref, dh_ref, a_ref, b_ref, gain_ref, mine_ref, theirs_ref, sum_mine, sum_theirs, held, sums
):
    x = x_ref[...].astype(F32)
    middle, scaled = stats(x)
    c = (x - middle) * scaled
    dn = a_ref[...].astype(F32) + b_ref[...].astype(F32)
    e = dn * gain_ref[...]
    held[...] = dh_ref[...] + scaled * (e - row_mean(e) - c * row_mean(e * c))
    width = D // 4
    core, side = place_ref[0], place_ref[1]
    here = pl.ds(pl.multiple_of((2 * side + core) * width, width), width)
    there = pl.ds(pl.multiple_of((2 * (1 - side) + core) * width, width), width)
    mine_ref[...] = held[:, here]
    theirs_ref[...] = held[:, there].astype(BF16)
    i = pl.program_id(0)
    add_up(sums, i == 0, jnp.concatenate([col_sum(dn * c), col_sum(dn)], axis=0))

    @pl.when(i == pl.num_programs(0) - 1)
    def _():
        sum_mine[...] = sums[:, here]
        sum_theirs[...] = sums[:, there]


def last(place, x, dh, a, b, gain):
    rows = x.shape[0]
    width = D // 4
    return pl.pallas_call(
        last_kernel,
        name="last",
        grid_spec=pltpu.PrefetchScalarGridSpec(
            num_scalar_prefetch=1,
            grid=(rows // TM,),
            in_specs=[row_spec(D)] * 4 + [gain[1]],
            out_specs=[row_spec(width), row_spec(width), fixed((2, width)), fixed((2, width))],
            scratch_shapes=[pltpu.VMEM((TM, D), F32), pltpu.VMEM((2, D), F32)],
        ),
        out_shape=[
            like((rows, width), F32),
            like((rows, width), BF16),
            like((2, width), F32),
            like((2, width), F32),
        ],
        compiler_params=params(1),
        cost_estimate=cost(20 * rows * D, 12 * rows * D),
    )(place, x, dh, a, b, gain[0])


def pack_kernel(*refs):
    out_ref = refs[-1]
    width = refs[0].shape[0]
    for at, ref in enumerate(refs[:-2]):
        out_ref[at, :] = ref[...]
    for at in range(4):
        out_ref[len(refs) - 2 + at, :] = refs[-2][width * at : width * (at + 1)]


def pack(vectors, long_vector):
    width = vectors[0].shape[0]
    return pl.pallas_call(
        pack_kernel,
        name="pack",
        out_shape=like((len(vectors) + 4, width), F32),
    )(*vectors, long_vector)


def unpack_kernel(place_ref, own, far, own_other, far_other, vec_ref, qkv_ref, tile_ref):
    core, side, half = place_ref[0], place_ref[1], place_ref[2]
    width = own.shape[1]
    one = width // 2

    def put(ref, at_side, at_core):
        at = pl.multiple_of((2 * at_side + at_core) * width, width)
        for k in range(6):
            vec_ref[k, :, pl.ds(at, width)] = ref[k : k + 1, :]

    put(own, side, core)
    put(far, 1 - side, core)
    put(own_other, side, 1 - core)
    put(far_other, 1 - side, 1 - core)
    qkv_ref[...] = jnp.zeros_like(qkv_ref)
    blocks = ((own, half), (far, half), (own, 1 - half), (far, 1 - half))
    for at, (ref, which) in enumerate(blocks):
        cut = pl.ds(pl.multiple_of(which * one, one), one)
        qkv_ref[:, 3 * one * at : 3 * one * at + one] = ref[6:7, cut]
        qkv_ref[:, 3 * one * at + 2 * one : 3 * one * (at + 1)] = ref[7:8, cut]
    order = (0, 1, 2, 3), (0, 2, 1, 3)
    for part in range(2):
        for at, index in enumerate(order[part]):
            ref, which = blocks[index]
            start = width * (4 * part + at)
            tile_ref[:, start : start + width] = ref[pl.ds(8 + 2 * which + part, 1), :]


def unpack(place, own, far, own_other, far_other):
    width = own.shape[1]
    return pl.pallas_call(
        unpack_kernel,
        name="unpack",
        in_specs=[pl.BlockSpec(memory_space=pltpu.SMEM)]
        + [pl.BlockSpec(memory_space=pltpu.VMEM)] * 4,
        out_shape=[like((6, 1, D), F32), like((1, 6 * width), F32), like((1, 8 * width), F32)],
    )(place, own, far, own_other, far_other)


def collect_kernel(place_ref, turn_ref, qkv_ref, up_ref, a_ref, b_ref, mine_ref, theirs_ref):
    core, side, half = place_ref[0], place_ref[1], place_ref[2]
    width = mine_ref.shape[1]
    one = width // 2
    for ref, at_side in ((mine_ref, side), (theirs_ref, 1 - side)):
        at = pl.ds(pl.multiple_of((2 * at_side + core) * width, width), width)
        ref[2:6, :] = turn_ref[:, at]
    mine_ref[10:12, :] = a_ref[...]
    theirs_ref[10:12, :] = b_ref[...]
    for at in range(4):
        ref = (mine_ref, theirs_ref)[at % 2]
        which = half if at < 2 else 1 - half
        cut = pl.ds(pl.multiple_of(which * one, one), one)
        ref[0:1, cut] = qkv_ref[:, 3 * one * at : 3 * one * at + one]
        ref[1:2, cut] = qkv_ref[:, 3 * one * at + 2 * one : 3 * one * (at + 1)]
    order = (0, 1, 2, 3), (0, 2, 1, 3)
    for part in range(2):
        for at, index in enumerate(order[part]):
            ref = (mine_ref, theirs_ref)[index % 2]
            which = half if index < 2 else 1 - half
            start = width * (4 * part + at)
            ref[pl.ds(6 + 2 * which + part, 1), :] = up_ref[:, start : start + width]


def collect(place, *sums):
    width = D // 4
    return pl.pallas_call(
        collect_kernel,
        name="collect",
        in_specs=[pl.BlockSpec(memory_space=pltpu.SMEM)]
        + [pl.BlockSpec(memory_space=pltpu.VMEM)] * 5,
        out_shape=[like((12, width), F32)] * 2,
    )(place, *sums)


def hand_out_kernel(a_ref, b_ref, *outs):
    sums = a_ref[...] + b_ref[...]
    width = a_ref.shape[1]
    for at in range(6):
        outs[at][...] = sums[at, :]
    for at in range(4):
        outs[6][width * at : width * (at + 1)] = sums[6 + at, :]
    for at in range(2):
        outs[7 + at][...] = sums[10 + at, :]


def hand_out(mine, got):
    width = mine.shape[1]
    one = like((width,), F32)
    return pl.pallas_call(
        hand_out_kernel,
        name="hand_out",
        out_shape=[one] * 6 + [like((4 * width,), F32)] + [one] * 2,
    )(mine, got)


def local(
    sizes,
    inputs,
    query_weight,
    key_weight,
    value_weight,
    query_bias,
    value_bias,
    out_weight,
    out_bias,
    up_weight,
    up_bias,
    down_weight,
    down_bias,
    first_gain,
    first_shift,
    second_gain,
    second_shift,
    cotangent,
):
    n_dp, n_row, n_xa, n_core = sizes
    my_x = lax.axis_index("xa")
    my_core = lax.axis_index("core")
    my_row = lax.axis_index("row")
    my_half = lax.axis_index("dp") % 2
    place = jnp.stack([my_core, my_x, my_half]).astype(jnp.int32)
    tokens_here, width = inputs.shape
    images = tokens_here // SEQ
    held = images // n_xa
    rows = held * PAD
    half = up_weight.shape[1] // 2
    quarter = half // 2
    heads_half = width // 2
    three = 3 * heads_half

    def swap(value, axis, size, bit=1):
        return lax.ppermute(value, axis, [(at, at ^ bit) for at in range(size)])

    def shifted(value, shift):
        return lax.ppermute(value, "row", [(at, (at + shift) % n_row) for at in range(n_row)])

    def across(value):
        return swap(value, "xa", n_xa)

    def beside(value):
        return swap(value, "core", n_core)

    def over(value):
        return swap(value, "dp", n_dp)

    def pick(value, at, axis):
        return lax.dynamic_index_in_dim(value, at, axis, keepdims=False)

    def in_order(mine, other, at):
        return jnp.where(at == 0, mine, other), jnp.where(at == 0, other, mine)

    def after(value, *others):
        return lax.optimization_barrier((value, *others))[0]

    def halves(value, axis):
        cut = value.shape[axis] // 2
        both = value.reshape(value.shape[:axis] + (2, cut) + value.shape[axis + 1 :])
        return pick(both, my_half, axis), pick(both, my_half ^ 1, axis)

    count = held * SEQ

    def send_tokens(value):
        return lax.dynamic_slice_in_dim(value, (my_x ^ 1) * count, count, 0)

    def wide_tokens(value, got):
        mine = lax.dynamic_slice_in_dim(value, my_x * count, count, 0)
        pair = jnp.concatenate([mine, got], axis=1).reshape(held, SEQ, 2 * width)
        pair = jnp.pad(pair, ((0, 0), (0, PAD - SEQ), (0, 0))).reshape(rows, 2 * width)
        other = beside(pair)
        left, right = in_order(pair, other, my_core)
        first_left, second_left = in_order(left[:, :width], left[:, width:], my_x)
        first_right, second_right = in_order(right[:, :width], right[:, width:], my_x)
        return jnp.concatenate([first_left, first_right, second_left, second_right], axis=1)

    attn_shard = jnp.concatenate(
        [halves(item, 1)[0] for item in (query_weight, key_weight, value_weight)]
        + [halves(out_weight, 0)[0].T],
        axis=1,
    )
    input_leaves = send_tokens(inputs)
    attn_shard = after(attn_shard, input_leaves)
    input_got = across(input_leaves)
    pieces = [attn_shard] + [shifted(attn_shard, shift) for shift in range(1, n_row)]
    cut = 2 * heads_half
    first_own = jnp.zeros((D, cut), BF16)
    second_own = jnp.zeros((D, cut), BF16)
    for shift, piece in enumerate(pieces):
        start = (my_row - shift) % n_row * (D // n_row)
        first_own = lax.dynamic_update_slice(first_own, piece[:, :cut], (start, 0))
        second_own = lax.dynamic_update_slice(second_own, piece[:, cut:], (start, 0))
    first_far, second_oth = across(first_own), over(second_own)
    first_oth, second_far = over(first_own), across(second_own)

    small = pack(
        (
            out_bias,
            down_bias,
            first_gain,
            first_shift,
            second_gain,
            second_shift,
            query_bias,
            value_bias,
        ),
        up_bias,
    )
    small_far = across(small)
    vectors, qkv_bias, tile_bias = unpack(
        place, small, after(small_far, first_own, second_own), beside(small), beside(small_far)
    )
    out_bias_all, down_bias_all, gain_one, shift_one, gain_two, shift_two = (
        (vectors, pl.BlockSpec((None, 1, D), lambda i, *_, at=at: (at, 0, 0))) for at in range(6)
    )
    wide_input = wide_tokens(inputs, after(input_got, first_own, second_own))
    first_far_oth = over(after(first_far, wide_input, qkv_bias))
    second_far_oth = across(after(second_oth, wide_input, qkv_bias))

    def gather(part):
        up_part = halves(up_weight, 1)[0][:, quarter * part : quarter * (part + 1)]
        down_part = halves(down_weight, 0)[0][quarter * part : quarter * (part + 1)].T
        shard = after(jnp.concatenate([up_part, down_part], axis=1), first_own, second_own)
        return lax.all_gather(shard, "row", axis=0, tiled=True)

    own_a, own_b = gather(0), gather(1)
    grad_got = across(after(send_tokens(cotangent), wide_input))

    wide_one, qkv, attn_weights = norm_qkv(
        wide_input,
        gain_one,
        shift_one,
        qkv_bias,
        (
            first_own,
            second_own,
            first_far,
            second_far,
            first_oth,
            second_oth,
            first_far_oth,
            second_far_oth,
        ),
    )
    oth_a, far_a = over(own_a), across(own_a)
    oth_b, far_b = over(own_b), across(own_b)
    attended, probs = attend(qkv)
    mixed = mm_nt(attended, attn_weights[:, 4 * three :]).astype(BF16)
    mixed_other = beside(mixed)
    wide_grad = wide_tokens(cotangent, after(grad_got, mixed))
    far_oth_a = over(after(far_a, mixed))
    middle_sum, wide_two = middle(
        wide_input, mixed, after(mixed_other, wide_grad), out_bias_all, gain_two, shift_two
    )
    far_oth_b = across(after(oth_b, wide_two))
    plan = (0, 1, 2, 3, 4, 6, 5, 7)
    gate, pre, low_mine, low_theirs, lifted_two, up_sums = mlp(
        place,
        wide_two,
        wide_grad,
        tile_bias,
        (own_a, far_a, oth_a, far_oth_a, own_b, far_b, oth_b, far_oth_b),
        plan,
    )

    def wide_add(mine, got):
        return (mine.astype(F32) + got.astype(F32)).astype(BF16)

    def same_half(value):
        if n_dp == 2:
            return value
        groups = [[at + bit for at in range(0, n_dp, 2)] for bit in range(2)]
        return lax.psum(value.astype(F32), "dp", axis_index_groups=groups).astype(BF16)

    def scatter(value):
        return lax.psum_scatter(value, "row", scatter_dimension=0, tiled=True)

    def tiles(value, first, end):
        return value[:, quarter * first : quarter * end]

    lifted_other = beside(lifted_two)
    low_other = beside(low_theirs)
    up_over = mm_tn(wide_two, tiles(pre, 2, 4)).astype(BF16)
    up_across = mm_tn(wide_two, tiles(pre, 6, 8)).astype(BF16)
    up_over_got, up_across_got = over(up_over), across(up_across)
    down_all = mm_tn(after(wide_grad, up_over, up_across), gate).astype(BF16)
    down_piece = scatter(down_all)

    middle_grad, attn_grad, head_grad, turn_sums, out_mine, out_theirs = turn(
        place,
        middle_sum,
        wide_grad,
        lifted_two,
        after(lifted_other, down_all),
        low_mine,
        low_other,
        gain_two,
        down_bias_all,
        attn_weights,
    )
    out_all = mm_tn(attn_grad, attended).astype(BF16)
    out_over_got = over(out_all[:, 2 * heads_half :])
    up_over_got, up_across_got, _ = lax.optimization_barrier((up_over_got, up_across_got, out_all))
    up_a = wide_add(mm_tn(wide_two, tiles(pre, 0, 2)), up_over_got)
    up_b = wide_add(mm_tn(wide_two, tiles(pre, 4, 6)), up_across_got)
    up_a_got, up_b_got = across(up_a[:, quarter:]), over(up_b[:, quarter:])
    out_got = across(after(out_theirs, up_a))
    dqkv, qkv_sums = attend_back(qkv, probs, after(head_grad, up_a, up_b))

    def to_feature_blocks(mine, got, dtype):
        first, second = in_order(mine.astype(dtype), got.astype(dtype), my_x)
        both = jnp.concatenate([first, second]).reshape(images, PAD, width)
        return both[:, :SEQ].reshape(tokens_here, width)

    split = 3 * three + cut
    far_oth_qk = mm_tn(wide_one, dqkv[:, 3 * three : split]).astype(BF16)
    far_oth_v = mm_tn(wide_one, dqkv[:, split:]).astype(BF16)
    qk_got, v_got = over(far_oth_qk), across(far_oth_v)
    lifted_one = mm_nt(
        after(dqkv, far_oth_qk, far_oth_v), attn_weights[:, : 4 * three]
    ).astype(BF16)
    lifted_one_other = beside(lifted_one)

    out_own = wide_add(out_all[:, : 2 * heads_half], after(out_over_got, lifted_one))
    out_far_got = across(out_own[:, heads_half:])
    near_oth = wide_add(
        mm_tn(wide_one, dqkv[:, 2 * three : 3 * three]),
        jnp.pad(after(v_got, out_own), ((0, 0), (cut, 0))),
    )
    near_oth_got = over(near_oth)
    far_own = wide_add(
        mm_tn(wide_one, dqkv[:, three : 2 * three]),
        jnp.pad(after(qk_got, near_oth), ((0, 0), (0, three - cut))),
    )
    far_own_got = across(far_own)
    near_own = mm_tn(after(wide_one, far_own), dqkv[:, :three])
    up_sum = jnp.concatenate(
        [
            wide_add(up_a[:, :quarter], after(up_a_got, far_own)),
            wide_add(up_b[:, :quarter], up_b_got),
            wide_add(out_own[:, :heads_half], out_far_got),
        ],
        axis=1,
    )
    up_piece = same_half(scatter(up_sum))
    input_mine, input_theirs, late_mine, late_theirs = last(
        place,
        wide_input,
        middle_grad,
        lifted_one,
        after(lifted_one_other, near_own, up_sum),
        gain_one,
    )
    mine_sums, theirs_sums = collect(
        place, turn_sums, qkv_sums, up_sums, late_mine, late_theirs
    )

    near_sum = (near_own + near_oth_got.astype(F32) + after(far_own_got, mine_sums).astype(F32)).astype(
        BF16
    )
    strip = D // n_row

    def rows_of(value, shift):
        return lax.dynamic_slice_in_dim(value, (my_row + shift) % n_row * strip, strip, 0)

    gots = [shifted(rows_of(near_sum, shift), shift) for shift in range(1, n_row)]
    input_got = across(after(input_theirs, near_sum))
    sums = mine_sums + across(after(theirs_sums, near_sum))
    steps = [("row", n_row, 1 << bit) for bit in range(n_row.bit_length() - 1)]
    steps += [("dp", n_dp, 1 << bit) for bit in range(n_dp.bit_length() - 1)]
    for step in steps[:-1]:
        sums = sums + swap(sums, *step)
    sums = hand_out(sums, swap(sums, *steps[-1]))
    outputs = to_feature_blocks(out_mine, after(out_got, near_sum), BF16)

    def some(value, *which):
        return jnp.concatenate([tiles(value, at, at + 1) for at in which], axis=1)

    down_piece = after(down_piece, near_sum)
    down_x = wide_add(some(down_piece, 0, 4, 2, 5), across(some(down_piece, 1, 6, 3, 7)))

    qkv_total = rows_of(near_sum, 0).astype(F32)
    for got in gots:
        qkv_total = qkv_total + got.astype(F32)
    qkv_piece = same_half(qkv_total.astype(BF16))
    qkv_other = over(qkv_piece)
    down_got = over(down_x)
    input_grad = to_feature_blocks(input_mine, input_got, F32)
    up_other = over(up_piece)

    down_total = down_x.astype(F32) + jnp.concatenate(
        [down_got[:, half:], down_got[:, :half]], axis=1
    ).astype(F32)
    if n_dp > 2:
        groups = [[at + bit for at in range(0, n_dp, 2)] for bit in range(2)]
        down_total = lax.psum(down_total, "dp", axis_index_groups=groups)
    down_first, down_second = in_order(down_total[:, :half], down_total[:, half:], my_half)
    down_grad = jnp.concatenate([down_first, down_second], axis=1).T

    def both_halves(mine, other, low, high):
        first, second = in_order(mine[:, low:high], other[:, low:high], my_half)
        return jnp.concatenate([first, second], axis=1).astype(F32)

    up_grad = both_halves(up_piece, up_other, 0, half)
    out_grad = both_halves(up_piece, up_other, half, half + heads_half).T
    query_grad, key_grad, value_grad = (
        both_halves(qkv_piece, qkv_other, heads_half * at, heads_half * (at + 1))
        for at in range(3)
    )

    return (
        outputs,
        input_grad,
        query_grad,
        key_grad,
        value_grad,
        sums[0],
        sums[1],
        out_grad,
        sums[2],
        up_grad,
        sums[6],
        down_grad,
        sums[3],
        sums[7],
        sums[8],
        sums[4],
        sums[5],
    )


def solution(mesh):
    n_dp, n_row, n_col = (mesh.shape[name] for name in ("dp", "row", "col"))
    sizes = (n_dp, n_row, n_col // 2, 2)
    split = Mesh(mesh.devices.reshape(sizes), ("dp", "row", "xa", "core"))
    col = ("xa", "core")
    tokens, rows, cols, vec = P(("dp", "row"), col), P("row", col), P(col, "row"), P(col)
    in_specs = (
        (tokens, rows, rows, rows, vec, vec, cols, vec, rows, vec, cols)
        + (vec,) * 5
        + (tokens,)
    )
    out_specs = (
        (tokens, tokens, rows, rows, rows, vec, vec, cols, vec, rows, vec, cols) + (vec,) * 5
    )

    def body(*args):
        return local(sizes, *args)

    return jax.shard_map(
        body, mesh=split, in_specs=in_specs, out_specs=out_specs, check_vma=False
    )
```

```python
import functools
import math

import jax
import jax.numpy as jnp
from jax import lax
from jax.experimental import pallas as pl
from jax.experimental.pallas import tpu as pltpu
from jax.sharding import Mesh, PartitionSpec as P


D = 1024
HD = 64
SEQ = 577
PAD = 592
TM = 296
EPS = 1e-06
F32 = jnp.float32
BF16 = jnp.bfloat16
VMEM_LIMIT = 60 * 1024 * 1024
ROOT_HALF = math.sqrt(0.5)
DENSITY = 1.0 / math.sqrt(2.0 * math.pi)


def mm(a, b):
    return lax.dot_general(a, b, (((1,), (0,)), ((), ())), preferred_element_type=F32)


def mm_nt(a, b):
    return lax.dot_general(a, b, (((1,), (1,)), ((), ())), preferred_element_type=F32)


def mm_tn(a, b):
    return lax.dot_general(a, b, (((0,), (0,)), ((), ())), preferred_element_type=F32)


def row_mean(v):
    return jnp.sum(v, axis=1, keepdims=True) * (1.0 / D)


def col_sum(v):
    return jnp.sum(v, axis=0, keepdims=True)


def stats(rows):
    middle = row_mean(rows)
    spread = row_mean(rows * rows) - middle * middle
    return middle, lax.rsqrt(spread + EPS)


def params(n):
    return pltpu.CompilerParams(
        dimension_semantics=("arbitrary",) * n, vmem_limit_bytes=VMEM_LIMIT
    )


def cost(flops, moved, exps=0):
    return pl.CostEstimate(flops=int(flops), bytes_accessed=int(moved), transcendentals=int(exps))


def like(shape, dtype):
    return jax.ShapeDtypeStruct(shape, dtype)


def row_spec(cols):
    return pl.BlockSpec((TM, cols), lambda i, *_: (i, 0))


def fixed(shape):
    return pl.BlockSpec(shape, lambda *_: (0,) * len(shape))


def held_once(shape):
    return pl.BlockSpec(shape, lambda *_: (0,) * len(shape), pipeline_mode=pl.Buffered(1))


def add_up(ref, first, part):
    @pl.when(first)
    def _():
        ref[...] = part

    @pl.when(jnp.logical_not(first))
    def _():
        ref[...] += part


def norm_qkv_kernel(x_ref, gain_ref, shift_ref, bias_ref, *refs):
    blocks, (n_ref, o_ref, w_ref) = refs[:8], refs[8:]
    one = blocks[1].shape[1] // 2

    @pl.when(pl.program_id(0) == 0)
    def _():
        for place in range(4):
            first, second = blocks[2 * place], blocks[2 * place + 1]
            start = 3 * one * place
            w_ref[:, start : start + 2 * one] = first[...]
            w_ref[:, start + 2 * one : start + 3 * one] = second[:, :one]
            w_ref[:, (12 + place) * one : (13 + place) * one] = second[:, one:]

    x = x_ref[...].astype(F32)
    middle, scaled = stats(x)
    n = (((x - middle) * scaled) * gain_ref[...] + shift_ref[...]).astype(BF16)
    n_ref[...] = n
    o_ref[...] = (mm(n, w_ref[:, : 12 * one]) + bias_ref[...]).astype(BF16)


def norm_qkv(x, gain, shift, bias, blocks):
    rows = x.shape[0]
    wide = blocks[0].shape[1]
    out = 6 * wide
    return pl.pallas_call(
        norm_qkv_kernel,
        grid=(rows // TM,),
        name="norm_qkv",
        in_specs=[row_spec(D), gain[1], shift[1], fixed((1, out))] + [held_once((D, wide))] * 8,
        out_specs=[row_spec(D), row_spec(out), held_once((D, 8 * wide))],
        out_shape=[like((rows, D), BF16), like((rows, out), BF16), like((D, 8 * wide), BF16)],
        compiler_params=params(1),
        cost_estimate=cost(2 * rows * D * out, 16 * rows * D),
    )(x, gain[0], shift[0], bias, *blocks)


def attend_kernel(qkv_ref, o_ref, p_ref):
    live = lax.broadcasted_iota(jnp.int32, (1, PAD), 1) < SEQ
    step = 2 * HD
    for h in range(2):
        q, k, v = (qkv_ref[:, step * w + HD * h : step * w + HD * (h + 1)] for w in range(3))
        s = mm_nt(q * jnp.asarray(0.125, BF16), k)
        s = jnp.where(live, s, -1e30)
        e = jnp.exp(s - jnp.max(s, axis=1, keepdims=True))
        p = (e * (1.0 / jnp.sum(e, axis=1, keepdims=True))).astype(BF16)
        p_ref[h] = p
        o_ref[:, HD * h : HD * (h + 1)] = mm(p, v).astype(BF16)


def attend(qkv):
    rows, cols = qkv.shape
    pairs = cols // (6 * HD)
    held = rows // PAD
    return pl.pallas_call(
        attend_kernel,
        grid=(pairs, held),
        name="attend",
        in_specs=[pl.BlockSpec((PAD, 6 * HD), lambda p, i: (i, p))],
        out_specs=[
            pl.BlockSpec((PAD, 2 * HD), lambda p, i: (i, p)),
            pl.BlockSpec((None, 2, PAD, PAD), lambda p, i: (i, p, 0, 0)),
        ],
        out_shape=[like((rows, cols // 3), BF16), like((held, 2 * pairs, PAD, PAD), BF16)],
        compiler_params=params(2),
        cost_estimate=cost(16 * rows * PAD * cols, 40 * rows * D, 4 * rows * PAD * pairs),
    )(qkv)


def attend_back_kernel(qkv_ref, p_ref, g_ref, d_ref, sum_ref):
    step = 2 * HD
    for h in range(2):
        q, k, v = (qkv_ref[:, step * w + HD * h : step * w + HD * (h + 1)] for w in range(3))
        g = g_ref[:, HD * h : HD * (h + 1)]
        pb = p_ref[h]
        p = pb.astype(F32)
        dp = mm_nt(g, v)
        z = jnp.sum(p * dp, axis=1, keepdims=True)
        ds = (p * (dp - z)).astype(BF16)
        parts = (mm(ds, k) * 0.125, mm_tn(ds, q) * 0.125, mm_tn(pb, g))
        for w, part in enumerate(parts):
            d_ref[:, step * w + HD * h : step * w + HD * (h + 1)] = part.astype(BF16)
    add_up(sum_ref, pl.program_id(1) == 0, col_sum(d_ref[...].astype(F32)))


def attend_back(qkv, probs, grads):
    rows, cols = qkv.shape
    pairs = cols // (6 * HD)
    held = rows // PAD
    three = pl.BlockSpec((PAD, 6 * HD), lambda p, i: (i, p))
    return pl.pallas_call(
        attend_back_kernel,
        grid=(pairs, held),
        name="attend_back",
        in_specs=[
            three,
            pl.BlockSpec((None, 2, PAD, PAD), lambda p, i: (i, p, 0, 0)),
            pl.BlockSpec((PAD, 2 * HD), lambda p, i: (i, p)),
        ],
        out_specs=[three, pl.BlockSpec((1, 6 * HD), lambda p, i: (0, p))],
        out_shape=[like((rows, cols), BF16), like((1, cols), F32)],
        compiler_params=params(2),
        cost_estimate=cost(20 * rows * PAD * cols, 50 * rows * D),
    )(qkv, probs, grads)


def middle_kernel(x_ref, a_ref, b_ref, bias_ref, gain_ref, shift_ref, h_ref, n_ref):
    h = x_ref[...].astype(F32) + (a_ref[...].astype(F32) + b_ref[...].astype(F32)) + bias_ref[...]
    h_ref[...] = h
    middle, scaled = stats(h)
    n_ref[...] = (((h - middle) * scaled) * gain_ref[...] + shift_ref[...]).astype(BF16)


def middle(x, a, b, bias, gain, shift):
    rows = x.shape[0]
    return pl.pallas_call(
        middle_kernel,
        grid=(rows // TM,),
        name="middle",
        in_specs=[row_spec(D)] * 3 + [bias[1], gain[1], shift[1]],
        out_specs=[row_spec(D)] * 2,
        out_shape=[like((rows, D), F32), like((rows, D), BF16)],
        compiler_params=params(1),
        cost_estimate=cost(20 * rows * D, 12 * rows * D),
    )(x, a, b, bias[0], gain[0], shift[0])


def mlp_kernel(final, place_ref, n_ref, dy_ref, bias_ref, *refs):
    packs = refs[:4]
    before = refs[4:6] if final else ()
    rest = refs[4 + len(before) :]
    g_ref, du_ref, bsum_ref = rest[:3]
    low_acc, lift_acc, buf, sems = rest[6:10] if final else rest[5:9]
    j = pl.program_id(0)
    tn = g_ref.shape[1]
    slot = lax.rem(j, 2)

    def load(tile, at):
        return pltpu.make_async_copy(packs[tile], buf.at[at], sems.at[at])

    def fetch(at):
        return pltpu.make_async_copy(before[at], rest[10 + at], sems.at[2 + at])

    @pl.when(j == 0)
    def _():
        load(0, 0).start()
        for at in range(len(before)):
            fetch(at).start()
        low_acc[...] = jnp.zeros_like(low_acc)
        lift_acc[...] = jnp.zeros_like(lift_acc)

    for tile in range(1, 4):

        @pl.when(j == tile - 1)
        def _(tile=tile):
            load(tile, tile % 2).start()

    load(0, slot).wait()
    up, down = buf[slot, :, :tn], buf[slot, :, tn:]
    u = mm(n_ref[...], up) + bias_ref[...]
    cdf = 0.5 * (1.0 + lax.erf(u * ROOT_HALF))
    g = (u * cdf).astype(BF16)
    slope = cdf + u * (jnp.exp(-0.5 * u * u) * DENSITY)
    g_ref[...] = g
    du = (mm(dy_ref[...], down) * slope).astype(BF16)
    du_ref[...] = du
    bsum_ref[...] = col_sum(du.astype(F32))
    low_acc[...] += mm_nt(g, down)
    lift_acc[...] += mm_nt(du, up)

    @pl.when(j == 3)
    def _():
        if not final:
            rest[3][...] = low_acc[...].astype(BF16)
            rest[4][...] = lift_acc[...].astype(BF16)
            return
        mine_ref, theirs_ref, lift_ref = rest[3:6]
        for at in range(2):
            fetch(at).wait()
        lift_ref[...] = (lift_acc[...] + rest[11][...].astype(F32)).astype(BF16)
        low_acc[...] += rest[10][...].astype(F32)
        width = D // 4
        core = place_ref[0]
        for far in range(2):
            low = pl.multiple_of((2 * far + core) * width, width)
            other = pl.multiple_of((2 * far + 1 - core) * width, width)
            mine_ref[:, far * width : (far + 1) * width] = low_acc[:, pl.ds(low, width)]
            theirs_ref[:, far * width : (far + 1) * width] = low_acc[:, pl.ds(other, width)].astype(
                BF16
            )


def mlp(place, n2, dy, bias, packs, before=()):
    rows = n2.shape[0]
    tn = packs[0].shape[1] // 2
    first_tile = 4 if before else 0
    whole = held_once((rows, D))
    half = held_once((rows, D // 2))
    tile = pl.BlockSpec((rows, tn), lambda j, *_: (0, j))
    swapped = pl.BlockSpec(
        (rows, tn), lambda j, *_: (0, jnp.where(j == 1, 2, jnp.where(j == 2, 1, j)))
    )
    thin = pl.BlockSpec((1, tn), lambda j, *_: (0, j))
    anywhere = pl.BlockSpec(memory_space=pl.ANY)
    out_specs = [swapped, tile, thin] + ([half, half, whole] if before else [whole, whole])
    out_shape = [like((rows, 4 * tn), BF16), like((rows, 4 * tn), BF16), like((1, 4 * tn), F32)]
    if before:
        out_shape += [like((rows, D // 2), F32), like((rows, D // 2), BF16), like((rows, D), BF16)]
    else:
        out_shape += [like((rows, D), BF16)] * 2
    return pl.pallas_call(
        functools.partial(mlp_kernel, bool(before)),
        name="mlp_second" if before else "mlp_first",
        grid_spec=pltpu.PrefetchScalarGridSpec(
            num_scalar_prefetch=1,
            grid=(4,),
            in_specs=[whole, whole, pl.BlockSpec((1, tn), lambda j, *_: (0, j + first_tile))]
            + [anywhere] * (4 + len(before)),
            out_specs=out_specs,
            scratch_shapes=[
                pltpu.VMEM((rows, D), F32),
                pltpu.VMEM((rows, D), F32),
                pltpu.VMEM((2, D, 2 * tn), BF16),
                pltpu.SemaphoreType.DMA((4,)),
            ]
            + [pltpu.VMEM((rows, D), BF16)] * len(before),
        ),
        out_shape=out_shape,
        compiler_params=params(1),
        cost_estimate=cost(32 * rows * D * tn, 20 * rows * D, 8 * rows * tn),
    )(place, n2, dy, bias, *packs, *before)


def turn_kernel(
    place_ref, h_ref, dy_ref, a_ref, b_ref, low_ref, other_ref, gain_ref, bias_ref, w_ref,
    dh_ref, da_ref, do_ref, sums_ref, mine_ref, theirs_ref, held,
):
    h = h_ref[...]
    held[...] = h + bias_ref[...]
    core, side = place_ref[0], place_ref[1]
    width = D // 4
    low = low_ref[...] + other_ref[...].astype(F32)
    for far in range(2):
        at = pl.ds(pl.multiple_of((2 * far + core) * width, width), width)
        out = (held[:, at] + low[:, far * width : (far + 1) * width]).astype(BF16)

        @pl.when(side == far)
        def _(out=out):
            mine_ref[...] = out

        @pl.when(side != far)
        def _(out=out):
            theirs_ref[...] = out

    middle, scaled = stats(h)
    c = (h - middle) * scaled
    dn = a_ref[...].astype(F32) + b_ref[...].astype(F32)
    dy = dy_ref[...].astype(F32)
    e = dn * gain_ref[...]
    dh = dy + scaled * (e - row_mean(e) - c * row_mean(e * c))
    dh_ref[...] = dh
    da = dh.astype(BF16)
    da_ref[...] = da
    do_ref[...] = mm(da, w_ref[...]).astype(BF16)
    part = jnp.concatenate(
        [col_sum(da.astype(F32)), col_sum(dy), col_sum(dn * c), col_sum(dn)], axis=0
    )
    add_up(sums_ref, pl.program_id(0) == 0, part)


def turn(place, h, dy, a, b, low_mine, low_other, gain, bias, weights):
    rows = h.shape[0]
    wide = weights.shape[1] // 4
    width = D // 4
    return pl.pallas_call(
        turn_kernel,
        name="turn",
        grid_spec=pltpu.PrefetchScalarGridSpec(
            num_scalar_prefetch=1,
            grid=(rows // TM,),
            in_specs=[row_spec(D)] * 4
            + [row_spec(D // 2)] * 2
            + [gain[1], bias[1]]
            + [pl.BlockSpec((D, wide), lambda i, *_: (0, 3), pipeline_mode=pl.Buffered(1))],
            out_specs=[
                row_spec(D),
                row_spec(D),
                row_spec(wide),
                fixed((4, D)),
                row_spec(width),
                row_spec(width),
            ],
            scratch_shapes=[pltpu.VMEM((TM, D), F32)],
        ),
        out_shape=[
            like((rows, D), F32),
            like((rows, D), BF16),
            like((rows, wide), BF16),
            like((4, D), F32),
            like((rows, width), BF16),
            like((rows, width), BF16),
        ],
        compiler_params=params(1),
        cost_estimate=cost(2 * rows * D * wide, 20 * rows * D),
    )(place, h, dy, a, b, low_mine, low_other, gain[0], bias[0], weights)


def last_kernel(
    place_ref, x_ref, dh_ref, a_ref, b_ref, gain_ref, mine_ref, theirs_ref, sum_mine, sum_theirs, held, sums
):
    x = x_ref[...].astype(F32)
    middle, scaled = stats(x)
    c = (x - middle) * scaled
    dn = a_ref[...].astype(F32) + b_ref[...].astype(F32)
    e = dn * gain_ref[...]
    held[...] = dh_ref[...] + scaled * (e - row_mean(e) - c * row_mean(e * c))
    width = D // 4
    core, side = place_ref[0], place_ref[1]
    here = pl.ds(pl.multiple_of((2 * side + core) * width, width), width)
    there = pl.ds(pl.multiple_of((2 * (1 - side) + core) * width, width), width)
    mine_ref[...] = held[:, here]
    theirs_ref[...] = held[:, there].astype(BF16)
    i = pl.program_id(0)
    add_up(sums, i == 0, jnp.concatenate([col_sum(dn * c), col_sum(dn)], axis=0))

    @pl.when(i == pl.num_programs(0) - 1)
    def _():
        sum_mine[...] = sums[:, here]
        sum_theirs[...] = sums[:, there]


def last(place, x, dh, a, b, gain):
    rows = x.shape[0]
    width = D // 4
    return pl.pallas_call(
        last_kernel,
        name="last",
        grid_spec=pltpu.PrefetchScalarGridSpec(
            num_scalar_prefetch=1,
            grid=(rows // TM,),
            in_specs=[row_spec(D)] * 4 + [gain[1]],
            out_specs=[row_spec(width), row_spec(width), fixed((2, width)), fixed((2, width))],
            scratch_shapes=[pltpu.VMEM((TM, D), F32), pltpu.VMEM((2, D), F32)],
        ),
        out_shape=[
            like((rows, width), F32),
            like((rows, width), BF16),
            like((2, width), F32),
            like((2, width), F32),
        ],
        compiler_params=params(1),
        cost_estimate=cost(20 * rows * D, 12 * rows * D),
    )(place, x, dh, a, b, gain[0])


def pack_kernel(*refs):
    out_ref = refs[-1]
    width = refs[0].shape[0]
    for at, ref in enumerate(refs[:-2]):
        out_ref[at, :] = ref[...]
    for at in range(4):
        out_ref[len(refs) - 2 + at, :] = refs[-2][width * at : width * (at + 1)]


def pack(vectors, long_vector):
    width = vectors[0].shape[0]
    return pl.pallas_call(
        pack_kernel,
        name="pack",
        out_shape=like((len(vectors) + 4, width), F32),
    )(*vectors, long_vector)


def unpack_kernel(place_ref, own, far, own_other, far_other, vec_ref, qkv_ref, tile_ref):
    core, side, half = place_ref[0], place_ref[1], place_ref[2]
    width = own.shape[1]
    one = width // 2

    def put(ref, at_side, at_core):
        at = pl.multiple_of((2 * at_side + at_core) * width, width)
        for k in range(6):
            vec_ref[k, :, pl.ds(at, width)] = ref[k : k + 1, :]

    put(own, side, core)
    put(far, 1 - side, core)
    put(own_other, side, 1 - core)
    put(far_other, 1 - side, 1 - core)
    qkv_ref[...] = jnp.zeros_like(qkv_ref)
    blocks = ((own, half), (far, half), (own, 1 - half), (far, 1 - half))
    for at, (ref, which) in enumerate(blocks):
        cut = pl.ds(pl.multiple_of(which * one, one), one)
        qkv_ref[:, 3 * one * at : 3 * one * at + one] = ref[6:7, cut]
        qkv_ref[:, 3 * one * at + 2 * one : 3 * one * (at + 1)] = ref[7:8, cut]
    order = (0, 1, 2, 3), (0, 2, 1, 3)
    for part in range(2):
        for at, index in enumerate(order[part]):
            ref, which = blocks[index]
            start = width * (4 * part + at)
            tile_ref[:, start : start + width] = ref[pl.ds(8 + 2 * which + part, 1), :]


def unpack(place, own, far, own_other, far_other):
    width = own.shape[1]
    return pl.pallas_call(
        unpack_kernel,
        name="unpack",
        in_specs=[pl.BlockSpec(memory_space=pltpu.SMEM)]
        + [pl.BlockSpec(memory_space=pltpu.VMEM)] * 4,
        out_shape=[like((6, 1, D), F32), like((1, 6 * width), F32), like((1, 8 * width), F32)],
    )(place, own, far, own_other, far_other)


def collect_kernel(
    place_ref, turn_ref, qkv_ref, up_a_ref, up_b_ref, a_ref, b_ref, mine_ref, theirs_ref
):
    core, side, half = place_ref[0], place_ref[1], place_ref[2]
    width = mine_ref.shape[1]
    one = width // 2
    for ref, at_side in ((mine_ref, side), (theirs_ref, 1 - side)):
        at = pl.ds(pl.multiple_of((2 * at_side + core) * width, width), width)
        ref[2:6, :] = turn_ref[:, at]
    mine_ref[10:12, :] = a_ref[...]
    theirs_ref[10:12, :] = b_ref[...]
    for at in range(4):
        ref = (mine_ref, theirs_ref)[at % 2]
        which = half if at < 2 else 1 - half
        cut = pl.ds(pl.multiple_of(which * one, one), one)
        ref[0:1, cut] = qkv_ref[:, 3 * one * at : 3 * one * at + one]
        ref[1:2, cut] = qkv_ref[:, 3 * one * at + 2 * one : 3 * one * (at + 1)]
    order = (0, 1, 2, 3), (0, 2, 1, 3)
    for part in range(2):
        for at, index in enumerate(order[part]):
            ref = (mine_ref, theirs_ref)[index % 2]
            which = half if index < 2 else 1 - half
            up_ref = (up_a_ref, up_b_ref)[part]
            ref[pl.ds(6 + 2 * which + part, 1), :] = up_ref[:, width * at : width * (at + 1)]


def collect(place, *sums):
    width = D // 4
    return pl.pallas_call(
        collect_kernel,
        name="collect",
        in_specs=[pl.BlockSpec(memory_space=pltpu.SMEM)]
        + [pl.BlockSpec(memory_space=pltpu.VMEM)] * 6,
        out_shape=[like((12, width), F32)] * 2,
    )(place, *sums)


def hand_out_kernel(a_ref, b_ref, *outs):
    sums = a_ref[...] + b_ref[...]
    width = a_ref.shape[1]
    for at in range(6):
        outs[at][...] = sums[at, :]
    for at in range(4):
        outs[6][width * at : width * (at + 1)] = sums[6 + at, :]
    for at in range(2):
        outs[7 + at][...] = sums[10 + at, :]


def hand_out(mine, got):
    width = mine.shape[1]
    one = like((width,), F32)
    return pl.pallas_call(
        hand_out_kernel,
        name="hand_out",
        out_shape=[one] * 6 + [like((4 * width,), F32)] + [one] * 2,
    )(mine, got)


def local(
    sizes,
    inputs,
    query_weight,
    key_weight,
    value_weight,
    query_bias,
    value_bias,
    out_weight,
    out_bias,
    up_weight,
    up_bias,
    down_weight,
    down_bias,
    first_gain,
    first_shift,
    second_gain,
    second_shift,
    cotangent,
):
    n_dp, n_row, n_xa, n_core = sizes
    my_x = lax.axis_index("xa")
    my_core = lax.axis_index("core")
    my_row = lax.axis_index("row")
    my_half = lax.axis_index("dp") % 2
    place = jnp.stack([my_core, my_x, my_half]).astype(jnp.int32)
    tokens_here, width = inputs.shape
    images = tokens_here // SEQ
    held = images // n_xa
    rows = held * PAD
    half = up_weight.shape[1] // 2
    quarter = half // 2
    heads_half = width // 2
    three = 3 * heads_half

    def swap(value, axis, size, bit=1):
        return lax.ppermute(value, axis, [(at, at ^ bit) for at in range(size)])

    def shifted(value, shift):
        return lax.ppermute(value, "row", [(at, (at + shift) % n_row) for at in range(n_row)])

    def across(value):
        return swap(value, "xa", n_xa)

    def beside(value):
        return swap(value, "core", n_core)

    def over(value):
        return swap(value, "dp", n_dp)

    def pick(value, at, axis):
        return lax.dynamic_index_in_dim(value, at, axis, keepdims=False)

    def in_order(mine, other, at):
        return jnp.where(at == 0, mine, other), jnp.where(at == 0, other, mine)

    def after(value, *others):
        return lax.optimization_barrier((value, *others))[0]

    def halves(value, axis):
        cut = value.shape[axis] // 2
        both = value.reshape(value.shape[:axis] + (2, cut) + value.shape[axis + 1 :])
        return pick(both, my_half, axis), pick(both, my_half ^ 1, axis)

    count = held * SEQ

    def send_tokens(value):
        return lax.dynamic_slice_in_dim(value, (my_x ^ 1) * count, count, 0)

    def wide_tokens(value, got):
        mine = lax.dynamic_slice_in_dim(value, my_x * count, count, 0)
        pair = jnp.concatenate([mine, got], axis=1).reshape(held, SEQ, 2 * width)
        pair = jnp.pad(pair, ((0, 0), (0, PAD - SEQ), (0, 0))).reshape(rows, 2 * width)
        other = beside(pair)
        left, right = in_order(pair, other, my_core)
        first_left, second_left = in_order(left[:, :width], left[:, width:], my_x)
        first_right, second_right = in_order(right[:, :width], right[:, width:], my_x)
        return jnp.concatenate([first_left, first_right, second_left, second_right], axis=1)

    attn_shard = jnp.concatenate(
        [halves(item, 1)[0] for item in (query_weight, key_weight, value_weight)]
        + [halves(out_weight, 0)[0].T],
        axis=1,
    )
    input_leaves = send_tokens(inputs)
    attn_shard = after(attn_shard, input_leaves)
    input_got = across(input_leaves)
    pieces = [attn_shard] + [shifted(attn_shard, shift) for shift in range(1, n_row)]
    cut = 2 * heads_half
    first_own = jnp.zeros((D, cut), BF16)
    second_own = jnp.zeros((D, cut), BF16)
    for shift, piece in enumerate(pieces):
        start = (my_row - shift) % n_row * (D // n_row)
        first_own = lax.dynamic_update_slice(first_own, piece[:, :cut], (start, 0))
        second_own = lax.dynamic_update_slice(second_own, piece[:, cut:], (start, 0))
    first_far, second_oth = across(first_own), over(second_own)
    first_oth, second_far = over(first_own), across(second_own)

    small = pack(
        (
            out_bias,
            down_bias,
            first_gain,
            first_shift,
            second_gain,
            second_shift,
            query_bias,
            value_bias,
        ),
        up_bias,
    )
    small_far = across(small)
    vectors, qkv_bias, tile_bias = unpack(
        place, small, after(small_far, first_own, second_own), beside(small), beside(small_far)
    )
    out_bias_all, down_bias_all, gain_one, shift_one, gain_two, shift_two = (
        (vectors, pl.BlockSpec((None, 1, D), lambda i, *_, at=at: (at, 0, 0))) for at in range(6)
    )
    wide_input = wide_tokens(inputs, after(input_got, first_own, second_own))
    first_far_oth = over(after(first_far, wide_input, qkv_bias))
    second_far_oth = across(after(second_oth, wide_input, qkv_bias))

    def gather(part):
        up_part = halves(up_weight, 1)[0][:, quarter * part : quarter * (part + 1)]
        down_part = halves(down_weight, 0)[0][quarter * part : quarter * (part + 1)].T
        shard = after(jnp.concatenate([up_part, down_part], axis=1), first_own, second_own)
        return lax.all_gather(shard, "row", axis=0, tiled=True)

    own_a, own_b = gather(0), gather(1)
    grad_got = across(after(send_tokens(cotangent), wide_input))

    wide_one, qkv, attn_weights = norm_qkv(
        wide_input,
        gain_one,
        shift_one,
        qkv_bias,
        (
            first_own,
            second_own,
            first_far,
            second_far,
            first_oth,
            second_oth,
            first_far_oth,
            second_far_oth,
        ),
    )
    oth_a, far_a = over(own_a), across(own_a)
    oth_b, far_b = over(own_b), across(own_b)
    attended, probs = attend(qkv)
    mixed = mm_nt(attended, attn_weights[:, 4 * three :]).astype(BF16)
    mixed_other = beside(mixed)
    wide_grad = wide_tokens(cotangent, after(grad_got, mixed))
    far_oth_a = over(after(far_a, mixed))
    middle_sum, wide_two = middle(
        wide_input, mixed, after(mixed_other, wide_grad), out_bias_all, gain_two, shift_two
    )
    far_oth_b = across(oth_b)

    def tiles(value, first, end):
        return value[:, quarter * first : quarter * end]

    gate_a, pre_a, up_sums_a, low_a, lift_a = mlp(
        place, wide_two, wide_grad, tile_bias, (own_a, far_a, oth_a, far_oth_a)
    )
    up_over = mm_tn(wide_two, tiles(pre_a, 2, 4)).astype(BF16)
    down_a = mm_tn(wide_grad, gate_a).astype(BF16)
    up_over_got = over(up_over)
    down_piece = lax.psum_scatter(down_a, "row", scatter_dimension=0, tiled=True)
    gate_b, pre_b, up_sums_b, low_mine, low_theirs, lifted_two = mlp(
        place,
        after(wide_two, up_over, down_a),
        wide_grad,
        tile_bias,
        (own_b, oth_b, far_b, far_oth_b),
        (low_a, lift_a),
    )

    def wide_add(mine, got):
        return (mine.astype(F32) + got.astype(F32)).astype(BF16)

    def same_half(value):
        if n_dp == 2:
            return value
        groups = [[at + bit for at in range(0, n_dp, 2)] for bit in range(2)]
        return lax.psum(value.astype(F32), "dp", axis_index_groups=groups).astype(BF16)

    def scatter(value):
        return lax.psum_scatter(value, "row", scatter_dimension=0, tiled=True)

    lifted_other = beside(lifted_two)
    low_other = beside(low_theirs)
    up_across = mm_tn(wide_two, tiles(pre_b, 2, 4)).astype(BF16)
    down_over = mm_tn(wide_grad, tiles(gate_b, 2, 4)).astype(BF16)
    up_across_got, down_over_got = across(up_across), over(down_over)

    middle_grad, attn_grad, head_grad, turn_sums, out_mine, out_theirs = turn(
        place,
        middle_sum,
        wide_grad,
        lifted_two,
        after(lifted_other, up_across, down_over),
        low_mine,
        low_other,
        gain_two,
        down_bias_all,
        attn_weights,
    )
    out_all = mm_tn(attn_grad, attended).astype(BF16)
    out_over_got = over(out_all[:, 2 * heads_half :])
    up_over_got, up_across_got, down_over_got, _ = lax.optimization_barrier(
        (up_over_got, up_across_got, down_over_got, out_all)
    )
    up_a = wide_add(mm_tn(wide_two, tiles(pre_a, 0, 2)), up_over_got)
    up_b = wide_add(mm_tn(wide_two, tiles(pre_b, 0, 2)), up_across_got)
    down_b = wide_add(mm_tn(wide_grad, tiles(gate_b, 0, 2)), down_over_got)
    up_a_got, up_b_got = across(up_a[:, quarter:]), over(up_b[:, quarter:])
    down_b_got = across(down_b[:, quarter:])
    out_got = across(after(out_theirs, down_b))
    dqkv, qkv_sums = attend_back(qkv, probs, after(head_grad, up_a, up_b, down_b))

    def to_feature_blocks(mine, got, dtype):
        first, second = in_order(mine.astype(dtype), got.astype(dtype), my_x)
        both = jnp.concatenate([first, second]).reshape(images, PAD, width)
        return both[:, :SEQ].reshape(tokens_here, width)

    down_piece = after(down_piece, dqkv)
    down_x_got = across(down_piece[:, half:])

    split = 3 * three + cut
    far_oth_qk = mm_tn(wide_one, dqkv[:, 3 * three : split]).astype(BF16)
    far_oth_v = mm_tn(wide_one, dqkv[:, split:]).astype(BF16)
    qk_got, v_got = over(far_oth_qk), across(far_oth_v)
    lifted_one = mm_nt(
        after(dqkv, far_oth_qk, far_oth_v), attn_weights[:, : 4 * three]
    ).astype(BF16)
    lifted_one_other = beside(lifted_one)

    out_own = wide_add(out_all[:, : 2 * heads_half], after(out_over_got, lifted_one))
    out_far_got = across(out_own[:, heads_half:])
    near_oth = wide_add(
        mm_tn(wide_one, dqkv[:, 2 * three : 3 * three]),
        jnp.pad(after(v_got, out_own), ((0, 0), (cut, 0))),
    )
    near_oth_got = over(near_oth)
    far_own = wide_add(
        mm_tn(wide_one, dqkv[:, three : 2 * three]),
        jnp.pad(after(qk_got, near_oth), ((0, 0), (0, three - cut))),
    )
    far_own_got = across(far_own)
    near_own = mm_tn(after(wide_one, far_own), dqkv[:, :three])
    up_sum = jnp.concatenate(
        [
            wide_add(up_a[:, :quarter], after(up_a_got, far_own)),
            wide_add(up_b[:, :quarter], up_b_got),
            wide_add(down_b[:, :quarter], down_b_got),
            wide_add(out_own[:, :heads_half], out_far_got),
        ],
        axis=1,
    )
    up_piece = same_half(scatter(up_sum))
    down_x = wide_add(down_piece[:, :half], after(down_x_got, far_own))
    down_y_got = over(down_x)
    input_mine, input_theirs, late_mine, late_theirs = last(
        place,
        wide_input,
        middle_grad,
        lifted_one,
        after(lifted_one_other, near_own, up_sum),
        gain_one,
    )
    mine_sums, theirs_sums = collect(
        place, turn_sums, qkv_sums, up_sums_a, up_sums_b, late_mine, late_theirs
    )

    near_sum = (near_own + near_oth_got.astype(F32) + after(far_own_got, mine_sums).astype(F32)).astype(
        BF16
    )
    strip = D // n_row

    def rows_of(value, shift):
        return lax.dynamic_slice_in_dim(value, (my_row + shift) % n_row * strip, strip, 0)

    gots = [shifted(rows_of(near_sum, shift), shift) for shift in range(1, n_row)]
    input_got = across(after(input_theirs, near_sum))
    sums = mine_sums + across(after(theirs_sums, near_sum))
    steps = [("row", n_row, 1 << bit) for bit in range(n_row.bit_length() - 1)]
    steps += [("dp", n_dp, 1 << bit) for bit in range(n_dp.bit_length() - 1)]
    for step in steps[:-1]:
        sums = sums + swap(sums, *step)
    sums = hand_out(sums, swap(sums, *steps[-1]))
    outputs = to_feature_blocks(out_mine, after(out_got, near_sum), BF16)

    qkv_total = rows_of(near_sum, 0).astype(F32)
    for got in gots:
        qkv_total = qkv_total + got.astype(F32)
    qkv_piece = same_half(qkv_total.astype(BF16))
    qkv_other = over(qkv_piece)
    input_grad = to_feature_blocks(input_mine, input_got, F32)
    up_other = over(up_piece)

    down_total = down_x.astype(F32) + jnp.concatenate(
        [down_y_got[:, quarter:], down_y_got[:, :quarter]], axis=1
    ).astype(F32)
    if n_dp > 2:
        groups = [[at + bit for at in range(0, n_dp, 2)] for bit in range(2)]
        down_total = lax.psum(down_total, "dp", axis_index_groups=groups)

    def down_half(first_part, second):
        return jnp.concatenate([first_part, tiles(second, 2, 3).astype(F32)], axis=1)

    down_first, down_second = in_order(
        down_half(down_total[:, :quarter], up_piece),
        down_half(down_total[:, quarter:], up_other),
        my_half,
    )
    down_grad = jnp.concatenate([down_first, down_second], axis=1).T

    def both_halves(mine, other, low, high):
        first, second = in_order(mine[:, low:high], other[:, low:high], my_half)
        return jnp.concatenate([first, second], axis=1).astype(F32)

    up_grad = both_halves(up_piece, up_other, 0, half)
    start = half + quarter
    out_grad = both_halves(up_piece, up_other, start, start + heads_half).T
    query_grad, key_grad, value_grad = (
        both_halves(qkv_piece, qkv_other, heads_half * at, heads_half * (at + 1))
        for at in range(3)
    )

    return (
        outputs,
        input_grad,
        query_grad,
        key_grad,
        value_grad,
        sums[0],
        sums[1],
        out_grad,
        sums[2],
        up_grad,
        sums[6],
        down_grad,
        sums[3],
        sums[7],
        sums[8],
        sums[4],
        sums[5],
    )


def solution(mesh):
    n_dp, n_row, n_col = (mesh.shape[name] for name in ("dp", "row", "col"))
    sizes = (n_dp, n_row, n_col // 2, 2)
    split = Mesh(mesh.devices.reshape(sizes), ("dp", "row", "xa", "core"))
    col = ("xa", "core")
    tokens, rows, cols, vec = P(("dp", "row"), col), P("row", col), P(col, "row"), P(col)
    in_specs = (
        (tokens, rows, rows, rows, vec, vec, cols, vec, rows, vec, cols)
        + (vec,) * 5
        + (tokens,)
    )
    out_specs = (
        (tokens, tokens, rows, rows, rows, vec, vec, cols, vec, rows, vec, cols) + (vec,) * 5
    )

    def body(*args):
        return local(sizes, *args)

    return jax.shard_map(
        body, mesh=split, in_specs=in_specs, out_specs=out_specs, check_vma=False
    )
```

```python
import functools
import math

import jax
import jax.numpy as jnp
from jax import lax
from jax.experimental import pallas as pl
from jax.experimental.pallas import tpu as pltpu
from jax.sharding import Mesh, PartitionSpec as P


D = 1024
HD = 64
SEQ = 577
PAD = 592
TM = 296
EPS = 1e-06
F32 = jnp.float32
BF16 = jnp.bfloat16
VMEM_LIMIT = 60 * 1024 * 1024
ROOT_HALF = math.sqrt(0.5)
DENSITY = 1.0 / math.sqrt(2.0 * math.pi)


def mm(a, b):
    return lax.dot_general(a, b, (((1,), (0,)), ((), ())), preferred_element_type=F32)


def mm_nt(a, b):
    return lax.dot_general(a, b, (((1,), (1,)), ((), ())), preferred_element_type=F32)


def mm_tn(a, b):
    return lax.dot_general(a, b, (((0,), (0,)), ((), ())), preferred_element_type=F32)


def row_mean(v):
    return jnp.sum(v, axis=1, keepdims=True) * (1.0 / D)


def col_sum(v):
    return jnp.sum(v, axis=0, keepdims=True)


def stats(rows):
    middle = row_mean(rows)
    spread = row_mean(rows * rows) - middle * middle
    return middle, lax.rsqrt(spread + EPS)


def params(n):
    return pltpu.CompilerParams(
        dimension_semantics=("arbitrary",) * n, vmem_limit_bytes=VMEM_LIMIT
    )


def cost(flops, moved, exps=0):
    return pl.CostEstimate(flops=int(flops), bytes_accessed=int(moved), transcendentals=int(exps))


def like(shape, dtype):
    return jax.ShapeDtypeStruct(shape, dtype)


def row_spec(cols):
    return pl.BlockSpec((TM, cols), lambda i, *_: (i, 0))


def fixed(shape):
    return pl.BlockSpec(shape, lambda *_: (0,) * len(shape))


def held_once(shape):
    return pl.BlockSpec(shape, lambda *_: (0,) * len(shape), pipeline_mode=pl.Buffered(1))


def add_up(ref, first, part):
    @pl.when(first)
    def _():
        ref[...] = part

    @pl.when(jnp.logical_not(first))
    def _():
        ref[...] += part


def norm_qkv_kernel(x_ref, gain_ref, shift_ref, bias_ref, *refs):
    blocks, (n_ref, o_ref, w_ref) = refs[:8], refs[8:]
    one = blocks[1].shape[1] // 2

    @pl.when(pl.program_id(0) == 0)
    def _():
        for place in range(4):
            first, second = blocks[2 * place], blocks[2 * place + 1]
            start = 3 * one * place
            w_ref[:, start : start + 2 * one] = first[...]
            w_ref[:, start + 2 * one : start + 3 * one] = second[:, :one]
            w_ref[:, (12 + place) * one : (13 + place) * one] = second[:, one:]

    x = x_ref[...].astype(F32)
    middle, scaled = stats(x)
    n = (((x - middle) * scaled) * gain_ref[...] + shift_ref[...]).astype(BF16)
    n_ref[...] = n
    o_ref[...] = (mm(n, w_ref[:, : 12 * one]) + bias_ref[...]).astype(BF16)


def norm_qkv(x, gain, shift, bias, blocks):
    rows = x.shape[0]
    wide = blocks[0].shape[1]
    out = 6 * wide
    return pl.pallas_call(
        norm_qkv_kernel,
        grid=(rows // TM,),
        name="norm_qkv",
        in_specs=[row_spec(D), gain[1], shift[1], fixed((1, out))] + [held_once((D, wide))] * 8,
        out_specs=[row_spec(D), row_spec(out), held_once((D, 8 * wide))],
        out_shape=[like((rows, D), BF16), like((rows, out), BF16), like((D, 8 * wide), BF16)],
        compiler_params=params(1),
        cost_estimate=cost(2 * rows * D * out, 16 * rows * D),
    )(x, gain[0], shift[0], bias, *blocks)


def attend_kernel(qkv_ref, o_ref, p_ref):
    live = lax.broadcasted_iota(jnp.int32, (1, PAD), 1) < SEQ
    step = 2 * HD
    for h in range(2):
        q, k, v = (qkv_ref[:, step * w + HD * h : step * w + HD * (h + 1)] for w in range(3))
        s = mm_nt(q * jnp.asarray(0.125, BF16), k)
        s = jnp.where(live, s, -1e30)
        e = jnp.exp(s - jnp.max(s, axis=1, keepdims=True))
        p = (e * (1.0 / jnp.sum(e, axis=1, keepdims=True))).astype(BF16)
        p_ref[h] = p
        o_ref[:, HD * h : HD * (h + 1)] = mm(p, v).astype(BF16)


def attend(qkv):
    rows, cols = qkv.shape
    pairs = cols // (6 * HD)
    held = rows // PAD
    return pl.pallas_call(
        attend_kernel,
        grid=(pairs, held),
        name="attend",
        in_specs=[pl.BlockSpec((PAD, 6 * HD), lambda p, i: (i, p))],
        out_specs=[
            pl.BlockSpec((PAD, 2 * HD), lambda p, i: (i, p)),
            pl.BlockSpec((None, 2, PAD, PAD), lambda p, i: (i, p, 0, 0)),
        ],
        out_shape=[like((rows, cols // 3), BF16), like((held, 2 * pairs, PAD, PAD), BF16)],
        compiler_params=params(2),
        cost_estimate=cost(16 * rows * PAD * cols, 40 * rows * D, 4 * rows * PAD * pairs),
    )(qkv)


def attend_back_kernel(qkv_ref, p_ref, g_ref, d_ref, sum_ref):
    step = 2 * HD
    for h in range(2):
        q, k, v = (qkv_ref[:, step * w + HD * h : step * w + HD * (h + 1)] for w in range(3))
        g = g_ref[:, HD * h : HD * (h + 1)]
        pb = p_ref[h]
        p = pb.astype(F32)
        dp = mm_nt(g, v)
        z = jnp.sum(p * dp, axis=1, keepdims=True)
        ds = (p * (dp - z)).astype(BF16)
        parts = (mm(ds, k) * 0.125, mm_tn(ds, q) * 0.125, mm_tn(pb, g))
        for w, part in enumerate(parts):
            d_ref[:, step * w + HD * h : step * w + HD * (h + 1)] = part.astype(BF16)
    add_up(sum_ref, pl.program_id(1) == 0, col_sum(d_ref[...].astype(F32)))


def attend_back(qkv, probs, grads):
    rows, cols = qkv.shape
    pairs = cols // (6 * HD)
    held = rows // PAD
    three = pl.BlockSpec((PAD, 6 * HD), lambda p, i: (i, p))
    return pl.pallas_call(
        attend_back_kernel,
        grid=(pairs, held),
        name="attend_back",
        in_specs=[
            three,
            pl.BlockSpec((None, 2, PAD, PAD), lambda p, i: (i, p, 0, 0)),
            pl.BlockSpec((PAD, 2 * HD), lambda p, i: (i, p)),
        ],
        out_specs=[three, pl.BlockSpec((1, 6 * HD), lambda p, i: (0, p))],
        out_shape=[like((rows, cols), BF16), like((1, cols), F32)],
        compiler_params=params(2),
        cost_estimate=cost(20 * rows * PAD * cols, 50 * rows * D),
    )(qkv, probs, grads)


def middle_kernel(x_ref, a_ref, b_ref, bias_ref, gain_ref, shift_ref, h_ref, n_ref):
    h = x_ref[...].astype(F32) + (a_ref[...].astype(F32) + b_ref[...].astype(F32)) + bias_ref[...]
    h_ref[...] = h
    middle, scaled = stats(h)
    n_ref[...] = (((h - middle) * scaled) * gain_ref[...] + shift_ref[...]).astype(BF16)


def middle(x, a, b, bias, gain, shift):
    rows = x.shape[0]
    return pl.pallas_call(
        middle_kernel,
        grid=(rows // TM,),
        name="middle",
        in_specs=[row_spec(D)] * 3 + [bias[1], gain[1], shift[1]],
        out_specs=[row_spec(D)] * 2,
        out_shape=[like((rows, D), F32), like((rows, D), BF16)],
        compiler_params=params(1),
        cost_estimate=cost(20 * rows * D, 12 * rows * D),
    )(x, a, b, bias[0], gain[0], shift[0])


def mlp_kernel(final, place_ref, n_ref, dy_ref, bias_ref, *refs):
    packs = refs[:4]
    before = refs[4:6] if final else ()
    rest = refs[4 + len(before) :]
    g_ref, du_ref, bsum_ref = rest[:3]
    low_acc, lift_acc, buf, sems = rest[6:10] if final else rest[5:9]
    j = pl.program_id(0)
    tn = g_ref.shape[1]
    slot = lax.rem(j, 2)

    def load(tile, at):
        return pltpu.make_async_copy(packs[tile], buf.at[at], sems.at[at])

    def fetch(at):
        return pltpu.make_async_copy(before[at], rest[10 + at], sems.at[2 + at])

    @pl.when(j == 0)
    def _():
        load(0, 0).start()
        for at in range(len(before)):
            fetch(at).start()
        low_acc[...] = jnp.zeros_like(low_acc)
        lift_acc[...] = jnp.zeros_like(lift_acc)

    for tile in range(1, 4):

        @pl.when(j == tile - 1)
        def _(tile=tile):
            load(tile, tile % 2).start()

    load(0, slot).wait()
    up, down = buf[slot, :, :tn], buf[slot, :, tn:]
    u = mm(n_ref[...], up) + bias_ref[...]
    cdf = 0.5 * (1.0 + lax.erf(u * ROOT_HALF))
    g = (u * cdf).astype(BF16)
    slope = cdf + u * (jnp.exp(-0.5 * u * u) * DENSITY)
    g_ref[...] = g
    du = (mm(dy_ref[...], down) * slope).astype(BF16)
    du_ref[...] = du
    bsum_ref[...] = col_sum(du.astype(F32))
    low_acc[...] += mm_nt(g, down)
    lift_acc[...] += mm_nt(du, up)

    @pl.when(j == 3)
    def _():
        if not final:
            rest[3][...] = low_acc[...].astype(BF16)
            rest[4][...] = lift_acc[...].astype(BF16)
            return
        mine_ref, theirs_ref, lift_ref = rest[3:6]
        for at in range(2):
            fetch(at).wait()
        lift_ref[...] = (lift_acc[...] + rest[11][...].astype(F32)).astype(BF16)
        low_acc[...] += rest[10][...].astype(F32)
        width = D // 4
        core = place_ref[0]
        for far in range(2):
            low = pl.multiple_of((2 * far + core) * width, width)
            other = pl.multiple_of((2 * far + 1 - core) * width, width)
            mine_ref[:, far * width : (far + 1) * width] = low_acc[:, pl.ds(low, width)]
            theirs_ref[:, far * width : (far + 1) * width] = low_acc[:, pl.ds(other, width)].astype(
                BF16
            )


def mlp(place, n2, dy, bias, packs, before=()):
    rows = n2.shape[0]
    tn = packs[0].shape[1] // 2
    first_tile = 4 if before else 0
    whole = held_once((rows, D))
    half = held_once((rows, D // 2))
    tile = pl.BlockSpec((rows, tn), lambda j, *_: (0, j))
    swapped = pl.BlockSpec(
        (rows, tn), lambda j, *_: (0, jnp.where(j == 1, 2, jnp.where(j == 2, 1, j)))
    )
    thin = pl.BlockSpec((1, tn), lambda j, *_: (0, j))
    anywhere = pl.BlockSpec(memory_space=pl.ANY)
    out_specs = [swapped, tile, thin] + ([half, half, whole] if before else [whole, whole])
    out_shape = [like((rows, 4 * tn), BF16), like((rows, 4 * tn), BF16), like((1, 4 * tn), F32)]
    if before:
        out_shape += [like((rows, D // 2), F32), like((rows, D // 2), BF16), like((rows, D), BF16)]
    else:
        out_shape += [like((rows, D), BF16)] * 2
    return pl.pallas_call(
        functools.partial(mlp_kernel, bool(before)),
        name="mlp_second" if before else "mlp_first",
        grid_spec=pltpu.PrefetchScalarGridSpec(
            num_scalar_prefetch=1,
            grid=(4,),
            in_specs=[whole, whole, pl.BlockSpec((1, tn), lambda j, *_: (0, j + first_tile))]
            + [anywhere] * (4 + len(before)),
            out_specs=out_specs,
            scratch_shapes=[
                pltpu.VMEM((rows, D), F32),
                pltpu.VMEM((rows, D), F32),
                pltpu.VMEM((2, D, 2 * tn), BF16),
                pltpu.SemaphoreType.DMA((4,)),
            ]
            + [pltpu.VMEM((rows, D), BF16)] * len(before),
        ),
        out_shape=out_shape,
        compiler_params=params(1),
        cost_estimate=cost(32 * rows * D * tn, 20 * rows * D, 8 * rows * tn),
    )(place, n2, dy, bias, *packs, *before)


def turn_kernel(
    place_ref, h_ref, dy_ref, a_ref, b_ref, low_ref, other_ref, gain_ref, bias_ref, w_ref,
    dh_ref, da_ref, do_ref, sums_ref, mine_ref, theirs_ref, held,
):
    h = h_ref[...]
    held[...] = h + bias_ref[...]
    core, side = place_ref[0], place_ref[1]
    width = D // 4
    low = low_ref[...] + other_ref[...].astype(F32)
    for far in range(2):
        at = pl.ds(pl.multiple_of((2 * far + core) * width, width), width)
        out = (held[:, at] + low[:, far * width : (far + 1) * width]).astype(BF16)

        @pl.when(side == far)
        def _(out=out):
            mine_ref[...] = out

        @pl.when(side != far)
        def _(out=out):
            theirs_ref[...] = out

    middle, scaled = stats(h)
    c = (h - middle) * scaled
    dn = a_ref[...].astype(F32) + b_ref[...].astype(F32)
    dy = dy_ref[...].astype(F32)
    e = dn * gain_ref[...]
    dh = dy + scaled * (e - row_mean(e) - c * row_mean(e * c))
    dh_ref[...] = dh
    da = dh.astype(BF16)
    da_ref[...] = da
    do_ref[...] = mm(da, w_ref[...]).astype(BF16)
    part = jnp.concatenate(
        [col_sum(da.astype(F32)), col_sum(dy), col_sum(dn * c), col_sum(dn)], axis=0
    )
    add_up(sums_ref, pl.program_id(0) == 0, part)


def turn(place, h, dy, a, b, low_mine, low_other, gain, bias, weights):
    rows = h.shape[0]
    wide = weights.shape[1] // 4
    width = D // 4
    return pl.pallas_call(
        turn_kernel,
        name="turn",
        grid_spec=pltpu.PrefetchScalarGridSpec(
            num_scalar_prefetch=1,
            grid=(rows // TM,),
            in_specs=[row_spec(D)] * 4
            + [row_spec(D // 2)] * 2
            + [gain[1], bias[1]]
            + [pl.BlockSpec((D, wide), lambda i, *_: (0, 3), pipeline_mode=pl.Buffered(1))],
            out_specs=[
                row_spec(D),
                row_spec(D),
                row_spec(wide),
                fixed((4, D)),
                row_spec(width),
                row_spec(width),
            ],
            scratch_shapes=[pltpu.VMEM((TM, D), F32)],
        ),
        out_shape=[
            like((rows, D), F32),
            like((rows, D), BF16),
            like((rows, wide), BF16),
            like((4, D), F32),
            like((rows, width), BF16),
            like((rows, width), BF16),
        ],
        compiler_params=params(1),
        cost_estimate=cost(2 * rows * D * wide, 20 * rows * D),
    )(place, h, dy, a, b, low_mine, low_other, gain[0], bias[0], weights)


def last_kernel(
    place_ref, x_ref, dh_ref, a_ref, b_ref, gain_ref, mine_ref, theirs_ref, sum_mine, sum_theirs, held, sums
):
    x = x_ref[...].astype(F32)
    middle, scaled = stats(x)
    c = (x - middle) * scaled
    dn = a_ref[...].astype(F32) + b_ref[...].astype(F32)
    e = dn * gain_ref[...]
    held[...] = dh_ref[...] + scaled * (e - row_mean(e) - c * row_mean(e * c))
    width = D // 4
    core, side = place_ref[0], place_ref[1]
    here = pl.ds(pl.multiple_of((2 * side + core) * width, width), width)
    there = pl.ds(pl.multiple_of((2 * (1 - side) + core) * width, width), width)
    mine_ref[...] = held[:, here]
    theirs_ref[...] = held[:, there].astype(BF16)
    i = pl.program_id(0)
    add_up(sums, i == 0, jnp.concatenate([col_sum(dn * c), col_sum(dn)], axis=0))

    @pl.when(i == pl.num_programs(0) - 1)
    def _():
        sum_mine[...] = sums[:, here]
        sum_theirs[...] = sums[:, there]


def last(place, x, dh, a, b, gain):
    rows = x.shape[0]
    width = D // 4
    return pl.pallas_call(
        last_kernel,
        name="last",
        grid_spec=pltpu.PrefetchScalarGridSpec(
            num_scalar_prefetch=1,
            grid=(rows // TM,),
            in_specs=[row_spec(D)] * 4 + [gain[1]],
            out_specs=[row_spec(width), row_spec(width), fixed((2, width)), fixed((2, width))],
            scratch_shapes=[pltpu.VMEM((TM, D), F32), pltpu.VMEM((2, D), F32)],
        ),
        out_shape=[
            like((rows, width), F32),
            like((rows, width), BF16),
            like((2, width), F32),
            like((2, width), F32),
        ],
        compiler_params=params(1),
        cost_estimate=cost(20 * rows * D, 12 * rows * D),
    )(place, x, dh, a, b, gain[0])


def join_kernel(*refs):
    out_ref = refs[-1]
    start = 0
    for mine, got in zip(refs[:-1:2], refs[1:-1:2]):
        width = got.shape[1]
        total = mine[...].astype(F32) + got[...].astype(F32)
        out_ref[:, start : start + width] = total.astype(BF16)
        start += width


def join(*parts):
    rows = parts[0].shape[0]
    tm = rows // 4
    widths = [item.shape[1] for item in parts[1::2]]
    return pl.pallas_call(
        join_kernel,
        grid=(4,),
        name="join",
        in_specs=[
            pl.BlockSpec((tm, width), lambda i: (i, 0)) for width in widths for _ in range(2)
        ],
        out_specs=pl.BlockSpec((tm, sum(widths)), lambda i: (i, 0)),
        out_shape=like((rows, sum(widths)), BF16),
        compiler_params=params(1),
        cost_estimate=cost(rows * sum(widths), 6 * rows * sum(widths)),
    )(*parts)


def pack_kernel(*refs):
    out_ref = refs[-1]
    width = refs[0].shape[0]
    for at, ref in enumerate(refs[:-2]):
        out_ref[at, :] = ref[...]
    for at in range(4):
        out_ref[len(refs) - 2 + at, :] = refs[-2][width * at : width * (at + 1)]


def pack(vectors, long_vector):
    width = vectors[0].shape[0]
    return pl.pallas_call(
        pack_kernel,
        name="pack",
        out_shape=like((len(vectors) + 4, width), F32),
    )(*vectors, long_vector)


def unpack_kernel(place_ref, own, far, own_other, far_other, vec_ref, qkv_ref, tile_ref):
    core, side, half = place_ref[0], place_ref[1], place_ref[2]
    width = own.shape[1]
    one = width // 2

    def put(ref, at_side, at_core):
        at = pl.multiple_of((2 * at_side + at_core) * width, width)
        for k in range(6):
            vec_ref[k, :, pl.ds(at, width)] = ref[k : k + 1, :]

    put(own, side, core)
    put(far, 1 - side, core)
    put(own_other, side, 1 - core)
    put(far_other, 1 - side, 1 - core)
    qkv_ref[...] = jnp.zeros_like(qkv_ref)
    blocks = ((own, half), (far, half), (own, 1 - half), (far, 1 - half))
    for at, (ref, which) in enumerate(blocks):
        cut = pl.ds(pl.multiple_of(which * one, one), one)
        qkv_ref[:, 3 * one * at : 3 * one * at + one] = ref[6:7, cut]
        qkv_ref[:, 3 * one * at + 2 * one : 3 * one * (at + 1)] = ref[7:8, cut]
    order = (0, 1, 2, 3), (0, 2, 1, 3)
    for part in range(2):
        for at, index in enumerate(order[part]):
            ref, which = blocks[index]
            start = width * (4 * part + at)
            tile_ref[:, start : start + width] = ref[pl.ds(8 + 2 * which + part, 1), :]


def unpack(place, own, far, own_other, far_other):
    width = own.shape[1]
    return pl.pallas_call(
        unpack_kernel,
        name="unpack",
        in_specs=[pl.BlockSpec(memory_space=pltpu.SMEM)]
        + [pl.BlockSpec(memory_space=pltpu.VMEM)] * 4,
        out_shape=[like((6, 1, D), F32), like((1, 6 * width), F32), like((1, 8 * width), F32)],
    )(place, own, far, own_other, far_other)


def collect_kernel(
    place_ref, turn_ref, qkv_ref, up_a_ref, up_b_ref, a_ref, b_ref, mine_ref, theirs_ref
):
    core, side, half = place_ref[0], place_ref[1], place_ref[2]
    width = mine_ref.shape[1]
    one = width // 2
    for ref, at_side in ((mine_ref, side), (theirs_ref, 1 - side)):
        at = pl.ds(pl.multiple_of((2 * at_side + core) * width, width), width)
        ref[2:6, :] = turn_ref[:, at]
    mine_ref[10:12, :] = a_ref[...]
    theirs_ref[10:12, :] = b_ref[...]
    for at in range(4):
        ref = (mine_ref, theirs_ref)[at % 2]
        which = half if at < 2 else 1 - half
        cut = pl.ds(pl.multiple_of(which * one, one), one)
        ref[0:1, cut] = qkv_ref[:, 3 * one * at : 3 * one * at + one]
        ref[1:2, cut] = qkv_ref[:, 3 * one * at + 2 * one : 3 * one * (at + 1)]
    order = (0, 1, 2, 3), (0, 2, 1, 3)
    for part in range(2):
        for at, index in enumerate(order[part]):
            ref = (mine_ref, theirs_ref)[index % 2]
            which = half if index < 2 else 1 - half
            up_ref = (up_a_ref, up_b_ref)[part]
            ref[pl.ds(6 + 2 * which + part, 1), :] = up_ref[:, width * at : width * (at + 1)]


def collect(place, *sums):
    width = D // 4
    return pl.pallas_call(
        collect_kernel,
        name="collect",
        in_specs=[pl.BlockSpec(memory_space=pltpu.SMEM)]
        + [pl.BlockSpec(memory_space=pltpu.VMEM)] * 6,
        out_shape=[like((12, width), F32)] * 2,
    )(place, *sums)


def hand_out_kernel(a_ref, b_ref, *outs):
    sums = a_ref[...] + b_ref[...]
    width = a_ref.shape[1]
    for at in range(6):
        outs[at][...] = sums[at, :]
    for at in range(4):
        outs[6][width * at : width * (at + 1)] = sums[6 + at, :]
    for at in range(2):
        outs[7 + at][...] = sums[10 + at, :]


def hand_out(mine, got):
    width = mine.shape[1]
    one = like((width,), F32)
    return pl.pallas_call(
        hand_out_kernel,
        name="hand_out",
        out_shape=[one] * 6 + [like((4 * width,), F32)] + [one] * 2,
    )(mine, got)


def local(
    sizes,
    inputs,
    query_weight,
    key_weight,
    value_weight,
    query_bias,
    value_bias,
    out_weight,
    out_bias,
    up_weight,
    up_bias,
    down_weight,
    down_bias,
    first_gain,
    first_shift,
    second_gain,
    second_shift,
    cotangent,
):
    n_dp, n_row, n_xa, n_core = sizes
    my_x = lax.axis_index("xa")
    my_core = lax.axis_index("core")
    my_row = lax.axis_index("row")
    my_half = lax.axis_index("dp") % 2
    place = jnp.stack([my_core, my_x, my_half]).astype(jnp.int32)
    tokens_here, width = inputs.shape
    images = tokens_here // SEQ
    held = images // n_xa
    rows = held * PAD
    half = up_weight.shape[1] // 2
    quarter = half // 2
    heads_half = width // 2
    three = 3 * heads_half

    def swap(value, axis, size, bit=1):
        return lax.ppermute(value, axis, [(at, at ^ bit) for at in range(size)])

    def shifted(value, shift):
        return lax.ppermute(value, "row", [(at, (at + shift) % n_row) for at in range(n_row)])

    def across(value):
        return swap(value, "xa", n_xa)

    def beside(value):
        return swap(value, "core", n_core)

    def over(value):
        return swap(value, "dp", n_dp)

    def pick(value, at, axis):
        return lax.dynamic_index_in_dim(value, at, axis, keepdims=False)

    def in_order(mine, other, at):
        return jnp.where(at == 0, mine, other), jnp.where(at == 0, other, mine)

    def after(value, *others):
        return lax.optimization_barrier((value, *others))[0]

    def halves(value, axis):
        cut = value.shape[axis] // 2
        both = value.reshape(value.shape[:axis] + (2, cut) + value.shape[axis + 1 :])
        return pick(both, my_half, axis), pick(both, my_half ^ 1, axis)

    count = held * SEQ

    def send_tokens(value):
        return lax.dynamic_slice_in_dim(value, (my_x ^ 1) * count, count, 0)

    def wide_tokens(value, got):
        mine = lax.dynamic_slice_in_dim(value, my_x * count, count, 0)
        pair = jnp.concatenate([mine, got], axis=1).reshape(held, SEQ, 2 * width)
        pair = jnp.pad(pair, ((0, 0), (0, PAD - SEQ), (0, 0))).reshape(rows, 2 * width)
        other = beside(pair)
        left, right = in_order(pair, other, my_core)
        first_left, second_left = in_order(left[:, :width], left[:, width:], my_x)
        first_right, second_right = in_order(right[:, :width], right[:, width:], my_x)
        return jnp.concatenate([first_left, first_right, second_left, second_right], axis=1)

    attn_shard = jnp.concatenate(
        [halves(item, 1)[0] for item in (query_weight, key_weight, value_weight)]
        + [halves(out_weight, 0)[0].T],
        axis=1,
    )
    input_leaves = send_tokens(inputs)
    attn_shard = after(attn_shard, input_leaves)
    input_got = across(input_leaves)
    pieces = [attn_shard] + [shifted(attn_shard, shift) for shift in range(1, n_row)]
    small = pack(
        (
            out_bias,
            down_bias,
            first_gain,
            first_shift,
            second_gain,
            second_shift,
            query_bias,
            value_bias,
        ),
        up_bias,
    )
    pieces = [pieces[0]] + [after(piece, small) for piece in pieces[1:]]
    cut = 2 * heads_half
    first_own = jnp.zeros((D, cut), BF16)
    second_own = jnp.zeros((D, cut), BF16)
    for shift, piece in enumerate(pieces):
        start = (my_row - shift) % n_row * (D // n_row)
        first_own = lax.dynamic_update_slice(first_own, piece[:, :cut], (start, 0))
        second_own = lax.dynamic_update_slice(second_own, piece[:, cut:], (start, 0))
    first_far, second_oth = across(first_own), over(second_own)
    first_oth, second_far = over(first_own), across(second_own)

    small_far = across(small)
    vectors, qkv_bias, tile_bias = unpack(
        place, small, after(small_far, first_own, second_own), beside(small), beside(small_far)
    )
    out_bias_all, down_bias_all, gain_one, shift_one, gain_two, shift_two = (
        (vectors, pl.BlockSpec((None, 1, D), lambda i, *_, at=at: (at, 0, 0))) for at in range(6)
    )
    wide_input = wide_tokens(inputs, after(input_got, first_own, second_own))
    first_far_oth = over(after(first_far, wide_input, qkv_bias))
    second_far_oth = across(after(second_oth, wide_input, qkv_bias))

    def gather(part):
        up_part = halves(up_weight, 1)[0][:, quarter * part : quarter * (part + 1)]
        down_part = halves(down_weight, 0)[0][quarter * part : quarter * (part + 1)].T
        shard = after(jnp.concatenate([up_part, down_part], axis=1), first_own, second_own)
        return lax.all_gather(shard, "row", axis=0, tiled=True)

    own_a, own_b = gather(0), gather(1)
    grad_got = across(after(send_tokens(cotangent), wide_input))

    wide_one, qkv, attn_weights = norm_qkv(
        wide_input,
        gain_one,
        shift_one,
        qkv_bias,
        (
            first_own,
            second_own,
            first_far,
            second_far,
            first_oth,
            second_oth,
            first_far_oth,
            second_far_oth,
        ),
    )
    oth_a, far_a = over(own_a), across(own_a)
    oth_b, far_b = over(own_b), across(own_b)
    attended, probs = attend(qkv)
    mixed = mm_nt(attended, attn_weights[:, 4 * three :]).astype(BF16)
    mixed_other = beside(mixed)
    wide_grad = wide_tokens(cotangent, after(grad_got, mixed))
    far_oth_a = over(far_a)
    middle_sum, wide_two = middle(
        wide_input, mixed, after(mixed_other, wide_grad), out_bias_all, gain_two, shift_two
    )
    far_oth_b = across(oth_b)

    def tiles(value, first, end):
        return value[:, quarter * first : quarter * end]

    gate_a, pre_a, up_sums_a, low_a, lift_a = mlp(
        place, wide_two, wide_grad, tile_bias, (own_a, far_a, oth_a, far_oth_a)
    )
    up_over = mm_tn(wide_two, tiles(pre_a, 2, 4)).astype(BF16)
    down_a = mm_tn(wide_grad, gate_a).astype(BF16)
    up_over_got = over(up_over)
    down_piece = lax.psum_scatter(down_a, "row", scatter_dimension=0, tiled=True)
    gate_b, pre_b, up_sums_b, low_mine, low_theirs, lifted_two = mlp(
        place,
        after(wide_two, up_over, down_a),
        wide_grad,
        tile_bias,
        (own_b, oth_b, far_b, far_oth_b),
        (low_a, lift_a),
    )

    def wide_add(mine, got):
        return (mine.astype(F32) + got.astype(F32)).astype(BF16)

    def same_half(value):
        if n_dp == 2:
            return value
        groups = [[at + bit for at in range(0, n_dp, 2)] for bit in range(2)]
        return lax.psum(value.astype(F32), "dp", axis_index_groups=groups).astype(BF16)

    def scatter(value):
        return lax.psum_scatter(value, "row", scatter_dimension=0, tiled=True)

    lifted_other = beside(lifted_two)
    low_other = beside(low_theirs)
    up_across = mm_tn(wide_two, tiles(pre_b, 2, 4)).astype(BF16)
    down_over = mm_tn(wide_grad, tiles(gate_b, 2, 4)).astype(BF16)
    up_across_got, down_over_got = across(up_across), over(down_over)
    down_x_got = across(after(down_piece, up_across, down_over)[:, half:])

    middle_grad, attn_grad, head_grad, turn_sums, out_mine, out_theirs = turn(
        place,
        middle_sum,
        wide_grad,
        lifted_two,
        after(lifted_other, up_across, down_over),
        low_mine,
        low_other,
        gain_two,
        down_bias_all,
        attn_weights,
    )
    out_all = mm_tn(attn_grad, attended).astype(BF16)
    out_over_got = over(out_all[:, 2 * heads_half :])
    up_over_got, up_across_got, down_over_got, _ = lax.optimization_barrier(
        (up_over_got, up_across_got, down_over_got, out_all)
    )
    up_a = wide_add(mm_tn(wide_two, tiles(pre_a, 0, 2)), up_over_got)
    up_b = wide_add(mm_tn(wide_two, tiles(pre_b, 0, 2)), up_across_got)
    down_b = wide_add(mm_tn(wide_grad, tiles(gate_b, 0, 2)), down_over_got)
    up_a_got, up_b_got = across(up_a[:, quarter:]), over(up_b[:, quarter:])
    out_own = wide_add(out_all[:, : 2 * heads_half], after(out_over_got, down_b))
    out_far_got = across(out_own[:, heads_half:])
    down_x = wide_add(down_piece[:, :half], after(down_x_got, down_b))
    down_y_got = over(down_x)
    down_b_got = across(down_b[:, quarter:])
    out_got = across(after(out_theirs, down_b))
    dqkv, qkv_sums = attend_back(qkv, probs, after(head_grad, up_a, up_b, out_own, down_x))
    up_sum = join(
        up_a, up_a_got, up_b, up_b_got, down_b, down_b_got, out_own, after(out_far_got, dqkv)
    )
    up_piece = same_half(scatter(up_sum))

    def to_feature_blocks(mine, got, dtype):
        first, second = in_order(mine.astype(dtype), got.astype(dtype), my_x)
        both = jnp.concatenate([first, second]).reshape(images, PAD, width)
        return both[:, :SEQ].reshape(tokens_here, width)

    split = 3 * three + cut
    dqkv = after(dqkv, up_sum)
    far_oth_qk = mm_tn(wide_one, dqkv[:, 3 * three : split]).astype(BF16)
    far_oth_v = mm_tn(wide_one, dqkv[:, split:]).astype(BF16)
    qk_got, v_got = over(far_oth_qk), across(far_oth_v)
    lifted_one = mm_nt(
        after(dqkv, far_oth_qk, far_oth_v), attn_weights[:, : 4 * three]
    ).astype(BF16)
    lifted_one_other = beside(lifted_one)

    near_oth = wide_add(
        mm_tn(wide_one, dqkv[:, 2 * three : 3 * three]),
        jnp.pad(after(v_got, lifted_one), ((0, 0), (cut, 0))),
    )
    near_oth_got = over(near_oth)
    far_own = wide_add(
        mm_tn(wide_one, dqkv[:, three : 2 * three]),
        jnp.pad(after(qk_got, near_oth), ((0, 0), (0, three - cut))),
    )
    far_own_got = across(far_own)
    near_own = mm_tn(after(wide_one, far_own), dqkv[:, :three])
    input_mine, input_theirs, late_mine, late_theirs = last(
        place, wide_input, middle_grad, lifted_one, after(lifted_one_other, near_own), gain_one
    )
    mine_sums, theirs_sums = collect(
        place, turn_sums, qkv_sums, up_sums_a, up_sums_b, late_mine, late_theirs
    )

    near_sum = (near_own + near_oth_got.astype(F32) + after(far_own_got, mine_sums).astype(F32)).astype(
        BF16
    )
    strip = D // n_row

    def rows_of(value, shift):
        return lax.dynamic_slice_in_dim(value, (my_row + shift) % n_row * strip, strip, 0)

    gots = [shifted(rows_of(near_sum, shift), shift) for shift in range(1, n_row)]
    input_got = across(after(input_theirs, near_sum))
    sums = mine_sums + across(after(theirs_sums, near_sum))
    steps = [("row", n_row, 1 << bit) for bit in range(n_row.bit_length() - 1)]
    steps += [("dp", n_dp, 1 << bit) for bit in range(n_dp.bit_length() - 1)]
    for step in steps[:-1]:
        sums = sums + swap(sums, *step)
    sums = hand_out(sums, swap(sums, *steps[-1]))
    outputs = to_feature_blocks(out_mine, after(out_got, near_sum), BF16)

    qkv_total = rows_of(near_sum, 0).astype(F32)
    for got in gots:
        qkv_total = qkv_total + got.astype(F32)
    qkv_piece = same_half(qkv_total.astype(BF16))
    qkv_other = over(qkv_piece)
    input_grad = to_feature_blocks(input_mine, input_got, F32)
    up_other = over(up_piece)

    down_total = down_x.astype(F32) + jnp.concatenate(
        [down_y_got[:, quarter:], down_y_got[:, :quarter]], axis=1
    ).astype(F32)
    if n_dp > 2:
        groups = [[at + bit for at in range(0, n_dp, 2)] for bit in range(2)]
        down_total = lax.psum(down_total, "dp", axis_index_groups=groups)

    def down_half(first_part, second):
        return jnp.concatenate([first_part, tiles(second, 2, 3).astype(F32)], axis=1)

    down_first, down_second = in_order(
        down_half(down_total[:, :quarter], up_piece),
        down_half(down_total[:, quarter:], up_other),
        my_half,
    )
    down_grad = jnp.concatenate([down_first, down_second], axis=1).T

    def both_halves(mine, other, low, high):
        first, second = in_order(mine[:, low:high], other[:, low:high], my_half)
        return jnp.concatenate([first, second], axis=1).astype(F32)

    up_grad = both_halves(up_piece, up_other, 0, half)
    start = half + quarter
    out_grad = both_halves(up_piece, up_other, start, start + heads_half).T
    query_grad, key_grad, value_grad = (
        both_halves(qkv_piece, qkv_other, heads_half * at, heads_half * (at + 1))
        for at in range(3)
    )

    return (
        outputs,
        input_grad,
        query_grad,
        key_grad,
        value_grad,
        sums[0],
        sums[1],
        out_grad,
        sums[2],
        up_grad,
        sums[6],
        down_grad,
        sums[3],
        sums[7],
        sums[8],
        sums[4],
        sums[5],
    )


def solution(mesh):
    n_dp, n_row, n_col = (mesh.shape[name] for name in ("dp", "row", "col"))
    sizes = (n_dp, n_row, n_col // 2, 2)
    split = Mesh(mesh.devices.reshape(sizes), ("dp", "row", "xa", "core"))
    col = ("xa", "core")
    tokens, rows, cols, vec = P(("dp", "row"), col), P("row", col), P(col, "row"), P(col)
    in_specs = (
        (tokens, rows, rows, rows, vec, vec, cols, vec, rows, vec, cols)
        + (vec,) * 5
        + (tokens,)
    )
    out_specs = (
        (tokens, tokens, rows, rows, rows, vec, vec, cols, vec, rows, vec, cols) + (vec,) * 5
    )

    def body(*args):
        return local(sizes, *args)

    return jax.shard_map(
        body, mesh=split, in_specs=in_specs, out_specs=out_specs, check_vma=False
    )
```

```python
import functools
import math

import jax
import jax.numpy as jnp
from jax import lax
from jax.experimental import pallas as pl
from jax.experimental.pallas import tpu as pltpu
from jax.sharding import Mesh, PartitionSpec as P


D = 1024
HD = 64
SEQ = 577
PAD = 592
TM = 296
EPS = 1e-06
F32 = jnp.float32
BF16 = jnp.bfloat16
VMEM_LIMIT = 60 * 1024 * 1024
ROOT_HALF = math.sqrt(0.5)
DENSITY = 1.0 / math.sqrt(2.0 * math.pi)


def mm(a, b):
    return lax.dot_general(a, b, (((1,), (0,)), ((), ())), preferred_element_type=F32)


def mm_nt(a, b):
    return lax.dot_general(a, b, (((1,), (1,)), ((), ())), preferred_element_type=F32)


def mm_tn(a, b):
    return lax.dot_general(a, b, (((0,), (0,)), ((), ())), preferred_element_type=F32)


def row_mean(v):
    return jnp.sum(v, axis=1, keepdims=True) * (1.0 / D)


def col_sum(v):
    return jnp.sum(v, axis=0, keepdims=True)


def stats(rows):
    middle = row_mean(rows)
    spread = row_mean(rows * rows) - middle * middle
    return middle, lax.rsqrt(spread + EPS)


def params(n):
    return pltpu.CompilerParams(
        dimension_semantics=("arbitrary",) * n, vmem_limit_bytes=VMEM_LIMIT
    )


def cost(flops, moved, exps=0):
    return pl.CostEstimate(flops=int(flops), bytes_accessed=int(moved), transcendentals=int(exps))


def like(shape, dtype):
    return jax.ShapeDtypeStruct(shape, dtype)


def row_spec(cols):
    return pl.BlockSpec((TM, cols), lambda i, *_: (i, 0))


def fixed(shape):
    return pl.BlockSpec(shape, lambda *_: (0,) * len(shape))


def held_once(shape):
    return pl.BlockSpec(shape, lambda *_: (0,) * len(shape), pipeline_mode=pl.Buffered(1))


def add_up(ref, first, part):
    @pl.when(first)
    def _():
        ref[...] = part

    @pl.when(jnp.logical_not(first))
    def _():
        ref[...] += part


def norm_qkv_kernel(place_ref, x_ref, gain_ref, shift_ref, bias_ref, *refs):
    pieces, (n_ref, o_ref, w_ref) = refs[:-3], refs[-3:]
    n_row = len(pieces) // 4
    strip, wide = pieces[0].shape
    one = wide // 4

    @pl.when(pl.program_id(0) == 0)
    def _():
        for shift in range(n_row):
            start = lax.rem(place_ref[3] - shift + n_row, n_row) * strip
            rows = pl.ds(pl.multiple_of(start, strip), strip)
            for block in range(4):
                piece = pieces[n_row * block + shift]
                w_ref[rows, 3 * one * block : 3 * one * (block + 1)] = piece[:, : 3 * one]
                w_ref[rows, (12 + block) * one : (13 + block) * one] = piece[:, 3 * one :]

    x = x_ref[...].astype(F32)
    middle, scaled = stats(x)
    n = (((x - middle) * scaled) * gain_ref[...] + shift_ref[...]).astype(BF16)
    n_ref[...] = n
    o_ref[...] = (mm(n, w_ref[:, : 12 * one]) + bias_ref[...]).astype(BF16)


def norm_qkv(place, x, gain, shift, bias, pieces):
    rows = x.shape[0]
    wide = pieces[0].shape[1]
    out = 3 * wide
    return pl.pallas_call(
        norm_qkv_kernel,
        name="norm_qkv",
        grid_spec=pltpu.PrefetchScalarGridSpec(
            num_scalar_prefetch=1,
            grid=(rows // TM,),
            in_specs=[row_spec(D), gain[1], shift[1], fixed((1, out))]
            + [held_once(pieces[0].shape)] * len(pieces),
            out_specs=[row_spec(D), row_spec(out), held_once((D, 4 * wide))],
        ),
        out_shape=[like((rows, D), BF16), like((rows, out), BF16), like((D, 4 * wide), BF16)],
        compiler_params=params(1),
        cost_estimate=cost(2 * rows * D * out, 16 * rows * D),
    )(place, x, gain[0], shift[0], bias, *pieces)


def attend_kernel(qkv_ref, o_ref, p_ref):
    live = lax.broadcasted_iota(jnp.int32, (1, PAD), 1) < SEQ
    step = 2 * HD
    items = [(h, slice(r, r + TM)) for h in range(2) for r in range(0, PAD, TM)]

    def score(h, rows):
        q = qkv_ref[rows, HD * h : HD * (h + 1)] * jnp.asarray(0.125, BF16)
        return mm_nt(q, qkv_ref[:, step + HD * h : step + HD * (h + 1)])

    scores = [score(*item) for item in items[:3]]
    for at, (h, rows) in enumerate(items):
        if at + 3 < len(items):
            scores.append(score(*items[at + 3]))
        s = jnp.where(live, scores[at], -1e30)
        e = jnp.exp(s - jnp.max(s, axis=1, keepdims=True))
        p = (e * (1.0 / jnp.sum(e, axis=1, keepdims=True))).astype(BF16)
        p_ref[h, rows, :] = p
        v = qkv_ref[:, 2 * step + HD * h : 2 * step + HD * (h + 1)]
        o_ref[rows, HD * h : HD * (h + 1)] = mm(p, v).astype(BF16)


def attend(qkv):
    rows, cols = qkv.shape
    pairs = cols // (6 * HD)
    held = rows // PAD
    return pl.pallas_call(
        attend_kernel,
        grid=(pairs, held),
        name="attend",
        in_specs=[pl.BlockSpec((PAD, 6 * HD), lambda p, i: (i, p))],
        out_specs=[
            pl.BlockSpec((PAD, 2 * HD), lambda p, i: (i, p)),
            pl.BlockSpec((None, 2, PAD, PAD), lambda p, i: (i, p, 0, 0)),
        ],
        out_shape=[like((rows, cols // 3), BF16), like((held, 2 * pairs, PAD, PAD), BF16)],
        compiler_params=params(2),
        cost_estimate=cost(16 * rows * PAD * cols, 40 * rows * D, 4 * rows * PAD * pairs),
    )(qkv)


def attend_back_kernel(qkv_ref, p_ref, g_ref, d_ref, sum_ref):
    step = 2 * HD

    def cut(h, w):
        return slice(step * w + HD * h, step * w + HD * (h + 1))

    grads = [g_ref[:, HD * h : HD * (h + 1)] for h in range(2)]
    dprobs = [mm_nt(grads[h], qkv_ref[:, cut(h, 2)]) for h in range(2)]
    dscores = []
    for h in range(2):
        p = p_ref[h].astype(F32)
        z = jnp.sum(p * dprobs[h], axis=1, keepdims=True)
        dscores.append((p * (dprobs[h] - z)).astype(BF16))
        d_ref[:, cut(h, 2)] = mm_tn(p_ref[h], grads[h]).astype(BF16)
    for h in range(2):
        d_ref[:, cut(h, 0)] = (mm(dscores[h], qkv_ref[:, cut(h, 1)]) * 0.125).astype(BF16)
        d_ref[:, cut(h, 1)] = (mm_tn(dscores[h], qkv_ref[:, cut(h, 0)]) * 0.125).astype(BF16)
    add_up(sum_ref, pl.program_id(1) == 0, col_sum(d_ref[...].astype(F32)))


def attend_back(qkv, probs, grads):
    rows, cols = qkv.shape
    pairs = cols // (6 * HD)
    held = rows // PAD
    three = pl.BlockSpec((PAD, 6 * HD), lambda p, i: (i, p))
    return pl.pallas_call(
        attend_back_kernel,
        grid=(pairs, held),
        name="attend_back",
        in_specs=[
            three,
            pl.BlockSpec((None, 2, PAD, PAD), lambda p, i: (i, p, 0, 0)),
            pl.BlockSpec((PAD, 2 * HD), lambda p, i: (i, p)),
        ],
        out_specs=[three, pl.BlockSpec((1, 6 * HD), lambda p, i: (0, p))],
        out_shape=[like((rows, cols), BF16), like((1, cols), F32)],
        compiler_params=params(2),
        cost_estimate=cost(20 * rows * PAD * cols, 50 * rows * D),
    )(qkv, probs, grads)


def middle_kernel(x_ref, a_ref, b_ref, bias_ref, gain_ref, shift_ref, h_ref, n_ref):
    h = x_ref[...].astype(F32) + (a_ref[...].astype(F32) + b_ref[...].astype(F32)) + bias_ref[...]
    h_ref[...] = h
    middle, scaled = stats(h)
    n_ref[...] = (((h - middle) * scaled) * gain_ref[...] + shift_ref[...]).astype(BF16)


def middle(x, a, b, bias, gain, shift):
    rows = x.shape[0]
    return pl.pallas_call(
        middle_kernel,
        grid=(rows // TM,),
        name="middle",
        in_specs=[row_spec(D)] * 3 + [bias[1], gain[1], shift[1]],
        out_specs=[row_spec(D)] * 2,
        out_shape=[like((rows, D), F32), like((rows, D), BF16)],
        compiler_params=params(1),
        cost_estimate=cost(20 * rows * D, 12 * rows * D),
    )(x, a, b, bias[0], gain[0], shift[0])


def mlp_kernel(final, place_ref, n_ref, dy_ref, bias_ref, *refs):
    packs = refs[:4]
    before = refs[4:6] if final else ()
    rest = refs[4 + len(before) :]
    g_ref, du_ref, bsum_ref = rest[:3]
    buf, sem = rest[6:8] if final else rest[5:7]
    i = pl.program_id(0)
    tn = g_ref.shape[1] // 4

    @pl.when(i == 0)
    def _():
        copies = []
        for tile in range(4):
            for part in range(2):
                copies.append(
                    pltpu.make_async_copy(
                        packs[tile].at[:, pl.ds(part * tn, tn)],
                        buf.at[part, :, pl.ds(tile * tn, tn)],
                        sem.at[part, tile],
                    )
                )
        for copy in copies:
            copy.start()
        for copy in copies:
            copy.wait()

    up, down = buf[0], buf[1]
    u = mm(n_ref[...], up) + bias_ref[...]
    cdf = 0.5 * (1.0 + lax.erf(u * ROOT_HALF))
    g = (u * cdf).astype(BF16)
    slope = cdf + u * (jnp.exp(-0.5 * u * u) * DENSITY)
    for at, tile in enumerate((0, 2, 1, 3)):
        g_ref[:, at * tn : (at + 1) * tn] = g[:, tile * tn : (tile + 1) * tn]
    du = (mm(dy_ref[...], down) * slope).astype(BF16)
    du_ref[...] = du
    add_up(bsum_ref, i == 0, col_sum(du.astype(F32)))
    low = mm_nt(g, down)
    lift = mm_nt(du, up)
    if not final:
        rest[3][...] = low.astype(BF16)
        rest[4][...] = lift.astype(BF16)
        return
    mine_ref, theirs_ref, lift_ref = rest[3:6]
    held = rest[8]
    lift_ref[...] = (lift + before[1][...].astype(F32)).astype(BF16)
    held[...] = low + before[0][...].astype(F32)
    width = D // 4
    core = place_ref[0]
    for far in range(2):
        here = pl.multiple_of((2 * far + core) * width, width)
        other = pl.multiple_of((2 * far + 1 - core) * width, width)
        mine_ref[:, far * width : (far + 1) * width] = held[:, pl.ds(here, width)]
        theirs_ref[:, far * width : (far + 1) * width] = held[:, pl.ds(other, width)].astype(BF16)


def mlp(place, n2, dy, bias, packs, before=()):
    rows = n2.shape[0]
    hid = 2 * packs[0].shape[1]
    part = 1 if before else 0

    def block(cols):
        return pl.BlockSpec((PAD, cols), lambda i, *_: (i, 0))

    out_specs = [block(hid), block(hid), fixed((1, hid))]
    out_shape = [like((rows, hid), BF16), like((rows, hid), BF16), like((1, hid), F32)]
    scratch = [pltpu.VMEM((2, D, hid), BF16), pltpu.SemaphoreType.DMA((2, 4))]
    if before:
        out_specs += [block(D // 2), block(D // 2), block(D)]
        out_shape += [like((rows, D // 2), F32), like((rows, D // 2), BF16), like((rows, D), BF16)]
        scratch += [pltpu.VMEM((PAD, D), F32)]
    else:
        out_specs += [block(D), block(D)]
        out_shape += [like((rows, D), BF16)] * 2
    return pl.pallas_call(
        functools.partial(mlp_kernel, bool(before)),
        name="mlp_second" if before else "mlp_first",
        grid_spec=pltpu.PrefetchScalarGridSpec(
            num_scalar_prefetch=1,
            grid=(rows // PAD,),
            in_specs=[block(D), block(D), pl.BlockSpec((1, hid), lambda i, *_: (0, part))]
            + [pl.BlockSpec(memory_space=pl.ANY)] * 4
            + [block(D)] * len(before),
            out_specs=out_specs,
            scratch_shapes=scratch,
        ),
        out_shape=out_shape,
        compiler_params=params(1),
        cost_estimate=cost(8 * rows * D * hid, 20 * rows * D, 2 * rows * hid),
    )(place, n2, dy, bias, *packs, *before)


def turn_kernel(
    place_ref, h_ref, dy_ref, a_ref, b_ref, low_ref, other_ref, gain_ref, bias_ref, w_ref,
    dh_ref, da_ref, do_ref, sums_ref, mine_ref, theirs_ref, held,
):
    h = h_ref[...]
    held[...] = h + bias_ref[...]
    core, side = place_ref[0], place_ref[1]
    width = D // 4
    low = low_ref[...] + other_ref[...].astype(F32)
    for far in range(2):
        at = pl.ds(pl.multiple_of((2 * far + core) * width, width), width)
        out = (held[:, at] + low[:, far * width : (far + 1) * width]).astype(BF16)

        @pl.when(side == far)
        def _(out=out):
            mine_ref[...] = out

        @pl.when(side != far)
        def _(out=out):
            theirs_ref[...] = out

    middle, scaled = stats(h)
    c = (h - middle) * scaled
    dn = a_ref[...].astype(F32) + b_ref[...].astype(F32)
    dy = dy_ref[...].astype(F32)
    e = dn * gain_ref[...]
    dh = dy + scaled * (e - row_mean(e) - c * row_mean(e * c))
    dh_ref[...] = dh
    da = dh.astype(BF16)
    da_ref[...] = da
    do_ref[...] = mm(da, w_ref[...]).astype(BF16)
    part = jnp.concatenate(
        [col_sum(da.astype(F32)), col_sum(dy), col_sum(dn * c), col_sum(dn)], axis=0
    )
    add_up(sums_ref, pl.program_id(0) == 0, part)


def turn(place, h, dy, a, b, low_mine, low_other, gain, bias, weights):
    rows = h.shape[0]
    wide = weights.shape[1] // 4
    width = D // 4
    return pl.pallas_call(
        turn_kernel,
        name="turn",
        grid_spec=pltpu.PrefetchScalarGridSpec(
            num_scalar_prefetch=1,
            grid=(rows // TM,),
            in_specs=[row_spec(D)] * 4
            + [row_spec(D // 2)] * 2
            + [gain[1], bias[1]]
            + [pl.BlockSpec((D, wide), lambda i, *_: (0, 3), pipeline_mode=pl.Buffered(1))],
            out_specs=[
                row_spec(D),
                row_spec(D),
                row_spec(wide),
                fixed((4, D)),
                row_spec(width),
                row_spec(width),
            ],
            scratch_shapes=[pltpu.VMEM((TM, D), F32)],
        ),
        out_shape=[
            like((rows, D), F32),
            like((rows, D), BF16),
            like((rows, wide), BF16),
            like((4, D), F32),
            like((rows, width), BF16),
            like((rows, width), BF16),
        ],
        compiler_params=params(1),
        cost_estimate=cost(2 * rows * D * wide, 20 * rows * D),
    )(place, h, dy, a, b, low_mine, low_other, gain[0], bias[0], weights)


def last_kernel(
    place_ref, x_ref, dh_ref, a_ref, b_ref, gain_ref, mine_ref, theirs_ref, sum_mine, sum_theirs, held, sums
):
    x = x_ref[...].astype(F32)
    middle, scaled = stats(x)
    c = (x - middle) * scaled
    dn = a_ref[...].astype(F32) + b_ref[...].astype(F32)
    e = dn * gain_ref[...]
    held[...] = dh_ref[...] + scaled * (e - row_mean(e) - c * row_mean(e * c))
    width = D // 4
    core, side = place_ref[0], place_ref[1]
    here = pl.ds(pl.multiple_of((2 * side + core) * width, width), width)
    there = pl.ds(pl.multiple_of((2 * (1 - side) + core) * width, width), width)
    mine_ref[...] = held[:, here]
    theirs_ref[...] = held[:, there].astype(BF16)
    i = pl.program_id(0)
    add_up(sums, i == 0, jnp.concatenate([col_sum(dn * c), col_sum(dn)], axis=0))

    @pl.when(i == pl.num_programs(0) - 1)
    def _():
        sum_mine[...] = sums[:, here]
        sum_theirs[...] = sums[:, there]


def last(place, x, dh, a, b, gain):
    rows = x.shape[0]
    width = D // 4
    return pl.pallas_call(
        last_kernel,
        name="last",
        grid_spec=pltpu.PrefetchScalarGridSpec(
            num_scalar_prefetch=1,
            grid=(rows // TM,),
            in_specs=[row_spec(D)] * 4 + [gain[1]],
            out_specs=[row_spec(width), row_spec(width), fixed((2, width)), fixed((2, width))],
            scratch_shapes=[pltpu.VMEM((TM, D), F32), pltpu.VMEM((2, D), F32)],
        ),
        out_shape=[
            like((rows, width), F32),
            like((rows, width), BF16),
            like((2, width), F32),
            like((2, width), F32),
        ],
        compiler_params=params(1),
        cost_estimate=cost(20 * rows * D, 12 * rows * D),
    )(place, x, dh, a, b, gain[0])


def join_kernel(*refs):
    out_ref = refs[-1]
    start = 0
    for mine, got in zip(refs[:-1:2], refs[1:-1:2]):
        width = got.shape[1]
        total = mine[...].astype(F32) + got[...].astype(F32)
        out_ref[:, start : start + width] = total.astype(BF16)
        start += width


def join(*parts):
    rows = parts[0].shape[0]
    tm = rows // 4
    widths = [item.shape[1] for item in parts[1::2]]
    return pl.pallas_call(
        join_kernel,
        grid=(4,),
        name="join",
        in_specs=[
            pl.BlockSpec((tm, width), lambda i: (i, 0)) for width in widths for _ in range(2)
        ],
        out_specs=pl.BlockSpec((tm, sum(widths)), lambda i: (i, 0)),
        out_shape=like((rows, sum(widths)), BF16),
        compiler_params=params(1),
        cost_estimate=cost(rows * sum(widths), 6 * rows * sum(widths)),
    )(*parts)


def pack_kernel(*refs):
    out_ref = refs[-1]
    width = refs[0].shape[0]
    for at, ref in enumerate(refs[:-2]):
        out_ref[at, :] = ref[...]
    for at in range(4):
        out_ref[len(refs) - 2 + at, :] = refs[-2][width * at : width * (at + 1)]


def pack(vectors, long_vector):
    width = vectors[0].shape[0]
    return pl.pallas_call(
        pack_kernel,
        name="pack",
        out_shape=like((len(vectors) + 4, width), F32),
    )(*vectors, long_vector)


def unpack_kernel(place_ref, own, far, own_other, far_other, vec_ref, qkv_ref, tile_ref):
    core, side, half = place_ref[0], place_ref[1], place_ref[2]
    width = own.shape[1]
    one = width // 2

    def put(ref, at_side, at_core):
        at = pl.multiple_of((2 * at_side + at_core) * width, width)
        for k in range(6):
            vec_ref[k, :, pl.ds(at, width)] = ref[k : k + 1, :]

    put(own, side, core)
    put(far, 1 - side, core)
    put(own_other, side, 1 - core)
    put(far_other, 1 - side, 1 - core)
    qkv_ref[...] = jnp.zeros_like(qkv_ref)
    blocks = ((own, half), (far, half), (own, 1 - half), (far, 1 - half))
    for at, (ref, which) in enumerate(blocks):
        cut = pl.ds(pl.multiple_of(which * one, one), one)
        qkv_ref[:, 3 * one * at : 3 * one * at + one] = ref[6:7, cut]
        qkv_ref[:, 3 * one * at + 2 * one : 3 * one * (at + 1)] = ref[7:8, cut]
    order = (0, 1, 2, 3), (0, 2, 1, 3)
    for part in range(2):
        for at, index in enumerate(order[part]):
            ref, which = blocks[index]
            start = width * (4 * part + at)
            tile_ref[:, start : start + width] = ref[pl.ds(8 + 2 * which + part, 1), :]


def unpack(place, own, far, own_other, far_other):
    width = own.shape[1]
    return pl.pallas_call(
        unpack_kernel,
        name="unpack",
        in_specs=[pl.BlockSpec(memory_space=pltpu.SMEM)]
        + [pl.BlockSpec(memory_space=pltpu.VMEM)] * 4,
        out_shape=[like((6, 1, D), F32), like((1, 6 * width), F32), like((1, 8 * width), F32)],
    )(place, own, far, own_other, far_other)


def collect_kernel(
    place_ref, turn_ref, qkv_ref, up_a_ref, up_b_ref, a_ref, b_ref, mine_ref, theirs_ref
):
    core, side, half = place_ref[0], place_ref[1], place_ref[2]
    width = mine_ref.shape[1]
    one = width // 2
    for ref, at_side in ((mine_ref, side), (theirs_ref, 1 - side)):
        at = pl.ds(pl.multiple_of((2 * at_side + core) * width, width), width)
        ref[2:6, :] = turn_ref[:, at]
    mine_ref[10:12, :] = a_ref[...]
    theirs_ref[10:12, :] = b_ref[...]
    for at in range(4):
        ref = (mine_ref, theirs_ref)[at % 2]
        which = half if at < 2 else 1 - half
        cut = pl.ds(pl.multiple_of(which * one, one), one)
        ref[0:1, cut] = qkv_ref[:, 3 * one * at : 3 * one * at + one]
        ref[1:2, cut] = qkv_ref[:, 3 * one * at + 2 * one : 3 * one * (at + 1)]
    order = (0, 1, 2, 3), (0, 2, 1, 3)
    for part in range(2):
        for at, index in enumerate(order[part]):
            ref = (mine_ref, theirs_ref)[index % 2]
            which = half if index < 2 else 1 - half
            up_ref = (up_a_ref, up_b_ref)[part]
            ref[pl.ds(6 + 2 * which + part, 1), :] = up_ref[:, width * at : width * (at + 1)]


def collect(place, *sums):
    width = D // 4
    return pl.pallas_call(
        collect_kernel,
        name="collect",
        in_specs=[pl.BlockSpec(memory_space=pltpu.SMEM)]
        + [pl.BlockSpec(memory_space=pltpu.VMEM)] * 6,
        out_shape=[like((12, width), F32)] * 2,
    )(place, *sums)


def hand_out_kernel(a_ref, b_ref, *outs):
    sums = a_ref[...] + b_ref[...]
    width = a_ref.shape[1]
    for at in range(6):
        outs[at][...] = sums[at, :]
    for at in range(4):
        outs[6][width * at : width * (at + 1)] = sums[6 + at, :]
    for at in range(2):
        outs[7 + at][...] = sums[10 + at, :]


def hand_out(mine, got):
    width = mine.shape[1]
    one = like((width,), F32)
    return pl.pallas_call(
        hand_out_kernel,
        name="hand_out",
        out_shape=[one] * 6 + [like((4 * width,), F32)] + [one] * 2,
    )(mine, got)


def local(
    sizes,
    inputs,
    query_weight,
    key_weight,
    value_weight,
    query_bias,
    value_bias,
    out_weight,
    out_bias,
    up_weight,
    up_bias,
    down_weight,
    down_bias,
    first_gain,
    first_shift,
    second_gain,
    second_shift,
    cotangent,
):
    n_dp, n_row, n_xa, n_core = sizes
    my_x = lax.axis_index("xa")
    my_core = lax.axis_index("core")
    my_row = lax.axis_index("row")
    my_half = lax.axis_index("dp") % 2
    place = jnp.stack([my_core, my_x, my_half, my_row]).astype(jnp.int32)
    tokens_here, width = inputs.shape
    images = tokens_here // SEQ
    held = images // n_xa
    rows = held * PAD
    half = up_weight.shape[1] // 2
    quarter = half // 2
    heads_half = width // 2
    three = 3 * heads_half

    def swap(value, axis, size, bit=1):
        return lax.ppermute(value, axis, [(at, at ^ bit) for at in range(size)])

    def shifted(value, shift):
        return lax.ppermute(value, "row", [(at, (at + shift) % n_row) for at in range(n_row)])

    def across(value):
        return swap(value, "xa", n_xa)

    def beside(value):
        return swap(value, "core", n_core)

    def over(value):
        return swap(value, "dp", n_dp)

    def pick(value, at, axis):
        return lax.dynamic_index_in_dim(value, at, axis, keepdims=False)

    def in_order(mine, other, at):
        return jnp.where(at == 0, mine, other), jnp.where(at == 0, other, mine)

    def after(value, *others):
        return lax.optimization_barrier((value, *others))[0]

    def halves(value, axis):
        cut = value.shape[axis] // 2
        both = value.reshape(value.shape[:axis] + (2, cut) + value.shape[axis + 1 :])
        return pick(both, my_half, axis), pick(both, my_half ^ 1, axis)

    count = held * SEQ

    def send_tokens(value):
        return lax.dynamic_slice_in_dim(value, (my_x ^ 1) * count, count, 0)

    def wide_tokens(value, got):
        mine = lax.dynamic_slice_in_dim(value, my_x * count, count, 0)
        pair = jnp.concatenate([mine, got], axis=1).reshape(held, SEQ, 2 * width)
        pair = jnp.pad(pair, ((0, 0), (0, PAD - SEQ), (0, 0))).reshape(rows, 2 * width)
        other = beside(pair)
        left, right = in_order(pair, other, my_core)
        first_left, second_left = in_order(left[:, :width], left[:, width:], my_x)
        first_right, second_right = in_order(right[:, :width], right[:, width:], my_x)
        return jnp.concatenate([first_left, first_right, second_left, second_right], axis=1)

    attn_shard = jnp.concatenate(
        [halves(item, 1)[0] for item in (query_weight, key_weight, value_weight)]
        + [halves(out_weight, 0)[0].T],
        axis=1,
    )
    input_leaves = send_tokens(inputs)
    attn_shard = after(attn_shard, input_leaves)
    input_got = across(input_leaves)
    pieces = [attn_shard] + [shifted(attn_shard, shift) for shift in range(1, n_row)]
    small = pack(
        (
            out_bias,
            down_bias,
            first_gain,
            first_shift,
            second_gain,
            second_shift,
            query_bias,
            value_bias,
        ),
        up_bias,
    )
    fars = [across(piece) for piece in pieces]
    oths = [over(piece) for piece in pieces]
    small_far = across(small)
    vectors, qkv_bias, tile_bias = unpack(
        place, small, after(small_far, pieces[-1]), beside(small), beside(small_far)
    )
    out_bias_all, down_bias_all, gain_one, shift_one, gain_two, shift_two = (
        (vectors, pl.BlockSpec((None, 1, D), lambda i, *_, at=at: (at, 0, 0))) for at in range(6)
    )
    wide_input = wide_tokens(inputs, after(input_got, pieces[-1]))
    far_oths = [over(far) for far in fars[:-1]]
    far_oths.append(across(after(oths[-1], wide_input, qkv_bias)))

    def gather(part):
        up_part = halves(up_weight, 1)[0][:, quarter * part : quarter * (part + 1)]
        down_part = halves(down_weight, 0)[0][quarter * part : quarter * (part + 1)].T
        shard = after(jnp.concatenate([up_part, down_part], axis=1), *pieces)
        return lax.all_gather(shard, "row", axis=0, tiled=True)

    own_a, own_b = gather(0), gather(1)
    grad_got = across(after(send_tokens(cotangent), wide_input))

    wide_one, qkv, attn_weights = norm_qkv(
        place, wide_input, gain_one, shift_one, qkv_bias, (*pieces, *fars, *oths, *far_oths)
    )
    oth_a, far_a = over(own_a), across(own_a)
    oth_b, far_b = over(own_b), across(own_b)
    attended, probs = attend(qkv)
    mixed = mm_nt(attended, attn_weights[:, 4 * three :]).astype(BF16)
    mixed_other = beside(mixed)
    wide_grad = wide_tokens(cotangent, after(grad_got, mixed))
    far_oth_a = over(far_a)
    middle_sum, wide_two = middle(wide_input, mixed, mixed_other, out_bias_all, gain_two, shift_two)
    far_oth_b = across(oth_b)

    def tiles(value, first, end):
        return value[:, quarter * first : quarter * end]

    gate_a, pre_a, up_sums_a, low_a, lift_a = mlp(
        place, wide_two, wide_grad, tile_bias, (own_a, far_a, oth_a, far_oth_a)
    )
    up_over = mm_tn(wide_two, tiles(pre_a, 2, 4)).astype(BF16)
    down_a = mm_tn(wide_grad, gate_a).astype(BF16)
    up_over_got = over(up_over)
    down_piece = lax.psum_scatter(down_a, "row", scatter_dimension=0, tiled=True)
    gate_b, pre_b, up_sums_b, low_mine, low_theirs, lifted_two = mlp(
        place,
        after(wide_two, up_over, down_a),
        wide_grad,
        tile_bias,
        (own_b, oth_b, far_b, far_oth_b),
        (low_a, lift_a),
    )

    def wide_add(mine, got):
        return (mine.astype(F32) + got.astype(F32)).astype(BF16)

    def same_half(value):
        if n_dp == 2:
            return value
        groups = [[at + bit for at in range(0, n_dp, 2)] for bit in range(2)]
        return lax.psum(value.astype(F32), "dp", axis_index_groups=groups).astype(BF16)

    def scatter(value):
        return lax.psum_scatter(value, "row", scatter_dimension=0, tiled=True)

    lifted_other = beside(lifted_two)
    low_other = beside(low_theirs)
    up_across = mm_tn(wide_two, tiles(pre_b, 2, 4)).astype(BF16)
    down_over = mm_tn(wide_grad, tiles(gate_b, 2, 4)).astype(BF16)
    up_across_got, down_over_got = across(up_across), over(down_over)
    down_x_got = across(after(down_piece, up_across, down_over)[:, half:])

    middle_grad, attn_grad, head_grad, turn_sums, out_mine, out_theirs = turn(
        place,
        middle_sum,
        wide_grad,
        lifted_two,
        after(lifted_other, up_across, down_over),
        low_mine,
        low_other,
        gain_two,
        down_bias_all,
        attn_weights,
    )
    out_all = mm_tn(attn_grad, attended).astype(BF16)
    out_over_got = over(out_all[:, 2 * heads_half :])
    up_over_got, up_across_got, down_over_got, _ = lax.optimization_barrier(
        (up_over_got, up_across_got, down_over_got, out_all)
    )
    up_a = wide_add(mm_tn(wide_two, tiles(pre_a, 0, 2)), up_over_got)
    up_b = wide_add(mm_tn(wide_two, tiles(pre_b, 0, 2)), up_across_got)
    down_b = wide_add(mm_tn(wide_grad, tiles(gate_b, 0, 2)), down_over_got)
    up_a_got, up_b_got = across(up_a[:, quarter:]), over(up_b[:, quarter:])
    out_own = wide_add(out_all[:, : 2 * heads_half], after(out_over_got, down_b))
    out_far_got = across(out_own[:, heads_half:])
    down_x = wide_add(down_piece[:, :half], after(down_x_got, down_b))
    down_y_got = over(down_x)
    down_b_got = across(down_b[:, quarter:])
    out_got = across(after(out_theirs, down_b))
    dqkv, qkv_sums = attend_back(qkv, probs, after(head_grad, up_a, up_b, out_own, down_x))
    up_sum = join(
        up_a, up_a_got, up_b, up_b_got, down_b, down_b_got, out_own, after(out_far_got, dqkv)
    )
    up_piece = same_half(scatter(up_sum))

    def to_feature_blocks(mine, got, dtype):
        first, second = in_order(mine.astype(dtype), got.astype(dtype), my_x)
        both = jnp.concatenate([first, second]).reshape(images, PAD, width)
        return both[:, :SEQ].reshape(tokens_here, width)

    cut = 2 * heads_half
    split = 3 * three + cut
    dqkv = after(dqkv, up_sum)
    far_oth_qk = mm_tn(wide_one, dqkv[:, 3 * three : split]).astype(BF16)
    far_oth_v = mm_tn(wide_one, dqkv[:, split:]).astype(BF16)
    qk_got, v_got = over(far_oth_qk), across(far_oth_v)
    lifted_one = mm_nt(
        after(dqkv, far_oth_qk, far_oth_v), attn_weights[:, : 4 * three]
    ).astype(BF16)
    lifted_one_other = beside(lifted_one)

    near_oth = wide_add(
        mm_tn(wide_one, dqkv[:, 2 * three : 3 * three]),
        jnp.pad(after(v_got, lifted_one), ((0, 0), (cut, 0))),
    )
    near_oth_got = over(near_oth)
    far_own = wide_add(
        mm_tn(wide_one, dqkv[:, three : 2 * three]),
        jnp.pad(after(qk_got, near_oth), ((0, 0), (0, three - cut))),
    )
    far_own_got = across(far_own)
    near_own = mm_tn(after(wide_one, far_own), dqkv[:, :three])
    input_mine, input_theirs, late_mine, late_theirs = last(
        place, wide_input, middle_grad, lifted_one, after(lifted_one_other, near_own), gain_one
    )
    mine_sums, theirs_sums = collect(
        place, turn_sums, qkv_sums, up_sums_a, up_sums_b, late_mine, late_theirs
    )

    near_sum = (near_own + near_oth_got.astype(F32) + after(far_own_got, mine_sums).astype(F32)).astype(
        BF16
    )
    strip = D // n_row

    def rows_of(value, shift):
        return lax.dynamic_slice_in_dim(value, (my_row + shift) % n_row * strip, strip, 0)

    gots = [shifted(rows_of(near_sum, shift), shift) for shift in range(1, n_row)]
    input_got = across(after(input_theirs, near_sum))
    sums = mine_sums + across(after(theirs_sums, near_sum))
    steps = [("row", n_row, 1 << bit) for bit in range(n_row.bit_length() - 1)]
    steps += [("dp", n_dp, 1 << bit) for bit in range(n_dp.bit_length() - 1)]
    for step in steps[:-1]:
        sums = sums + swap(sums, *step)
    sums = hand_out(sums, swap(sums, *steps[-1]))
    outputs = to_feature_blocks(out_mine, after(out_got, near_sum), BF16)

    qkv_total = rows_of(near_sum, 0).astype(F32)
    for got in gots:
        qkv_total = qkv_total + got.astype(F32)
    qkv_piece = same_half(qkv_total.astype(BF16))
    qkv_other = over(qkv_piece)
    input_grad = to_feature_blocks(input_mine, input_got, F32)
    up_other = over(up_piece)

    down_total = down_x.astype(F32) + jnp.concatenate(
        [down_y_got[:, quarter:], down_y_got[:, :quarter]], axis=1
    ).astype(F32)
    if n_dp > 2:
        groups = [[at + bit for at in range(0, n_dp, 2)] for bit in range(2)]
        down_total = lax.psum(down_total, "dp", axis_index_groups=groups)

    def down_half(first_part, second):
        return jnp.concatenate([first_part, tiles(second, 2, 3).astype(F32)], axis=1)

    down_first, down_second = in_order(
        down_half(down_total[:, :quarter], up_piece),
        down_half(down_total[:, quarter:], up_other),
        my_half,
    )
    down_grad = jnp.concatenate([down_first, down_second], axis=1).T

    def both_halves(mine, other, low, high):
        first, second = in_order(mine[:, low:high], other[:, low:high], my_half)
        return jnp.concatenate([first, second], axis=1).astype(F32)

    up_grad = both_halves(up_piece, up_other, 0, half)
    start = half + quarter
    out_grad = both_halves(up_piece, up_other, start, start + heads_half).T
    query_grad, key_grad, value_grad = (
        both_halves(qkv_piece, qkv_other, heads_half * at, heads_half * (at + 1))
        for at in range(3)
    )

    return (
        outputs,
        input_grad,
        query_grad,
        key_grad,
        value_grad,
        sums[0],
        sums[1],
        out_grad,
        sums[2],
        up_grad,
        sums[6],
        down_grad,
        sums[3],
        sums[7],
        sums[8],
        sums[4],
        sums[5],
    )


def solution(mesh):
    n_dp, n_row, n_col = (mesh.shape[name] for name in ("dp", "row", "col"))
    sizes = (n_dp, n_row, n_col // 2, 2)
    split = Mesh(mesh.devices.reshape(sizes), ("dp", "row", "xa", "core"))
    col = ("xa", "core")
    tokens, rows, cols, vec = P(("dp", "row"), col), P("row", col), P(col, "row"), P(col)
    in_specs = (
        (tokens, rows, rows, rows, vec, vec, cols, vec, rows, vec, cols)
        + (vec,) * 5
        + (tokens,)
    )
    out_specs = (
        (tokens, tokens, rows, rows, rows, vec, vec, cols, vec, rows, vec, cols) + (vec,) * 5
    )

    def body(*args):
        return local(sizes, *args)

    return jax.shard_map(
        body, mesh=split, in_specs=in_specs, out_specs=out_specs, check_vma=False
    )
```

```python
import functools
import math

import jax
import jax.numpy as jnp
from jax import lax
from jax.experimental import pallas as pl
from jax.experimental.pallas import tpu as pltpu
from jax.sharding import Mesh, PartitionSpec as P


D = 1024
HD = 64
SEQ = 577
PAD = 592
TM = 296
EPS = 1e-06
F32 = jnp.float32
BF16 = jnp.bfloat16
VMEM_LIMIT = 60 * 1024 * 1024
ROOT_HALF = math.sqrt(0.5)
DENSITY = 1.0 / math.sqrt(2.0 * math.pi)


def mm(a, b):
    return lax.dot_general(a, b, (((1,), (0,)), ((), ())), preferred_element_type=F32)


def mm_nt(a, b):
    return lax.dot_general(a, b, (((1,), (1,)), ((), ())), preferred_element_type=F32)


def mm_tn(a, b):
    return lax.dot_general(a, b, (((0,), (0,)), ((), ())), preferred_element_type=F32)


def row_mean(v):
    return jnp.sum(v, axis=1, keepdims=True) * (1.0 / D)


def col_sum(v):
    return jnp.sum(v, axis=0, keepdims=True)


def stats(rows):
    middle = row_mean(rows)
    spread = row_mean(rows * rows) - middle * middle
    return middle, lax.rsqrt(spread + EPS)


def params(n):
    return pltpu.CompilerParams(
        dimension_semantics=("arbitrary",) * n, vmem_limit_bytes=VMEM_LIMIT
    )


def cost(flops, moved, exps=0):
    return pl.CostEstimate(flops=int(flops), bytes_accessed=int(moved), transcendentals=int(exps))


def like(shape, dtype):
    return jax.ShapeDtypeStruct(shape, dtype)


def row_spec(cols):
    return pl.BlockSpec((TM, cols), lambda i, *_: (i, 0))


def fixed(shape):
    return pl.BlockSpec(shape, lambda *_: (0,) * len(shape))


def held_once(shape):
    return pl.BlockSpec(shape, lambda *_: (0,) * len(shape), pipeline_mode=pl.Buffered(1))


def add_up(ref, first, part):
    @pl.when(first)
    def _():
        ref[...] = part

    @pl.when(jnp.logical_not(first))
    def _():
        ref[...] += part


def norm_qkv_kernel(place_ref, x_ref, gain_ref, shift_ref, bias_ref, *refs):
    pieces, (n_ref, o_ref, w_ref) = refs[:-3], refs[-3:]
    n_row = len(pieces) // 4
    strip, wide = pieces[0].shape
    one = wide // 4

    @pl.when(pl.program_id(0) == 0)
    def _():
        for shift in range(n_row):
            start = lax.rem(place_ref[3] - shift + n_row, n_row) * strip
            rows = pl.ds(pl.multiple_of(start, strip), strip)
            for block in range(4):
                piece = pieces[n_row * block + shift]
                w_ref[rows, 3 * one * block : 3 * one * (block + 1)] = piece[:, : 3 * one]
                w_ref[rows, (12 + block) * one : (13 + block) * one] = piece[:, 3 * one :]

    x = x_ref[...].astype(F32)
    middle, scaled = stats(x)
    n = (((x - middle) * scaled) * gain_ref[...] + shift_ref[...]).astype(BF16)
    n_ref[...] = n
    o_ref[...] = (mm(n, w_ref[:, : 12 * one]) + bias_ref[...]).astype(BF16)


def norm_qkv(place, x, gain, shift, bias, pieces):
    rows = x.shape[0]
    wide = pieces[0].shape[1]
    out = 3 * wide
    return pl.pallas_call(
        norm_qkv_kernel,
        name="norm_qkv",
        grid_spec=pltpu.PrefetchScalarGridSpec(
            num_scalar_prefetch=1,
            grid=(rows // TM,),
            in_specs=[row_spec(D), gain[1], shift[1], fixed((1, out))]
            + [held_once(pieces[0].shape)] * len(pieces),
            out_specs=[row_spec(D), row_spec(out), held_once((D, 4 * wide))],
        ),
        out_shape=[like((rows, D), BF16), like((rows, out), BF16), like((D, 4 * wide), BF16)],
        compiler_params=params(1),
        cost_estimate=cost(2 * rows * D * out, 16 * rows * D),
    )(place, x, gain[0], shift[0], bias, *pieces)


def attend_kernel(qkv_ref, o_ref, p_ref):
    live = lax.broadcasted_iota(jnp.int32, (1, PAD), 1) < SEQ
    step = 2 * HD
    items = [(h, slice(r, r + TM)) for h in range(2) for r in range(0, PAD, TM)]

    def score(h, rows):
        q = qkv_ref[rows, HD * h : HD * (h + 1)] * jnp.asarray(0.125, BF16)
        return mm_nt(q, qkv_ref[:, step + HD * h : step + HD * (h + 1)])

    scores = [score(*item) for item in items[:3]]
    for at, (h, rows) in enumerate(items):
        if at + 3 < len(items):
            scores.append(score(*items[at + 3]))
        s = jnp.where(live, scores[at], -1e30)
        e = jnp.exp(s - jnp.max(s, axis=1, keepdims=True))
        p = (e * (1.0 / jnp.sum(e, axis=1, keepdims=True))).astype(BF16)
        p_ref[h, rows, :] = p
        v = qkv_ref[:, 2 * step + HD * h : 2 * step + HD * (h + 1)]
        o_ref[rows, HD * h : HD * (h + 1)] = mm(p, v).astype(BF16)


def attend(qkv, before=()):
    rows, cols = qkv.shape
    pairs = cols // (6 * HD)
    held = rows // PAD
    start = pairs // 2 if before else 0

    def kernel(*refs):
        attend_kernel(refs[0], refs[-2], refs[-1])

    return pl.pallas_call(
        kernel,
        grid=(pairs // 2, held),
        name="attend",
        in_specs=[pl.BlockSpec((PAD, 6 * HD), lambda p, i: (i, p + start))]
        + [pl.BlockSpec(memory_space=pl.ANY)] * len(before),
        out_specs=[
            pl.BlockSpec((PAD, 2 * HD), lambda p, i: (i, p + start)),
            pl.BlockSpec((None, 2, PAD, PAD), lambda p, i: (i, p + start, 0, 0)),
        ],
        out_shape=[like((rows, cols // 3), BF16), like((held, 2 * pairs, PAD, PAD), BF16)],
        input_output_aliases={1: 0, 2: 1} if before else {},
        compiler_params=params(2),
        cost_estimate=cost(8 * rows * PAD * cols, 20 * rows * D, 2 * rows * PAD * pairs),
    )(qkv, *before)


def attend_back_kernel(qkv_ref, p_ref, g_ref, d_ref, sum_ref):
    step = 2 * HD

    def cut(h, w):
        return slice(step * w + HD * h, step * w + HD * (h + 1))

    grads = [g_ref[:, HD * h : HD * (h + 1)] for h in range(2)]
    dprobs = [mm_nt(grads[h], qkv_ref[:, cut(h, 2)]) for h in range(2)]
    dscores = []
    for h in range(2):
        p = p_ref[h].astype(F32)
        z = jnp.sum(p * dprobs[h], axis=1, keepdims=True)
        dscores.append((p * (dprobs[h] - z)).astype(BF16))
        d_ref[:, cut(h, 2)] = mm_tn(p_ref[h], grads[h]).astype(BF16)
    for h in range(2):
        d_ref[:, cut(h, 0)] = (mm(dscores[h], qkv_ref[:, cut(h, 1)]) * 0.125).astype(BF16)
        d_ref[:, cut(h, 1)] = (mm_tn(dscores[h], qkv_ref[:, cut(h, 0)]) * 0.125).astype(BF16)
    add_up(sum_ref, pl.program_id(1) == 0, col_sum(d_ref[...].astype(F32)))


def attend_back(qkv, probs, grads):
    rows, cols = qkv.shape
    pairs = cols // (6 * HD)
    held = rows // PAD
    three = pl.BlockSpec((PAD, 6 * HD), lambda p, i: (i, p))
    return pl.pallas_call(
        attend_back_kernel,
        grid=(pairs, held),
        name="attend_back",
        in_specs=[
            three,
            pl.BlockSpec((None, 2, PAD, PAD), lambda p, i: (i, p, 0, 0)),
            pl.BlockSpec((PAD, 2 * HD), lambda p, i: (i, p)),
        ],
        out_specs=[three, pl.BlockSpec((1, 6 * HD), lambda p, i: (0, p))],
        out_shape=[like((rows, cols), BF16), like((1, cols), F32)],
        compiler_params=params(2),
        cost_estimate=cost(20 * rows * PAD * cols, 50 * rows * D),
    )(qkv, probs, grads)


def middle_kernel(x_ref, a_ref, b_ref, bias_ref, gain_ref, shift_ref, h_ref, n_ref):
    h = x_ref[...].astype(F32) + (a_ref[...].astype(F32) + b_ref[...].astype(F32)) + bias_ref[...]
    h_ref[...] = h
    middle, scaled = stats(h)
    n_ref[...] = (((h - middle) * scaled) * gain_ref[...] + shift_ref[...]).astype(BF16)


def middle(x, a, b, bias, gain, shift):
    rows = x.shape[0]
    return pl.pallas_call(
        middle_kernel,
        grid=(rows // TM,),
        name="middle",
        in_specs=[row_spec(D)] * 3 + [bias[1], gain[1], shift[1]],
        out_specs=[row_spec(D)] * 2,
        out_shape=[like((rows, D), F32), like((rows, D), BF16)],
        compiler_params=params(1),
        cost_estimate=cost(20 * rows * D, 12 * rows * D),
    )(x, a, b, bias[0], gain[0], shift[0])


def mlp_kernel(final, split, place_ref, n_ref, dy_ref, bias_ref, *refs):
    packs = refs[:5]
    before = refs[5:7] if final else ()
    rest = refs[5 + len(before) :]
    g_ref, du_ref, bsum_ref = rest[:3]
    buf, sem = rest[6:8] if final else rest[5:7]
    i = pl.program_id(0)
    tn = g_ref.shape[1] // 4

    @pl.when(i == 0)
    def _():
        copies = []
        for tile in range(4):
            for part in range(2):
                if tile == 3 and split:
                    source = packs[tile + part]
                else:
                    source = packs[tile].at[:, pl.ds(part * tn, tn)]
                copies.append(
                    pltpu.make_async_copy(
                        source,
                        buf.at[part, :, pl.ds(tile * tn, tn)],
                        sem.at[part, tile],
                    )
                )
        for copy in copies:
            copy.start()
        for copy in copies:
            copy.wait()

    up, down = buf[0], buf[1]
    u = mm(n_ref[...], up) + bias_ref[...]
    cdf = 0.5 * (1.0 + lax.erf(u * ROOT_HALF))
    g = (u * cdf).astype(BF16)
    slope = cdf + u * (jnp.exp(-0.5 * u * u) * DENSITY)
    for at, tile in enumerate((0, 2, 1, 3)):
        g_ref[:, at * tn : (at + 1) * tn] = g[:, tile * tn : (tile + 1) * tn]
    du = (mm(dy_ref[...], down) * slope).astype(BF16)
    du_ref[...] = du
    add_up(bsum_ref, i == 0, col_sum(du.astype(F32)))
    low = mm_nt(g, down)
    lift = mm_nt(du, up)
    if not final:
        rest[3][...] = low.astype(BF16)
        rest[4][...] = lift.astype(BF16)
        return
    mine_ref, theirs_ref, lift_ref = rest[3:6]
    held = rest[8]
    lift_ref[...] = (lift + before[1][...].astype(F32)).astype(BF16)
    held[...] = low + before[0][...].astype(F32)
    width = D // 4
    core = place_ref[0]
    for far in range(2):
        here = pl.multiple_of((2 * far + core) * width, width)
        other = pl.multiple_of((2 * far + 1 - core) * width, width)
        mine_ref[:, far * width : (far + 1) * width] = held[:, pl.ds(here, width)]
        theirs_ref[:, far * width : (far + 1) * width] = held[:, pl.ds(other, width)].astype(BF16)


def mlp(place, n2, dy, bias, packs, before=()):
    split = len(packs) == 5
    packs = packs if split else (*packs, packs[-1])
    rows = n2.shape[0]
    hid = 2 * packs[0].shape[1]
    part = 1 if before else 0

    def block(cols):
        return pl.BlockSpec((PAD, cols), lambda i, *_: (i, 0))

    out_specs = [block(hid), block(hid), fixed((1, hid))]
    out_shape = [like((rows, hid), BF16), like((rows, hid), BF16), like((1, hid), F32)]
    scratch = [pltpu.VMEM((2, D, hid), BF16), pltpu.SemaphoreType.DMA((2, 4))]
    if before:
        out_specs += [block(D // 2), block(D // 2), block(D)]
        out_shape += [like((rows, D // 2), F32), like((rows, D // 2), BF16), like((rows, D), BF16)]
        scratch += [pltpu.VMEM((PAD, D), F32)]
    else:
        out_specs += [block(D), block(D)]
        out_shape += [like((rows, D), BF16)] * 2
    return pl.pallas_call(
        functools.partial(mlp_kernel, bool(before), split),
        name="mlp_second" if before else "mlp_first",
        grid_spec=pltpu.PrefetchScalarGridSpec(
            num_scalar_prefetch=1,
            grid=(rows // PAD,),
            in_specs=[block(D), block(D), pl.BlockSpec((1, hid), lambda i, *_: (0, part))]
            + [pl.BlockSpec(memory_space=pl.ANY)] * 5
            + [block(D)] * len(before),
            out_specs=out_specs,
            scratch_shapes=scratch,
        ),
        out_shape=out_shape,
        compiler_params=params(1),
        cost_estimate=cost(8 * rows * D * hid, 20 * rows * D, 2 * rows * hid),
    )(place, n2, dy, bias, *packs, *before)


def turn_kernel(
    place_ref, h_ref, dy_ref, a_ref, b_ref, low_ref, other_ref, gain_ref, bias_ref, w_ref,
    dh_ref, da_ref, do_ref, sums_ref, mine_ref, theirs_ref, held,
):
    h = h_ref[...]
    held[...] = h + bias_ref[...]
    core, side = place_ref[0], place_ref[1]
    width = D // 4
    low = low_ref[...] + other_ref[...].astype(F32)
    for far in range(2):
        at = pl.ds(pl.multiple_of((2 * far + core) * width, width), width)
        out = (held[:, at] + low[:, far * width : (far + 1) * width]).astype(BF16)

        @pl.when(side == far)
        def _(out=out):
            mine_ref[...] = out

        @pl.when(side != far)
        def _(out=out):
            theirs_ref[...] = out

    middle, scaled = stats(h)
    c = (h - middle) * scaled
    dn = a_ref[...].astype(F32) + b_ref[...].astype(F32)
    dy = dy_ref[...].astype(F32)
    e = dn * gain_ref[...]
    dh = dy + scaled * (e - row_mean(e) - c * row_mean(e * c))
    dh_ref[...] = dh
    da = dh.astype(BF16)
    da_ref[...] = da
    do_ref[...] = mm(da, w_ref[...]).astype(BF16)
    part = jnp.concatenate(
        [col_sum(da.astype(F32)), col_sum(dy), col_sum(dn * c), col_sum(dn)], axis=0
    )
    add_up(sums_ref, pl.program_id(0) == 0, part)


def turn(place, h, dy, a, b, low_mine, low_other, gain, bias, weights):
    rows = h.shape[0]
    wide = weights.shape[1] // 4
    width = D // 4
    return pl.pallas_call(
        turn_kernel,
        name="turn",
        grid_spec=pltpu.PrefetchScalarGridSpec(
            num_scalar_prefetch=1,
            grid=(rows // TM,),
            in_specs=[row_spec(D)] * 4
            + [row_spec(D // 2)] * 2
            + [gain[1], bias[1]]
            + [pl.BlockSpec((D, wide), lambda i, *_: (0, 3), pipeline_mode=pl.Buffered(1))],
            out_specs=[
                row_spec(D),
                row_spec(D),
                row_spec(wide),
                fixed((4, D)),
                row_spec(width),
                row_spec(width),
            ],
            scratch_shapes=[pltpu.VMEM((TM, D), F32)],
        ),
        out_shape=[
            like((rows, D), F32),
            like((rows, D), BF16),
            like((rows, wide), BF16),
            like((4, D), F32),
            like((rows, width), BF16),
            like((rows, width), BF16),
        ],
        compiler_params=params(1),
        cost_estimate=cost(2 * rows * D * wide, 20 * rows * D),
    )(place, h, dy, a, b, low_mine, low_other, gain[0], bias[0], weights)


def last_kernel(
    place_ref, x_ref, dh_ref, a_ref, b_ref, gain_ref, mine_ref, theirs_ref, sum_mine, sum_theirs, held, sums
):
    x = x_ref[...].astype(F32)
    middle, scaled = stats(x)
    c = (x - middle) * scaled
    dn = a_ref[...].astype(F32) + b_ref[...].astype(F32)
    e = dn * gain_ref[...]
    held[...] = dh_ref[...] + scaled * (e - row_mean(e) - c * row_mean(e * c))
    width = D // 4
    core, side = place_ref[0], place_ref[1]
    here = pl.ds(pl.multiple_of((2 * side + core) * width, width), width)
    there = pl.ds(pl.multiple_of((2 * (1 - side) + core) * width, width), width)
    mine_ref[...] = held[:, here]
    theirs_ref[...] = held[:, there].astype(BF16)
    i = pl.program_id(0)
    add_up(sums, i == 0, jnp.concatenate([col_sum(dn * c), col_sum(dn)], axis=0))

    @pl.when(i == pl.num_programs(0) - 1)
    def _():
        sum_mine[...] = sums[:, here]
        sum_theirs[...] = sums[:, there]


def last(place, x, dh, a, b, gain):
    rows = x.shape[0]
    width = D // 4
    return pl.pallas_call(
        last_kernel,
        name="last",
        grid_spec=pltpu.PrefetchScalarGridSpec(
            num_scalar_prefetch=1,
            grid=(rows // TM,),
            in_specs=[row_spec(D)] * 4 + [gain[1]],
            out_specs=[row_spec(width), row_spec(width), fixed((2, width)), fixed((2, width))],
            scratch_shapes=[pltpu.VMEM((TM, D), F32), pltpu.VMEM((2, D), F32)],
        ),
        out_shape=[
            like((rows, width), F32),
            like((rows, width), BF16),
            like((2, width), F32),
            like((2, width), F32),
        ],
        compiler_params=params(1),
        cost_estimate=cost(20 * rows * D, 12 * rows * D),
    )(place, x, dh, a, b, gain[0])


def join_kernel(*refs):
    out_ref = refs[-1]
    start = 0
    for mine, got in zip(refs[:-1:2], refs[1:-1:2]):
        width = got.shape[1]
        total = mine[...].astype(F32) + got[...].astype(F32)
        out_ref[:, start : start + width] = total.astype(BF16)
        start += width


def join(*parts):
    rows = parts[0].shape[0]
    tm = rows // 4
    widths = [item.shape[1] for item in parts[1::2]]
    return pl.pallas_call(
        join_kernel,
        grid=(4,),
        name="join",
        in_specs=[
            pl.BlockSpec((tm, width), lambda i: (i, 0)) for width in widths for _ in range(2)
        ],
        out_specs=pl.BlockSpec((tm, sum(widths)), lambda i: (i, 0)),
        out_shape=like((rows, sum(widths)), BF16),
        compiler_params=params(1),
        cost_estimate=cost(rows * sum(widths), 6 * rows * sum(widths)),
    )(*parts)


def pack_kernel(*refs):
    out_ref = refs[-1]
    width = refs[0].shape[0]
    for at, ref in enumerate(refs[:-2]):
        out_ref[at, :] = ref[...]
    for at in range(4):
        out_ref[len(refs) - 2 + at, :] = refs[-2][width * at : width * (at + 1)]


def pack(vectors, long_vector):
    width = vectors[0].shape[0]
    return pl.pallas_call(
        pack_kernel,
        name="pack",
        out_shape=like((len(vectors) + 4, width), F32),
    )(*vectors, long_vector)


def unpack_kernel(place_ref, own, far, own_other, far_other, vec_ref, qkv_ref, tile_ref):
    core, side, half = place_ref[0], place_ref[1], place_ref[2]
    width = own.shape[1]
    one = width // 2

    def put(ref, at_side, at_core):
        at = pl.multiple_of((2 * at_side + at_core) * width, width)
        for k in range(6):
            vec_ref[k, :, pl.ds(at, width)] = ref[k : k + 1, :]

    put(own, side, core)
    put(far, 1 - side, core)
    put(own_other, side, 1 - core)
    put(far_other, 1 - side, 1 - core)
    qkv_ref[...] = jnp.zeros_like(qkv_ref)
    blocks = ((own, half), (far, half), (own, 1 - half), (far, 1 - half))
    for at, (ref, which) in enumerate(blocks):
        cut = pl.ds(pl.multiple_of(which * one, one), one)
        qkv_ref[:, 3 * one * at : 3 * one * at + one] = ref[6:7, cut]
        qkv_ref[:, 3 * one * at + 2 * one : 3 * one * (at + 1)] = ref[7:8, cut]
    order = (0, 1, 2, 3), (0, 2, 1, 3)
    for part in range(2):
        for at, index in enumerate(order[part]):
            ref, which = blocks[index]
            start = width * (4 * part + at)
            tile_ref[:, start : start + width] = ref[pl.ds(8 + 2 * which + part, 1), :]


def unpack(place, own, far, own_other, far_other):
    width = own.shape[1]
    return pl.pallas_call(
        unpack_kernel,
        name="unpack",
        in_specs=[pl.BlockSpec(memory_space=pltpu.SMEM)]
        + [pl.BlockSpec(memory_space=pltpu.VMEM)] * 4,
        out_shape=[like((6, 1, D), F32), like((1, 6 * width), F32), like((1, 8 * width), F32)],
    )(place, own, far, own_other, far_other)


def collect_kernel(
    place_ref, turn_ref, qkv_ref, up_a_ref, up_b_ref, a_ref, b_ref, mine_ref, theirs_ref
):
    core, side, half = place_ref[0], place_ref[1], place_ref[2]
    width = mine_ref.shape[1]
    one = width // 2
    for ref, at_side in ((mine_ref, side), (theirs_ref, 1 - side)):
        at = pl.ds(pl.multiple_of((2 * at_side + core) * width, width), width)
        ref[2:6, :] = turn_ref[:, at]
    mine_ref[10:12, :] = a_ref[...]
    theirs_ref[10:12, :] = b_ref[...]
    for at in range(4):
        ref = (mine_ref, theirs_ref)[at % 2]
        which = half if at < 2 else 1 - half
        cut = pl.ds(pl.multiple_of(which * one, one), one)
        ref[0:1, cut] = qkv_ref[:, 3 * one * at : 3 * one * at + one]
        ref[1:2, cut] = qkv_ref[:, 3 * one * at + 2 * one : 3 * one * (at + 1)]
    order = (0, 1, 2, 3), (0, 2, 1, 3)
    for part in range(2):
        for at, index in enumerate(order[part]):
            ref = (mine_ref, theirs_ref)[index % 2]
            which = half if index < 2 else 1 - half
            up_ref = (up_a_ref, up_b_ref)[part]
            ref[pl.ds(6 + 2 * which + part, 1), :] = up_ref[:, width * at : width * (at + 1)]


def collect(place, *sums):
    width = D // 4
    return pl.pallas_call(
        collect_kernel,
        name="collect",
        in_specs=[pl.BlockSpec(memory_space=pltpu.SMEM)]
        + [pl.BlockSpec(memory_space=pltpu.VMEM)] * 6,
        out_shape=[like((12, width), F32)] * 2,
    )(place, *sums)


def hand_out_kernel(a_ref, b_ref, *outs):
    sums = a_ref[...] + b_ref[...]
    width = a_ref.shape[1]
    for at in range(6):
        outs[at][...] = sums[at, :]
    for at in range(4):
        outs[6][width * at : width * (at + 1)] = sums[6 + at, :]
    for at in range(2):
        outs[7 + at][...] = sums[10 + at, :]


def hand_out(mine, got):
    width = mine.shape[1]
    one = like((width,), F32)
    return pl.pallas_call(
        hand_out_kernel,
        name="hand_out",
        out_shape=[one] * 6 + [like((4 * width,), F32)] + [one] * 2,
    )(mine, got)


def local(
    sizes,
    inputs,
    query_weight,
    key_weight,
    value_weight,
    query_bias,
    value_bias,
    out_weight,
    out_bias,
    up_weight,
    up_bias,
    down_weight,
    down_bias,
    first_gain,
    first_shift,
    second_gain,
    second_shift,
    cotangent,
):
    n_dp, n_row, n_xa, n_core = sizes
    my_x = lax.axis_index("xa")
    my_core = lax.axis_index("core")
    my_row = lax.axis_index("row")
    my_half = lax.axis_index("dp") % 2
    place = jnp.stack([my_core, my_x, my_half, my_row]).astype(jnp.int32)
    tokens_here, width = inputs.shape
    images = tokens_here // SEQ
    held = images // n_xa
    rows = held * PAD
    half = up_weight.shape[1] // 2
    quarter = half // 2
    heads_half = width // 2
    three = 3 * heads_half

    def swap(value, axis, size, bit=1):
        return lax.ppermute(value, axis, [(at, at ^ bit) for at in range(size)])

    def shifted(value, shift):
        return lax.ppermute(value, "row", [(at, (at + shift) % n_row) for at in range(n_row)])

    def across(value):
        return swap(value, "xa", n_xa)

    def beside(value):
        return swap(value, "core", n_core)

    def over(value):
        return swap(value, "dp", n_dp)

    def pick(value, at, axis):
        return lax.dynamic_index_in_dim(value, at, axis, keepdims=False)

    def in_order(mine, other, at):
        return jnp.where(at == 0, mine, other), jnp.where(at == 0, other, mine)

    def after(value, *others):
        return lax.optimization_barrier((value, *others))[0]

    def halves(value, axis):
        cut = value.shape[axis] // 2
        both = value.reshape(value.shape[:axis] + (2, cut) + value.shape[axis + 1 :])
        return pick(both, my_half, axis), pick(both, my_half ^ 1, axis)

    count = held * SEQ

    def send_tokens(value):
        return lax.dynamic_slice_in_dim(value, (my_x ^ 1) * count, count, 0)

    def wide_tokens(value, got):
        mine = lax.dynamic_slice_in_dim(value, my_x * count, count, 0)
        pair = jnp.concatenate([mine, got], axis=1).reshape(held, SEQ, 2 * width)
        pair = jnp.pad(pair, ((0, 0), (0, PAD - SEQ), (0, 0))).reshape(rows, 2 * width)
        other = beside(pair)
        left, right = in_order(pair, other, my_core)
        first_left, second_left = in_order(left[:, :width], left[:, width:], my_x)
        first_right, second_right = in_order(right[:, :width], right[:, width:], my_x)
        return jnp.concatenate([first_left, first_right, second_left, second_right], axis=1)

    attn_shard = jnp.concatenate(
        [halves(item, 1)[0] for item in (query_weight, key_weight, value_weight)]
        + [halves(out_weight, 0)[0].T],
        axis=1,
    )
    input_leaves = send_tokens(inputs)
    attn_shard = after(attn_shard, input_leaves)
    input_got = across(input_leaves)
    pieces = [attn_shard] + [shifted(attn_shard, shift) for shift in range(1, n_row)]
    small = pack(
        (
            out_bias,
            down_bias,
            first_gain,
            first_shift,
            second_gain,
            second_shift,
            query_bias,
            value_bias,
        ),
        up_bias,
    )
    fars = [across(piece) for piece in pieces]
    oths = [over(piece) for piece in pieces]
    small_far = across(small)
    vectors, qkv_bias, tile_bias = unpack(
        place, small, after(small_far, pieces[-1]), beside(small), beside(small_far)
    )
    out_bias_all, down_bias_all, gain_one, shift_one, gain_two, shift_two = (
        (vectors, pl.BlockSpec((None, 1, D), lambda i, *_, at=at: (at, 0, 0))) for at in range(6)
    )
    wide_input = wide_tokens(inputs, after(input_got, pieces[-1]))
    far_oths = [over(far) for far in fars[:-1]]
    far_oths.append(across(after(oths[-1], wide_input, qkv_bias)))

    def gather(part):
        up_part = halves(up_weight, 1)[0][:, quarter * part : quarter * (part + 1)]
        down_part = halves(down_weight, 0)[0][quarter * part : quarter * (part + 1)].T
        shard = after(jnp.concatenate([up_part, down_part], axis=1), *pieces)
        return lax.all_gather(shard, "row", axis=0, tiled=True)

    own_a, own_b = gather(0), gather(1)
    grad_got = across(after(send_tokens(cotangent), wide_input))

    wide_one, qkv, attn_weights = norm_qkv(
        place, wide_input, gain_one, shift_one, qkv_bias, (*pieces, *fars, *oths, *far_oths)
    )
    oth_a, far_a = over(own_a), across(own_a)
    oth_b, far_b = over(own_b), across(own_b)
    first_heads = attend(qkv)
    attended, probs = attend(qkv, first_heads)
    mixed = mm_nt(attended, attn_weights[:, 4 * three :]).astype(BF16)
    mixed_other = beside(mixed)
    wide_grad = wide_tokens(cotangent, after(grad_got, mixed))
    far_oth_a = over(far_a)
    middle_sum, wide_two = middle(wide_input, mixed, mixed_other, out_bias_all, gain_two, shift_two)
    up_far_oth_b = over(far_b[:, :quarter])
    down_far_oth_b = across(oth_b[:, quarter:])

    def tiles(value, first, end):
        return value[:, quarter * first : quarter * end]

    gate_a, pre_a, up_sums_a, low_a, lift_a = mlp(
        place, wide_two, wide_grad, tile_bias, (own_a, far_a, oth_a, far_oth_a)
    )
    up_over = mm_tn(wide_two, tiles(pre_a, 2, 4)).astype(BF16)
    down_a = mm_tn(wide_grad, gate_a).astype(BF16)
    up_over_got = over(up_over)
    down_piece = lax.psum_scatter(down_a, "row", scatter_dimension=0, tiled=True)
    gate_b, pre_b, up_sums_b, low_mine, low_theirs, lifted_two = mlp(
        place,
        after(wide_two, up_over, down_a),
        wide_grad,
        tile_bias,
        (own_b, oth_b, far_b, up_far_oth_b, down_far_oth_b),
        (low_a, lift_a),
    )

    def wide_add(mine, got):
        return (mine.astype(F32) + got.astype(F32)).astype(BF16)

    def same_half(value):
        if n_dp == 2:
            return value
        groups = [[at + bit for at in range(0, n_dp, 2)] for bit in range(2)]
        return lax.psum(value.astype(F32), "dp", axis_index_groups=groups).astype(BF16)

    def scatter(value):
        return lax.psum_scatter(value, "row", scatter_dimension=0, tiled=True)

    lifted_other = beside(lifted_two)
    low_other = beside(low_theirs)
    up_across = mm_tn(wide_two, tiles(pre_b, 2, 4)).astype(BF16)
    down_over = mm_tn(wide_grad, tiles(gate_b, 2, 4)).astype(BF16)
    up_across_got, down_over_got = across(up_across), over(down_over)
    down_x_got = across(after(down_piece, up_across, down_over)[:, half:])

    middle_grad, attn_grad, head_grad, turn_sums, out_mine, out_theirs = turn(
        place,
        middle_sum,
        wide_grad,
        lifted_two,
        after(lifted_other, up_across, down_over),
        low_mine,
        low_other,
        gain_two,
        down_bias_all,
        attn_weights,
    )
    out_all = mm_tn(attn_grad, attended).astype(BF16)
    out_over_got = over(out_all[:, 2 * heads_half :])
    up_over_got, up_across_got, down_over_got, _ = lax.optimization_barrier(
        (up_over_got, up_across_got, down_over_got, out_all)
    )
    up_a = wide_add(mm_tn(wide_two, tiles(pre_a, 0, 2)), up_over_got)
    up_b = wide_add(mm_tn(wide_two, tiles(pre_b, 0, 2)), up_across_got)
    down_b = wide_add(mm_tn(wide_grad, tiles(gate_b, 0, 2)), down_over_got)
    up_a_got, up_b_got = across(up_a[:, quarter:]), over(up_b[:, quarter:])
    out_own = wide_add(out_all[:, : 2 * heads_half], after(out_over_got, down_b))
    out_far_got = across(out_own[:, heads_half:])
    down_x = wide_add(down_piece[:, :half], after(down_x_got, down_b))
    down_y_got = over(down_x)
    down_b_got = across(down_b[:, quarter:])
    out_got = across(after(out_theirs, down_b))
    dqkv, qkv_sums = attend_back(qkv, probs, after(head_grad, up_a, up_b, out_own, down_x))
    up_sum = join(
        up_a, up_a_got, up_b, up_b_got, down_b, down_b_got, out_own, after(out_far_got, dqkv)
    )
    up_piece = same_half(scatter(up_sum))

    def to_feature_blocks(mine, got, dtype):
        first, second = in_order(mine.astype(dtype), got.astype(dtype), my_x)
        both = jnp.concatenate([first, second]).reshape(images, PAD, width)
        return both[:, :SEQ].reshape(tokens_here, width)

    cut = 2 * heads_half
    split = 3 * three + cut
    dqkv = after(dqkv, up_sum)
    far_oth_qk = mm_tn(wide_one, dqkv[:, 3 * three : split]).astype(BF16)
    far_oth_v = mm_tn(wide_one, dqkv[:, split:]).astype(BF16)
    qk_got, v_got = over(far_oth_qk), across(far_oth_v)
    lifted_one = mm_nt(
        after(dqkv, far_oth_qk, far_oth_v), attn_weights[:, : 4 * three]
    ).astype(BF16)
    lifted_one_other = beside(lifted_one)

    near_oth = wide_add(
        mm_tn(wide_one, dqkv[:, 2 * three : 3 * three]),
        jnp.pad(after(v_got, lifted_one), ((0, 0), (cut, 0))),
    )
    near_oth_got = over(near_oth)
    far_own = wide_add(
        mm_tn(wide_one, dqkv[:, three : 2 * three]),
        jnp.pad(after(qk_got, near_oth), ((0, 0), (0, three - cut))),
    )
    far_own_got = across(far_own)
    near_own = mm_tn(after(wide_one, far_own), dqkv[:, :three])
    input_mine, input_theirs, late_mine, late_theirs = last(
        place, wide_input, middle_grad, lifted_one, after(lifted_one_other, near_own), gain_one
    )
    mine_sums, theirs_sums = collect(
        place, turn_sums, qkv_sums, up_sums_a, up_sums_b, late_mine, late_theirs
    )

    near_sum = (near_own + near_oth_got.astype(F32) + after(far_own_got, mine_sums).astype(F32)).astype(
        BF16
    )
    strip = D // n_row

    def rows_of(value, shift):
        return lax.dynamic_slice_in_dim(value, (my_row + shift) % n_row * strip, strip, 0)

    gots = [shifted(rows_of(near_sum, shift), shift) for shift in range(1, n_row)]
    input_got = across(after(input_theirs, near_sum))
    sums = mine_sums + across(after(theirs_sums, near_sum))
    steps = [("row", n_row, 1 << bit) for bit in range(n_row.bit_length() - 1)]
    steps += [("dp", n_dp, 1 << bit) for bit in range(n_dp.bit_length() - 1)]
    for step in steps[:-1]:
        sums = sums + swap(sums, *step)
        sums = after(sums, up_piece)
    sums = hand_out(sums, swap(sums, *steps[-1]))
    outputs = to_feature_blocks(out_mine, after(out_got, near_sum), BF16)

    qkv_total = rows_of(near_sum, 0).astype(F32)
    for got in gots:
        qkv_total = qkv_total + got.astype(F32)
    qkv_piece = same_half(qkv_total.astype(BF16))
    qkv_other = over(qkv_piece)
    input_grad = to_feature_blocks(input_mine, input_got, F32)
    up_other = over(up_piece)

    down_total = down_x.astype(F32) + jnp.concatenate(
        [down_y_got[:, quarter:], down_y_got[:, :quarter]], axis=1
    ).astype(F32)
    if n_dp > 2:
        groups = [[at + bit for at in range(0, n_dp, 2)] for bit in range(2)]
        down_total = lax.psum(down_total, "dp", axis_index_groups=groups)

    def down_half(first_part, second):
        return jnp.concatenate([first_part, tiles(second, 2, 3).astype(F32)], axis=1)

    down_first, down_second = in_order(
        down_half(down_total[:, :quarter], up_piece),
        down_half(down_total[:, quarter:], up_other),
        my_half,
    )
    down_grad = jnp.concatenate([down_first, down_second], axis=1).T

    def both_halves(mine, other, low, high):
        first, second = in_order(mine[:, low:high], other[:, low:high], my_half)
        return jnp.concatenate([first, second], axis=1).astype(F32)

    up_grad = both_halves(up_piece, up_other, 0, half)
    start = half + quarter
    out_grad = both_halves(up_piece, up_other, start, start + heads_half).T
    query_grad, key_grad, value_grad = (
        both_halves(qkv_piece, qkv_other, heads_half * at, heads_half * (at + 1))
        for at in range(3)
    )

    return (
        outputs,
        input_grad,
        query_grad,
        key_grad,
        value_grad,
        sums[0],
        sums[1],
        out_grad,
        sums[2],
        up_grad,
        sums[6],
        down_grad,
        sums[3],
        sums[7],
        sums[8],
        sums[4],
        sums[5],
    )


def solution(mesh):
    n_dp, n_row, n_col = (mesh.shape[name] for name in ("dp", "row", "col"))
    sizes = (n_dp, n_row, n_col // 2, 2)
    split = Mesh(mesh.devices.reshape(sizes), ("dp", "row", "xa", "core"))
    col = ("xa", "core")
    tokens, rows, cols, vec = P(("dp", "row"), col), P("row", col), P(col, "row"), P(col)
    in_specs = (
        (tokens, rows, rows, rows, vec, vec, cols, vec, rows, vec, cols)
        + (vec,) * 5
        + (tokens,)
    )
    out_specs = (
        (tokens, tokens, rows, rows, rows, vec, vec, cols, vec, rows, vec, cols) + (vec,) * 5
    )

    def body(*args):
        return local(sizes, *args)

    return jax.shard_map(
        body, mesh=split, in_specs=in_specs, out_specs=out_specs, check_vma=False
    )
```

```python
import functools
import math

import jax
import jax.numpy as jnp
from jax import lax
from jax.experimental import pallas as pl
from jax.experimental.pallas import tpu as pltpu
from jax.sharding import Mesh, PartitionSpec as P


D = 1024
HD = 64
SEQ = 577
PAD = 592
TM = 296
EPS = 1e-06
F32 = jnp.float32
BF16 = jnp.bfloat16
VMEM_LIMIT = 60 * 1024 * 1024
ROOT_HALF = math.sqrt(0.5)
DENSITY = 1.0 / math.sqrt(2.0 * math.pi)


def mm(a, b):
    return lax.dot_general(a, b, (((1,), (0,)), ((), ())), preferred_element_type=F32)


def mm_nt(a, b):
    return lax.dot_general(a, b, (((1,), (1,)), ((), ())), preferred_element_type=F32)


def mm_tn(a, b):
    return lax.dot_general(a, b, (((0,), (0,)), ((), ())), preferred_element_type=F32)


def row_mean(v):
    return jnp.sum(v, axis=1, keepdims=True) * (1.0 / D)


def col_sum(v):
    return jnp.sum(v, axis=0, keepdims=True)


def stats(rows):
    middle = row_mean(rows)
    spread = row_mean(rows * rows) - middle * middle
    return middle, lax.rsqrt(spread + EPS)


def params(n):
    return pltpu.CompilerParams(
        dimension_semantics=("arbitrary",) * n, vmem_limit_bytes=VMEM_LIMIT
    )


def cost(flops, moved, exps=0):
    return pl.CostEstimate(flops=int(flops), bytes_accessed=int(moved), transcendentals=int(exps))


def like(shape, dtype):
    return jax.ShapeDtypeStruct(shape, dtype)


def row_spec(cols):
    return pl.BlockSpec((TM, cols), lambda i, *_: (i, 0))


def fixed(shape):
    return pl.BlockSpec(shape, lambda *_: (0,) * len(shape))


def held_once(shape):
    return pl.BlockSpec(shape, lambda *_: (0,) * len(shape), pipeline_mode=pl.Buffered(1))


def add_up(ref, first, part):
    @pl.when(first)
    def _():
        ref[...] = part

    @pl.when(jnp.logical_not(first))
    def _():
        ref[...] += part


def norm_qkv_kernel(place_ref, x_ref, gain_ref, shift_ref, bias_ref, *refs):
    pieces, (n_ref, o_ref, w_ref) = refs[:-3], refs[-3:]
    n_row = len(pieces) // 4
    strip, wide = pieces[0].shape
    one = wide // 4

    @pl.when(pl.program_id(0) == 0)
    def _():
        for shift in range(n_row):
            start = lax.rem(place_ref[3] - shift + n_row, n_row) * strip
            rows = pl.ds(pl.multiple_of(start, strip), strip)
            for block in range(4):
                piece = pieces[n_row * block + shift]
                w_ref[rows, 3 * one * block : 3 * one * (block + 1)] = piece[:, : 3 * one]
                w_ref[rows, (12 + block) * one : (13 + block) * one] = piece[:, 3 * one :]

    x = x_ref[...].astype(F32)
    middle, scaled = stats(x)
    n = (((x - middle) * scaled) * gain_ref[...] + shift_ref[...]).astype(BF16)
    n_ref[...] = n
    o_ref[...] = (mm(n, w_ref[:, : 12 * one]) + bias_ref[...]).astype(BF16)


def norm_qkv(place, x, gain, shift, bias, pieces):
    rows = x.shape[0]
    wide = pieces[0].shape[1]
    out = 3 * wide
    return pl.pallas_call(
        norm_qkv_kernel,
        name="norm_qkv",
        grid_spec=pltpu.PrefetchScalarGridSpec(
            num_scalar_prefetch=1,
            grid=(rows // TM,),
            in_specs=[row_spec(D), gain[1], shift[1], fixed((1, out))]
            + [held_once(pieces[0].shape)] * len(pieces),
            out_specs=[row_spec(D), row_spec(out), held_once((D, 4 * wide))],
        ),
        out_shape=[like((rows, D), BF16), like((rows, out), BF16), like((D, 4 * wide), BF16)],
        compiler_params=params(1),
        cost_estimate=cost(2 * rows * D * out, 16 * rows * D),
    )(place, x, gain[0], shift[0], bias, *pieces)


def attend_kernel(qkv_ref, o_ref, p_ref):
    live = lax.broadcasted_iota(jnp.int32, (1, PAD), 1) < SEQ
    step = 2 * HD
    items = [(h, slice(r, r + TM)) for h in range(2) for r in range(0, PAD, TM)]

    def score(h, rows):
        q = qkv_ref[rows, HD * h : HD * (h + 1)] * jnp.asarray(0.125, BF16)
        return mm_nt(q, qkv_ref[:, step + HD * h : step + HD * (h + 1)])

    scores = [score(*item) for item in items[:3]]
    for at, (h, rows) in enumerate(items):
        if at + 3 < len(items):
            scores.append(score(*items[at + 3]))
        s = jnp.where(live, scores[at], -1e30)
        e = jnp.exp(s - jnp.max(s, axis=1, keepdims=True))
        p = (e * (1.0 / jnp.sum(e, axis=1, keepdims=True))).astype(BF16)
        p_ref[h, rows, :] = p
        v = qkv_ref[:, 2 * step + HD * h : 2 * step + HD * (h + 1)]
        o_ref[rows, HD * h : HD * (h + 1)] = mm(p, v).astype(BF16)


def attend(qkv, before=()):
    rows, cols = qkv.shape
    pairs = cols // (6 * HD)
    held = rows // PAD
    start = pairs // 2 if before else 0

    def kernel(*refs):
        attend_kernel(refs[0], refs[-2], refs[-1])

    return pl.pallas_call(
        kernel,
        grid=(pairs // 2, held),
        name="attend",
        in_specs=[pl.BlockSpec((PAD, 6 * HD), lambda p, i: (i, p + start))]
        + [pl.BlockSpec(memory_space=pl.ANY)] * len(before),
        out_specs=[
            pl.BlockSpec((PAD, 2 * HD), lambda p, i: (i, p + start)),
            pl.BlockSpec((None, 2, PAD, PAD), lambda p, i: (i, p + start, 0, 0)),
        ],
        out_shape=[like((rows, cols // 3), BF16), like((held, 2 * pairs, PAD, PAD), BF16)],
        input_output_aliases={1: 0, 2: 1} if before else {},
        compiler_params=params(2),
        cost_estimate=cost(8 * rows * PAD * cols, 20 * rows * D, 2 * rows * PAD * pairs),
    )(qkv, *before)


def attend_back_kernel(qkv_ref, p_ref, g_ref, d_ref, sum_ref):
    step = 2 * HD

    def cut(h, w):
        return slice(step * w + HD * h, step * w + HD * (h + 1))

    grads = [g_ref[:, HD * h : HD * (h + 1)] for h in range(2)]
    dprobs = [mm_nt(grads[h], qkv_ref[:, cut(h, 2)]) for h in range(2)]
    dscores = []
    for h in range(2):
        p = p_ref[h].astype(F32)
        z = jnp.sum(p * dprobs[h], axis=1, keepdims=True)
        dscores.append((p * (dprobs[h] - z)).astype(BF16))
        d_ref[:, cut(h, 2)] = mm_tn(p_ref[h], grads[h]).astype(BF16)
    for h in range(2):
        d_ref[:, cut(h, 0)] = (mm(dscores[h], qkv_ref[:, cut(h, 1)]) * 0.125).astype(BF16)
        d_ref[:, cut(h, 1)] = (mm_tn(dscores[h], qkv_ref[:, cut(h, 0)]) * 0.125).astype(BF16)
    add_up(sum_ref, pl.program_id(1) == 0, col_sum(d_ref[...].astype(F32)))


def attend_back(qkv, probs, grads):
    rows, cols = qkv.shape
    pairs = cols // (6 * HD)
    held = rows // PAD
    three = pl.BlockSpec((PAD, 6 * HD), lambda p, i: (i, p))
    return pl.pallas_call(
        attend_back_kernel,
        grid=(pairs, held),
        name="attend_back",
        in_specs=[
            three,
            pl.BlockSpec((None, 2, PAD, PAD), lambda p, i: (i, p, 0, 0)),
            pl.BlockSpec((PAD, 2 * HD), lambda p, i: (i, p)),
        ],
        out_specs=[three, pl.BlockSpec((1, 6 * HD), lambda p, i: (0, p))],
        out_shape=[like((rows, cols), BF16), like((1, cols), F32)],
        compiler_params=params(2),
        cost_estimate=cost(20 * rows * PAD * cols, 50 * rows * D),
    )(qkv, probs, grads)


def middle_kernel(x_ref, a_ref, b_ref, bias_ref, gain_ref, shift_ref, h_ref, n_ref):
    h = x_ref[...].astype(F32) + (a_ref[...].astype(F32) + b_ref[...].astype(F32)) + bias_ref[...]
    h_ref[...] = h
    middle, scaled = stats(h)
    n_ref[...] = (((h - middle) * scaled) * gain_ref[...] + shift_ref[...]).astype(BF16)


def middle(x, a, b, bias, gain, shift):
    rows = x.shape[0]
    return pl.pallas_call(
        middle_kernel,
        grid=(rows // TM,),
        name="middle",
        in_specs=[row_spec(D)] * 3 + [bias[1], gain[1], shift[1]],
        out_specs=[row_spec(D)] * 2,
        out_shape=[like((rows, D), F32), like((rows, D), BF16)],
        compiler_params=params(1),
        cost_estimate=cost(20 * rows * D, 12 * rows * D),
    )(x, a, b, bias[0], gain[0], shift[0])


def mlp_kernel(final, split, place_ref, n_ref, dy_ref, bias_ref, *refs):
    packs = refs[:5]
    before = refs[5:7] if final else ()
    rest = refs[5 + len(before) :]
    g_ref, du_ref, bsum_ref = rest[:3]
    buf, sem = rest[6:8] if final else rest[5:7]
    i = pl.program_id(0)
    tn = g_ref.shape[1] // 4

    @pl.when(i == 0)
    def _():
        copies = []
        for tile in range(4):
            for part in range(2):
                if tile == 3 and split:
                    source = packs[tile + part]
                else:
                    source = packs[tile].at[:, pl.ds(part * tn, tn)]
                copies.append(
                    pltpu.make_async_copy(
                        source,
                        buf.at[part, :, pl.ds(tile * tn, tn)],
                        sem.at[part, tile],
                    )
                )
        for copy in copies:
            copy.start()
        for copy in copies:
            copy.wait()

    up, down = buf[0], buf[1]
    u = mm(n_ref[...], up) + bias_ref[...]
    cdf = 0.5 * (1.0 + lax.erf(u * ROOT_HALF))
    g = (u * cdf).astype(BF16)
    slope = cdf + u * (jnp.exp(-0.5 * u * u) * DENSITY)
    for at, tile in enumerate((0, 2, 1, 3)):
        g_ref[:, at * tn : (at + 1) * tn] = g[:, tile * tn : (tile + 1) * tn]
    du = (mm(dy_ref[...], down) * slope).astype(BF16)
    du_ref[...] = du
    add_up(bsum_ref, i == 0, col_sum(du.astype(F32)))
    low = mm_nt(g, down)
    lift = mm_nt(du, up)
    if not final:
        rest[3][...] = low.astype(BF16)
        rest[4][...] = lift.astype(BF16)
        return
    mine_ref, theirs_ref, lift_ref = rest[3:6]
    held = rest[8]
    lift_ref[...] = (lift + before[1][...].astype(F32)).astype(BF16)
    held[...] = low + before[0][...].astype(F32)
    width = D // 4
    core = place_ref[0]
    for far in range(2):
        here = pl.multiple_of((2 * far + core) * width, width)
        other = pl.multiple_of((2 * far + 1 - core) * width, width)
        mine_ref[:, far * width : (far + 1) * width] = held[:, pl.ds(here, width)]
        theirs_ref[:, far * width : (far + 1) * width] = held[:, pl.ds(other, width)].astype(BF16)


def mlp(place, n2, dy, bias, packs, before=()):
    split = len(packs) == 5
    packs = packs if split else (*packs, packs[-1])
    rows = n2.shape[0]
    hid = 2 * packs[0].shape[1]
    part = 1 if before else 0

    def block(cols):
        return pl.BlockSpec((PAD, cols), lambda i, *_: (i, 0))

    out_specs = [block(hid), block(hid), fixed((1, hid))]
    out_shape = [like((rows, hid), BF16), like((rows, hid), BF16), like((1, hid), F32)]
    scratch = [pltpu.VMEM((2, D, hid), BF16), pltpu.SemaphoreType.DMA((2, 4))]
    if before:
        out_specs += [block(D // 2), block(D // 2), block(D)]
        out_shape += [like((rows, D // 2), F32), like((rows, D // 2), BF16), like((rows, D), BF16)]
        scratch += [pltpu.VMEM((PAD, D), F32)]
    else:
        out_specs += [block(D), block(D)]
        out_shape += [like((rows, D), BF16)] * 2
    return pl.pallas_call(
        functools.partial(mlp_kernel, bool(before), split),
        name="mlp_second" if before else "mlp_first",
        grid_spec=pltpu.PrefetchScalarGridSpec(
            num_scalar_prefetch=1,
            grid=(rows // PAD,),
            in_specs=[block(D), block(D), pl.BlockSpec((1, hid), lambda i, *_: (0, part))]
            + [pl.BlockSpec(memory_space=pl.ANY)] * 5
            + [block(D)] * len(before),
            out_specs=out_specs,
            scratch_shapes=scratch,
        ),
        out_shape=out_shape,
        compiler_params=params(1),
        cost_estimate=cost(8 * rows * D * hid, 20 * rows * D, 2 * rows * hid),
    )(place, n2, dy, bias, *packs, *before)


def turn_kernel(
    place_ref, h_ref, dy_ref, a_ref, b_ref, low_ref, other_ref, gain_ref, bias_ref, w_ref,
    dh_ref, da_ref, do_ref, sums_ref, mine_ref, theirs_ref, held,
):
    h = h_ref[...]
    held[...] = h + bias_ref[...]
    core, side = place_ref[0], place_ref[1]
    width = D // 4
    low = low_ref[...] + other_ref[...].astype(F32)
    for far in range(2):
        at = pl.ds(pl.multiple_of((2 * far + core) * width, width), width)
        out = (held[:, at] + low[:, far * width : (far + 1) * width]).astype(BF16)

        @pl.when(side == far)
        def _(out=out):
            mine_ref[...] = out

        @pl.when(side != far)
        def _(out=out):
            theirs_ref[...] = out

    middle, scaled = stats(h)
    c = (h - middle) * scaled
    dn = a_ref[...].astype(F32) + b_ref[...].astype(F32)
    dy = dy_ref[...].astype(F32)
    e = dn * gain_ref[...]
    dh = dy + scaled * (e - row_mean(e) - c * row_mean(e * c))
    dh_ref[...] = dh
    da = dh.astype(BF16)
    da_ref[...] = da
    do_ref[...] = mm(da, w_ref[...]).astype(BF16)
    part = jnp.concatenate(
        [col_sum(da.astype(F32)), col_sum(dy), col_sum(dn * c), col_sum(dn)], axis=0
    )
    add_up(sums_ref, pl.program_id(0) == 0, part)


def turn(place, h, dy, a, b, low_mine, low_other, gain, bias, weights):
    rows = h.shape[0]
    wide = weights.shape[1] // 4
    width = D // 4
    return pl.pallas_call(
        turn_kernel,
        name="turn",
        grid_spec=pltpu.PrefetchScalarGridSpec(
            num_scalar_prefetch=1,
            grid=(rows // TM,),
            in_specs=[row_spec(D)] * 4
            + [row_spec(D // 2)] * 2
            + [gain[1], bias[1]]
            + [pl.BlockSpec((D, wide), lambda i, *_: (0, 3), pipeline_mode=pl.Buffered(1))],
            out_specs=[
                row_spec(D),
                row_spec(D),
                row_spec(wide),
                fixed((4, D)),
                row_spec(width),
                row_spec(width),
            ],
            scratch_shapes=[pltpu.VMEM((TM, D), F32)],
        ),
        out_shape=[
            like((rows, D), F32),
            like((rows, D), BF16),
            like((rows, wide), BF16),
            like((4, D), F32),
            like((rows, width), BF16),
            like((rows, width), BF16),
        ],
        compiler_params=params(1),
        cost_estimate=cost(2 * rows * D * wide, 20 * rows * D),
    )(place, h, dy, a, b, low_mine, low_other, gain[0], bias[0], weights)


def last_kernel(
    place_ref, x_ref, dh_ref, a_ref, b_ref, gain_ref, mine_ref, theirs_ref, sum_mine, sum_theirs, held, sums
):
    x = x_ref[...].astype(F32)
    middle, scaled = stats(x)
    c = (x - middle) * scaled
    dn = a_ref[...].astype(F32) + b_ref[...].astype(F32)
    e = dn * gain_ref[...]
    held[...] = dh_ref[...] + scaled * (e - row_mean(e) - c * row_mean(e * c))
    width = D // 4
    core, side = place_ref[0], place_ref[1]
    here = pl.ds(pl.multiple_of((2 * side + core) * width, width), width)
    there = pl.ds(pl.multiple_of((2 * (1 - side) + core) * width, width), width)
    mine_ref[...] = held[:, here]
    theirs_ref[...] = held[:, there].astype(BF16)
    i = pl.program_id(0)
    add_up(sums, i == 0, jnp.concatenate([col_sum(dn * c), col_sum(dn)], axis=0))

    @pl.when(i == pl.num_programs(0) - 1)
    def _():
        sum_mine[...] = sums[:, here]
        sum_theirs[...] = sums[:, there]


def last(place, x, dh, a, b, gain):
    rows = x.shape[0]
    width = D // 4
    return pl.pallas_call(
        last_kernel,
        name="last",
        grid_spec=pltpu.PrefetchScalarGridSpec(
            num_scalar_prefetch=1,
            grid=(rows // TM,),
            in_specs=[row_spec(D)] * 4 + [gain[1]],
            out_specs=[row_spec(width), row_spec(width), fixed((2, width)), fixed((2, width))],
            scratch_shapes=[pltpu.VMEM((TM, D), F32), pltpu.VMEM((2, D), F32)],
        ),
        out_shape=[
            like((rows, width), F32),
            like((rows, width), BF16),
            like((2, width), F32),
            like((2, width), F32),
        ],
        compiler_params=params(1),
        cost_estimate=cost(20 * rows * D, 12 * rows * D),
    )(place, x, dh, a, b, gain[0])


def join_kernel(*refs):
    out_ref = refs[-1]
    start = 0
    for mine, got in zip(refs[:-1:2], refs[1:-1:2]):
        width = got.shape[1]
        total = mine[...].astype(F32) + got[...].astype(F32)
        out_ref[:, start : start + width] = total.astype(BF16)
        start += width


def join(*parts):
    rows = parts[0].shape[0]
    tm = rows // 4
    widths = [item.shape[1] for item in parts[1::2]]
    return pl.pallas_call(
        join_kernel,
        grid=(4,),
        name="join",
        in_specs=[
            pl.BlockSpec((tm, width), lambda i: (i, 0)) for width in widths for _ in range(2)
        ],
        out_specs=pl.BlockSpec((tm, sum(widths)), lambda i: (i, 0)),
        out_shape=like((rows, sum(widths)), BF16),
        compiler_params=params(1),
        cost_estimate=cost(rows * sum(widths), 6 * rows * sum(widths)),
    )(*parts)


def pack_kernel(*refs):
    out_ref = refs[-1]
    width = refs[0].shape[0]
    for at, ref in enumerate(refs[:-2]):
        out_ref[at, :] = ref[...]
    for at in range(4):
        out_ref[len(refs) - 2 + at, :] = refs[-2][width * at : width * (at + 1)]


def pack(vectors, long_vector):
    width = vectors[0].shape[0]
    return pl.pallas_call(
        pack_kernel,
        name="pack",
        out_shape=like((len(vectors) + 4, width), F32),
    )(*vectors, long_vector)


def unpack_kernel(place_ref, own, far, own_other, far_other, vec_ref, qkv_ref, tile_ref):
    core, side, half = place_ref[0], place_ref[1], place_ref[2]
    width = own.shape[1]
    one = width // 2

    def put(ref, at_side, at_core):
        at = pl.multiple_of((2 * at_side + at_core) * width, width)
        for k in range(6):
            vec_ref[k, :, pl.ds(at, width)] = ref[k : k + 1, :]

    put(own, side, core)
    put(far, 1 - side, core)
    put(own_other, side, 1 - core)
    put(far_other, 1 - side, 1 - core)
    qkv_ref[...] = jnp.zeros_like(qkv_ref)
    blocks = ((own, half), (far, half), (own, 1 - half), (far, 1 - half))
    for at, (ref, which) in enumerate(blocks):
        cut = pl.ds(pl.multiple_of(which * one, one), one)
        qkv_ref[:, 3 * one * at : 3 * one * at + one] = ref[6:7, cut]
        qkv_ref[:, 3 * one * at + 2 * one : 3 * one * (at + 1)] = ref[7:8, cut]
    order = (0, 1, 2, 3), (0, 2, 1, 3)
    for part in range(2):
        for at, index in enumerate(order[part]):
            ref, which = blocks[index]
            start = width * (4 * part + at)
            tile_ref[:, start : start + width] = ref[pl.ds(8 + 2 * which + part, 1), :]


def unpack(place, own, far, own_other, far_other):
    width = own.shape[1]
    return pl.pallas_call(
        unpack_kernel,
        name="unpack",
        in_specs=[pl.BlockSpec(memory_space=pltpu.SMEM)]
        + [pl.BlockSpec(memory_space=pltpu.VMEM)] * 4,
        out_shape=[like((6, 1, D), F32), like((1, 6 * width), F32), like((1, 8 * width), F32)],
    )(place, own, far, own_other, far_other)


def collect_kernel(
    place_ref, turn_ref, qkv_ref, up_a_ref, up_b_ref, a_ref, b_ref, mine_ref, theirs_ref
):
    core, side, half = place_ref[0], place_ref[1], place_ref[2]
    width = mine_ref.shape[1]
    one = width // 2
    for ref, at_side in ((mine_ref, side), (theirs_ref, 1 - side)):
        at = pl.ds(pl.multiple_of((2 * at_side + core) * width, width), width)
        ref[2:6, :] = turn_ref[:, at]
    mine_ref[10:12, :] = a_ref[...]
    theirs_ref[10:12, :] = b_ref[...]
    for at in range(4):
        ref = (mine_ref, theirs_ref)[at % 2]
        which = half if at < 2 else 1 - half
        cut = pl.ds(pl.multiple_of(which * one, one), one)
        ref[0:1, cut] = qkv_ref[:, 3 * one * at : 3 * one * at + one]
        ref[1:2, cut] = qkv_ref[:, 3 * one * at + 2 * one : 3 * one * (at + 1)]
    order = (0, 1, 2, 3), (0, 2, 1, 3)
    for part in range(2):
        for at, index in enumerate(order[part]):
            ref = (mine_ref, theirs_ref)[index % 2]
            which = half if index < 2 else 1 - half
            up_ref = (up_a_ref, up_b_ref)[part]
            ref[pl.ds(6 + 2 * which + part, 1), :] = up_ref[:, width * at : width * (at + 1)]


def collect(place, *sums):
    width = D // 4
    return pl.pallas_call(
        collect_kernel,
        name="collect",
        in_specs=[pl.BlockSpec(memory_space=pltpu.SMEM)]
        + [pl.BlockSpec(memory_space=pltpu.VMEM)] * 6,
        out_shape=[like((12, width), F32)] * 2,
    )(place, *sums)


def hand_out_kernel(a_ref, b_ref, *outs):
    sums = a_ref[...] + b_ref[...]
    width = a_ref.shape[1]
    for at in range(6):
        outs[at][...] = sums[at, :]
    for at in range(4):
        outs[6][width * at : width * (at + 1)] = sums[6 + at, :]
    for at in range(2):
        outs[7 + at][...] = sums[10 + at, :]


def hand_out(mine, got):
    width = mine.shape[1]
    one = like((width,), F32)
    return pl.pallas_call(
        hand_out_kernel,
        name="hand_out",
        out_shape=[one] * 6 + [like((4 * width,), F32)] + [one] * 2,
    )(mine, got)


def local(
    sizes,
    inputs,
    query_weight,
    key_weight,
    value_weight,
    query_bias,
    value_bias,
    out_weight,
    out_bias,
    up_weight,
    up_bias,
    down_weight,
    down_bias,
    first_gain,
    first_shift,
    second_gain,
    second_shift,
    cotangent,
):
    n_dp, n_row, n_xa, n_core = sizes
    my_x = lax.axis_index("xa")
    my_core = lax.axis_index("core")
    my_row = lax.axis_index("row")
    my_half = lax.axis_index("dp") % 2
    place = jnp.stack([my_core, my_x, my_half, my_row]).astype(jnp.int32)
    tokens_here, width = inputs.shape
    images = tokens_here // SEQ
    held = images // n_xa
    rows = held * PAD
    half = up_weight.shape[1] // 2
    quarter = half // 2
    heads_half = width // 2
    three = 3 * heads_half

    def swap(value, axis, size, bit=1):
        return lax.ppermute(value, axis, [(at, at ^ bit) for at in range(size)])

    def shifted(value, shift):
        return lax.ppermute(value, "row", [(at, (at + shift) % n_row) for at in range(n_row)])

    def across(value):
        return swap(value, "xa", n_xa)

    def beside(value):
        return swap(value, "core", n_core)

    def over(value):
        return swap(value, "dp", n_dp)

    def pick(value, at, axis):
        return lax.dynamic_index_in_dim(value, at, axis, keepdims=False)

    def in_order(mine, other, at):
        return jnp.where(at == 0, mine, other), jnp.where(at == 0, other, mine)

    def after(value, *others):
        return lax.optimization_barrier((value, *others))[0]

    def halves(value, axis):
        cut = value.shape[axis] // 2
        both = value.reshape(value.shape[:axis] + (2, cut) + value.shape[axis + 1 :])
        return pick(both, my_half, axis), pick(both, my_half ^ 1, axis)

    count = held * SEQ

    def send_tokens(value):
        return lax.dynamic_slice_in_dim(value, (my_x ^ 1) * count, count, 0)

    def wide_tokens(value, got):
        mine = lax.dynamic_slice_in_dim(value, my_x * count, count, 0)
        pair = jnp.concatenate([mine, got], axis=1).reshape(held, SEQ, 2 * width)
        pair = jnp.pad(pair, ((0, 0), (0, PAD - SEQ), (0, 0))).reshape(rows, 2 * width)
        other = beside(pair)
        left, right = in_order(pair, other, my_core)
        first_left, second_left = in_order(left[:, :width], left[:, width:], my_x)
        first_right, second_right = in_order(right[:, :width], right[:, width:], my_x)
        return jnp.concatenate([first_left, first_right, second_left, second_right], axis=1)

    attn_shard = jnp.concatenate(
        [halves(item, 1)[0] for item in (query_weight, key_weight, value_weight)]
        + [halves(out_weight, 0)[0].T],
        axis=1,
    )
    input_leaves = send_tokens(inputs)
    attn_shard = after(attn_shard, input_leaves)
    input_got = across(input_leaves)
    pieces = [attn_shard] + [shifted(attn_shard, shift) for shift in range(1, n_row)]
    small = pack(
        (
            out_bias,
            down_bias,
            first_gain,
            first_shift,
            second_gain,
            second_shift,
            query_bias,
            value_bias,
        ),
        up_bias,
    )
    fars = [across(piece) for piece in pieces]
    oths = [over(piece) for piece in pieces]
    small_far = across(small)
    vectors, qkv_bias, tile_bias = unpack(
        place, small, after(small_far, pieces[-1]), beside(small), beside(small_far)
    )
    out_bias_all, down_bias_all, gain_one, shift_one, gain_two, shift_two = (
        (vectors, pl.BlockSpec((None, 1, D), lambda i, *_, at=at: (at, 0, 0))) for at in range(6)
    )
    wide_input = wide_tokens(inputs, after(input_got, pieces[-1]))
    far_oths = [over(far) for far in fars[:-1]]
    far_oths.append(across(after(oths[-1], wide_input, qkv_bias)))

    def gather(part):
        up_part = halves(up_weight, 1)[0][:, quarter * part : quarter * (part + 1)]
        down_part = halves(down_weight, 0)[0][quarter * part : quarter * (part + 1)].T
        shard = after(jnp.concatenate([up_part, down_part], axis=1), *pieces)
        return lax.all_gather(shard, "row", axis=0, tiled=True)

    own_a, own_b = gather(0), gather(1)
    grad_got = across(after(send_tokens(cotangent), wide_input))

    wide_one, qkv, attn_weights = norm_qkv(
        place, wide_input, gain_one, shift_one, qkv_bias, (*pieces, *fars, *oths, *far_oths)
    )
    oth_a, far_a = over(own_a), across(own_a)
    oth_b, far_b = over(own_b), across(own_b)
    first_heads = attend(qkv)
    attended, probs = attend(qkv, first_heads)
    mixed = mm_nt(attended, attn_weights[:, 4 * three :]).astype(BF16)
    mixed_other = beside(mixed)
    wide_grad = wide_tokens(cotangent, after(grad_got, mixed))
    far_oth_a = over(far_a)
    middle_sum, wide_two = middle(wide_input, mixed, mixed_other, out_bias_all, gain_two, shift_two)
    up_far_oth_b = over(far_b[:, :quarter])
    down_far_oth_b = across(oth_b[:, quarter:])

    def tiles(value, first, end):
        return value[:, quarter * first : quarter * end]

    gate_a, pre_a, up_sums_a, low_a, lift_a = mlp(
        place, wide_two, wide_grad, tile_bias, (own_a, far_a, oth_a, far_oth_a)
    )
    up_over = mm_tn(wide_two, tiles(pre_a, 2, 4)).astype(BF16)
    down_a = mm_tn(wide_grad, gate_a).astype(BF16)
    up_over_got = over(up_over)
    down_piece = lax.psum_scatter(down_a, "row", scatter_dimension=0, tiled=True)
    gate_b, pre_b, up_sums_b, low_mine, low_theirs, lifted_two = mlp(
        place,
        after(wide_two, up_over, down_a),
        wide_grad,
        tile_bias,
        (own_b, oth_b, far_b, up_far_oth_b, down_far_oth_b),
        (low_a, lift_a),
    )

    def wide_add(mine, got):
        return (mine.astype(F32) + got.astype(F32)).astype(BF16)

    def same_half(value):
        if n_dp == 2:
            return value
        groups = [[at + bit for at in range(0, n_dp, 2)] for bit in range(2)]
        return lax.psum(value.astype(F32), "dp", axis_index_groups=groups).astype(BF16)

    def scatter(value):
        return lax.psum_scatter(value, "row", scatter_dimension=0, tiled=True)

    lifted_other = beside(lifted_two)
    low_other = beside(low_theirs)
    up_across = mm_tn(wide_two, tiles(pre_b, 2, 4)).astype(BF16)
    down_over = mm_tn(wide_grad, tiles(gate_b, 2, 4)).astype(BF16)
    up_across_got, down_over_got = across(up_across), over(down_over)

    middle_grad, attn_grad, head_grad, turn_sums, out_mine, out_theirs = turn(
        place,
        middle_sum,
        wide_grad,
        lifted_two,
        after(lifted_other, up_across, down_over),
        low_mine,
        low_other,
        gain_two,
        down_bias_all,
        attn_weights,
    )
    out_all = mm_tn(attn_grad, attended).astype(BF16)
    out_over_got = over(out_all[:, 2 * heads_half :])
    down_x_got = across(after(down_piece, attn_grad)[:, half:])
    up_over_got, up_across_got, down_over_got, _ = lax.optimization_barrier(
        (up_over_got, up_across_got, down_over_got, out_all)
    )
    up_a = wide_add(mm_tn(wide_two, tiles(pre_a, 0, 2)), up_over_got)
    up_b = wide_add(mm_tn(wide_two, tiles(pre_b, 0, 2)), up_across_got)
    down_b = wide_add(mm_tn(wide_grad, tiles(gate_b, 0, 2)), down_over_got)
    up_a_got, up_b_got = across(up_a[:, quarter:]), over(up_b[:, quarter:])
    out_own = wide_add(out_all[:, : 2 * heads_half], after(out_over_got, down_b))
    out_far_got = across(out_own[:, heads_half:])
    down_x = wide_add(down_piece[:, :half], after(down_x_got, down_b))
    down_y_got = over(down_x)
    down_b_got = across(down_b[:, quarter:])
    out_got = across(after(out_theirs, down_b))
    dqkv, qkv_sums = attend_back(qkv, probs, after(head_grad, up_a, up_b, out_own, down_x))

    def to_feature_blocks(mine, got, dtype):
        first, second = in_order(mine.astype(dtype), got.astype(dtype), my_x)
        both = jnp.concatenate([first, second]).reshape(images, PAD, width)
        return both[:, :SEQ].reshape(tokens_here, width)

    cut = 2 * heads_half
    split = 3 * three + cut
    far_oth_qk = mm_tn(wide_one, dqkv[:, 3 * three : split]).astype(BF16)
    far_oth_v = mm_tn(after(wide_one, far_oth_qk), dqkv[:, split:]).astype(BF16)
    qk_got, v_got = over(far_oth_qk), across(far_oth_v)
    up_sum = join(
        up_a, up_a_got, up_b, up_b_got, down_b, down_b_got, out_own, after(out_far_got, far_oth_v)
    )
    up_piece = same_half(scatter(up_sum))
    lifted_one = mm_nt(
        after(dqkv, far_oth_qk, far_oth_v, up_sum), attn_weights[:, : 4 * three]
    ).astype(BF16)
    lifted_one_other = beside(lifted_one)

    far_own = wide_add(
        mm_tn(wide_one, dqkv[:, three : 2 * three]),
        jnp.pad(after(qk_got, lifted_one), ((0, 0), (0, three - cut))),
    )
    far_own_got = across(far_own)
    near_oth = wide_add(
        mm_tn(wide_one, dqkv[:, 2 * three : 3 * three]),
        jnp.pad(after(v_got, far_own), ((0, 0), (cut, 0))),
    )
    near_oth_got = over(near_oth)
    near_own = mm_tn(after(wide_one, near_oth), dqkv[:, :three])
    input_mine, input_theirs, late_mine, late_theirs = last(
        place, wide_input, middle_grad, lifted_one, after(lifted_one_other, near_own), gain_one
    )
    mine_sums, theirs_sums = collect(
        place, turn_sums, qkv_sums, up_sums_a, up_sums_b, late_mine, late_theirs
    )

    near_sum = (near_own + near_oth_got.astype(F32) + after(far_own_got, mine_sums).astype(F32)).astype(
        BF16
    )
    strip = D // n_row

    def rows_of(value, shift):
        return lax.dynamic_slice_in_dim(value, (my_row + shift) % n_row * strip, strip, 0)

    gots = [shifted(rows_of(near_sum, shift), shift) for shift in range(1, n_row)]
    input_got = across(after(input_theirs, near_sum))
    sums = mine_sums + across(after(theirs_sums, near_sum))
    steps = [("row", n_row, 1 << bit) for bit in range(n_row.bit_length() - 1)]
    steps += [("dp", n_dp, 1 << bit) for bit in range(n_dp.bit_length() - 1)]
    for step in steps[:-1]:
        sums = sums + swap(sums, *step)
    sums = hand_out(sums, swap(sums, *steps[-1]))
    outputs = to_feature_blocks(out_mine, after(out_got, near_sum), BF16)

    qkv_total = rows_of(near_sum, 0).astype(F32)
    for got in gots:
        qkv_total = qkv_total + got.astype(F32)
    qkv_piece = same_half(qkv_total.astype(BF16))
    qkv_other = over(qkv_piece)
    input_grad = to_feature_blocks(input_mine, input_got, F32)
    up_other = over(up_piece)

    down_total = down_x.astype(F32) + jnp.concatenate(
        [down_y_got[:, quarter:], down_y_got[:, :quarter]], axis=1
    ).astype(F32)
    if n_dp > 2:
        groups = [[at + bit for at in range(0, n_dp, 2)] for bit in range(2)]
        down_total = lax.psum(down_total, "dp", axis_index_groups=groups)

    def down_half(first_part, second):
        return jnp.concatenate([first_part, tiles(second, 2, 3).astype(F32)], axis=1)

    down_first, down_second = in_order(
        down_half(down_total[:, :quarter], up_piece),
        down_half(down_total[:, quarter:], up_other),
        my_half,
    )
    down_grad = jnp.concatenate([down_first, down_second], axis=1).T

    def both_halves(mine, other, low, high):
        first, second = in_order(mine[:, low:high], other[:, low:high], my_half)
        return jnp.concatenate([first, second], axis=1).astype(F32)

    up_grad = both_halves(up_piece, up_other, 0, half)
    start = half + quarter
    out_grad = both_halves(up_piece, up_other, start, start + heads_half).T
    query_grad, key_grad, value_grad = (
        both_halves(qkv_piece, qkv_other, heads_half * at, heads_half * (at + 1))
        for at in range(3)
    )

    return (
        outputs,
        input_grad,
        query_grad,
        key_grad,
        value_grad,
        sums[0],
        sums[1],
        out_grad,
        sums[2],
        up_grad,
        sums[6],
        down_grad,
        sums[3],
        sums[7],
        sums[8],
        sums[4],
        sums[5],
    )


def solution(mesh):
    n_dp, n_row, n_col = (mesh.shape[name] for name in ("dp", "row", "col"))
    sizes = (n_dp, n_row, n_col // 2, 2)
    split = Mesh(mesh.devices.reshape(sizes), ("dp", "row", "xa", "core"))
    col = ("xa", "core")
    tokens, rows, cols, vec = P(("dp", "row"), col), P("row", col), P(col, "row"), P(col)
    in_specs = (
        (tokens, rows, rows, rows, vec, vec, cols, vec, rows, vec, cols)
        + (vec,) * 5
        + (tokens,)
    )
    out_specs = (
        (tokens, tokens, rows, rows, rows, vec, vec, cols, vec, rows, vec, cols) + (vec,) * 5
    )

    def body(*args):
        return local(sizes, *args)

    return jax.shard_map(
        body, mesh=split, in_specs=in_specs, out_specs=out_specs, check_vma=False
    )
```

```python
import functools
import math

import jax
import jax.numpy as jnp
from jax import lax
from jax.experimental import pallas as pl
from jax.experimental.pallas import tpu as pltpu
from jax.sharding import Mesh, PartitionSpec as P


D = 1024
HD = 64
SEQ = 577
PAD = 592
TM = 296
EPS = 1e-06
F32 = jnp.float32
BF16 = jnp.bfloat16
VMEM_LIMIT = 60 * 1024 * 1024
ROOT_HALF = math.sqrt(0.5)
DENSITY = 1.0 / math.sqrt(2.0 * math.pi)


def mm(a, b):
    return lax.dot_general(a, b, (((1,), (0,)), ((), ())), preferred_element_type=F32)


def mm_nt(a, b):
    return lax.dot_general(a, b, (((1,), (1,)), ((), ())), preferred_element_type=F32)


def mm_tn(a, b):
    return lax.dot_general(a, b, (((0,), (0,)), ((), ())), preferred_element_type=F32)


def row_mean(v):
    return jnp.sum(v, axis=1, keepdims=True) * (1.0 / D)


def col_sum(v):
    return jnp.sum(v, axis=0, keepdims=True)


def stats(rows):
    middle = row_mean(rows)
    spread = row_mean(rows * rows) - middle * middle
    return middle, lax.rsqrt(spread + EPS)


def params(n):
    return pltpu.CompilerParams(
        dimension_semantics=("arbitrary",) * n, vmem_limit_bytes=VMEM_LIMIT
    )


def cost(flops, moved, exps=0):
    return pl.CostEstimate(flops=int(flops), bytes_accessed=int(moved), transcendentals=int(exps))


def like(shape, dtype):
    return jax.ShapeDtypeStruct(shape, dtype)


def row_spec(cols):
    return pl.BlockSpec((TM, cols), lambda i, *_: (i, 0))


def fixed(shape):
    return pl.BlockSpec(shape, lambda *_: (0,) * len(shape))


def held_once(shape):
    return pl.BlockSpec(shape, lambda *_: (0,) * len(shape), pipeline_mode=pl.Buffered(1))


def add_up(ref, first, part):
    @pl.when(first)
    def _():
        ref[...] = part

    @pl.when(jnp.logical_not(first))
    def _():
        ref[...] += part


def norm_qkv_kernel(place_ref, x_ref, gain_ref, shift_ref, bias_ref, *refs):
    pieces, (n_ref, o_ref, w_ref) = refs[:-3], refs[-3:]
    n_row = len(pieces) // 4
    strip, wide = pieces[0].shape
    one = wide // 4

    @pl.when(pl.program_id(0) == 0)
    def _():
        for shift in range(n_row):
            start = lax.rem(place_ref[3] - shift + n_row, n_row) * strip
            rows = pl.ds(pl.multiple_of(start, strip), strip)
            for block in range(4):
                piece = pieces[n_row * block + shift]
                w_ref[rows, 3 * one * block : 3 * one * (block + 1)] = piece[:, : 3 * one]
                w_ref[rows, (12 + block) * one : (13 + block) * one] = piece[:, 3 * one :]

    x = x_ref[...].astype(F32)
    middle, scaled = stats(x)
    n = (((x - middle) * scaled) * gain_ref[...] + shift_ref[...]).astype(BF16)
    n_ref[...] = n
    o_ref[...] = (mm(n, w_ref[:, : 12 * one]) + bias_ref[...]).astype(BF16)


def norm_qkv(place, x, gain, shift, bias, pieces):
    rows = x.shape[0]
    wide = pieces[0].shape[1]
    out = 3 * wide
    return pl.pallas_call(
        norm_qkv_kernel,
        name="norm_qkv",
        grid_spec=pltpu.PrefetchScalarGridSpec(
            num_scalar_prefetch=1,
            grid=(rows // TM,),
            in_specs=[row_spec(D), gain[1], shift[1], fixed((1, out))]
            + [held_once(pieces[0].shape)] * len(pieces),
            out_specs=[row_spec(D), row_spec(out), held_once((D, 4 * wide))],
        ),
        out_shape=[like((rows, D), BF16), like((rows, out), BF16), like((D, 4 * wide), BF16)],
        compiler_params=params(1),
        cost_estimate=cost(2 * rows * D * out, 16 * rows * D),
    )(place, x, gain[0], shift[0], bias, *pieces)


def attend_kernel(qkv_ref, o_ref, p_ref):
    live = lax.broadcasted_iota(jnp.int32, (1, PAD), 1) < SEQ
    step = 2 * HD
    items = [(h, slice(r, r + TM)) for h in range(2) for r in range(0, PAD, TM)]

    def score(h, rows):
        q = qkv_ref[rows, HD * h : HD * (h + 1)] * jnp.asarray(0.125, BF16)
        return mm_nt(q, qkv_ref[:, step + HD * h : step + HD * (h + 1)])

    scores = [score(*item) for item in items[:3]]
    for at, (h, rows) in enumerate(items):
        if at + 3 < len(items):
            scores.append(score(*items[at + 3]))
        s = jnp.where(live, scores[at], -1e30)
        e = jnp.exp(s - jnp.max(s, axis=1, keepdims=True))
        p = (e * (1.0 / jnp.sum(e, axis=1, keepdims=True))).astype(BF16)
        p_ref[h, rows, :] = p
        v = qkv_ref[:, 2 * step + HD * h : 2 * step + HD * (h + 1)]
        o_ref[rows, HD * h : HD * (h + 1)] = mm(p, v).astype(BF16)


def attend(qkv, before=()):
    rows, cols = qkv.shape
    pairs = cols // (6 * HD)
    held = rows // PAD
    start = pairs // 2 if before else 0

    def kernel(*refs):
        attend_kernel(refs[0], refs[-2], refs[-1])

    return pl.pallas_call(
        kernel,
        grid=(pairs // 2, held),
        name="attend",
        in_specs=[pl.BlockSpec((PAD, 6 * HD), lambda p, i: (i, p + start))]
        + [pl.BlockSpec(memory_space=pl.ANY)] * len(before),
        out_specs=[
            pl.BlockSpec((PAD, 2 * HD), lambda p, i: (i, p + start)),
            pl.BlockSpec((None, 2, PAD, PAD), lambda p, i: (i, p + start, 0, 0)),
        ],
        out_shape=[like((rows, cols // 3), BF16), like((held, 2 * pairs, PAD, PAD), BF16)],
        input_output_aliases={1: 0, 2: 1} if before else {},
        compiler_params=params(2),
        cost_estimate=cost(8 * rows * PAD * cols, 20 * rows * D, 2 * rows * PAD * pairs),
    )(qkv, *before)


def attend_back_kernel(qkv_ref, p_ref, g_ref, d_ref, sum_ref):
    step = 2 * HD

    def cut(h, w):
        return slice(step * w + HD * h, step * w + HD * (h + 1))

    grads = [g_ref[:, HD * h : HD * (h + 1)] for h in range(2)]
    dprobs = [mm_nt(grads[h], qkv_ref[:, cut(h, 2)]) for h in range(2)]
    dscores = []
    for h in range(2):
        p = p_ref[h].astype(F32)
        z = jnp.sum(p * dprobs[h], axis=1, keepdims=True)
        dscores.append((p * (dprobs[h] - z)).astype(BF16))
        d_ref[:, cut(h, 2)] = mm_tn(p_ref[h], grads[h]).astype(BF16)
    for h in range(2):
        d_ref[:, cut(h, 0)] = (mm(dscores[h], qkv_ref[:, cut(h, 1)]) * 0.125).astype(BF16)
        d_ref[:, cut(h, 1)] = (mm_tn(dscores[h], qkv_ref[:, cut(h, 0)]) * 0.125).astype(BF16)
    add_up(sum_ref, pl.program_id(1) == 0, col_sum(d_ref[...].astype(F32)))


def attend_back(qkv, probs, grads):
    rows, cols = qkv.shape
    pairs = cols // (6 * HD)
    held = rows // PAD
    three = pl.BlockSpec((PAD, 6 * HD), lambda p, i: (i, p))
    return pl.pallas_call(
        attend_back_kernel,
        grid=(pairs, held),
        name="attend_back",
        in_specs=[
            three,
            pl.BlockSpec((None, 2, PAD, PAD), lambda p, i: (i, p, 0, 0)),
            pl.BlockSpec((PAD, 2 * HD), lambda p, i: (i, p)),
        ],
        out_specs=[three, pl.BlockSpec((1, 6 * HD), lambda p, i: (0, p))],
        out_shape=[like((rows, cols), BF16), like((1, cols), F32)],
        compiler_params=params(2),
        cost_estimate=cost(20 * rows * PAD * cols, 50 * rows * D),
    )(qkv, probs, grads)


def middle_kernel(x_ref, a_ref, b_ref, bias_ref, gain_ref, shift_ref, h_ref, n_ref):
    h = x_ref[...].astype(F32) + (a_ref[...].astype(F32) + b_ref[...].astype(F32)) + bias_ref[...]
    h_ref[...] = h
    middle, scaled = stats(h)
    n_ref[...] = (((h - middle) * scaled) * gain_ref[...] + shift_ref[...]).astype(BF16)


def middle(x, a, b, bias, gain, shift):
    rows = x.shape[0]
    return pl.pallas_call(
        middle_kernel,
        grid=(rows // TM,),
        name="middle",
        in_specs=[row_spec(D)] * 3 + [bias[1], gain[1], shift[1]],
        out_specs=[row_spec(D)] * 2,
        out_shape=[like((rows, D), F32), like((rows, D), BF16)],
        compiler_params=params(1),
        cost_estimate=cost(20 * rows * D, 12 * rows * D),
    )(x, a, b, bias[0], gain[0], shift[0])


def mlp_kernel(final, split, place_ref, n_ref, dy_ref, bias_ref, *refs):
    packs = refs[:5]
    before = refs[5:7] if final else ()
    rest = refs[5 + len(before) :]
    g_ref, du_ref, bsum_ref = rest[:3]
    buf, sem = rest[6:8] if final else rest[5:7]
    i = pl.program_id(0)
    tn = g_ref.shape[1] // 4

    @pl.when(i == 0)
    def _():
        copies = []
        for tile in range(4):
            for part in range(2):
                if tile == 3 and split:
                    source = packs[tile + part]
                else:
                    source = packs[tile].at[:, pl.ds(part * tn, tn)]
                copies.append(
                    pltpu.make_async_copy(
                        source,
                        buf.at[part, :, pl.ds(tile * tn, tn)],
                        sem.at[part, tile],
                    )
                )
        for copy in copies:
            copy.start()
        for copy in copies:
            copy.wait()

    up, down = buf[0], buf[1]
    u = mm(n_ref[...], up) + bias_ref[...]
    cdf = 0.5 * (1.0 + lax.erf(u * ROOT_HALF))
    g = (u * cdf).astype(BF16)
    slope = cdf + u * (jnp.exp(-0.5 * u * u) * DENSITY)
    for at, tile in enumerate((0, 2, 1, 3)):
        g_ref[:, at * tn : (at + 1) * tn] = g[:, tile * tn : (tile + 1) * tn]
    du = (mm(dy_ref[...], down) * slope).astype(BF16)
    du_ref[...] = du
    add_up(bsum_ref, i == 0, col_sum(du.astype(F32)))
    low = mm_nt(g, down)
    lift = mm_nt(du, up)
    if not final:
        rest[3][...] = low.astype(BF16)
        rest[4][...] = lift.astype(BF16)
        return
    mine_ref, theirs_ref, lift_ref = rest[3:6]
    held = rest[8]
    lift_ref[...] = (lift + before[1][...].astype(F32)).astype(BF16)
    held[...] = low + before[0][...].astype(F32)
    width = D // 4
    core = place_ref[0]
    for far in range(2):
        here = pl.multiple_of((2 * far + core) * width, width)
        other = pl.multiple_of((2 * far + 1 - core) * width, width)
        mine_ref[:, far * width : (far + 1) * width] = held[:, pl.ds(here, width)]
        theirs_ref[:, far * width : (far + 1) * width] = held[:, pl.ds(other, width)].astype(BF16)


def mlp(place, n2, dy, bias, packs, before=()):
    split = len(packs) == 5
    packs = packs if split else (*packs, packs[-1])
    rows = n2.shape[0]
    hid = 2 * packs[0].shape[1]
    part = 1 if before else 0

    def block(cols):
        return pl.BlockSpec((PAD, cols), lambda i, *_: (i, 0))

    out_specs = [block(hid), block(hid), fixed((1, hid))]
    out_shape = [like((rows, hid), BF16), like((rows, hid), BF16), like((1, hid), F32)]
    scratch = [pltpu.VMEM((2, D, hid), BF16), pltpu.SemaphoreType.DMA((2, 4))]
    if before:
        out_specs += [block(D // 2), block(D // 2), block(D)]
        out_shape += [like((rows, D // 2), F32), like((rows, D // 2), BF16), like((rows, D), BF16)]
        scratch += [pltpu.VMEM((PAD, D), F32)]
    else:
        out_specs += [block(D), block(D)]
        out_shape += [like((rows, D), BF16)] * 2
    return pl.pallas_call(
        functools.partial(mlp_kernel, bool(before), split),
        name="mlp_second" if before else "mlp_first",
        grid_spec=pltpu.PrefetchScalarGridSpec(
            num_scalar_prefetch=1,
            grid=(rows // PAD,),
            in_specs=[block(D), block(D), pl.BlockSpec((1, hid), lambda i, *_: (0, part))]
            + [pl.BlockSpec(memory_space=pl.ANY)] * 5
            + [block(D)] * len(before),
            out_specs=out_specs,
            scratch_shapes=scratch,
        ),
        out_shape=out_shape,
        compiler_params=params(1),
        cost_estimate=cost(8 * rows * D * hid, 20 * rows * D, 2 * rows * hid),
    )(place, n2, dy, bias, *packs, *before)


def turn_kernel(
    place_ref, h_ref, dy_ref, a_ref, b_ref, low_ref, other_ref, gain_ref, bias_ref, w_ref,
    dh_ref, da_ref, do_ref, sums_ref, mine_ref, theirs_ref, held,
):
    h = h_ref[...]
    held[...] = h + bias_ref[...]
    core, side = place_ref[0], place_ref[1]
    width = D // 4
    low = low_ref[...] + other_ref[...].astype(F32)
    for far in range(2):
        at = pl.ds(pl.multiple_of((2 * far + core) * width, width), width)
        out = (held[:, at] + low[:, far * width : (far + 1) * width]).astype(BF16)

        @pl.when(side == far)
        def _(out=out):
            mine_ref[...] = out

        @pl.when(side != far)
        def _(out=out):
            theirs_ref[...] = out

    middle, scaled = stats(h)
    c = (h - middle) * scaled
    dn = a_ref[...].astype(F32) + b_ref[...].astype(F32)
    dy = dy_ref[...].astype(F32)
    e = dn * gain_ref[...]
    dh = dy + scaled * (e - row_mean(e) - c * row_mean(e * c))
    dh_ref[...] = dh
    da = dh.astype(BF16)
    da_ref[...] = da
    do_ref[...] = mm(da, w_ref[...]).astype(BF16)
    part = jnp.concatenate(
        [col_sum(da.astype(F32)), col_sum(dy), col_sum(dn * c), col_sum(dn)], axis=0
    )
    add_up(sums_ref, pl.program_id(0) == 0, part)


def turn(place, h, dy, a, b, low_mine, low_other, gain, bias, weights):
    rows = h.shape[0]
    wide = weights.shape[1] // 4
    width = D // 4
    return pl.pallas_call(
        turn_kernel,
        name="turn",
        grid_spec=pltpu.PrefetchScalarGridSpec(
            num_scalar_prefetch=1,
            grid=(rows // TM,),
            in_specs=[row_spec(D)] * 4
            + [row_spec(D // 2)] * 2
            + [gain[1], bias[1]]
            + [pl.BlockSpec((D, wide), lambda i, *_: (0, 3), pipeline_mode=pl.Buffered(1))],
            out_specs=[
                row_spec(D),
                row_spec(D),
                row_spec(wide),
                fixed((4, D)),
                row_spec(width),
                row_spec(width),
            ],
            scratch_shapes=[pltpu.VMEM((TM, D), F32)],
        ),
        out_shape=[
            like((rows, D), F32),
            like((rows, D), BF16),
            like((rows, wide), BF16),
            like((4, D), F32),
            like((rows, width), BF16),
            like((rows, width), BF16),
        ],
        compiler_params=params(1),
        cost_estimate=cost(2 * rows * D * wide, 20 * rows * D),
    )(place, h, dy, a, b, low_mine, low_other, gain[0], bias[0], weights)


def last_kernel(
    place_ref, x_ref, dh_ref, a_ref, b_ref, gain_ref, mine_ref, theirs_ref, sum_mine, sum_theirs, held, sums
):
    x = x_ref[...].astype(F32)
    middle, scaled = stats(x)
    c = (x - middle) * scaled
    dn = a_ref[...].astype(F32) + b_ref[...].astype(F32)
    e = dn * gain_ref[...]
    held[...] = dh_ref[...] + scaled * (e - row_mean(e) - c * row_mean(e * c))
    width = D // 4
    core, side = place_ref[0], place_ref[1]
    here = pl.ds(pl.multiple_of((2 * side + core) * width, width), width)
    there = pl.ds(pl.multiple_of((2 * (1 - side) + core) * width, width), width)
    mine_ref[...] = held[:, here]
    theirs_ref[...] = held[:, there].astype(BF16)
    i = pl.program_id(0)
    add_up(sums, i == 0, jnp.concatenate([col_sum(dn * c), col_sum(dn)], axis=0))

    @pl.when(i == pl.num_programs(0) - 1)
    def _():
        sum_mine[...] = sums[:, here]
        sum_theirs[...] = sums[:, there]


def last(place, x, dh, a, b, gain):
    rows = x.shape[0]
    width = D // 4
    return pl.pallas_call(
        last_kernel,
        name="last",
        grid_spec=pltpu.PrefetchScalarGridSpec(
            num_scalar_prefetch=1,
            grid=(rows // TM,),
            in_specs=[row_spec(D)] * 4 + [gain[1]],
            out_specs=[row_spec(width), row_spec(width), fixed((2, width)), fixed((2, width))],
            scratch_shapes=[pltpu.VMEM((TM, D), F32), pltpu.VMEM((2, D), F32)],
        ),
        out_shape=[
            like((rows, width), F32),
            like((rows, width), BF16),
            like((2, width), F32),
            like((2, width), F32),
        ],
        compiler_params=params(1),
        cost_estimate=cost(20 * rows * D, 12 * rows * D),
    )(place, x, dh, a, b, gain[0])


def join_kernel(*refs):
    out_ref = refs[-1]
    start = 0
    for mine, got in zip(refs[:-1:2], refs[1:-1:2]):
        width = got.shape[1]
        total = mine[...].astype(F32) + got[...].astype(F32)
        out_ref[:, start : start + width] = total.astype(BF16)
        start += width


def join(*parts):
    rows = parts[0].shape[0]
    tm = rows // 4
    widths = [item.shape[1] for item in parts[1::2]]
    return pl.pallas_call(
        join_kernel,
        grid=(4,),
        name="join",
        in_specs=[
            pl.BlockSpec((tm, width), lambda i: (i, 0)) for width in widths for _ in range(2)
        ],
        out_specs=pl.BlockSpec((tm, sum(widths)), lambda i: (i, 0)),
        out_shape=like((rows, sum(widths)), BF16),
        compiler_params=params(1),
        cost_estimate=cost(rows * sum(widths), 6 * rows * sum(widths)),
    )(*parts)


def pack_kernel(*refs):
    out_ref = refs[-1]
    width = refs[0].shape[0]
    for at, ref in enumerate(refs[:-2]):
        out_ref[at, :] = ref[...]
    for at in range(4):
        out_ref[len(refs) - 2 + at, :] = refs[-2][width * at : width * (at + 1)]


def pack(vectors, long_vector):
    width = vectors[0].shape[0]
    return pl.pallas_call(
        pack_kernel,
        name="pack",
        out_shape=like((len(vectors) + 4, width), F32),
    )(*vectors, long_vector)


def unpack_kernel(place_ref, own, far, own_other, far_other, vec_ref, qkv_ref, tile_ref):
    core, side, half = place_ref[0], place_ref[1], place_ref[2]
    width = own.shape[1]
    one = width // 2

    def put(ref, at_side, at_core):
        at = pl.multiple_of((2 * at_side + at_core) * width, width)
        for k in range(6):
            vec_ref[k, :, pl.ds(at, width)] = ref[k : k + 1, :]

    put(own, side, core)
    put(far, 1 - side, core)
    put(own_other, side, 1 - core)
    put(far_other, 1 - side, 1 - core)
    qkv_ref[...] = jnp.zeros_like(qkv_ref)
    blocks = ((own, half), (far, half), (own, 1 - half), (far, 1 - half))
    for at, (ref, which) in enumerate(blocks):
        cut = pl.ds(pl.multiple_of(which * one, one), one)
        qkv_ref[:, 3 * one * at : 3 * one * at + one] = ref[6:7, cut]
        qkv_ref[:, 3 * one * at + 2 * one : 3 * one * (at + 1)] = ref[7:8, cut]
    order = (0, 1, 2, 3), (0, 2, 1, 3)
    for part in range(2):
        for at, index in enumerate(order[part]):
            ref, which = blocks[index]
            start = width * (4 * part + at)
            tile_ref[:, start : start + width] = ref[pl.ds(8 + 2 * which + part, 1), :]


def unpack(place, own, far, own_other, far_other):
    width = own.shape[1]
    return pl.pallas_call(
        unpack_kernel,
        name="unpack",
        in_specs=[pl.BlockSpec(memory_space=pltpu.SMEM)]
        + [pl.BlockSpec(memory_space=pltpu.VMEM)] * 4,
        out_shape=[like((6, 1, D), F32), like((1, 6 * width), F32), like((1, 8 * width), F32)],
    )(place, own, far, own_other, far_other)


def collect_kernel(
    place_ref, turn_ref, qkv_ref, up_a_ref, up_b_ref, a_ref, b_ref, mine_ref, theirs_ref
):
    core, side, half = place_ref[0], place_ref[1], place_ref[2]
    width = mine_ref.shape[1]
    one = width // 2
    for ref, at_side in ((mine_ref, side), (theirs_ref, 1 - side)):
        at = pl.ds(pl.multiple_of((2 * at_side + core) * width, width), width)
        ref[2:6, :] = turn_ref[:, at]
    mine_ref[10:12, :] = a_ref[...]
    theirs_ref[10:12, :] = b_ref[...]
    for at in range(4):
        ref = (mine_ref, theirs_ref)[at % 2]
        which = half if at < 2 else 1 - half
        cut = pl.ds(pl.multiple_of(which * one, one), one)
        ref[0:1, cut] = qkv_ref[:, 3 * one * at : 3 * one * at + one]
        ref[1:2, cut] = qkv_ref[:, 3 * one * at + 2 * one : 3 * one * (at + 1)]
    order = (0, 1, 2, 3), (0, 2, 1, 3)
    for part in range(2):
        for at, index in enumerate(order[part]):
            ref = (mine_ref, theirs_ref)[index % 2]
            which = half if index < 2 else 1 - half
            up_ref = (up_a_ref, up_b_ref)[part]
            ref[pl.ds(6 + 2 * which + part, 1), :] = up_ref[:, width * at : width * (at + 1)]


def collect(place, *sums):
    width = D // 4
    return pl.pallas_call(
        collect_kernel,
        name="collect",
        in_specs=[pl.BlockSpec(memory_space=pltpu.SMEM)]
        + [pl.BlockSpec(memory_space=pltpu.VMEM)] * 6,
        out_shape=[like((12, width), F32)] * 2,
    )(place, *sums)


def hand_out_kernel(a_ref, b_ref, *outs):
    sums = a_ref[...] + b_ref[...]
    width = a_ref.shape[1]
    for at in range(6):
        outs[at][...] = sums[at, :]
    for at in range(4):
        outs[6][width * at : width * (at + 1)] = sums[6 + at, :]
    for at in range(2):
        outs[7 + at][...] = sums[10 + at, :]


def hand_out(mine, got):
    width = mine.shape[1]
    one = like((width,), F32)
    return pl.pallas_call(
        hand_out_kernel,
        name="hand_out",
        out_shape=[one] * 6 + [like((4 * width,), F32)] + [one] * 2,
    )(mine, got)


def place_mlp_kernel(swapped, place_ref, mine_ref, other_ref, a_ref, b_ref, up_ref, down_ref, out_ref):
    half = place_ref[2]
    width = up_ref.shape[1] // 2
    quarter = width // 2
    heads = out_ref.shape[0] // 2
    for ref, at in ((mine_ref, half), (other_ref, 1 - half)):
        up_ref[:, pl.ds(pl.multiple_of(at * width, width), width)] = ref[:, :width].astype(F32)
        down_ref[pl.ds(pl.multiple_of(at * width + quarter, quarter), quarter), :] = (
            ref[:, width : width + quarter].astype(F32).T
        )
        out_ref[pl.ds(pl.multiple_of(at * heads, heads), heads), :] = (
            ref[:, width + quarter :].astype(F32).T
        )
    for part, at in ((0, half), (1, 1 - half)):
        from_b = 1 - part if swapped else part
        total = a_ref[:, part * quarter : (part + 1) * quarter].astype(F32)
        total = total + b_ref[:, from_b * quarter : (from_b + 1) * quarter].astype(F32)
        down_ref[pl.ds(pl.multiple_of(at * width, width), quarter), :] = total.T


def place_mlp(place, mine, other, a, b, swapped):
    strip, cols = mine.shape
    quarter = a.shape[1] // 2
    heads = cols - 3 * quarter
    return pl.pallas_call(
        functools.partial(place_mlp_kernel, swapped),
        name="place_mlp",
        in_specs=[pl.BlockSpec(memory_space=pltpu.SMEM)]
        + [pl.BlockSpec(memory_space=pltpu.VMEM)] * 4,
        out_shape=[
            like((strip, 4 * quarter), F32),
            like((4 * quarter, strip), F32),
            like((2 * heads, strip), F32),
        ],
    )(place, mine, other, a, b)


def place_qkv_kernel(place_ref, mine_ref, other_ref, *outs):
    half = place_ref[2]
    heads = outs[0].shape[1] // 2
    for ref, at in ((mine_ref, half), (other_ref, 1 - half)):
        here = pl.ds(pl.multiple_of(at * heads, heads), heads)
        for w in range(3):
            outs[w][:, here] = ref[:, heads * w : heads * (w + 1)].astype(F32)


def place_qkv(place, mine, other):
    strip, cols = mine.shape
    return pl.pallas_call(
        place_qkv_kernel,
        name="place_qkv",
        in_specs=[pl.BlockSpec(memory_space=pltpu.SMEM)]
        + [pl.BlockSpec(memory_space=pltpu.VMEM)] * 2,
        out_shape=[like((strip, cols // 3 * 2), F32)] * 3,
    )(place, mine, other)


def local(
    sizes,
    inputs,
    query_weight,
    key_weight,
    value_weight,
    query_bias,
    value_bias,
    out_weight,
    out_bias,
    up_weight,
    up_bias,
    down_weight,
    down_bias,
    first_gain,
    first_shift,
    second_gain,
    second_shift,
    cotangent,
):
    n_dp, n_row, n_xa, n_core = sizes
    my_x = lax.axis_index("xa")
    my_core = lax.axis_index("core")
    my_row = lax.axis_index("row")
    my_half = lax.axis_index("dp") % 2
    place = jnp.stack([my_core, my_x, my_half, my_row]).astype(jnp.int32)
    tokens_here, width = inputs.shape
    images = tokens_here // SEQ
    held = images // n_xa
    rows = held * PAD
    half = up_weight.shape[1] // 2
    quarter = half // 2
    heads_half = width // 2
    three = 3 * heads_half

    def swap(value, axis, size, bit=1):
        return lax.ppermute(value, axis, [(at, at ^ bit) for at in range(size)])

    def shifted(value, shift):
        return lax.ppermute(value, "row", [(at, (at + shift) % n_row) for at in range(n_row)])

    def across(value):
        return swap(value, "xa", n_xa)

    def beside(value):
        return swap(value, "core", n_core)

    def over(value):
        return swap(value, "dp", n_dp)

    def pick(value, at, axis):
        return lax.dynamic_index_in_dim(value, at, axis, keepdims=False)

    def in_order(mine, other, at):
        return jnp.where(at == 0, mine, other), jnp.where(at == 0, other, mine)

    def after(value, *others):
        return lax.optimization_barrier((value, *others))[0]

    def halves(value, axis):
        cut = value.shape[axis] // 2
        both = value.reshape(value.shape[:axis] + (2, cut) + value.shape[axis + 1 :])
        return pick(both, my_half, axis), pick(both, my_half ^ 1, axis)

    count = held * SEQ

    def send_tokens(value):
        return lax.dynamic_slice_in_dim(value, (my_x ^ 1) * count, count, 0)

    def wide_tokens(value, got):
        mine = lax.dynamic_slice_in_dim(value, my_x * count, count, 0)
        pair = jnp.concatenate([mine, got], axis=1).reshape(held, SEQ, 2 * width)
        pair = jnp.pad(pair, ((0, 0), (0, PAD - SEQ), (0, 0))).reshape(rows, 2 * width)
        other = beside(pair)
        left, right = in_order(pair, other, my_core)
        first_left, second_left = in_order(left[:, :width], left[:, width:], my_x)
        first_right, second_right = in_order(right[:, :width], right[:, width:], my_x)
        return jnp.concatenate([first_left, first_right, second_left, second_right], axis=1)

    attn_shard = jnp.concatenate(
        [halves(item, 1)[0] for item in (query_weight, key_weight, value_weight)]
        + [halves(out_weight, 0)[0].T],
        axis=1,
    )
    input_leaves = send_tokens(inputs)
    attn_shard = after(attn_shard, input_leaves)
    input_got = across(input_leaves)
    pieces = [attn_shard] + [shifted(attn_shard, shift) for shift in range(1, n_row)]
    small = pack(
        (
            out_bias,
            down_bias,
            first_gain,
            first_shift,
            second_gain,
            second_shift,
            query_bias,
            value_bias,
        ),
        up_bias,
    )
    fars = [across(piece) for piece in pieces]
    oths = [over(piece) for piece in pieces]
    small_far = across(small)
    vectors, qkv_bias, tile_bias = unpack(
        place, small, after(small_far, pieces[-1]), beside(small), beside(small_far)
    )
    out_bias_all, down_bias_all, gain_one, shift_one, gain_two, shift_two = (
        (vectors, pl.BlockSpec((None, 1, D), lambda i, *_, at=at: (at, 0, 0))) for at in range(6)
    )
    wide_input = wide_tokens(inputs, after(input_got, pieces[-1]))
    far_oths = [over(far) for far in fars[:-1]]
    far_oths.append(across(after(oths[-1], wide_input, qkv_bias)))

    def gather(part):
        up_part = halves(up_weight, 1)[0][:, quarter * part : quarter * (part + 1)]
        down_part = halves(down_weight, 0)[0][quarter * part : quarter * (part + 1)].T
        shard = after(jnp.concatenate([up_part, down_part], axis=1), *pieces)
        return lax.all_gather(shard, "row", axis=0, tiled=True)

    own_a, own_b = gather(0), gather(1)
    grad_got = across(after(send_tokens(cotangent), wide_input))

    wide_one, qkv, attn_weights = norm_qkv(
        place, wide_input, gain_one, shift_one, qkv_bias, (*pieces, *fars, *oths, *far_oths)
    )
    oth_a, far_a = over(own_a), across(own_a)
    oth_b, far_b = over(own_b), across(own_b)
    first_heads = attend(qkv)
    attended, probs = attend(qkv, first_heads)
    mixed = mm_nt(attended, attn_weights[:, 4 * three :]).astype(BF16)
    mixed_other = beside(mixed)
    wide_grad = wide_tokens(cotangent, after(grad_got, mixed))
    far_oth_a = over(far_a)
    middle_sum, wide_two = middle(wide_input, mixed, mixed_other, out_bias_all, gain_two, shift_two)
    up_far_oth_b = over(far_b[:, :quarter])
    down_far_oth_b = across(oth_b[:, quarter:])

    def tiles(value, first, end):
        return value[:, quarter * first : quarter * end]

    gate_a, pre_a, up_sums_a, low_a, lift_a = mlp(
        place, wide_two, wide_grad, tile_bias, (own_a, far_a, oth_a, far_oth_a)
    )
    up_over = mm_tn(wide_two, tiles(pre_a, 2, 4)).astype(BF16)
    down_a = mm_tn(wide_grad, gate_a).astype(BF16)
    up_over_got = over(up_over)
    down_piece = lax.psum_scatter(down_a, "row", scatter_dimension=0, tiled=True)
    gate_b, pre_b, up_sums_b, low_mine, low_theirs, lifted_two = mlp(
        place,
        after(wide_two, up_over, down_a),
        wide_grad,
        tile_bias,
        (own_b, oth_b, far_b, up_far_oth_b, down_far_oth_b),
        (low_a, lift_a),
    )

    def wide_add(mine, got):
        return (mine.astype(F32) + got.astype(F32)).astype(BF16)

    def same_half(value):
        if n_dp == 2:
            return value
        groups = [[at + bit for at in range(0, n_dp, 2)] for bit in range(2)]
        return lax.psum(value.astype(F32), "dp", axis_index_groups=groups).astype(BF16)

    def scatter(value):
        return lax.psum_scatter(value, "row", scatter_dimension=0, tiled=True)

    lifted_other = beside(lifted_two)
    low_other = beside(low_theirs)
    up_across = mm_tn(wide_two, tiles(pre_b, 2, 4)).astype(BF16)
    down_over = mm_tn(wide_grad, tiles(gate_b, 2, 4)).astype(BF16)
    up_across_got, down_over_got = across(up_across), over(down_over)

    middle_grad, attn_grad, head_grad, turn_sums, out_mine, out_theirs = turn(
        place,
        middle_sum,
        wide_grad,
        lifted_two,
        after(lifted_other, up_across, down_over),
        low_mine,
        low_other,
        gain_two,
        down_bias_all,
        attn_weights,
    )
    out_all = mm_tn(attn_grad, attended).astype(BF16)
    out_over_got = over(out_all[:, 2 * heads_half :])
    down_x_got = across(after(down_piece, attn_grad)[:, half:])
    up_over_got, up_across_got, down_over_got, _ = lax.optimization_barrier(
        (up_over_got, up_across_got, down_over_got, out_all)
    )
    up_a = wide_add(mm_tn(wide_two, tiles(pre_a, 0, 2)), up_over_got)
    up_b = wide_add(mm_tn(wide_two, tiles(pre_b, 0, 2)), up_across_got)
    down_b = wide_add(mm_tn(wide_grad, tiles(gate_b, 0, 2)), down_over_got)
    up_a_got, up_b_got = across(up_a[:, quarter:]), over(up_b[:, quarter:])
    out_own = wide_add(out_all[:, : 2 * heads_half], after(out_over_got, down_b))
    out_far_got = across(out_own[:, heads_half:])
    down_x = wide_add(down_piece[:, :half], after(down_x_got, down_b))
    down_y_got = over(down_x)
    down_b_got = across(down_b[:, quarter:])
    out_got = across(after(out_theirs, down_b))
    dqkv, qkv_sums = attend_back(qkv, probs, after(head_grad, up_a, up_b, out_own, down_x))

    def to_feature_blocks(mine, got, dtype):
        first, second = in_order(mine.astype(dtype), got.astype(dtype), my_x)
        both = jnp.concatenate([first, second]).reshape(images, PAD, width)
        return both[:, :SEQ].reshape(tokens_here, width)

    cut = 2 * heads_half
    split = 3 * three + cut
    far_oth_qk = mm_tn(wide_one, dqkv[:, 3 * three : split]).astype(BF16)
    far_oth_v = mm_tn(after(wide_one, far_oth_qk), dqkv[:, split:]).astype(BF16)
    qk_got, v_got = over(far_oth_qk), across(far_oth_v)
    up_sum = join(
        up_a, up_a_got, up_b, up_b_got, down_b, down_b_got, out_own, after(out_far_got, far_oth_v)
    )
    up_piece = same_half(scatter(up_sum))
    near_oth = wide_add(
        mm_tn(wide_one, dqkv[:, 2 * three : 3 * three]),
        jnp.pad(after(v_got, up_sum), ((0, 0), (cut, 0))),
    )
    near_oth_got = over(near_oth)
    far_own = wide_add(
        mm_tn(wide_one, dqkv[:, three : 2 * three]),
        jnp.pad(after(qk_got, near_oth), ((0, 0), (0, three - cut))),
    )
    far_own_got = across(far_own)
    lifted_one = mm_nt(
        after(dqkv, far_own), attn_weights[:, : 4 * three]
    ).astype(BF16)
    lifted_one_other = beside(lifted_one)

    near_own = mm_tn(after(wide_one, lifted_one), dqkv[:, :three])
    input_mine, input_theirs, late_mine, late_theirs = last(
        place, wide_input, middle_grad, lifted_one, after(lifted_one_other, near_own), gain_one
    )
    mine_sums, theirs_sums = collect(
        place, turn_sums, qkv_sums, up_sums_a, up_sums_b, late_mine, late_theirs
    )

    near_sum = (near_own + near_oth_got.astype(F32) + after(far_own_got, mine_sums).astype(F32)).astype(
        BF16
    )
    strip = D // n_row

    def rows_of(value, shift):
        return lax.dynamic_slice_in_dim(value, (my_row + shift) % n_row * strip, strip, 0)

    gots = [shifted(rows_of(near_sum, shift), shift) for shift in range(1, n_row)]
    input_got = across(after(input_theirs, near_sum))
    sums = mine_sums + across(after(theirs_sums, near_sum))
    steps = [("row", n_row, 1 << bit) for bit in range(n_row.bit_length() - 1)]
    steps += [("dp", n_dp, 1 << bit) for bit in range(n_dp.bit_length() - 1)]
    for step in steps[:-1]:
        sums = sums + swap(sums, *step)
    sums = hand_out(sums, swap(sums, *steps[-1]))
    outputs = to_feature_blocks(out_mine, after(out_got, near_sum), BF16)

    qkv_total = rows_of(near_sum, 0).astype(F32)
    for got in gots:
        qkv_total = qkv_total + got.astype(F32)
    qkv_piece = same_half(qkv_total.astype(BF16))
    qkv_other = over(qkv_piece)
    input_grad = to_feature_blocks(input_mine, input_got, F32)
    up_other = over(up_piece)

    if n_dp > 2:
        down_total = down_x.astype(F32) + jnp.concatenate(
            [down_y_got[:, quarter:], down_y_got[:, :quarter]], axis=1
        ).astype(F32)
        groups = [[at + bit for at in range(0, n_dp, 2)] for bit in range(2)]
        down_total = lax.psum(down_total, "dp", axis_index_groups=groups)
        parts = (down_total, jnp.zeros_like(down_total))
    else:
        parts = (down_x, down_y_got)
    up_grad, down_grad, out_grad = place_mlp(place, up_piece, up_other, *parts, n_dp == 2)
    query_grad, key_grad, value_grad = place_qkv(
        place, qkv_piece, after(qkv_other, up_grad)
    )

    return (
        outputs,
        input_grad,
        query_grad,
        key_grad,
        value_grad,
        sums[0],
        sums[1],
        out_grad,
        sums[2],
        up_grad,
        sums[6],
        down_grad,
        sums[3],
        sums[7],
        sums[8],
        sums[4],
        sums[5],
    )


def solution(mesh):
    n_dp, n_row, n_col = (mesh.shape[name] for name in ("dp", "row", "col"))
    sizes = (n_dp, n_row, n_col // 2, 2)
    split = Mesh(mesh.devices.reshape(sizes), ("dp", "row", "xa", "core"))
    col = ("xa", "core")
    tokens, rows, cols, vec = P(("dp", "row"), col), P("row", col), P(col, "row"), P(col)
    in_specs = (
        (tokens, rows, rows, rows, vec, vec, cols, vec, rows, vec, cols)
        + (vec,) * 5
        + (tokens,)
    )
    out_specs = (
        (tokens, tokens, rows, rows, rows, vec, vec, cols, vec, rows, vec, cols) + (vec,) * 5
    )

    def body(*args):
        return local(sizes, *args)

    return jax.shard_map(
        body, mesh=split, in_specs=in_specs, out_specs=out_specs, check_vma=False
    )
```

```python
import functools
import math

import jax
import jax.numpy as jnp
from jax import lax
from jax.experimental import pallas as pl
from jax.experimental.pallas import tpu as pltpu
from jax.sharding import Mesh, PartitionSpec as P


D = 1024
HD = 64
SEQ = 577
PAD = 592
TM = 296
EPS = 1e-06
F32 = jnp.float32
BF16 = jnp.bfloat16
VMEM_LIMIT = 60 * 1024 * 1024
ROOT_HALF = math.sqrt(0.5)
DENSITY = 1.0 / math.sqrt(2.0 * math.pi)


def mm(a, b):
    return lax.dot_general(a, b, (((1,), (0,)), ((), ())), preferred_element_type=F32)


def mm_nt(a, b):
    return lax.dot_general(a, b, (((1,), (1,)), ((), ())), preferred_element_type=F32)


def mm_tn(a, b):
    return lax.dot_general(a, b, (((0,), (0,)), ((), ())), preferred_element_type=F32)


def row_mean(v):
    return jnp.sum(v, axis=1, keepdims=True) * (1.0 / D)


def col_sum(v):
    return jnp.sum(v, axis=0, keepdims=True)


def stats(rows):
    middle = row_mean(rows)
    spread = row_mean(rows * rows) - middle * middle
    return middle, lax.rsqrt(spread + EPS)


def params(n):
    return pltpu.CompilerParams(
        dimension_semantics=("arbitrary",) * n, vmem_limit_bytes=VMEM_LIMIT
    )


def cost(flops, moved, exps=0):
    return pl.CostEstimate(flops=int(flops), bytes_accessed=int(moved), transcendentals=int(exps))


def like(shape, dtype):
    return jax.ShapeDtypeStruct(shape, dtype)


def row_spec(cols):
    return pl.BlockSpec((TM, cols), lambda i, *_: (i, 0))


def fixed(shape):
    return pl.BlockSpec(shape, lambda *_: (0,) * len(shape))


def held_once(shape):
    return pl.BlockSpec(shape, lambda *_: (0,) * len(shape), pipeline_mode=pl.Buffered(1))


def add_up(ref, first, part):
    @pl.when(first)
    def _():
        ref[...] = part

    @pl.when(jnp.logical_not(first))
    def _():
        ref[...] += part


def norm_qkv_kernel(place_ref, x_ref, gain_ref, shift_ref, bias_ref, *refs):
    pieces, (n_ref, o_ref, w_ref) = refs[:-3], refs[-3:]
    n_row = len(pieces) // 4
    strip, wide = pieces[0].shape
    one = wide // 4

    @pl.when(pl.program_id(0) == 0)
    def _():
        for shift in range(n_row):
            start = lax.rem(place_ref[3] - shift + n_row, n_row) * strip
            rows = pl.ds(pl.multiple_of(start, strip), strip)
            for block in range(4):
                piece = pieces[n_row * block + shift]
                w_ref[rows, 3 * one * block : 3 * one * (block + 1)] = piece[:, : 3 * one]
                w_ref[rows, (12 + block) * one : (13 + block) * one] = piece[:, 3 * one :]

    x = x_ref[...].astype(F32)
    middle, scaled = stats(x)
    n = (((x - middle) * scaled) * gain_ref[...] + shift_ref[...]).astype(BF16)
    n_ref[...] = n
    o_ref[...] = (mm(n, w_ref[:, : 12 * one]) + bias_ref[...]).astype(BF16)


def norm_qkv(place, x, gain, shift, bias, pieces):
    rows = x.shape[0]
    wide = pieces[0].shape[1]
    out = 3 * wide
    return pl.pallas_call(
        norm_qkv_kernel,
        name="norm_qkv",
        grid_spec=pltpu.PrefetchScalarGridSpec(
            num_scalar_prefetch=1,
            grid=(rows // TM,),
            in_specs=[row_spec(D), gain[1], shift[1], fixed((1, out))]
            + [held_once(pieces[0].shape)] * len(pieces),
            out_specs=[row_spec(D), row_spec(out), held_once((D, 4 * wide))],
        ),
        out_shape=[like((rows, D), BF16), like((rows, out), BF16), like((D, 4 * wide), BF16)],
        compiler_params=params(1),
        cost_estimate=cost(2 * rows * D * out, 16 * rows * D),
    )(place, x, gain[0], shift[0], bias, *pieces)


def attend_kernel(qkv_ref, o_ref, p_ref):
    live = lax.broadcasted_iota(jnp.int32, (1, PAD), 1) < SEQ
    step = 2 * HD
    items = [(h, slice(r, r + TM)) for h in range(2) for r in range(0, PAD, TM)]

    def score(h, rows):
        q = qkv_ref[rows, HD * h : HD * (h + 1)] * jnp.asarray(0.125, BF16)
        return mm_nt(q, qkv_ref[:, step + HD * h : step + HD * (h + 1)])

    scores = [score(*item) for item in items[:3]]
    for at, (h, rows) in enumerate(items):
        if at + 3 < len(items):
            scores.append(score(*items[at + 3]))
        s = jnp.where(live, scores[at], -1e30)
        e = jnp.exp(s - jnp.max(s, axis=1, keepdims=True))
        p = (e * (1.0 / jnp.sum(e, axis=1, keepdims=True))).astype(BF16)
        p_ref[h, rows, :] = p
        v = qkv_ref[:, 2 * step + HD * h : 2 * step + HD * (h + 1)]
        o_ref[rows, HD * h : HD * (h + 1)] = mm(p, v).astype(BF16)


def attend(qkv, before=()):
    rows, cols = qkv.shape
    pairs = cols // (6 * HD)
    held = rows // PAD
    start = pairs // 2 if before else 0

    def kernel(*refs):
        attend_kernel(refs[0], refs[-2], refs[-1])

    return pl.pallas_call(
        kernel,
        grid=(pairs // 2, held),
        name="attend",
        in_specs=[pl.BlockSpec((PAD, 6 * HD), lambda p, i: (i, p + start))]
        + [pl.BlockSpec(memory_space=pl.ANY)] * len(before),
        out_specs=[
            pl.BlockSpec((PAD, 2 * HD), lambda p, i: (i, p + start)),
            pl.BlockSpec((None, 2, PAD, PAD), lambda p, i: (i, p + start, 0, 0)),
        ],
        out_shape=[like((rows, cols // 3), BF16), like((held, 2 * pairs, PAD, PAD), BF16)],
        input_output_aliases={1: 0, 2: 1} if before else {},
        compiler_params=params(2),
        cost_estimate=cost(8 * rows * PAD * cols, 20 * rows * D, 2 * rows * PAD * pairs),
    )(qkv, *before)


def attend_back_kernel(qkv_ref, p_ref, g_ref, d_ref, sum_ref):
    step = 2 * HD

    def cut(h, w):
        return slice(step * w + HD * h, step * w + HD * (h + 1))

    grads = [g_ref[:, HD * h : HD * (h + 1)] for h in range(2)]
    dprobs = [mm_nt(grads[h], qkv_ref[:, cut(h, 2)]) for h in range(2)]
    dscores = []
    for h in range(2):
        p = p_ref[h].astype(F32)
        z = jnp.sum(p * dprobs[h], axis=1, keepdims=True)
        dscores.append((p * (dprobs[h] - z)).astype(BF16))
        d_ref[:, cut(h, 2)] = mm_tn(p_ref[h], grads[h]).astype(BF16)
    for h in range(2):
        d_ref[:, cut(h, 0)] = (mm(dscores[h], qkv_ref[:, cut(h, 1)]) * 0.125).astype(BF16)
        d_ref[:, cut(h, 1)] = (mm_tn(dscores[h], qkv_ref[:, cut(h, 0)]) * 0.125).astype(BF16)
    add_up(sum_ref, pl.program_id(1) == 0, col_sum(d_ref[...].astype(F32)))


def attend_back(qkv, probs, grads):
    rows, cols = qkv.shape
    pairs = cols // (6 * HD)
    held = rows // PAD
    three = pl.BlockSpec((PAD, 6 * HD), lambda p, i: (i, p))
    return pl.pallas_call(
        attend_back_kernel,
        grid=(pairs, held),
        name="attend_back",
        in_specs=[
            three,
            pl.BlockSpec((None, 2, PAD, PAD), lambda p, i: (i, p, 0, 0)),
            pl.BlockSpec((PAD, 2 * HD), lambda p, i: (i, p)),
        ],
        out_specs=[three, pl.BlockSpec((1, 6 * HD), lambda p, i: (0, p))],
        out_shape=[like((rows, cols), BF16), like((1, cols), F32)],
        compiler_params=params(2),
        cost_estimate=cost(20 * rows * PAD * cols, 50 * rows * D),
    )(qkv, probs, grads)


def middle_kernel(x_ref, a_ref, b_ref, bias_ref, gain_ref, shift_ref, h_ref, n_ref):
    h = x_ref[...].astype(F32) + (a_ref[...].astype(F32) + b_ref[...].astype(F32)) + bias_ref[...]
    h_ref[...] = h
    middle, scaled = stats(h)
    n_ref[...] = (((h - middle) * scaled) * gain_ref[...] + shift_ref[...]).astype(BF16)


def middle(x, a, b, bias, gain, shift):
    rows = x.shape[0]
    return pl.pallas_call(
        middle_kernel,
        grid=(rows // TM,),
        name="middle",
        in_specs=[row_spec(D)] * 3 + [bias[1], gain[1], shift[1]],
        out_specs=[row_spec(D)] * 2,
        out_shape=[like((rows, D), F32), like((rows, D), BF16)],
        compiler_params=params(1),
        cost_estimate=cost(20 * rows * D, 12 * rows * D),
    )(x, a, b, bias[0], gain[0], shift[0])


def mlp_kernel(final, split, place_ref, n_ref, dy_ref, bias_ref, *refs):
    packs = refs[:5]
    before = refs[5:7] if final else ()
    rest = refs[5 + len(before) :]
    g_ref, du_ref, bsum_ref = rest[:3]
    buf, sem = rest[6:8] if final else rest[5:7]
    i = pl.program_id(0)
    tn = g_ref.shape[1] // 4

    @pl.when(i == 0)
    def _():
        copies = []
        for tile in range(4):
            for part in range(2):
                if tile == 3 and split:
                    source = packs[tile + part]
                else:
                    source = packs[tile].at[:, pl.ds(part * tn, tn)]
                copies.append(
                    pltpu.make_async_copy(
                        source,
                        buf.at[part, :, pl.ds(tile * tn, tn)],
                        sem.at[part, tile],
                    )
                )
        for copy in copies:
            copy.start()
        for copy in copies:
            copy.wait()

    up, down = buf[0], buf[1]
    u = mm(n_ref[...], up) + bias_ref[...]
    cdf = 0.5 * (1.0 + lax.erf(u * ROOT_HALF))
    g = (u * cdf).astype(BF16)
    slope = cdf + u * (jnp.exp(-0.5 * u * u) * DENSITY)
    for at, tile in enumerate((0, 2, 1, 3)):
        g_ref[:, at * tn : (at + 1) * tn] = g[:, tile * tn : (tile + 1) * tn]
    du = (mm(dy_ref[...], down) * slope).astype(BF16)
    du_ref[...] = du
    add_up(bsum_ref, i == 0, col_sum(du.astype(F32)))
    low = mm_nt(g, down)
    lift = mm_nt(du, up)
    if not final:
        rest[3][...] = low.astype(BF16)
        rest[4][...] = lift.astype(BF16)
        return
    mine_ref, theirs_ref, lift_ref = rest[3:6]
    held = rest[8]
    lift_ref[...] = (lift + before[1][...].astype(F32)).astype(BF16)
    held[...] = low + before[0][...].astype(F32)
    width = D // 4
    core = place_ref[0]
    for far in range(2):
        here = pl.multiple_of((2 * far + core) * width, width)
        other = pl.multiple_of((2 * far + 1 - core) * width, width)
        mine_ref[:, far * width : (far + 1) * width] = held[:, pl.ds(here, width)]
        theirs_ref[:, far * width : (far + 1) * width] = held[:, pl.ds(other, width)].astype(BF16)


def mlp(place, n2, dy, bias, packs, before=()):
    split = len(packs) == 5
    packs = packs if split else (*packs, packs[-1])
    rows = n2.shape[0]
    hid = 2 * packs[0].shape[1]
    part = 1 if before else 0

    def block(cols):
        return pl.BlockSpec((PAD, cols), lambda i, *_: (i, 0))

    out_specs = [block(hid), block(hid), fixed((1, hid))]
    out_shape = [like((rows, hid), BF16), like((rows, hid), BF16), like((1, hid), F32)]
    scratch = [pltpu.VMEM((2, D, hid), BF16), pltpu.SemaphoreType.DMA((2, 4))]
    if before:
        out_specs += [block(D // 2), block(D // 2), block(D)]
        out_shape += [like((rows, D // 2), F32), like((rows, D // 2), BF16), like((rows, D), BF16)]
        scratch += [pltpu.VMEM((PAD, D), F32)]
    else:
        out_specs += [block(D), block(D)]
        out_shape += [like((rows, D), BF16)] * 2
    return pl.pallas_call(
        functools.partial(mlp_kernel, bool(before), split),
        name="mlp_second" if before else "mlp_first",
        grid_spec=pltpu.PrefetchScalarGridSpec(
            num_scalar_prefetch=1,
            grid=(rows // PAD,),
            in_specs=[block(D), block(D), pl.BlockSpec((1, hid), lambda i, *_: (0, part))]
            + [pl.BlockSpec(memory_space=pl.ANY)] * 5
            + [block(D)] * len(before),
            out_specs=out_specs,
            scratch_shapes=scratch,
        ),
        out_shape=out_shape,
        compiler_params=params(1),
        cost_estimate=cost(8 * rows * D * hid, 20 * rows * D, 2 * rows * hid),
    )(place, n2, dy, bias, *packs, *before)


def turn_kernel(
    place_ref, h_ref, dy_ref, a_ref, b_ref, low_ref, other_ref, gain_ref, bias_ref, w_ref,
    dh_ref, da_ref, do_ref, sums_ref, mine_ref, theirs_ref, held,
):
    h = h_ref[...]
    held[...] = h + bias_ref[...]
    core, side = place_ref[0], place_ref[1]
    width = D // 4
    low = low_ref[...] + other_ref[...].astype(F32)
    for far in range(2):
        at = pl.ds(pl.multiple_of((2 * far + core) * width, width), width)
        out = (held[:, at] + low[:, far * width : (far + 1) * width]).astype(BF16)

        @pl.when(side == far)
        def _(out=out):
            mine_ref[...] = out

        @pl.when(side != far)
        def _(out=out):
            theirs_ref[...] = out

    middle, scaled = stats(h)
    c = (h - middle) * scaled
    dn = a_ref[...].astype(F32) + b_ref[...].astype(F32)
    dy = dy_ref[...].astype(F32)
    e = dn * gain_ref[...]
    dh = dy + scaled * (e - row_mean(e) - c * row_mean(e * c))
    dh_ref[...] = dh
    da = dh.astype(BF16)
    da_ref[...] = da
    do_ref[...] = mm(da, w_ref[...]).astype(BF16)
    part = jnp.concatenate(
        [col_sum(da.astype(F32)), col_sum(dy), col_sum(dn * c), col_sum(dn)], axis=0
    )
    add_up(sums_ref, pl.program_id(0) == 0, part)


def turn(place, h, dy, a, b, low_mine, low_other, gain, bias, weights):
    rows = h.shape[0]
    wide = weights.shape[1] // 4
    width = D // 4
    return pl.pallas_call(
        turn_kernel,
        name="turn",
        grid_spec=pltpu.PrefetchScalarGridSpec(
            num_scalar_prefetch=1,
            grid=(rows // TM,),
            in_specs=[row_spec(D)] * 4
            + [row_spec(D // 2)] * 2
            + [gain[1], bias[1]]
            + [pl.BlockSpec((D, wide), lambda i, *_: (0, 3), pipeline_mode=pl.Buffered(1))],
            out_specs=[
                row_spec(D),
                row_spec(D),
                row_spec(wide),
                fixed((4, D)),
                row_spec(width),
                row_spec(width),
            ],
            scratch_shapes=[pltpu.VMEM((TM, D), F32)],
        ),
        out_shape=[
            like((rows, D), F32),
            like((rows, D), BF16),
            like((rows, wide), BF16),
            like((4, D), F32),
            like((rows, width), BF16),
            like((rows, width), BF16),
        ],
        compiler_params=params(1),
        cost_estimate=cost(2 * rows * D * wide, 20 * rows * D),
    )(place, h, dy, a, b, low_mine, low_other, gain[0], bias[0], weights)


def last_kernel(
    place_ref, x_ref, dh_ref, a_ref, b_ref, gain_ref, mine_ref, theirs_ref, sum_mine, sum_theirs, held, sums
):
    x = x_ref[...].astype(F32)
    middle, scaled = stats(x)
    c = (x - middle) * scaled
    dn = a_ref[...].astype(F32) + b_ref[...].astype(F32)
    e = dn * gain_ref[...]
    held[...] = dh_ref[...] + scaled * (e - row_mean(e) - c * row_mean(e * c))
    width = D // 4
    core, side = place_ref[0], place_ref[1]
    here = pl.ds(pl.multiple_of((2 * side + core) * width, width), width)
    there = pl.ds(pl.multiple_of((2 * (1 - side) + core) * width, width), width)
    mine_ref[...] = held[:, here]
    theirs_ref[...] = held[:, there].astype(BF16)
    i = pl.program_id(0)
    add_up(sums, i == 0, jnp.concatenate([col_sum(dn * c), col_sum(dn)], axis=0))

    @pl.when(i == pl.num_programs(0) - 1)
    def _():
        sum_mine[...] = sums[:, here]
        sum_theirs[...] = sums[:, there]


def last(place, x, dh, a, b, gain):
    rows = x.shape[0]
    width = D // 4
    return pl.pallas_call(
        last_kernel,
        name="last",
        grid_spec=pltpu.PrefetchScalarGridSpec(
            num_scalar_prefetch=1,
            grid=(rows // TM,),
            in_specs=[row_spec(D)] * 4 + [gain[1]],
            out_specs=[row_spec(width), row_spec(width), fixed((2, width)), fixed((2, width))],
            scratch_shapes=[pltpu.VMEM((TM, D), F32), pltpu.VMEM((2, D), F32)],
        ),
        out_shape=[
            like((rows, width), F32),
            like((rows, width), BF16),
            like((2, width), F32),
            like((2, width), F32),
        ],
        compiler_params=params(1),
        cost_estimate=cost(20 * rows * D, 12 * rows * D),
    )(place, x, dh, a, b, gain[0])


def join_kernel(*refs):
    out_ref = refs[-1]
    start = 0
    for mine, got in zip(refs[:-1:2], refs[1:-1:2]):
        width = got.shape[1]
        total = mine[...].astype(F32) + got[...].astype(F32)
        out_ref[:, start : start + width] = total.astype(BF16)
        start += width


def join(*parts):
    rows = parts[0].shape[0]
    tm = rows // 4
    widths = [item.shape[1] for item in parts[1::2]]
    return pl.pallas_call(
        join_kernel,
        grid=(4,),
        name="join",
        in_specs=[
            pl.BlockSpec((tm, width), lambda i: (i, 0)) for width in widths for _ in range(2)
        ],
        out_specs=pl.BlockSpec((tm, sum(widths)), lambda i: (i, 0)),
        out_shape=like((rows, sum(widths)), BF16),
        compiler_params=params(1),
        cost_estimate=cost(rows * sum(widths), 6 * rows * sum(widths)),
    )(*parts)


def pack_kernel(*refs):
    out_ref = refs[-1]
    width = refs[0].shape[0]
    for at, ref in enumerate(refs[:-2]):
        out_ref[at, :] = ref[...]
    for at in range(4):
        out_ref[len(refs) - 2 + at, :] = refs[-2][width * at : width * (at + 1)]


def pack(vectors, long_vector):
    width = vectors[0].shape[0]
    return pl.pallas_call(
        pack_kernel,
        name="pack",
        out_shape=like((len(vectors) + 4, width), F32),
    )(*vectors, long_vector)


def unpack_kernel(place_ref, own, far, own_other, far_other, vec_ref, qkv_ref, tile_ref):
    core, side, half = place_ref[0], place_ref[1], place_ref[2]
    width = own.shape[1]
    one = width // 2

    def put(ref, at_side, at_core):
        at = pl.multiple_of((2 * at_side + at_core) * width, width)
        for k in range(6):
            vec_ref[k, :, pl.ds(at, width)] = ref[k : k + 1, :]

    put(own, side, core)
    put(far, 1 - side, core)
    put(own_other, side, 1 - core)
    put(far_other, 1 - side, 1 - core)
    qkv_ref[...] = jnp.zeros_like(qkv_ref)
    blocks = ((own, half), (far, half), (own, 1 - half), (far, 1 - half))
    for at, (ref, which) in enumerate(blocks):
        cut = pl.ds(pl.multiple_of(which * one, one), one)
        qkv_ref[:, 3 * one * at : 3 * one * at + one] = ref[6:7, cut]
        qkv_ref[:, 3 * one * at + 2 * one : 3 * one * (at + 1)] = ref[7:8, cut]
    order = (0, 1, 2, 3), (0, 2, 1, 3)
    for part in range(2):
        for at, index in enumerate(order[part]):
            ref, which = blocks[index]
            start = width * (4 * part + at)
            tile_ref[:, start : start + width] = ref[pl.ds(8 + 2 * which + part, 1), :]


def unpack(place, own, far, own_other, far_other):
    width = own.shape[1]
    return pl.pallas_call(
        unpack_kernel,
        name="unpack",
        in_specs=[pl.BlockSpec(memory_space=pltpu.SMEM)]
        + [pl.BlockSpec(memory_space=pltpu.VMEM)] * 4,
        out_shape=[like((6, 1, D), F32), like((1, 6 * width), F32), like((1, 8 * width), F32)],
    )(place, own, far, own_other, far_other)


def collect_kernel(
    place_ref, turn_ref, qkv_ref, up_a_ref, up_b_ref, a_ref, b_ref, mine_ref, theirs_ref
):
    core, side, half = place_ref[0], place_ref[1], place_ref[2]
    width = mine_ref.shape[1]
    one = width // 2
    for ref, at_side in ((mine_ref, side), (theirs_ref, 1 - side)):
        at = pl.ds(pl.multiple_of((2 * at_side + core) * width, width), width)
        ref[2:6, :] = turn_ref[:, at]
    mine_ref[10:12, :] = a_ref[...]
    theirs_ref[10:12, :] = b_ref[...]
    for at in range(4):
        ref = (mine_ref, theirs_ref)[at % 2]
        which = half if at < 2 else 1 - half
        cut = pl.ds(pl.multiple_of(which * one, one), one)
        ref[0:1, cut] = qkv_ref[:, 3 * one * at : 3 * one * at + one]
        ref[1:2, cut] = qkv_ref[:, 3 * one * at + 2 * one : 3 * one * (at + 1)]
    order = (0, 1, 2, 3), (0, 2, 1, 3)
    for part in range(2):
        for at, index in enumerate(order[part]):
            ref = (mine_ref, theirs_ref)[index % 2]
            which = half if index < 2 else 1 - half
            up_ref = (up_a_ref, up_b_ref)[part]
            ref[pl.ds(6 + 2 * which + part, 1), :] = up_ref[:, width * at : width * (at + 1)]


def collect(place, *sums):
    width = D // 4
    return pl.pallas_call(
        collect_kernel,
        name="collect",
        in_specs=[pl.BlockSpec(memory_space=pltpu.SMEM)]
        + [pl.BlockSpec(memory_space=pltpu.VMEM)] * 6,
        out_shape=[like((12, width), F32)] * 2,
    )(place, *sums)


def hand_out_kernel(a_ref, b_ref, *outs):
    sums = a_ref[...] + b_ref[...]
    width = a_ref.shape[1]
    for at in range(6):
        outs[at][...] = sums[at, :]
    for at in range(4):
        outs[6][width * at : width * (at + 1)] = sums[6 + at, :]
    for at in range(2):
        outs[7 + at][...] = sums[10 + at, :]


def hand_out(mine, got):
    width = mine.shape[1]
    one = like((width,), F32)
    return pl.pallas_call(
        hand_out_kernel,
        name="hand_out",
        out_shape=[one] * 6 + [like((4 * width,), F32)] + [one] * 2,
    )(mine, got)


def place_mlp_kernel(swapped, place_ref, mine_ref, other_ref, a_ref, b_ref, up_ref, down_ref, out_ref):
    half = place_ref[2]
    width = up_ref.shape[1] // 2
    quarter = width // 2
    heads = out_ref.shape[0] // 2
    for ref, at in ((mine_ref, half), (other_ref, 1 - half)):
        up_ref[:, pl.ds(pl.multiple_of(at * width, width), width)] = ref[:, :width].astype(F32)
        down_ref[pl.ds(pl.multiple_of(at * width + quarter, quarter), quarter), :] = (
            ref[:, width : width + quarter].astype(F32).T
        )
        out_ref[pl.ds(pl.multiple_of(at * heads, heads), heads), :] = (
            ref[:, width + quarter :].astype(F32).T
        )
    for part, at in ((0, half), (1, 1 - half)):
        from_b = 1 - part if swapped else part
        total = a_ref[:, part * quarter : (part + 1) * quarter].astype(F32)
        total = total + b_ref[:, from_b * quarter : (from_b + 1) * quarter].astype(F32)
        down_ref[pl.ds(pl.multiple_of(at * width, width), quarter), :] = total.T


def place_mlp(place, mine, other, a, b, swapped):
    strip, cols = mine.shape
    quarter = a.shape[1] // 2
    heads = cols - 3 * quarter
    return pl.pallas_call(
        functools.partial(place_mlp_kernel, swapped),
        name="place_mlp",
        in_specs=[pl.BlockSpec(memory_space=pltpu.SMEM)]
        + [pl.BlockSpec(memory_space=pltpu.VMEM)] * 4,
        out_shape=[
            like((strip, 4 * quarter), F32),
            like((4 * quarter, strip), F32),
            like((2 * heads, strip), F32),
        ],
    )(place, mine, other, a, b)


def place_qkv_kernel(place_ref, mine_ref, other_ref, *outs):
    half = place_ref[2]
    heads = outs[0].shape[1] // 2
    for ref, at in ((mine_ref, half), (other_ref, 1 - half)):
        here = pl.ds(pl.multiple_of(at * heads, heads), heads)
        for w in range(3):
            outs[w][:, here] = ref[:, heads * w : heads * (w + 1)].astype(F32)


def place_qkv(place, mine, other):
    strip, cols = mine.shape
    return pl.pallas_call(
        place_qkv_kernel,
        name="place_qkv",
        in_specs=[pl.BlockSpec(memory_space=pltpu.SMEM)]
        + [pl.BlockSpec(memory_space=pltpu.VMEM)] * 2,
        out_shape=[like((strip, cols // 3 * 2), F32)] * 3,
    )(place, mine, other)


def local(
    sizes,
    inputs,
    query_weight,
    key_weight,
    value_weight,
    query_bias,
    value_bias,
    out_weight,
    out_bias,
    up_weight,
    up_bias,
    down_weight,
    down_bias,
    first_gain,
    first_shift,
    second_gain,
    second_shift,
    cotangent,
):
    n_dp, n_row, n_xa, n_core = sizes
    my_x = lax.axis_index("xa")
    my_core = lax.axis_index("core")
    my_row = lax.axis_index("row")
    my_half = lax.axis_index("dp") % 2
    place = jnp.stack([my_core, my_x, my_half, my_row]).astype(jnp.int32)
    tokens_here, width = inputs.shape
    images = tokens_here // SEQ
    held = images // n_xa
    rows = held * PAD
    half = up_weight.shape[1] // 2
    quarter = half // 2
    heads_half = width // 2
    three = 3 * heads_half

    def swap(value, axis, size, bit=1):
        return lax.ppermute(value, axis, [(at, at ^ bit) for at in range(size)])

    def shifted(value, shift):
        return lax.ppermute(value, "row", [(at, (at + shift) % n_row) for at in range(n_row)])

    def across(value):
        return swap(value, "xa", n_xa)

    def beside(value):
        return swap(value, "core", n_core)

    def over(value):
        return swap(value, "dp", n_dp)

    def pick(value, at, axis):
        return lax.dynamic_index_in_dim(value, at, axis, keepdims=False)

    def in_order(mine, other, at):
        return jnp.where(at == 0, mine, other), jnp.where(at == 0, other, mine)

    def after(value, *others):
        return lax.optimization_barrier((value, *others))[0]

    def halves(value, axis):
        cut = value.shape[axis] // 2
        both = value.reshape(value.shape[:axis] + (2, cut) + value.shape[axis + 1 :])
        return pick(both, my_half, axis), pick(both, my_half ^ 1, axis)

    count = held * SEQ

    def send_tokens(value):
        return lax.dynamic_slice_in_dim(value, (my_x ^ 1) * count, count, 0)

    def wide_tokens(value, got):
        mine = lax.dynamic_slice_in_dim(value, my_x * count, count, 0)
        pair = jnp.concatenate([mine, got], axis=1).reshape(held, SEQ, 2 * width)
        pair = jnp.pad(pair, ((0, 0), (0, PAD - SEQ), (0, 0))).reshape(rows, 2 * width)
        other = beside(pair)
        left, right = in_order(pair, other, my_core)
        first_left, second_left = in_order(left[:, :width], left[:, width:], my_x)
        first_right, second_right = in_order(right[:, :width], right[:, width:], my_x)
        return jnp.concatenate([first_left, first_right, second_left, second_right], axis=1)

    attn_shard = jnp.concatenate(
        [halves(item, 1)[0] for item in (query_weight, key_weight, value_weight)]
        + [halves(out_weight, 0)[0].T],
        axis=1,
    )
    input_leaves = send_tokens(inputs)
    attn_shard = after(attn_shard, input_leaves)
    input_got = across(input_leaves)
    pieces = [attn_shard] + [shifted(attn_shard, shift) for shift in range(1, n_row)]
    small = pack(
        (
            out_bias,
            down_bias,
            first_gain,
            first_shift,
            second_gain,
            second_shift,
            query_bias,
            value_bias,
        ),
        up_bias,
    )
    fars = [across(piece) for piece in pieces]
    oths = [over(piece) for piece in pieces]
    small_far = across(small)
    vectors, qkv_bias, tile_bias = unpack(
        place, small, after(small_far, pieces[-1]), beside(small), beside(small_far)
    )
    out_bias_all, down_bias_all, gain_one, shift_one, gain_two, shift_two = (
        (vectors, pl.BlockSpec((None, 1, D), lambda i, *_, at=at: (at, 0, 0))) for at in range(6)
    )
    wide_input = wide_tokens(inputs, after(input_got, pieces[-1]))
    far_oths = [over(far) for far in fars[:-1]]
    far_oths.append(across(after(oths[-1], wide_input, qkv_bias)))

    def gather(part):
        up_part = halves(up_weight, 1)[0][:, quarter * part : quarter * (part + 1)]
        down_part = halves(down_weight, 0)[0][quarter * part : quarter * (part + 1)].T
        shard = after(jnp.concatenate([up_part, down_part], axis=1), *pieces)
        return lax.all_gather(shard, "row", axis=0, tiled=True)

    own_a, own_b = gather(0), gather(1)
    grad_got = across(after(send_tokens(cotangent), wide_input))

    wide_one, qkv, attn_weights = norm_qkv(
        place, wide_input, gain_one, shift_one, qkv_bias, (*pieces, *fars, *oths, *far_oths)
    )
    oth_a, far_a = over(own_a), across(own_a)
    oth_b, far_b = over(own_b), across(own_b)
    first_heads = attend(qkv)
    attended, probs = attend(qkv, first_heads)
    mixed = mm_nt(attended, attn_weights[:, 4 * three :]).astype(BF16)
    mixed_other = beside(mixed)
    wide_grad = wide_tokens(cotangent, after(grad_got, mixed))
    far_oth_a = over(far_a)
    middle_sum, wide_two = middle(wide_input, mixed, mixed_other, out_bias_all, gain_two, shift_two)
    up_far_oth_b = over(far_b[:, :quarter])
    down_far_oth_b = across(oth_b[:, quarter:])

    def tiles(value, first, end):
        return value[:, quarter * first : quarter * end]

    gate_a, pre_a, up_sums_a, low_a, lift_a = mlp(
        place, wide_two, wide_grad, tile_bias, (own_a, far_a, oth_a, far_oth_a)
    )
    up_over = mm_tn(wide_two, tiles(pre_a, 2, 4)).astype(BF16)
    down_a = mm_tn(wide_grad, gate_a).astype(BF16)
    up_over_got = over(up_over)
    down_piece = lax.psum_scatter(down_a, "row", scatter_dimension=0, tiled=True)
    gate_b, pre_b, up_sums_b, low_mine, low_theirs, lifted_two = mlp(
        place,
        after(wide_two, up_over, down_a),
        wide_grad,
        tile_bias,
        (own_b, oth_b, far_b, up_far_oth_b, down_far_oth_b),
        (low_a, lift_a),
    )

    def wide_add(mine, got):
        return (mine.astype(F32) + got.astype(F32)).astype(BF16)

    def same_half(value):
        if n_dp == 2:
            return value
        groups = [[at + bit for at in range(0, n_dp, 2)] for bit in range(2)]
        return lax.psum(value.astype(F32), "dp", axis_index_groups=groups).astype(BF16)

    def scatter(value):
        return lax.psum_scatter(value, "row", scatter_dimension=0, tiled=True)

    lifted_other = beside(lifted_two)
    low_other = beside(low_theirs)
    up_across = mm_tn(wide_two, tiles(pre_b, 2, 4)).astype(BF16)
    down_over = mm_tn(wide_grad, tiles(gate_b, 2, 4)).astype(BF16)
    up_across_got, down_over_got = across(up_across), over(down_over)

    middle_grad, attn_grad, head_grad, turn_sums, out_mine, out_theirs = turn(
        place,
        middle_sum,
        wide_grad,
        lifted_two,
        after(lifted_other, up_across, down_over),
        low_mine,
        low_other,
        gain_two,
        down_bias_all,
        attn_weights,
    )
    out_all = mm_tn(attn_grad, attended).astype(BF16)
    out_over_got = over(out_all[:, 2 * heads_half :])
    down_x_got = across(after(down_piece, attn_grad)[:, half:])
    up_over_got, up_across_got, down_over_got, _ = lax.optimization_barrier(
        (up_over_got, up_across_got, down_over_got, out_all)
    )
    up_a = wide_add(mm_tn(wide_two, tiles(pre_a, 0, 2)), up_over_got)
    up_b = wide_add(mm_tn(wide_two, tiles(pre_b, 0, 2)), up_across_got)
    down_b = wide_add(mm_tn(wide_grad, tiles(gate_b, 0, 2)), down_over_got)
    up_a_got, up_b_got = across(up_a[:, quarter:]), over(up_b[:, quarter:])
    out_own = wide_add(out_all[:, : 2 * heads_half], after(out_over_got, down_b))
    out_far_got = across(out_own[:, heads_half:])
    down_x = wide_add(down_piece[:, :half], after(down_x_got, down_b))
    down_y_got = over(down_x)
    down_b_got = across(down_b[:, quarter:])
    out_got = across(after(out_theirs, down_b))
    dqkv, qkv_sums = attend_back(qkv, probs, after(head_grad, up_a, up_b, out_own, down_x))

    def to_feature_blocks(mine, got, dtype):
        first, second = in_order(mine.astype(dtype), got.astype(dtype), my_x)
        both = jnp.concatenate([first, second]).reshape(images, PAD, width)
        return both[:, :SEQ].reshape(tokens_here, width)

    cut = 2 * heads_half
    split = 3 * three + cut
    far_oth_qk = mm_tn(wide_one, dqkv[:, 3 * three : split]).astype(BF16)
    far_oth_v = mm_tn(after(wide_one, far_oth_qk), dqkv[:, split:]).astype(BF16)
    qk_got, v_got = over(far_oth_qk), across(far_oth_v)
    up_sum = join(
        up_a, up_a_got, up_b, up_b_got, down_b, down_b_got, out_own, after(out_far_got, far_oth_v)
    )
    up_piece = same_half(scatter(up_sum))
    near_oth = wide_add(
        mm_tn(wide_one, dqkv[:, 2 * three : 3 * three]),
        jnp.pad(after(v_got, up_sum), ((0, 0), (cut, 0))),
    )
    near_oth_got = over(near_oth)
    far_own = wide_add(
        mm_tn(wide_one, dqkv[:, three : 2 * three]),
        jnp.pad(after(qk_got, near_oth), ((0, 0), (0, three - cut))),
    )
    far_own_got = across(far_own)
    lifted_one = mm_nt(
        after(dqkv, far_own), attn_weights[:, : 4 * three]
    ).astype(BF16)
    lifted_one_other = beside(lifted_one)

    near_own = mm_tn(after(wide_one, lifted_one), dqkv[:, :three])
    input_mine, input_theirs, late_mine, late_theirs = last(
        place, wide_input, middle_grad, lifted_one, after(lifted_one_other, near_own), gain_one
    )
    mine_sums, theirs_sums = collect(
        place, turn_sums, qkv_sums, up_sums_a, up_sums_b, late_mine, late_theirs
    )

    near_sum = (near_own + near_oth_got.astype(F32) + after(far_own_got, mine_sums).astype(F32)).astype(
        BF16
    )
    strip = D // n_row

    def rows_of(value, shift):
        return lax.dynamic_slice_in_dim(value, (my_row + shift) % n_row * strip, strip, 0)

    gots = [shifted(rows_of(near_sum, shift), shift) for shift in range(1, n_row)]
    input_got = across(after(input_theirs, near_sum))
    sums = mine_sums + across(after(theirs_sums, near_sum))
    steps = [("row", n_row, 1 << bit) for bit in range(n_row.bit_length() - 1)]
    steps += [("dp", n_dp, 1 << bit) for bit in range(n_dp.bit_length() - 1)]
    for step in steps[:-1]:
        sums = sums + swap(sums, *step)
    sums_got = swap(sums, *steps[-1])
    outputs = to_feature_blocks(out_mine, after(out_got, near_sum), BF16)

    qkv_total = rows_of(near_sum, 0).astype(F32)
    for got in gots:
        qkv_total = qkv_total + got.astype(F32)
    qkv_piece = same_half(qkv_total.astype(BF16))
    qkv_other = over(qkv_piece)
    input_grad = to_feature_blocks(input_mine, input_got, F32)
    up_other = over(up_piece)

    if n_dp > 2:
        down_total = down_x.astype(F32) + jnp.concatenate(
            [down_y_got[:, quarter:], down_y_got[:, :quarter]], axis=1
        ).astype(F32)
        groups = [[at + bit for at in range(0, n_dp, 2)] for bit in range(2)]
        down_total = lax.psum(down_total, "dp", axis_index_groups=groups)
        parts = (down_total, jnp.zeros_like(down_total))
    else:
        parts = (down_x, down_y_got)
    up_grad, down_grad, out_grad = place_mlp(place, up_piece, up_other, *parts, n_dp == 2)
    sums = hand_out(sums, after(sums_got, up_grad, input_grad))
    query_grad, key_grad, value_grad = place_qkv(
        place, qkv_piece, after(qkv_other, up_grad, input_grad)
    )

    return (
        outputs,
        input_grad,
        query_grad,
        key_grad,
        value_grad,
        sums[0],
        sums[1],
        out_grad,
        sums[2],
        up_grad,
        sums[6],
        down_grad,
        sums[3],
        sums[7],
        sums[8],
        sums[4],
        sums[5],
    )


def solution(mesh):
    n_dp, n_row, n_col = (mesh.shape[name] for name in ("dp", "row", "col"))
    sizes = (n_dp, n_row, n_col // 2, 2)
    split = Mesh(mesh.devices.reshape(sizes), ("dp", "row", "xa", "core"))
    col = ("xa", "core")
    tokens, rows, cols, vec = P(("dp", "row"), col), P("row", col), P(col, "row"), P(col)
    in_specs = (
        (tokens, rows, rows, rows, vec, vec, cols, vec, rows, vec, cols)
        + (vec,) * 5
        + (tokens,)
    )
    out_specs = (
        (tokens, tokens, rows, rows, rows, vec, vec, cols, vec, rows, vec, cols) + (vec,) * 5
    )

    def body(*args):
        return local(sizes, *args)

    return jax.shard_map(
        body, mesh=split, in_specs=in_specs, out_specs=out_specs, check_vma=False
    )
```

```python
import functools
import math

import jax
import jax.numpy as jnp
from jax import lax
from jax.experimental import pallas as pl
from jax.experimental.pallas import tpu as pltpu
from jax.sharding import Mesh, PartitionSpec as P


D = 1024
HD = 64
SEQ = 577
PAD = 592
TM = 296
EPS = 1e-06
F32 = jnp.float32
BF16 = jnp.bfloat16
VMEM_LIMIT = 60 * 1024 * 1024
ROOT_HALF = math.sqrt(0.5)
DENSITY = 1.0 / math.sqrt(2.0 * math.pi)


def mm(a, b):
    return lax.dot_general(a, b, (((1,), (0,)), ((), ())), preferred_element_type=F32)


def mm_nt(a, b):
    return lax.dot_general(a, b, (((1,), (1,)), ((), ())), preferred_element_type=F32)


def mm_tn(a, b):
    return lax.dot_general(a, b, (((0,), (0,)), ((), ())), preferred_element_type=F32)


def row_mean(v):
    return jnp.sum(v, axis=1, keepdims=True) * (1.0 / D)


def col_sum(v):
    return jnp.sum(v, axis=0, keepdims=True)


def stats(rows):
    middle = row_mean(rows)
    spread = row_mean(rows * rows) - middle * middle
    return middle, lax.rsqrt(spread + EPS)


def params(n):
    return pltpu.CompilerParams(
        dimension_semantics=("arbitrary",) * n, vmem_limit_bytes=VMEM_LIMIT
    )


def cost(flops, moved, exps=0):
    return pl.CostEstimate(flops=int(flops), bytes_accessed=int(moved), transcendentals=int(exps))


def like(shape, dtype):
    return jax.ShapeDtypeStruct(shape, dtype)


def row_spec(cols):
    return pl.BlockSpec((TM, cols), lambda i, *_: (i, 0))


def fixed(shape):
    return pl.BlockSpec(shape, lambda *_: (0,) * len(shape))


def held_once(shape):
    return pl.BlockSpec(shape, lambda *_: (0,) * len(shape), pipeline_mode=pl.Buffered(1))


def add_up(ref, first, part):
    @pl.when(first)
    def _():
        ref[...] = part

    @pl.when(jnp.logical_not(first))
    def _():
        ref[...] += part


def norm_qkv_kernel(place_ref, x_ref, gain_ref, shift_ref, bias_ref, *refs):
    pieces, (n_ref, o_ref, w_ref) = refs[:-3], refs[-3:]
    n_row = len(pieces) // 4
    strip, wide = pieces[0].shape
    one = wide // 4

    @pl.when(pl.program_id(0) == 0)
    def _():
        for shift in range(n_row):
            start = lax.rem(place_ref[3] - shift + n_row, n_row) * strip
            rows = pl.ds(pl.multiple_of(start, strip), strip)
            for block in range(4):
                piece = pieces[n_row * block + shift]
                w_ref[rows, 3 * one * block : 3 * one * (block + 1)] = piece[:, : 3 * one]
                w_ref[rows, (12 + block) * one : (13 + block) * one] = piece[:, 3 * one :]

    x = x_ref[...].astype(F32)
    middle, scaled = stats(x)
    n = (((x - middle) * scaled) * gain_ref[...] + shift_ref[...]).astype(BF16)
    n_ref[...] = n
    o_ref[...] = (mm(n, w_ref[:, : 12 * one]) + bias_ref[...]).astype(BF16)


def norm_qkv(place, x, gain, shift, bias, pieces):
    rows = x.shape[0]
    wide = pieces[0].shape[1]
    out = 3 * wide
    return pl.pallas_call(
        norm_qkv_kernel,
        name="norm_qkv",
        grid_spec=pltpu.PrefetchScalarGridSpec(
            num_scalar_prefetch=1,
            grid=(rows // TM,),
            in_specs=[row_spec(D), gain[1], shift[1], fixed((1, out))]
            + [held_once(pieces[0].shape)] * len(pieces),
            out_specs=[row_spec(D), row_spec(out), held_once((D, 4 * wide))],
        ),
        out_shape=[like((rows, D), BF16), like((rows, out), BF16), like((D, 4 * wide), BF16)],
        compiler_params=params(1),
        cost_estimate=cost(2 * rows * D * out, 16 * rows * D),
    )(place, x, gain[0], shift[0], bias, *pieces)


def attend_kernel(qkv_ref, o_ref, p_ref):
    live = lax.broadcasted_iota(jnp.int32, (1, PAD), 1) < SEQ
    step = 2 * HD
    items = [(h, slice(r, r + TM)) for h in range(2) for r in range(0, PAD, TM)]

    def score(h, rows):
        q = qkv_ref[rows, HD * h : HD * (h + 1)] * jnp.asarray(0.125, BF16)
        return mm_nt(q, qkv_ref[:, step + HD * h : step + HD * (h + 1)])

    scores = [score(*item) for item in items[:3]]
    for at, (h, rows) in enumerate(items):
        if at + 3 < len(items):
            scores.append(score(*items[at + 3]))
        s = jnp.where(live, scores[at], -1e30)
        e = jnp.exp(s - jnp.max(s, axis=1, keepdims=True))
        p = (e * (1.0 / jnp.sum(e, axis=1, keepdims=True))).astype(BF16)
        p_ref[h, rows, :] = p
        v = qkv_ref[:, 2 * step + HD * h : 2 * step + HD * (h + 1)]
        o_ref[rows, HD * h : HD * (h + 1)] = mm(p, v).astype(BF16)


def attend(qkv, before=()):
    rows, cols = qkv.shape
    pairs = cols // (6 * HD)
    held = rows // PAD
    start = pairs // 2 if before else 0

    def kernel(*refs):
        attend_kernel(refs[0], refs[-2], refs[-1])

    return pl.pallas_call(
        kernel,
        grid=(pairs // 2, held),
        name="attend",
        in_specs=[pl.BlockSpec((PAD, 6 * HD), lambda p, i: (i, p + start))]
        + [pl.BlockSpec(memory_space=pl.ANY)] * len(before),
        out_specs=[
            pl.BlockSpec((PAD, 2 * HD), lambda p, i: (i, p + start)),
            pl.BlockSpec((None, 2, PAD, PAD), lambda p, i: (i, p + start, 0, 0)),
        ],
        out_shape=[like((rows, cols // 3), BF16), like((held, 2 * pairs, PAD, PAD), BF16)],
        input_output_aliases={1: 0, 2: 1} if before else {},
        compiler_params=params(2),
        cost_estimate=cost(8 * rows * PAD * cols, 20 * rows * D, 2 * rows * PAD * pairs),
    )(qkv, *before)


def attend_back_kernel(qkv_ref, p_ref, g_ref, d_ref, sum_ref):
    step = 2 * HD

    def cut(h, w):
        return slice(step * w + HD * h, step * w + HD * (h + 1))

    grads = [g_ref[:, HD * h : HD * (h + 1)] for h in range(2)]
    dprobs = [mm_nt(grads[h], qkv_ref[:, cut(h, 2)]) for h in range(2)]
    dscores = []
    for h in range(2):
        p = p_ref[h].astype(F32)
        z = jnp.sum(p * dprobs[h], axis=1, keepdims=True)
        dscores.append((p * (dprobs[h] - z)).astype(BF16))
        d_ref[:, cut(h, 2)] = mm_tn(p_ref[h], grads[h]).astype(BF16)
    for h in range(2):
        d_ref[:, cut(h, 0)] = (mm(dscores[h], qkv_ref[:, cut(h, 1)]) * 0.125).astype(BF16)
        d_ref[:, cut(h, 1)] = (mm_tn(dscores[h], qkv_ref[:, cut(h, 0)]) * 0.125).astype(BF16)
    add_up(sum_ref, pl.program_id(1) == 0, col_sum(d_ref[...].astype(F32)))


def attend_back(qkv, probs, grads):
    rows, cols = qkv.shape
    pairs = cols // (6 * HD)
    held = rows // PAD
    three = pl.BlockSpec((PAD, 6 * HD), lambda p, i: (i, p))
    return pl.pallas_call(
        attend_back_kernel,
        grid=(pairs, held),
        name="attend_back",
        in_specs=[
            three,
            pl.BlockSpec((None, 2, PAD, PAD), lambda p, i: (i, p, 0, 0)),
            pl.BlockSpec((PAD, 2 * HD), lambda p, i: (i, p)),
        ],
        out_specs=[three, pl.BlockSpec((1, 6 * HD), lambda p, i: (0, p))],
        out_shape=[like((rows, cols), BF16), like((1, cols), F32)],
        compiler_params=params(2),
        cost_estimate=cost(20 * rows * PAD * cols, 50 * rows * D),
    )(qkv, probs, grads)


def middle_kernel(x_ref, a_ref, b_ref, bias_ref, gain_ref, shift_ref, h_ref, n_ref):
    h = x_ref[...].astype(F32) + (a_ref[...].astype(F32) + b_ref[...].astype(F32)) + bias_ref[...]
    h_ref[...] = h
    middle, scaled = stats(h)
    n_ref[...] = (((h - middle) * scaled) * gain_ref[...] + shift_ref[...]).astype(BF16)


def middle(x, a, b, bias, gain, shift):
    rows = x.shape[0]
    return pl.pallas_call(
        middle_kernel,
        grid=(rows // TM,),
        name="middle",
        in_specs=[row_spec(D)] * 3 + [bias[1], gain[1], shift[1]],
        out_specs=[row_spec(D)] * 2,
        out_shape=[like((rows, D), F32), like((rows, D), BF16)],
        compiler_params=params(1),
        cost_estimate=cost(20 * rows * D, 12 * rows * D),
    )(x, a, b, bias[0], gain[0], shift[0])


def mlp_kernel(final, split, place_ref, n_ref, dy_ref, bias_ref, *refs):
    packs = refs[:5]
    before = refs[5:7] if final else ()
    rest = refs[5 + len(before) :]
    g_ref, du_ref, bsum_ref = rest[:3]
    buf, sem = rest[6:8] if final else rest[5:7]
    i = pl.program_id(0)
    tn = g_ref.shape[1] // 4

    @pl.when(i == 0)
    def _():
        copies = []
        for tile in range(4):
            for part in range(2):
                if tile == 3 and split:
                    source = packs[tile + part]
                else:
                    source = packs[tile].at[:, pl.ds(part * tn, tn)]
                copies.append(
                    pltpu.make_async_copy(
                        source,
                        buf.at[part, :, pl.ds(tile * tn, tn)],
                        sem.at[part, tile],
                    )
                )
        for copy in copies:
            copy.start()
        for copy in copies:
            copy.wait()

    up, down = buf[0], buf[1]
    u = mm(n_ref[...], up) + bias_ref[...]
    cdf = 0.5 * (1.0 + lax.erf(u * ROOT_HALF))
    g = (u * cdf).astype(BF16)
    slope = cdf + u * (jnp.exp(-0.5 * u * u) * DENSITY)
    for at, tile in enumerate((0, 2, 1, 3)):
        g_ref[:, at * tn : (at + 1) * tn] = g[:, tile * tn : (tile + 1) * tn]
    du = (mm(dy_ref[...], down) * slope).astype(BF16)
    du_ref[...] = du
    add_up(bsum_ref, i == 0, col_sum(du.astype(F32)))
    low = mm_nt(g, down)
    lift = mm_nt(du, up)
    if not final:
        rest[3][...] = low.astype(BF16)
        rest[4][...] = lift.astype(BF16)
        return
    mine_ref, theirs_ref, lift_ref = rest[3:6]
    held = rest[8]
    lift_ref[...] = (lift + before[1][...].astype(F32)).astype(BF16)
    held[...] = low + before[0][...].astype(F32)
    width = D // 4
    core = place_ref[0]
    for far in range(2):
        here = pl.multiple_of((2 * far + core) * width, width)
        other = pl.multiple_of((2 * far + 1 - core) * width, width)
        mine_ref[:, far * width : (far + 1) * width] = held[:, pl.ds(here, width)]
        theirs_ref[:, far * width : (far + 1) * width] = held[:, pl.ds(other, width)].astype(BF16)


def mlp(place, n2, dy, bias, packs, before=()):
    split = len(packs) == 5
    packs = packs if split else (*packs, packs[-1])
    rows = n2.shape[0]
    hid = 2 * packs[0].shape[1]
    part = 1 if before else 0

    def block(cols):
        return pl.BlockSpec((PAD, cols), lambda i, *_: (i, 0))

    out_specs = [block(hid), block(hid), fixed((1, hid))]
    out_shape = [like((rows, hid), BF16), like((rows, hid), BF16), like((1, hid), F32)]
    scratch = [pltpu.VMEM((2, D, hid), BF16), pltpu.SemaphoreType.DMA((2, 4))]
    if before:
        out_specs += [block(D // 2), block(D // 2), block(D)]
        out_shape += [like((rows, D // 2), F32), like((rows, D // 2), BF16), like((rows, D), BF16)]
        scratch += [pltpu.VMEM((PAD, D), F32)]
    else:
        out_specs += [block(D), block(D)]
        out_shape += [like((rows, D), BF16)] * 2
    return pl.pallas_call(
        functools.partial(mlp_kernel, bool(before), split),
        name="mlp_second" if before else "mlp_first",
        grid_spec=pltpu.PrefetchScalarGridSpec(
            num_scalar_prefetch=1,
            grid=(rows // PAD,),
            in_specs=[block(D), block(D), pl.BlockSpec((1, hid), lambda i, *_: (0, part))]
            + [pl.BlockSpec(memory_space=pl.ANY)] * 5
            + [block(D)] * len(before),
            out_specs=out_specs,
            scratch_shapes=scratch,
        ),
        out_shape=out_shape,
        compiler_params=params(1),
        cost_estimate=cost(8 * rows * D * hid, 20 * rows * D, 2 * rows * hid),
    )(place, n2, dy, bias, *packs, *before)


def turn_kernel(
    place_ref, h_ref, dy_ref, a_ref, b_ref, low_ref, other_ref, gain_ref, bias_ref, w_ref,
    dh_ref, da_ref, do_ref, sums_ref, mine_ref, theirs_ref, held,
):
    h = h_ref[...]
    held[...] = h + bias_ref[...]
    core, side = place_ref[0], place_ref[1]
    width = D // 4
    low = low_ref[...] + other_ref[...].astype(F32)
    for far in range(2):
        at = pl.ds(pl.multiple_of((2 * far + core) * width, width), width)
        out = (held[:, at] + low[:, far * width : (far + 1) * width]).astype(BF16)

        @pl.when(side == far)
        def _(out=out):
            mine_ref[...] = out

        @pl.when(side != far)
        def _(out=out):
            theirs_ref[...] = out

    middle, scaled = stats(h)
    c = (h - middle) * scaled
    dn = a_ref[...].astype(F32) + b_ref[...].astype(F32)
    dy = dy_ref[...].astype(F32)
    e = dn * gain_ref[...]
    dh = dy + scaled * (e - row_mean(e) - c * row_mean(e * c))
    dh_ref[...] = dh
    da = dh.astype(BF16)
    da_ref[...] = da
    do_ref[...] = mm(da, w_ref[...]).astype(BF16)
    part = jnp.concatenate(
        [col_sum(da.astype(F32)), col_sum(dy), col_sum(dn * c), col_sum(dn)], axis=0
    )
    add_up(sums_ref, pl.program_id(0) == 0, part)


def turn(place, h, dy, a, b, low_mine, low_other, gain, bias, weights):
    rows = h.shape[0]
    wide = weights.shape[1] // 4
    width = D // 4
    return pl.pallas_call(
        turn_kernel,
        name="turn",
        grid_spec=pltpu.PrefetchScalarGridSpec(
            num_scalar_prefetch=1,
            grid=(rows // TM,),
            in_specs=[row_spec(D)] * 4
            + [row_spec(D // 2)] * 2
            + [gain[1], bias[1]]
            + [pl.BlockSpec((D, wide), lambda i, *_: (0, 3), pipeline_mode=pl.Buffered(1))],
            out_specs=[
                row_spec(D),
                row_spec(D),
                row_spec(wide),
                fixed((4, D)),
                row_spec(width),
                row_spec(width),
            ],
            scratch_shapes=[pltpu.VMEM((TM, D), F32)],
        ),
        out_shape=[
            like((rows, D), F32),
            like((rows, D), BF16),
            like((rows, wide), BF16),
            like((4, D), F32),
            like((rows, width), BF16),
            like((rows, width), BF16),
        ],
        compiler_params=params(1),
        cost_estimate=cost(2 * rows * D * wide, 20 * rows * D),
    )(place, h, dy, a, b, low_mine, low_other, gain[0], bias[0], weights)


def last_kernel(
    place_ref, x_ref, dh_ref, a_ref, b_ref, gain_ref, mine_ref, theirs_ref, sum_mine, sum_theirs, held, sums
):
    x = x_ref[...].astype(F32)
    middle, scaled = stats(x)
    c = (x - middle) * scaled
    dn = a_ref[...].astype(F32) + b_ref[...].astype(F32)
    e = dn * gain_ref[...]
    held[...] = dh_ref[...] + scaled * (e - row_mean(e) - c * row_mean(e * c))
    width = D // 4
    core, side = place_ref[0], place_ref[1]
    here = pl.ds(pl.multiple_of((2 * side + core) * width, width), width)
    there = pl.ds(pl.multiple_of((2 * (1 - side) + core) * width, width), width)
    mine_ref[...] = held[:, here]
    theirs_ref[...] = held[:, there].astype(BF16)
    i = pl.program_id(0)
    add_up(sums, i == 0, jnp.concatenate([col_sum(dn * c), col_sum(dn)], axis=0))

    @pl.when(i == pl.num_programs(0) - 1)
    def _():
        sum_mine[...] = sums[:, here]
        sum_theirs[...] = sums[:, there]


def last(place, x, dh, a, b, gain):
    rows = x.shape[0]
    width = D // 4
    return pl.pallas_call(
        last_kernel,
        name="last",
        grid_spec=pltpu.PrefetchScalarGridSpec(
            num_scalar_prefetch=1,
            grid=(rows // TM,),
            in_specs=[row_spec(D)] * 4 + [gain[1]],
            out_specs=[row_spec(width), row_spec(width), fixed((2, width)), fixed((2, width))],
            scratch_shapes=[pltpu.VMEM((TM, D), F32), pltpu.VMEM((2, D), F32)],
        ),
        out_shape=[
            like((rows, width), F32),
            like((rows, width), BF16),
            like((2, width), F32),
            like((2, width), F32),
        ],
        compiler_params=params(1),
        cost_estimate=cost(20 * rows * D, 12 * rows * D),
    )(place, x, dh, a, b, gain[0])


def join_kernel(*refs):
    out_ref = refs[-1]
    start = 0
    for mine, got in zip(refs[:-1:2], refs[1:-1:2]):
        width = got.shape[1]
        total = mine[...].astype(F32) + got[...].astype(F32)
        out_ref[:, start : start + width] = total.astype(BF16)
        start += width


def join(*parts):
    rows = parts[0].shape[0]
    tm = rows // 4
    widths = [item.shape[1] for item in parts[1::2]]
    return pl.pallas_call(
        join_kernel,
        grid=(4,),
        name="join",
        in_specs=[
            pl.BlockSpec((tm, width), lambda i: (i, 0)) for width in widths for _ in range(2)
        ],
        out_specs=pl.BlockSpec((tm, sum(widths)), lambda i: (i, 0)),
        out_shape=like((rows, sum(widths)), BF16),
        compiler_params=params(1),
        cost_estimate=cost(rows * sum(widths), 6 * rows * sum(widths)),
    )(*parts)


def pack_kernel(*refs):
    out_ref = refs[-1]
    width = refs[0].shape[0]
    for at, ref in enumerate(refs[:-2]):
        out_ref[at, :] = ref[...]
    for at in range(4):
        out_ref[len(refs) - 2 + at, :] = refs[-2][width * at : width * (at + 1)]


def pack(vectors, long_vector):
    width = vectors[0].shape[0]
    return pl.pallas_call(
        pack_kernel,
        name="pack",
        out_shape=like((len(vectors) + 4, width), F32),
    )(*vectors, long_vector)


def unpack_kernel(place_ref, own, far, own_other, far_other, vec_ref, qkv_ref, tile_ref):
    core, side, half = place_ref[0], place_ref[1], place_ref[2]
    width = own.shape[1]
    one = width // 2

    def put(ref, at_side, at_core):
        at = pl.multiple_of((2 * at_side + at_core) * width, width)
        for k in range(6):
            vec_ref[k, :, pl.ds(at, width)] = ref[k : k + 1, :]

    put(own, side, core)
    put(far, 1 - side, core)
    put(own_other, side, 1 - core)
    put(far_other, 1 - side, 1 - core)
    qkv_ref[...] = jnp.zeros_like(qkv_ref)
    blocks = ((own, half), (far, half), (own, 1 - half), (far, 1 - half))
    for at, (ref, which) in enumerate(blocks):
        cut = pl.ds(pl.multiple_of(which * one, one), one)
        qkv_ref[:, 3 * one * at : 3 * one * at + one] = ref[6:7, cut]
        qkv_ref[:, 3 * one * at + 2 * one : 3 * one * (at + 1)] = ref[7:8, cut]
    order = (0, 1, 2, 3), (0, 2, 1, 3)
    for part in range(2):
        for at, index in enumerate(order[part]):
            ref, which = blocks[index]
            start = width * (4 * part + at)
            tile_ref[:, start : start + width] = ref[pl.ds(8 + 2 * which + part, 1), :]


def unpack(place, own, far, own_other, far_other):
    width = own.shape[1]
    return pl.pallas_call(
        unpack_kernel,
        name="unpack",
        in_specs=[pl.BlockSpec(memory_space=pltpu.SMEM)]
        + [pl.BlockSpec(memory_space=pltpu.VMEM)] * 4,
        out_shape=[like((6, 1, D), F32), like((1, 6 * width), F32), like((1, 8 * width), F32)],
    )(place, own, far, own_other, far_other)


def collect_kernel(
    place_ref, turn_ref, qkv_ref, up_a_ref, up_b_ref, a_ref, b_ref, mine_ref, theirs_ref
):
    core, side, half = place_ref[0], place_ref[1], place_ref[2]
    width = mine_ref.shape[1]
    one = width // 2
    for ref, at_side in ((mine_ref, side), (theirs_ref, 1 - side)):
        at = pl.ds(pl.multiple_of((2 * at_side + core) * width, width), width)
        ref[2:6, :] = turn_ref[:, at]
    mine_ref[10:12, :] = a_ref[...]
    theirs_ref[10:12, :] = b_ref[...]
    for at in range(4):
        ref = (mine_ref, theirs_ref)[at % 2]
        which = half if at < 2 else 1 - half
        cut = pl.ds(pl.multiple_of(which * one, one), one)
        ref[0:1, cut] = qkv_ref[:, 3 * one * at : 3 * one * at + one]
        ref[1:2, cut] = qkv_ref[:, 3 * one * at + 2 * one : 3 * one * (at + 1)]
    order = (0, 1, 2, 3), (0, 2, 1, 3)
    for part in range(2):
        for at, index in enumerate(order[part]):
            ref = (mine_ref, theirs_ref)[index % 2]
            which = half if index < 2 else 1 - half
            up_ref = (up_a_ref, up_b_ref)[part]
            ref[pl.ds(6 + 2 * which + part, 1), :] = up_ref[:, width * at : width * (at + 1)]


def collect(place, *sums):
    width = D // 4
    return pl.pallas_call(
        collect_kernel,
        name="collect",
        in_specs=[pl.BlockSpec(memory_space=pltpu.SMEM)]
        + [pl.BlockSpec(memory_space=pltpu.VMEM)] * 6,
        out_shape=[like((12, width), F32)] * 2,
    )(place, *sums)


def hand_out_kernel(a_ref, b_ref, *outs):
    sums = a_ref[...] + b_ref[...]
    width = a_ref.shape[1]
    for at in range(6):
        outs[at][...] = sums[at, :]
    for at in range(4):
        outs[6][width * at : width * (at + 1)] = sums[6 + at, :]
    for at in range(2):
        outs[7 + at][...] = sums[10 + at, :]


def hand_out(mine, got):
    width = mine.shape[1]
    one = like((width,), F32)
    return pl.pallas_call(
        hand_out_kernel,
        name="hand_out",
        out_shape=[one] * 6 + [like((4 * width,), F32)] + [one] * 2,
    )(mine, got)


def place_mlp_kernel(swapped, place_ref, mine_ref, other_ref, a_ref, b_ref, up_ref, down_ref, out_ref):
    half = place_ref[2]
    width = up_ref.shape[1] // 2
    quarter = width // 2
    heads = out_ref.shape[0] // 2
    for ref, at in ((mine_ref, half), (other_ref, 1 - half)):
        up_ref[:, pl.ds(pl.multiple_of(at * width, width), width)] = ref[:, :width].astype(F32)
        down_ref[pl.ds(pl.multiple_of(at * width + quarter, quarter), quarter), :] = (
            ref[:, width : width + quarter].astype(F32).T
        )
        out_ref[pl.ds(pl.multiple_of(at * heads, heads), heads), :] = (
            ref[:, width + quarter :].astype(F32).T
        )
    for part, at in ((0, half), (1, 1 - half)):
        from_b = 1 - part if swapped else part
        total = a_ref[:, part * quarter : (part + 1) * quarter].astype(F32)
        total = total + b_ref[:, from_b * quarter : (from_b + 1) * quarter].astype(F32)
        down_ref[pl.ds(pl.multiple_of(at * width, width), quarter), :] = total.T


def place_mlp(place, mine, other, a, b, swapped):
    strip, cols = mine.shape
    quarter = a.shape[1] // 2
    heads = cols - 3 * quarter
    return pl.pallas_call(
        functools.partial(place_mlp_kernel, swapped),
        name="place_mlp",
        in_specs=[pl.BlockSpec(memory_space=pltpu.SMEM)]
        + [pl.BlockSpec(memory_space=pltpu.VMEM)] * 4,
        out_shape=[
            like((strip, 4 * quarter), F32),
            like((4 * quarter, strip), F32),
            like((2 * heads, strip), F32),
        ],
    )(place, mine, other, a, b)


def place_qkv_kernel(place_ref, mine_ref, other_ref, *outs):
    half = place_ref[2]
    heads = outs[0].shape[1] // 2
    for ref, at in ((mine_ref, half), (other_ref, 1 - half)):
        here = pl.ds(pl.multiple_of(at * heads, heads), heads)
        for w in range(3):
            outs[w][:, here] = ref[:, heads * w : heads * (w + 1)].astype(F32)


def place_qkv(place, mine, other):
    strip, cols = mine.shape
    return pl.pallas_call(
        place_qkv_kernel,
        name="place_qkv",
        in_specs=[pl.BlockSpec(memory_space=pltpu.SMEM)]
        + [pl.BlockSpec(memory_space=pltpu.VMEM)] * 2,
        out_shape=[like((strip, cols // 3 * 2), F32)] * 3,
    )(place, mine, other)


def local(
    sizes,
    inputs,
    query_weight,
    key_weight,
    value_weight,
    query_bias,
    value_bias,
    out_weight,
    out_bias,
    up_weight,
    up_bias,
    down_weight,
    down_bias,
    first_gain,
    first_shift,
    second_gain,
    second_shift,
    cotangent,
):
    n_dp, n_row, n_xa, n_core = sizes
    my_x = lax.axis_index("xa")
    my_core = lax.axis_index("core")
    my_row = lax.axis_index("row")
    my_half = lax.axis_index("dp") % 2
    place = jnp.stack([my_core, my_x, my_half, my_row]).astype(jnp.int32)
    tokens_here, width = inputs.shape
    images = tokens_here // SEQ
    held = images // n_xa
    rows = held * PAD
    half = up_weight.shape[1] // 2
    quarter = half // 2
    heads_half = width // 2
    three = 3 * heads_half

    def swap(value, axis, size, bit=1):
        return lax.ppermute(value, axis, [(at, at ^ bit) for at in range(size)])

    def shifted(value, shift):
        return lax.ppermute(value, "row", [(at, (at + shift) % n_row) for at in range(n_row)])

    def across(value):
        return swap(value, "xa", n_xa)

    def beside(value):
        return swap(value, "core", n_core)

    def over(value):
        return swap(value, "dp", n_dp)

    def pick(value, at, axis):
        return lax.dynamic_index_in_dim(value, at, axis, keepdims=False)

    def in_order(mine, other, at):
        return jnp.where(at == 0, mine, other), jnp.where(at == 0, other, mine)

    def after(value, *others):
        return lax.optimization_barrier((value, *others))[0]

    def halves(value, axis):
        cut = value.shape[axis] // 2
        both = value.reshape(value.shape[:axis] + (2, cut) + value.shape[axis + 1 :])
        return pick(both, my_half, axis), pick(both, my_half ^ 1, axis)

    count = held * SEQ

    def send_tokens(value):
        return lax.dynamic_slice_in_dim(value, (my_x ^ 1) * count, count, 0)

    def wide_tokens(value, got):
        mine = lax.dynamic_slice_in_dim(value, my_x * count, count, 0)
        pair = jnp.concatenate([mine, got], axis=1).reshape(held, SEQ, 2 * width)
        pair = jnp.pad(pair, ((0, 0), (0, PAD - SEQ), (0, 0))).reshape(rows, 2 * width)
        other = beside(pair)
        left, right = in_order(pair, other, my_core)
        first_left, second_left = in_order(left[:, :width], left[:, width:], my_x)
        first_right, second_right = in_order(right[:, :width], right[:, width:], my_x)
        return jnp.concatenate([first_left, first_right, second_left, second_right], axis=1)

    attn_shard = jnp.concatenate(
        [halves(item, 1)[0] for item in (query_weight, key_weight, value_weight)]
        + [halves(out_weight, 0)[0].T],
        axis=1,
    )
    input_leaves = send_tokens(inputs)
    attn_shard = after(attn_shard, input_leaves)
    input_got = across(input_leaves)
    pieces = [attn_shard] + [shifted(attn_shard, shift) for shift in range(1, n_row)]
    small = pack(
        (
            out_bias,
            down_bias,
            first_gain,
            first_shift,
            second_gain,
            second_shift,
            query_bias,
            value_bias,
        ),
        up_bias,
    )
    fars = [across(piece) for piece in pieces]
    oths = [over(piece) for piece in pieces]
    small_far = across(small)
    vectors, qkv_bias, tile_bias = unpack(
        place, small, after(small_far, pieces[-1]), beside(small), beside(small_far)
    )
    out_bias_all, down_bias_all, gain_one, shift_one, gain_two, shift_two = (
        (vectors, pl.BlockSpec((None, 1, D), lambda i, *_, at=at: (at, 0, 0))) for at in range(6)
    )
    wide_input = wide_tokens(inputs, after(input_got, pieces[-1]))
    far_oths = [
        across(after(oths[at], wide_input, qkv_bias))
        if at % 2
        else over(fars[at])
        for at in range(n_row)
    ]

    def gather(part):
        up_part = halves(up_weight, 1)[0][:, quarter * part : quarter * (part + 1)]
        down_part = halves(down_weight, 0)[0][quarter * part : quarter * (part + 1)].T
        shard = after(jnp.concatenate([up_part, down_part], axis=1), *pieces)
        return lax.all_gather(shard, "row", axis=0, tiled=True)

    own_a, own_b = gather(0), gather(1)
    grad_got = across(after(send_tokens(cotangent), wide_input))

    wide_one, qkv, attn_weights = norm_qkv(
        place, wide_input, gain_one, shift_one, qkv_bias, (*pieces, *fars, *oths, *far_oths)
    )
    oth_a, far_a = over(own_a), across(own_a)
    oth_b, far_b = over(own_b), across(own_b)
    first_heads = attend(qkv)
    attended, probs = attend(qkv, first_heads)
    mixed = mm_nt(attended, attn_weights[:, 4 * three :]).astype(BF16)
    mixed_other = beside(mixed)
    wide_grad = wide_tokens(cotangent, after(grad_got, mixed))
    far_oth_a = over(far_a)
    middle_sum, wide_two = middle(wide_input, mixed, mixed_other, out_bias_all, gain_two, shift_two)
    up_far_oth_b = over(far_b[:, :quarter])
    down_far_oth_b = across(oth_b[:, quarter:])

    def tiles(value, first, end):
        return value[:, quarter * first : quarter * end]

    gate_a, pre_a, up_sums_a, low_a, lift_a = mlp(
        place, wide_two, wide_grad, tile_bias, (own_a, far_a, oth_a, far_oth_a)
    )
    up_over = mm_tn(wide_two, tiles(pre_a, 2, 4)).astype(BF16)
    down_a = mm_tn(wide_grad, gate_a).astype(BF16)
    up_over_got = over(up_over)
    down_piece = lax.psum_scatter(down_a, "row", scatter_dimension=0, tiled=True)
    gate_b, pre_b, up_sums_b, low_mine, low_theirs, lifted_two = mlp(
        place,
        after(wide_two, up_over, down_a),
        wide_grad,
        tile_bias,
        (own_b, oth_b, far_b, up_far_oth_b, down_far_oth_b),
        (low_a, lift_a),
    )

    def wide_add(mine, got):
        return (mine.astype(F32) + got.astype(F32)).astype(BF16)

    def same_half(value):
        if n_dp == 2:
            return value
        groups = [[at + bit for at in range(0, n_dp, 2)] for bit in range(2)]
        return lax.psum(value.astype(F32), "dp", axis_index_groups=groups).astype(BF16)

    def scatter(value):
        return lax.psum_scatter(value, "row", scatter_dimension=0, tiled=True)

    lifted_other = beside(lifted_two)
    low_other = beside(low_theirs)
    up_across = mm_tn(wide_two, tiles(pre_b, 2, 4)).astype(BF16)
    down_over = mm_tn(wide_grad, tiles(gate_b, 2, 4)).astype(BF16)
    up_across_got, down_over_got = across(up_across), over(down_over)

    middle_grad, attn_grad, head_grad, turn_sums, out_mine, out_theirs = turn(
        place,
        middle_sum,
        wide_grad,
        lifted_two,
        after(lifted_other, up_across, down_over),
        low_mine,
        low_other,
        gain_two,
        down_bias_all,
        attn_weights,
    )
    out_all = mm_tn(attn_grad, attended).astype(BF16)
    out_over_got = over(out_all[:, 2 * heads_half :])
    down_x_got = across(after(down_piece, attn_grad)[:, half:])
    up_over_got, up_across_got, down_over_got, _ = lax.optimization_barrier(
        (up_over_got, up_across_got, down_over_got, out_all)
    )
    up_a = wide_add(mm_tn(wide_two, tiles(pre_a, 0, 2)), up_over_got)
    up_b = wide_add(mm_tn(wide_two, tiles(pre_b, 0, 2)), up_across_got)
    down_b = wide_add(mm_tn(wide_grad, tiles(gate_b, 0, 2)), down_over_got)
    up_a_got, up_b_got = across(up_a[:, quarter:]), over(up_b[:, quarter:])
    out_own = wide_add(out_all[:, : 2 * heads_half], after(out_over_got, down_b))
    out_far_got = across(out_own[:, heads_half:])
    down_x = wide_add(down_piece[:, :half], after(down_x_got, down_b))
    down_y_got = over(down_x)
    down_b_got = across(down_b[:, quarter:])
    out_got = across(after(out_theirs, down_b))
    dqkv, qkv_sums = attend_back(qkv, probs, after(head_grad, up_a, up_b, out_own, down_x))

    def to_feature_blocks(mine, got, dtype):
        first, second = in_order(mine.astype(dtype), got.astype(dtype), my_x)
        both = jnp.concatenate([first, second]).reshape(images, PAD, width)
        return both[:, :SEQ].reshape(tokens_here, width)

    cut = 2 * heads_half
    split = 3 * three + cut
    far_oth_qk = mm_tn(wide_one, dqkv[:, 3 * three : split]).astype(BF16)
    far_oth_v = mm_tn(after(wide_one, far_oth_qk), dqkv[:, split:]).astype(BF16)
    qk_got, v_got = over(far_oth_qk), across(far_oth_v)
    up_sum = join(
        up_a, up_a_got, up_b, up_b_got, down_b, down_b_got, out_own, after(out_far_got, far_oth_v)
    )
    up_piece = same_half(scatter(up_sum))
    near_oth = wide_add(
        mm_tn(wide_one, dqkv[:, 2 * three : 3 * three]),
        jnp.pad(after(v_got, up_sum), ((0, 0), (cut, 0))),
    )
    near_oth_got = over(near_oth)
    far_own = wide_add(
        mm_tn(wide_one, dqkv[:, three : 2 * three]),
        jnp.pad(after(qk_got, near_oth), ((0, 0), (0, three - cut))),
    )
    far_own_got = across(far_own)
    lifted_one = mm_nt(
        after(dqkv, far_own), attn_weights[:, : 4 * three]
    ).astype(BF16)
    lifted_one_other = beside(lifted_one)

    near_own = mm_tn(after(wide_one, lifted_one), dqkv[:, :three])
    input_mine, input_theirs, late_mine, late_theirs = last(
        place, wide_input, middle_grad, lifted_one, after(lifted_one_other, near_own), gain_one
    )
    mine_sums, theirs_sums = collect(
        place, turn_sums, qkv_sums, up_sums_a, up_sums_b, late_mine, late_theirs
    )

    near_sum = (near_own + near_oth_got.astype(F32) + after(far_own_got, mine_sums).astype(F32)).astype(
        BF16
    )
    strip = D // n_row

    def rows_of(value, shift):
        return lax.dynamic_slice_in_dim(value, (my_row + shift) % n_row * strip, strip, 0)

    gots = [shifted(rows_of(near_sum, shift), shift) for shift in range(1, n_row)]
    input_got = across(after(input_theirs, near_sum))
    sums = mine_sums + across(after(theirs_sums, near_sum))
    steps = [("row", n_row, 1 << bit) for bit in range(n_row.bit_length() - 1)]
    steps += [("dp", n_dp, 1 << bit) for bit in range(n_dp.bit_length() - 1)]
    for step in steps[:-1]:
        sums = sums + swap(sums, *step)
    sums_got = swap(sums, *steps[-1])
    outputs = to_feature_blocks(out_mine, after(out_got, near_sum), BF16)

    qkv_total = rows_of(near_sum, 0).astype(F32)
    for got in gots:
        qkv_total = qkv_total + got.astype(F32)
    qkv_piece = same_half(qkv_total.astype(BF16))
    qkv_other = over(qkv_piece)
    input_grad = to_feature_blocks(input_mine, input_got, F32)
    up_other = over(up_piece)

    if n_dp > 2:
        down_total = down_x.astype(F32) + jnp.concatenate(
            [down_y_got[:, quarter:], down_y_got[:, :quarter]], axis=1
        ).astype(F32)
        groups = [[at + bit for at in range(0, n_dp, 2)] for bit in range(2)]
        down_total = lax.psum(down_total, "dp", axis_index_groups=groups)
        parts = (down_total, jnp.zeros_like(down_total))
    else:
        parts = (down_x, down_y_got)
    up_grad, down_grad, out_grad = place_mlp(place, up_piece, up_other, *parts, n_dp == 2)
    sums = hand_out(sums, after(sums_got, up_grad, input_grad))
    query_grad, key_grad, value_grad = place_qkv(
        place, qkv_piece, after(qkv_other, up_grad, input_grad)
    )

    return (
        outputs,
        input_grad,
        query_grad,
        key_grad,
        value_grad,
        sums[0],
        sums[1],
        out_grad,
        sums[2],
        up_grad,
        sums[6],
        down_grad,
        sums[3],
        sums[7],
        sums[8],
        sums[4],
        sums[5],
    )


def solution(mesh):
    n_dp, n_row, n_col = (mesh.shape[name] for name in ("dp", "row", "col"))
    sizes = (n_dp, n_row, n_col // 2, 2)
    split = Mesh(mesh.devices.reshape(sizes), ("dp", "row", "xa", "core"))
    col = ("xa", "core")
    tokens, rows, cols, vec = P(("dp", "row"), col), P("row", col), P(col, "row"), P(col)
    in_specs = (
        (tokens, rows, rows, rows, vec, vec, cols, vec, rows, vec, cols)
        + (vec,) * 5
        + (tokens,)
    )
    out_specs = (
        (tokens, tokens, rows, rows, rows, vec, vec, cols, vec, rows, vec, cols) + (vec,) * 5
    )

    def body(*args):
        return local(sizes, *args)

    return jax.shard_map(
        body, mesh=split, in_specs=in_specs, out_specs=out_specs, check_vma=False
    )
```

```python
import functools
import math

import jax
import jax.numpy as jnp
from jax import lax
from jax.experimental import pallas as pl
from jax.experimental.pallas import tpu as pltpu
from jax.sharding import Mesh, PartitionSpec as P


D = 1024
HD = 64
SEQ = 577
PAD = 592
TM = 296
EPS = 1e-06
F32 = jnp.float32
BF16 = jnp.bfloat16
VMEM_LIMIT = 60 * 1024 * 1024
ROOT_HALF = math.sqrt(0.5)
DENSITY = 1.0 / math.sqrt(2.0 * math.pi)


def mm(a, b):
    return lax.dot_general(a, b, (((1,), (0,)), ((), ())), preferred_element_type=F32)


def mm_nt(a, b):
    return lax.dot_general(a, b, (((1,), (1,)), ((), ())), preferred_element_type=F32)


def mm_tn(a, b):
    return lax.dot_general(a, b, (((0,), (0,)), ((), ())), preferred_element_type=F32)


def row_mean(v):
    return jnp.sum(v, axis=1, keepdims=True) * (1.0 / D)


def col_sum(v):
    return jnp.sum(v, axis=0, keepdims=True)


def stats(rows):
    middle = row_mean(rows)
    spread = row_mean(rows * rows) - middle * middle
    return middle, lax.rsqrt(spread + EPS)


def params(n):
    return pltpu.CompilerParams(
        dimension_semantics=("arbitrary",) * n, vmem_limit_bytes=VMEM_LIMIT
    )


def cost(flops, moved, exps=0):
    return pl.CostEstimate(flops=int(flops), bytes_accessed=int(moved), transcendentals=int(exps))


def like(shape, dtype):
    return jax.ShapeDtypeStruct(shape, dtype)


def row_spec(cols):
    return pl.BlockSpec((TM, cols), lambda i, *_: (i, 0))


def fixed(shape):
    return pl.BlockSpec(shape, lambda *_: (0,) * len(shape))


def held_once(shape):
    return pl.BlockSpec(shape, lambda *_: (0,) * len(shape), pipeline_mode=pl.Buffered(1))


def add_up(ref, first, part):
    @pl.when(first)
    def _():
        ref[...] = part

    @pl.when(jnp.logical_not(first))
    def _():
        ref[...] += part


def norm_qkv_kernel(place_ref, x_ref, gain_ref, shift_ref, bias_ref, *refs):
    pieces, (n_ref, o_ref, w_ref) = refs[:-3], refs[-3:]
    n_row = len(pieces) // 4
    strip, wide = pieces[0].shape
    one = wide // 4

    @pl.when(pl.program_id(0) == 0)
    def _():
        for shift in range(n_row):
            start = lax.rem(place_ref[3] - shift + n_row, n_row) * strip
            rows = pl.ds(pl.multiple_of(start, strip), strip)
            for block in range(4):
                piece = pieces[n_row * block + shift]
                w_ref[rows, 3 * one * block : 3 * one * (block + 1)] = piece[:, : 3 * one]
                w_ref[rows, (12 + block) * one : (13 + block) * one] = piece[:, 3 * one :]

    x = x_ref[...].astype(F32)
    middle, scaled = stats(x)
    n = (((x - middle) * scaled) * gain_ref[...] + shift_ref[...]).astype(BF16)
    n_ref[...] = n
    o_ref[...] = (mm(n, w_ref[:, : 12 * one]) + bias_ref[...]).astype(BF16)


def norm_qkv(place, x, gain, shift, bias, pieces):
    rows = x.shape[0]
    wide = pieces[0].shape[1]
    out = 3 * wide
    return pl.pallas_call(
        norm_qkv_kernel,
        name="norm_qkv",
        grid_spec=pltpu.PrefetchScalarGridSpec(
            num_scalar_prefetch=1,
            grid=(rows // TM,),
            in_specs=[row_spec(D), gain[1], shift[1], fixed((1, out))]
            + [held_once(pieces[0].shape)] * len(pieces),
            out_specs=[row_spec(D), row_spec(out), held_once((D, 4 * wide))],
        ),
        out_shape=[like((rows, D), BF16), like((rows, out), BF16), like((D, 4 * wide), BF16)],
        compiler_params=params(1),
        cost_estimate=cost(2 * rows * D * out, 16 * rows * D),
    )(place, x, gain[0], shift[0], bias, *pieces)


def attend_kernel(qkv_ref, o_ref, p_ref):
    live = lax.broadcasted_iota(jnp.int32, (1, PAD), 1) < SEQ
    step = 2 * HD
    items = [(h, slice(r, r + TM)) for h in range(2) for r in range(0, PAD, TM)]

    def score(h, rows):
        q = qkv_ref[rows, HD * h : HD * (h + 1)] * jnp.asarray(0.125, BF16)
        return mm_nt(q, qkv_ref[:, step + HD * h : step + HD * (h + 1)])

    scores = [score(*item) for item in items[:3]]
    for at, (h, rows) in enumerate(items):
        if at + 3 < len(items):
            scores.append(score(*items[at + 3]))
        s = jnp.where(live, scores[at], -1e30)
        e = jnp.exp(s - jnp.max(s, axis=1, keepdims=True))
        p = (e * (1.0 / jnp.sum(e, axis=1, keepdims=True))).astype(BF16)
        p_ref[h, rows, :] = p
        v = qkv_ref[:, 2 * step + HD * h : 2 * step + HD * (h + 1)]
        o_ref[rows, HD * h : HD * (h + 1)] = mm(p, v).astype(BF16)


def attend(qkv, before=()):
    rows, cols = qkv.shape
    pairs = cols // (6 * HD)
    held = rows // PAD
    start = pairs // 2 if before else 0

    def kernel(*refs):
        attend_kernel(refs[0], refs[-2], refs[-1])

    return pl.pallas_call(
        kernel,
        grid=(pairs // 2, held),
        name="attend",
        in_specs=[pl.BlockSpec((PAD, 6 * HD), lambda p, i: (i, p + start))]
        + [pl.BlockSpec(memory_space=pl.ANY)] * len(before),
        out_specs=[
            pl.BlockSpec((PAD, 2 * HD), lambda p, i: (i, p + start)),
            pl.BlockSpec((None, 2, PAD, PAD), lambda p, i: (i, p + start, 0, 0)),
        ],
        out_shape=[like((rows, cols // 3), BF16), like((held, 2 * pairs, PAD, PAD), BF16)],
        input_output_aliases={1: 0, 2: 1} if before else {},
        compiler_params=params(2),
        cost_estimate=cost(8 * rows * PAD * cols, 20 * rows * D, 2 * rows * PAD * pairs),
    )(qkv, *before)


def attend_back_kernel(qkv_ref, p_ref, g_ref, d_ref, sum_ref):
    step = 2 * HD

    def cut(h, w):
        return slice(step * w + HD * h, step * w + HD * (h + 1))

    grads = [g_ref[:, HD * h : HD * (h + 1)] for h in range(2)]
    dprobs = [mm_nt(grads[h], qkv_ref[:, cut(h, 2)]) for h in range(2)]
    dscores = []
    for h in range(2):
        p = p_ref[h].astype(F32)
        z = jnp.sum(p * dprobs[h], axis=1, keepdims=True)
        dscores.append((p * (dprobs[h] - z)).astype(BF16))
        d_ref[:, cut(h, 2)] = mm_tn(p_ref[h], grads[h]).astype(BF16)
    for h in range(2):
        d_ref[:, cut(h, 0)] = (mm(dscores[h], qkv_ref[:, cut(h, 1)]) * 0.125).astype(BF16)
        d_ref[:, cut(h, 1)] = (mm_tn(dscores[h], qkv_ref[:, cut(h, 0)]) * 0.125).astype(BF16)
    add_up(sum_ref, pl.program_id(1) == 0, col_sum(d_ref[...].astype(F32)))


def attend_back(qkv, probs, grads):
    rows, cols = qkv.shape
    pairs = cols // (6 * HD)
    held = rows // PAD
    three = pl.BlockSpec((PAD, 6 * HD), lambda p, i: (i, p))
    return pl.pallas_call(
        attend_back_kernel,
        grid=(pairs, held),
        name="attend_back",
        in_specs=[
            three,
            pl.BlockSpec((None, 2, PAD, PAD), lambda p, i: (i, p, 0, 0)),
            pl.BlockSpec((PAD, 2 * HD), lambda p, i: (i, p)),
        ],
        out_specs=[three, pl.BlockSpec((1, 6 * HD), lambda p, i: (0, p))],
        out_shape=[like((rows, cols), BF16), like((1, cols), F32)],
        compiler_params=params(2),
        cost_estimate=cost(20 * rows * PAD * cols, 50 * rows * D),
    )(qkv, probs, grads)


def middle_kernel(x_ref, a_ref, b_ref, bias_ref, gain_ref, shift_ref, h_ref, n_ref):
    h = x_ref[...].astype(F32) + (a_ref[...].astype(F32) + b_ref[...].astype(F32)) + bias_ref[...]
    h_ref[...] = h
    middle, scaled = stats(h)
    n_ref[...] = (((h - middle) * scaled) * gain_ref[...] + shift_ref[...]).astype(BF16)


def middle(x, a, b, bias, gain, shift):
    rows = x.shape[0]
    return pl.pallas_call(
        middle_kernel,
        grid=(rows // TM,),
        name="middle",
        in_specs=[row_spec(D)] * 3 + [bias[1], gain[1], shift[1]],
        out_specs=[row_spec(D)] * 2,
        out_shape=[like((rows, D), F32), like((rows, D), BF16)],
        compiler_params=params(1),
        cost_estimate=cost(20 * rows * D, 12 * rows * D),
    )(x, a, b, bias[0], gain[0], shift[0])


def mlp_kernel(final, split, place_ref, n_ref, dy_ref, bias_ref, *refs):
    packs = refs[:5]
    before = refs[5:7] if final else ()
    rest = refs[5 + len(before) :]
    g_ref, du_ref, bsum_ref = rest[:3]
    buf, sem = rest[6:8] if final else rest[5:7]
    i = pl.program_id(0)
    tn = g_ref.shape[1] // 4

    @pl.when(i == 0)
    def _():
        copies = []
        for tile in range(4):
            for part in range(2):
                if tile == 3 and split:
                    source = packs[tile + part]
                else:
                    source = packs[tile].at[:, pl.ds(part * tn, tn)]
                copies.append(
                    pltpu.make_async_copy(
                        source,
                        buf.at[part, :, pl.ds(tile * tn, tn)],
                        sem.at[part, tile],
                    )
                )
        for copy in copies:
            copy.start()
        for copy in copies:
            copy.wait()

    up, down = buf[0], buf[1]
    u = mm(n_ref[...], up) + bias_ref[...]
    cdf = 0.5 * (1.0 + lax.erf(u * ROOT_HALF))
    g = (u * cdf).astype(BF16)
    slope = cdf + u * (jnp.exp(-0.5 * u * u) * DENSITY)
    for at, tile in enumerate((0, 2, 1, 3)):
        g_ref[:, at * tn : (at + 1) * tn] = g[:, tile * tn : (tile + 1) * tn]
    du = (mm(dy_ref[...], down) * slope).astype(BF16)
    du_ref[...] = du
    add_up(bsum_ref, i == 0, col_sum(du.astype(F32)))
    low = mm_nt(g, down)
    lift = mm_nt(du, up)
    if not final:
        rest[3][...] = low.astype(BF16)
        rest[4][...] = lift.astype(BF16)
        return
    mine_ref, theirs_ref, lift_ref = rest[3:6]
    held = rest[8]
    lift_ref[...] = (lift + before[1][...].astype(F32)).astype(BF16)
    held[...] = low + before[0][...].astype(F32)
    width = D // 4
    core = place_ref[0]
    for far in range(2):
        here = pl.multiple_of((2 * far + core) * width, width)
        other = pl.multiple_of((2 * far + 1 - core) * width, width)
        mine_ref[:, far * width : (far + 1) * width] = held[:, pl.ds(here, width)]
        theirs_ref[:, far * width : (far + 1) * width] = held[:, pl.ds(other, width)].astype(BF16)


def mlp(place, n2, dy, bias, packs, before=()):
    split = len(packs) == 5
    packs = packs if split else (*packs, packs[-1])
    rows = n2.shape[0]
    hid = 2 * packs[0].shape[1]
    part = 1 if before else 0

    def block(cols):
        return pl.BlockSpec((PAD, cols), lambda i, *_: (i, 0))

    out_specs = [block(hid), block(hid), fixed((1, hid))]
    out_shape = [like((rows, hid), BF16), like((rows, hid), BF16), like((1, hid), F32)]
    scratch = [pltpu.VMEM((2, D, hid), BF16), pltpu.SemaphoreType.DMA((2, 4))]
    if before:
        out_specs += [block(D // 2), block(D // 2), block(D)]
        out_shape += [like((rows, D // 2), F32), like((rows, D // 2), BF16), like((rows, D), BF16)]
        scratch += [pltpu.VMEM((PAD, D), F32)]
    else:
        out_specs += [block(D), block(D)]
        out_shape += [like((rows, D), BF16)] * 2
    return pl.pallas_call(
        functools.partial(mlp_kernel, bool(before), split),
        name="mlp_second" if before else "mlp_first",
        grid_spec=pltpu.PrefetchScalarGridSpec(
            num_scalar_prefetch=1,
            grid=(rows // PAD,),
            in_specs=[block(D), block(D), pl.BlockSpec((1, hid), lambda i, *_: (0, part))]
            + [pl.BlockSpec(memory_space=pl.ANY)] * 5
            + [block(D)] * len(before),
            out_specs=out_specs,
            scratch_shapes=scratch,
        ),
        out_shape=out_shape,
        compiler_params=params(1),
        cost_estimate=cost(8 * rows * D * hid, 20 * rows * D, 2 * rows * hid),
    )(place, n2, dy, bias, *packs, *before)


def turn_kernel(
    place_ref, h_ref, dy_ref, a_ref, b_ref, low_ref, other_ref, gain_ref, bias_ref, w_ref,
    dh_ref, da_ref, do_ref, sums_ref, mine_ref, theirs_ref, held,
):
    h = h_ref[...]
    held[...] = h + bias_ref[...]
    core, side = place_ref[0], place_ref[1]
    width = D // 4
    low = low_ref[...] + other_ref[...].astype(F32)
    for far in range(2):
        at = pl.ds(pl.multiple_of((2 * far + core) * width, width), width)
        out = (held[:, at] + low[:, far * width : (far + 1) * width]).astype(BF16)

        @pl.when(side == far)
        def _(out=out):
            mine_ref[...] = out

        @pl.when(side != far)
        def _(out=out):
            theirs_ref[...] = out

    middle, scaled = stats(h)
    c = (h - middle) * scaled
    dn = a_ref[...].astype(F32) + b_ref[...].astype(F32)
    dy = dy_ref[...].astype(F32)
    e = dn * gain_ref[...]
    dh = dy + scaled * (e - row_mean(e) - c * row_mean(e * c))
    dh_ref[...] = dh
    da = dh.astype(BF16)
    da_ref[...] = da
    do_ref[...] = mm(da, w_ref[...]).astype(BF16)
    part = jnp.concatenate(
        [col_sum(da.astype(F32)), col_sum(dy), col_sum(dn * c), col_sum(dn)], axis=0
    )
    add_up(sums_ref, pl.program_id(0) == 0, part)


def turn(place, h, dy, a, b, low_mine, low_other, gain, bias, weights):
    rows = h.shape[0]
    wide = weights.shape[1] // 4
    width = D // 4
    return pl.pallas_call(
        turn_kernel,
        name="turn",
        grid_spec=pltpu.PrefetchScalarGridSpec(
            num_scalar_prefetch=1,
            grid=(rows // TM,),
            in_specs=[row_spec(D)] * 4
            + [row_spec(D // 2)] * 2
            + [gain[1], bias[1]]
            + [pl.BlockSpec((D, wide), lambda i, *_: (0, 3), pipeline_mode=pl.Buffered(1))],
            out_specs=[
                row_spec(D),
                row_spec(D),
                row_spec(wide),
                fixed((4, D)),
                row_spec(width),
                row_spec(width),
            ],
            scratch_shapes=[pltpu.VMEM((TM, D), F32)],
        ),
        out_shape=[
            like((rows, D), F32),
            like((rows, D), BF16),
            like((rows, wide), BF16),
            like((4, D), F32),
            like((rows, width), BF16),
            like((rows, width), BF16),
        ],
        compiler_params=params(1),
        cost_estimate=cost(2 * rows * D * wide, 20 * rows * D),
    )(place, h, dy, a, b, low_mine, low_other, gain[0], bias[0], weights)


def last_kernel(
    place_ref, x_ref, dh_ref, a_ref, b_ref, gain_ref, mine_ref, theirs_ref, sum_mine, sum_theirs, held, sums
):
    x = x_ref[...].astype(F32)
    middle, scaled = stats(x)
    c = (x - middle) * scaled
    dn = a_ref[...].astype(F32) + b_ref[...].astype(F32)
    e = dn * gain_ref[...]
    held[...] = dh_ref[...] + scaled * (e - row_mean(e) - c * row_mean(e * c))
    width = D // 4
    core, side = place_ref[0], place_ref[1]
    here = pl.ds(pl.multiple_of((2 * side + core) * width, width), width)
    there = pl.ds(pl.multiple_of((2 * (1 - side) + core) * width, width), width)
    mine_ref[...] = held[:, here]
    theirs_ref[...] = held[:, there].astype(BF16)
    i = pl.program_id(0)
    add_up(sums, i == 0, jnp.concatenate([col_sum(dn * c), col_sum(dn)], axis=0))

    @pl.when(i == pl.num_programs(0) - 1)
    def _():
        sum_mine[...] = sums[:, here]
        sum_theirs[...] = sums[:, there]


def last(place, x, dh, a, b, gain):
    rows = x.shape[0]
    width = D // 4
    return pl.pallas_call(
        last_kernel,
        name="last",
        grid_spec=pltpu.PrefetchScalarGridSpec(
            num_scalar_prefetch=1,
            grid=(rows // TM,),
            in_specs=[row_spec(D)] * 4 + [gain[1]],
            out_specs=[row_spec(width), row_spec(width), fixed((2, width)), fixed((2, width))],
            scratch_shapes=[pltpu.VMEM((TM, D), F32), pltpu.VMEM((2, D), F32)],
        ),
        out_shape=[
            like((rows, width), F32),
            like((rows, width), BF16),
            like((2, width), F32),
            like((2, width), F32),
        ],
        compiler_params=params(1),
        cost_estimate=cost(20 * rows * D, 12 * rows * D),
    )(place, x, dh, a, b, gain[0])


def join_kernel(*refs):
    out_ref = refs[-1]
    start = 0
    for mine, got in zip(refs[:-1:2], refs[1:-1:2]):
        width = got.shape[1]
        total = mine[...].astype(F32) + got[...].astype(F32)
        out_ref[:, start : start + width] = total.astype(BF16)
        start += width


def join(*parts):
    rows = parts[0].shape[0]
    tm = rows // 4
    widths = [item.shape[1] for item in parts[1::2]]
    return pl.pallas_call(
        join_kernel,
        grid=(4,),
        name="join",
        in_specs=[
            pl.BlockSpec((tm, width), lambda i: (i, 0)) for width in widths for _ in range(2)
        ],
        out_specs=pl.BlockSpec((tm, sum(widths)), lambda i: (i, 0)),
        out_shape=like((rows, sum(widths)), BF16),
        compiler_params=params(1),
        cost_estimate=cost(rows * sum(widths), 6 * rows * sum(widths)),
    )(*parts)


def pack_kernel(*refs):
    out_ref = refs[-1]
    width = refs[0].shape[0]
    for at, ref in enumerate(refs[:-2]):
        out_ref[at, :] = ref[...]
    for at in range(4):
        out_ref[len(refs) - 2 + at, :] = refs[-2][width * at : width * (at + 1)]


def pack(vectors, long_vector):
    width = vectors[0].shape[0]
    return pl.pallas_call(
        pack_kernel,
        name="pack",
        out_shape=like((len(vectors) + 4, width), F32),
    )(*vectors, long_vector)


def unpack_kernel(place_ref, own, far, own_other, far_other, vec_ref, qkv_ref, tile_ref):
    core, side, half = place_ref[0], place_ref[1], place_ref[2]
    width = own.shape[1]
    one = width // 2

    def put(ref, at_side, at_core):
        at = pl.multiple_of((2 * at_side + at_core) * width, width)
        for k in range(6):
            vec_ref[k, :, pl.ds(at, width)] = ref[k : k + 1, :]

    put(own, side, core)
    put(far, 1 - side, core)
    put(own_other, side, 1 - core)
    put(far_other, 1 - side, 1 - core)
    qkv_ref[...] = jnp.zeros_like(qkv_ref)
    blocks = ((own, half), (far, half), (own, 1 - half), (far, 1 - half))
    for at, (ref, which) in enumerate(blocks):
        cut = pl.ds(pl.multiple_of(which * one, one), one)
        qkv_ref[:, 3 * one * at : 3 * one * at + one] = ref[6:7, cut]
        qkv_ref[:, 3 * one * at + 2 * one : 3 * one * (at + 1)] = ref[7:8, cut]
    order = (0, 1, 2, 3), (0, 2, 1, 3)
    for part in range(2):
        for at, index in enumerate(order[part]):
            ref, which = blocks[index]
            start = width * (4 * part + at)
            tile_ref[:, start : start + width] = ref[pl.ds(8 + 2 * which + part, 1), :]


def unpack(place, own, far, own_other, far_other):
    width = own.shape[1]
    return pl.pallas_call(
        unpack_kernel,
        name="unpack",
        in_specs=[pl.BlockSpec(memory_space=pltpu.SMEM)]
        + [pl.BlockSpec(memory_space=pltpu.VMEM)] * 4,
        out_shape=[like((6, 1, D), F32), like((1, 6 * width), F32), like((1, 8 * width), F32)],
    )(place, own, far, own_other, far_other)


def collect_kernel(
    place_ref, turn_ref, qkv_ref, up_a_ref, up_b_ref, a_ref, b_ref, mine_ref, theirs_ref
):
    core, side, half = place_ref[0], place_ref[1], place_ref[2]
    width = mine_ref.shape[1]
    one = width // 2
    for ref, at_side in ((mine_ref, side), (theirs_ref, 1 - side)):
        at = pl.ds(pl.multiple_of((2 * at_side + core) * width, width), width)
        ref[2:6, :] = turn_ref[:, at]
    mine_ref[10:12, :] = a_ref[...]
    theirs_ref[10:12, :] = b_ref[...]
    for at in range(4):
        ref = (mine_ref, theirs_ref)[at % 2]
        which = half if at < 2 else 1 - half
        cut = pl.ds(pl.multiple_of(which * one, one), one)
        ref[0:1, cut] = qkv_ref[:, 3 * one * at : 3 * one * at + one]
        ref[1:2, cut] = qkv_ref[:, 3 * one * at + 2 * one : 3 * one * (at + 1)]
    order = (0, 1, 2, 3), (0, 2, 1, 3)
    for part in range(2):
        for at, index in enumerate(order[part]):
            ref = (mine_ref, theirs_ref)[index % 2]
            which = half if index < 2 else 1 - half
            up_ref = (up_a_ref, up_b_ref)[part]
            ref[pl.ds(6 + 2 * which + part, 1), :] = up_ref[:, width * at : width * (at + 1)]


def collect(place, *sums):
    width = D // 4
    return pl.pallas_call(
        collect_kernel,
        name="collect",
        in_specs=[pl.BlockSpec(memory_space=pltpu.SMEM)]
        + [pl.BlockSpec(memory_space=pltpu.VMEM)] * 6,
        out_shape=[like((12, width), F32)] * 2,
    )(place, *sums)


def hand_out_kernel(a_ref, b_ref, *outs):
    sums = a_ref[...] + b_ref[...]
    width = a_ref.shape[1]
    for at in range(6):
        outs[at][...] = sums[at, :]
    for at in range(4):
        outs[6][width * at : width * (at + 1)] = sums[6 + at, :]
    for at in range(2):
        outs[7 + at][...] = sums[10 + at, :]


def hand_out(mine, got):
    width = mine.shape[1]
    one = like((width,), F32)
    return pl.pallas_call(
        hand_out_kernel,
        name="hand_out",
        out_shape=[one] * 6 + [like((4 * width,), F32)] + [one] * 2,
    )(mine, got)


def place_mlp_kernel(swapped, place_ref, mine_ref, other_ref, a_ref, b_ref, up_ref, down_ref, out_ref):
    half = place_ref[2]
    width = up_ref.shape[1] // 2
    quarter = width // 2
    heads = out_ref.shape[0] // 2
    for ref, at in ((mine_ref, half), (other_ref, 1 - half)):
        up_ref[:, pl.ds(pl.multiple_of(at * width, width), width)] = ref[:, :width].astype(F32)
        down_ref[pl.ds(pl.multiple_of(at * width + quarter, quarter), quarter), :] = (
            ref[:, width : width + quarter].astype(F32).T
        )
        out_ref[pl.ds(pl.multiple_of(at * heads, heads), heads), :] = (
            ref[:, width + quarter :].astype(F32).T
        )
    for part, at in ((0, half), (1, 1 - half)):
        from_b = 1 - part if swapped else part
        total = a_ref[:, part * quarter : (part + 1) * quarter].astype(F32)
        total = total + b_ref[:, from_b * quarter : (from_b + 1) * quarter].astype(F32)
        down_ref[pl.ds(pl.multiple_of(at * width, width), quarter), :] = total.T


def place_mlp(place, mine, other, a, b, swapped):
    strip, cols = mine.shape
    quarter = a.shape[1] // 2
    heads = cols - 3 * quarter
    return pl.pallas_call(
        functools.partial(place_mlp_kernel, swapped),
        name="place_mlp",
        in_specs=[pl.BlockSpec(memory_space=pltpu.SMEM)]
        + [pl.BlockSpec(memory_space=pltpu.VMEM)] * 4,
        out_shape=[
            like((strip, 4 * quarter), F32),
            like((4 * quarter, strip), F32),
            like((2 * heads, strip), F32),
        ],
    )(place, mine, other, a, b)


def place_qkv_kernel(place_ref, mine_ref, other_ref, *outs):
    half = place_ref[2]
    heads = outs[0].shape[1] // 2
    for ref, at in ((mine_ref, half), (other_ref, 1 - half)):
        here = pl.ds(pl.multiple_of(at * heads, heads), heads)
        for w in range(3):
            outs[w][:, here] = ref[:, heads * w : heads * (w + 1)].astype(F32)


def place_qkv(place, mine, other):
    strip, cols = mine.shape
    return pl.pallas_call(
        place_qkv_kernel,
        name="place_qkv",
        in_specs=[pl.BlockSpec(memory_space=pltpu.SMEM)]
        + [pl.BlockSpec(memory_space=pltpu.VMEM)] * 2,
        out_shape=[like((strip, cols // 3 * 2), F32)] * 3,
    )(place, mine, other)


def local(
    sizes,
    inputs,
    query_weight,
    key_weight,
    value_weight,
    query_bias,
    value_bias,
    out_weight,
    out_bias,
    up_weight,
    up_bias,
    down_weight,
    down_bias,
    first_gain,
    first_shift,
    second_gain,
    second_shift,
    cotangent,
):
    n_dp, n_row, n_xa, n_core = sizes
    my_x = lax.axis_index("xa")
    my_core = lax.axis_index("core")
    my_row = lax.axis_index("row")
    my_half = lax.axis_index("dp") % 2
    place = jnp.stack([my_core, my_x, my_half, my_row]).astype(jnp.int32)
    tokens_here, width = inputs.shape
    images = tokens_here // SEQ
    held = images // n_xa
    rows = held * PAD
    half = up_weight.shape[1] // 2
    quarter = half // 2
    heads_half = width // 2
    three = 3 * heads_half

    def swap(value, axis, size, bit=1):
        return lax.ppermute(value, axis, [(at, at ^ bit) for at in range(size)])

    def shifted(value, shift):
        return lax.ppermute(value, "row", [(at, (at + shift) % n_row) for at in range(n_row)])

    def across(value):
        return swap(value, "xa", n_xa)

    def beside(value):
        return swap(value, "core", n_core)

    def over(value):
        return swap(value, "dp", n_dp)

    def pick(value, at, axis):
        return lax.dynamic_index_in_dim(value, at, axis, keepdims=False)

    def in_order(mine, other, at):
        return jnp.where(at == 0, mine, other), jnp.where(at == 0, other, mine)

    def after(value, *others):
        return lax.optimization_barrier((value, *others))[0]

    def halves(value, axis):
        cut = value.shape[axis] // 2
        both = value.reshape(value.shape[:axis] + (2, cut) + value.shape[axis + 1 :])
        return pick(both, my_half, axis), pick(both, my_half ^ 1, axis)

    count = held * SEQ

    def send_tokens(value):
        return lax.dynamic_slice_in_dim(value, (my_x ^ 1) * count, count, 0)

    def wide_tokens(value, got):
        mine = lax.dynamic_slice_in_dim(value, my_x * count, count, 0)
        pair = jnp.concatenate([mine, got], axis=1).reshape(held, SEQ, 2 * width)
        pair = jnp.pad(pair, ((0, 0), (0, PAD - SEQ), (0, 0))).reshape(rows, 2 * width)
        other = beside(pair)
        left, right = in_order(pair, other, my_core)
        first_left, second_left = in_order(left[:, :width], left[:, width:], my_x)
        first_right, second_right = in_order(right[:, :width], right[:, width:], my_x)
        return jnp.concatenate([first_left, first_right, second_left, second_right], axis=1)

    attn_shard = jnp.concatenate(
        [halves(item, 1)[0] for item in (query_weight, key_weight, value_weight)]
        + [halves(out_weight, 0)[0].T],
        axis=1,
    )
    input_leaves = send_tokens(inputs)
    attn_shard = after(attn_shard, input_leaves)
    input_got = across(input_leaves)
    pieces = [attn_shard] + [shifted(attn_shard, shift) for shift in range(1, n_row)]
    small = pack(
        (
            out_bias,
            down_bias,
            first_gain,
            first_shift,
            second_gain,
            second_shift,
            query_bias,
            value_bias,
        ),
        up_bias,
    )
    fars = [across(piece) for piece in pieces]
    oths = [over(piece) for piece in pieces]
    small_far = across(small)
    vectors, qkv_bias, tile_bias = unpack(
        place, small, after(small_far, pieces[-1]), beside(small), beside(small_far)
    )
    out_bias_all, down_bias_all, gain_one, shift_one, gain_two, shift_two = (
        (vectors, pl.BlockSpec((None, 1, D), lambda i, *_, at=at: (at, 0, 0))) for at in range(6)
    )
    wide_input = wide_tokens(inputs, after(input_got, pieces[-1]))
    far_oths = [
        across(after(oths[at], wide_input, qkv_bias))
        if at % 2
        else over(fars[at])
        for at in range(n_row)
    ]

    def gather(part):
        up_part = halves(up_weight, 1)[0][:, quarter * part : quarter * (part + 1)]
        down_part = halves(down_weight, 0)[0][quarter * part : quarter * (part + 1)].T
        shard = after(jnp.concatenate([up_part, down_part], axis=1), *pieces)
        return lax.all_gather(shard, "row", axis=0, tiled=True)

    own_a, own_b = gather(0), gather(1)
    grad_got = across(after(send_tokens(cotangent), wide_input))

    wide_one, qkv, attn_weights = norm_qkv(
        place, wide_input, gain_one, shift_one, qkv_bias, (*pieces, *fars, *oths, *far_oths)
    )
    oth_a, far_a = over(own_a), across(own_a)
    oth_b, far_b = over(own_b), across(own_b)
    first_heads = attend(qkv)
    attended, probs = attend(qkv, first_heads)
    mixed = mm_nt(attended, attn_weights[:, 4 * three :]).astype(BF16)
    mixed_other = beside(mixed)
    wide_grad = wide_tokens(cotangent, after(grad_got, mixed))
    far_oth_a = over(far_a)
    middle_sum, wide_two = middle(wide_input, mixed, mixed_other, out_bias_all, gain_two, shift_two)
    up_far_oth_b = over(far_b[:, :quarter])
    down_far_oth_b = across(oth_b[:, quarter:])

    def tiles(value, first, end):
        return value[:, quarter * first : quarter * end]

    gate_a, pre_a, up_sums_a, low_a, lift_a = mlp(
        place, wide_two, wide_grad, tile_bias, (own_a, far_a, oth_a, far_oth_a)
    )
    up_over = mm_tn(wide_two, tiles(pre_a, 2, 4)).astype(BF16)
    down_a = mm_tn(wide_grad, gate_a).astype(BF16)
    up_over_got = over(up_over)
    down_piece = lax.psum_scatter(down_a, "row", scatter_dimension=0, tiled=True)
    gate_b, pre_b, up_sums_b, low_mine, low_theirs, lifted_two = mlp(
        place,
        after(wide_two, up_over, down_a),
        wide_grad,
        tile_bias,
        (own_b, oth_b, far_b, up_far_oth_b, down_far_oth_b),
        (low_a, lift_a),
    )

    def wide_add(mine, got):
        return (mine.astype(F32) + got.astype(F32)).astype(BF16)

    def same_half(value):
        if n_dp == 2:
            return value
        groups = [[at + bit for at in range(0, n_dp, 2)] for bit in range(2)]
        return lax.psum(value.astype(F32), "dp", axis_index_groups=groups).astype(BF16)

    def scatter(value):
        return lax.psum_scatter(value, "row", scatter_dimension=0, tiled=True)

    lifted_other = beside(lifted_two)
    low_other = beside(low_theirs)
    up_across = mm_tn(wide_two, tiles(pre_b, 2, 4)).astype(BF16)
    down_over = mm_tn(wide_grad, tiles(gate_b, 2, 4)).astype(BF16)
    up_across_got, down_over_got = across(up_across), over(down_over)

    middle_grad, attn_grad, head_grad, turn_sums, out_mine, out_theirs = turn(
        place,
        middle_sum,
        wide_grad,
        lifted_two,
        after(lifted_other, up_across, down_over),
        low_mine,
        low_other,
        gain_two,
        down_bias_all,
        attn_weights,
    )
    out_all = mm_tn(attn_grad, attended).astype(BF16)
    out_over_got = over(out_all[:, 2 * heads_half :])
    down_x_got = across(after(down_piece, attn_grad)[:, half:])
    up_over_got, up_across_got, down_over_got, _ = lax.optimization_barrier(
        (up_over_got, up_across_got, down_over_got, out_all)
    )
    up_a = wide_add(mm_tn(wide_two, tiles(pre_a, 0, 2)), up_over_got)
    up_b = wide_add(mm_tn(wide_two, tiles(pre_b, 0, 2)), up_across_got)
    down_b = wide_add(mm_tn(wide_grad, tiles(gate_b, 0, 2)), down_over_got)
    up_a_got, up_b_got = across(up_a[:, quarter:]), over(up_b[:, quarter:])
    out_own = wide_add(out_all[:, : 2 * heads_half], after(out_over_got, down_b))
    out_far_got = across(out_own[:, heads_half:])
    down_x = wide_add(down_piece[:, :half], after(down_x_got, down_b))
    down_y_got = over(down_x)
    down_b_got = across(down_b[:, quarter:])
    out_got = across(after(out_theirs, down_b))
    dqkv, qkv_sums = attend_back(qkv, probs, after(head_grad, up_a, up_b, out_own, down_x))

    def to_feature_blocks(mine, got, dtype):
        first, second = in_order(mine.astype(dtype), got.astype(dtype), my_x)
        both = jnp.concatenate([first, second]).reshape(images, PAD, width)
        return both[:, :SEQ].reshape(tokens_here, width)

    cut = 2 * heads_half
    split = 3 * three + cut
    far_oth_qk = mm_tn(wide_one, dqkv[:, 3 * three : split]).astype(BF16)
    far_oth_v = mm_tn(after(wide_one, far_oth_qk), dqkv[:, split:]).astype(BF16)
    qk_got, v_got = over(far_oth_qk), across(far_oth_v)
    up_sum = join(
        up_a, up_a_got, up_b, up_b_got, down_b, down_b_got, out_own, after(out_far_got, far_oth_v)
    )
    up_piece = same_half(scatter(up_sum))
    lifted_one = mm_nt(
        after(dqkv, up_sum), attn_weights[:, : 4 * three]
    ).astype(BF16)
    lifted_one_other = beside(lifted_one)

    near_oth = wide_add(
        mm_tn(wide_one, dqkv[:, 2 * three : 3 * three]),
        jnp.pad(after(v_got, lifted_one), ((0, 0), (cut, 0))),
    )
    near_oth_got = over(near_oth)
    far_own = wide_add(
        mm_tn(wide_one, dqkv[:, three : 2 * three]),
        jnp.pad(after(qk_got, near_oth), ((0, 0), (0, three - cut))),
    )
    far_own_got = across(far_own)
    near_own = mm_tn(after(wide_one, far_own), dqkv[:, :three])
    input_mine, input_theirs, late_mine, late_theirs = last(
        place, wide_input, middle_grad, lifted_one, after(lifted_one_other, near_own), gain_one
    )
    mine_sums, theirs_sums = collect(
        place, turn_sums, qkv_sums, up_sums_a, up_sums_b, late_mine, late_theirs
    )

    near_sum = (near_own + near_oth_got.astype(F32) + after(far_own_got, mine_sums).astype(F32)).astype(
        BF16
    )
    strip = D // n_row

    def rows_of(value, shift):
        return lax.dynamic_slice_in_dim(value, (my_row + shift) % n_row * strip, strip, 0)

    gots = [shifted(rows_of(near_sum, shift), shift) for shift in range(1, n_row)]
    input_got = across(after(input_theirs, near_sum))
    sums = mine_sums + across(after(theirs_sums, near_sum))
    steps = [("row", n_row, 1 << bit) for bit in range(n_row.bit_length() - 1)]
    steps += [("dp", n_dp, 1 << bit) for bit in range(n_dp.bit_length() - 1)]
    for step in steps[:-1]:
        sums = sums + swap(sums, *step)
    sums_got = swap(sums, *steps[-1])
    outputs = to_feature_blocks(out_mine, after(out_got, near_sum), BF16)

    qkv_total = rows_of(near_sum, 0).astype(F32)
    for got in gots:
        qkv_total = qkv_total + got.astype(F32)
    qkv_piece = same_half(qkv_total.astype(BF16))
    qkv_other = over(qkv_piece)
    input_grad = to_feature_blocks(input_mine, input_got, F32)
    up_other = over(up_piece)

    if n_dp > 2:
        down_total = down_x.astype(F32) + jnp.concatenate(
            [down_y_got[:, quarter:], down_y_got[:, :quarter]], axis=1
        ).astype(F32)
        groups = [[at + bit for at in range(0, n_dp, 2)] for bit in range(2)]
        down_total = lax.psum(down_total, "dp", axis_index_groups=groups)
        parts = (down_total, jnp.zeros_like(down_total))
    else:
        parts = (down_x, down_y_got)
    up_grad, down_grad, out_grad = place_mlp(place, up_piece, up_other, *parts, n_dp == 2)
    sums = hand_out(sums, after(sums_got, up_grad, input_grad))
    query_grad, key_grad, value_grad = place_qkv(
        place, qkv_piece, after(qkv_other, up_grad, input_grad)
    )

    return (
        outputs,
        input_grad,
        query_grad,
        key_grad,
        value_grad,
        sums[0],
        sums[1],
        out_grad,
        sums[2],
        up_grad,
        sums[6],
        down_grad,
        sums[3],
        sums[7],
        sums[8],
        sums[4],
        sums[5],
    )


def solution(mesh):
    n_dp, n_row, n_col = (mesh.shape[name] for name in ("dp", "row", "col"))
    sizes = (n_dp, n_row, n_col // 2, 2)
    split = Mesh(mesh.devices.reshape(sizes), ("dp", "row", "xa", "core"))
    col = ("xa", "core")
    tokens, rows, cols, vec = P(("dp", "row"), col), P("row", col), P(col, "row"), P(col)
    in_specs = (
        (tokens, rows, rows, rows, vec, vec, cols, vec, rows, vec, cols)
        + (vec,) * 5
        + (tokens,)
    )
    out_specs = (
        (tokens, tokens, rows, rows, rows, vec, vec, cols, vec, rows, vec, cols) + (vec,) * 5
    )

    def body(*args):
        return local(sizes, *args)

    return jax.shard_map(
        body, mesh=split, in_specs=in_specs, out_specs=out_specs, check_vma=False
    )
```

```python
import functools
import math

import jax
import jax.numpy as jnp
from jax import lax
from jax.experimental import pallas as pl
from jax.experimental.pallas import tpu as pltpu
from jax.sharding import Mesh, PartitionSpec as P


D = 1024
HD = 64
SEQ = 577
PAD = 592
TM = 296
EPS = 1e-06
F32 = jnp.float32
BF16 = jnp.bfloat16
VMEM_LIMIT = 60 * 1024 * 1024
ROOT_HALF = math.sqrt(0.5)
DENSITY = 1.0 / math.sqrt(2.0 * math.pi)


def mm(a, b):
    return lax.dot_general(a, b, (((1,), (0,)), ((), ())), preferred_element_type=F32)


def mm_nt(a, b):
    return lax.dot_general(a, b, (((1,), (1,)), ((), ())), preferred_element_type=F32)


def mm_tn(a, b):
    return lax.dot_general(a, b, (((0,), (0,)), ((), ())), preferred_element_type=F32)


def row_mean(v):
    return jnp.sum(v, axis=1, keepdims=True) * (1.0 / D)


def col_sum(v):
    return jnp.sum(v, axis=0, keepdims=True)


def stats(rows):
    middle = row_mean(rows)
    spread = row_mean(rows * rows) - middle * middle
    return middle, lax.rsqrt(spread + EPS)


def params(n):
    return pltpu.CompilerParams(
        dimension_semantics=("arbitrary",) * n, vmem_limit_bytes=VMEM_LIMIT
    )


def cost(flops, moved, exps=0):
    return pl.CostEstimate(flops=int(flops), bytes_accessed=int(moved), transcendentals=int(exps))


def like(shape, dtype):
    return jax.ShapeDtypeStruct(shape, dtype)


def row_spec(cols):
    return pl.BlockSpec((TM, cols), lambda i, *_: (i, 0))


def fixed(shape):
    return pl.BlockSpec(shape, lambda *_: (0,) * len(shape))


def held_once(shape):
    return pl.BlockSpec(shape, lambda *_: (0,) * len(shape), pipeline_mode=pl.Buffered(1))


def add_up(ref, first, part):
    @pl.when(first)
    def _():
        ref[...] = part

    @pl.when(jnp.logical_not(first))
    def _():
        ref[...] += part


def norm_qkv_kernel(place_ref, x_ref, gain_ref, shift_ref, bias_ref, *refs):
    pieces, (n_ref, o_ref, w_ref) = refs[:-3], refs[-3:]
    n_row = len(pieces) // 4
    strip, wide = pieces[0].shape
    one = wide // 4

    @pl.when(pl.program_id(0) == 0)
    def _():
        for shift in range(n_row):
            start = lax.rem(place_ref[3] - shift + n_row, n_row) * strip
            rows = pl.ds(pl.multiple_of(start, strip), strip)
            for block in range(4):
                piece = pieces[n_row * block + shift]
                w_ref[rows, 3 * one * block : 3 * one * (block + 1)] = piece[:, : 3 * one]
                w_ref[rows, (12 + block) * one : (13 + block) * one] = piece[:, 3 * one :]

    x = x_ref[...].astype(F32)
    middle, scaled = stats(x)
    n = (((x - middle) * scaled) * gain_ref[...] + shift_ref[...]).astype(BF16)
    n_ref[...] = n
    o_ref[...] = (mm(n, w_ref[:, : 12 * one]) + bias_ref[...]).astype(BF16)


def norm_qkv(place, x, gain, shift, bias, pieces):
    rows = x.shape[0]
    wide = pieces[0].shape[1]
    out = 3 * wide
    return pl.pallas_call(
        norm_qkv_kernel,
        name="norm_qkv",
        grid_spec=pltpu.PrefetchScalarGridSpec(
            num_scalar_prefetch=1,
            grid=(rows // TM,),
            in_specs=[row_spec(D), gain[1], shift[1], fixed((1, out))]
            + [held_once(pieces[0].shape)] * len(pieces),
            out_specs=[row_spec(D), row_spec(out), held_once((D, 4 * wide))],
        ),
        out_shape=[like((rows, D), BF16), like((rows, out), BF16), like((D, 4 * wide), BF16)],
        compiler_params=params(1),
        cost_estimate=cost(2 * rows * D * out, 16 * rows * D),
    )(place, x, gain[0], shift[0], bias, *pieces)


def attend_kernel(qkv_ref, o_ref, p_ref):
    live = lax.broadcasted_iota(jnp.int32, (1, PAD), 1) < SEQ
    step = 2 * HD
    items = [(h, slice(r, r + TM)) for h in range(2) for r in range(0, PAD, TM)]

    def score(h, rows):
        q = qkv_ref[rows, HD * h : HD * (h + 1)] * jnp.asarray(0.125, BF16)
        return mm_nt(q, qkv_ref[:, step + HD * h : step + HD * (h + 1)])

    scores = [score(*item) for item in items[:3]]
    for at, (h, rows) in enumerate(items):
        if at + 3 < len(items):
            scores.append(score(*items[at + 3]))
        s = jnp.where(live, scores[at], -1e30)
        e = jnp.exp(s - jnp.max(s, axis=1, keepdims=True))
        p = (e * (1.0 / jnp.sum(e, axis=1, keepdims=True))).astype(BF16)
        p_ref[h, rows, :] = p
        v = qkv_ref[:, 2 * step + HD * h : 2 * step + HD * (h + 1)]
        o_ref[rows, HD * h : HD * (h + 1)] = mm(p, v).astype(BF16)


def attend(qkv, before=()):
    rows, cols = qkv.shape
    pairs = cols // (6 * HD)
    held = rows // PAD
    start = pairs // 2 if before else 0

    def kernel(*refs):
        attend_kernel(refs[0], refs[-2], refs[-1])

    return pl.pallas_call(
        kernel,
        grid=(pairs // 2, held),
        name="attend",
        in_specs=[pl.BlockSpec((PAD, 6 * HD), lambda p, i: (i, p + start))]
        + [pl.BlockSpec(memory_space=pl.ANY)] * len(before),
        out_specs=[
            pl.BlockSpec((PAD, 2 * HD), lambda p, i: (i, p + start)),
            pl.BlockSpec((None, 2, PAD, PAD), lambda p, i: (i, p + start, 0, 0)),
        ],
        out_shape=[like((rows, cols // 3), BF16), like((held, 2 * pairs, PAD, PAD), BF16)],
        input_output_aliases={1: 0, 2: 1} if before else {},
        compiler_params=params(2),
        cost_estimate=cost(8 * rows * PAD * cols, 20 * rows * D, 2 * rows * PAD * pairs),
    )(qkv, *before)


def attend_back_kernel(qkv_ref, p_ref, g_ref, d_ref, sum_ref):
    step = 2 * HD

    def cut(h, w):
        return slice(step * w + HD * h, step * w + HD * (h + 1))

    grads = [g_ref[:, HD * h : HD * (h + 1)] for h in range(2)]
    dprobs = [mm_nt(grads[h], qkv_ref[:, cut(h, 2)]) for h in range(2)]
    dscores = []
    for h in range(2):
        p = p_ref[h].astype(F32)
        z = jnp.sum(p * dprobs[h], axis=1, keepdims=True)
        dscores.append((p * (dprobs[h] - z)).astype(BF16))
        d_ref[:, cut(h, 2)] = mm_tn(p_ref[h], grads[h]).astype(BF16)
    for h in range(2):
        d_ref[:, cut(h, 0)] = (mm(dscores[h], qkv_ref[:, cut(h, 1)]) * 0.125).astype(BF16)
        d_ref[:, cut(h, 1)] = (mm_tn(dscores[h], qkv_ref[:, cut(h, 0)]) * 0.125).astype(BF16)
    add_up(sum_ref, pl.program_id(1) == 0, col_sum(d_ref[...].astype(F32)))


def attend_back(qkv, probs, grads):
    rows, cols = qkv.shape
    pairs = cols // (6 * HD)
    held = rows // PAD
    three = pl.BlockSpec((PAD, 6 * HD), lambda p, i: (i, p))
    return pl.pallas_call(
        attend_back_kernel,
        grid=(pairs, held),
        name="attend_back",
        in_specs=[
            three,
            pl.BlockSpec((None, 2, PAD, PAD), lambda p, i: (i, p, 0, 0)),
            pl.BlockSpec((PAD, 2 * HD), lambda p, i: (i, p)),
        ],
        out_specs=[three, pl.BlockSpec((1, 6 * HD), lambda p, i: (0, p))],
        out_shape=[like((rows, cols), BF16), like((1, cols), F32)],
        compiler_params=params(2),
        cost_estimate=cost(20 * rows * PAD * cols, 50 * rows * D),
    )(qkv, probs, grads)


def middle_kernel(x_ref, a_ref, b_ref, bias_ref, gain_ref, shift_ref, h_ref, n_ref):
    h = x_ref[...].astype(F32) + (a_ref[...].astype(F32) + b_ref[...].astype(F32)) + bias_ref[...]
    h_ref[...] = h
    middle, scaled = stats(h)
    n_ref[...] = (((h - middle) * scaled) * gain_ref[...] + shift_ref[...]).astype(BF16)


def middle(x, a, b, bias, gain, shift):
    rows = x.shape[0]
    return pl.pallas_call(
        middle_kernel,
        grid=(rows // TM,),
        name="middle",
        in_specs=[row_spec(D)] * 3 + [bias[1], gain[1], shift[1]],
        out_specs=[row_spec(D)] * 2,
        out_shape=[like((rows, D), F32), like((rows, D), BF16)],
        compiler_params=params(1),
        cost_estimate=cost(20 * rows * D, 12 * rows * D),
    )(x, a, b, bias[0], gain[0], shift[0])


def mlp_kernel(final, split, place_ref, n_ref, dy_ref, bias_ref, *refs):
    packs = refs[:5]
    before = refs[5:7] if final else ()
    rest = refs[5 + len(before) :]
    g_ref, du_ref, bsum_ref = rest[:3]
    buf, sem = rest[6:8] if final else rest[5:7]
    i = pl.program_id(0)
    tn = g_ref.shape[1] // 4

    @pl.when(i == 0)
    def _():
        copies = []
        for tile in range(4):
            for part in range(2):
                if tile == 3 and split:
                    source = packs[tile + part]
                else:
                    source = packs[tile].at[:, pl.ds(part * tn, tn)]
                copies.append(
                    pltpu.make_async_copy(
                        source,
                        buf.at[part, :, pl.ds(tile * tn, tn)],
                        sem.at[part, tile],
                    )
                )
        for copy in copies:
            copy.start()
        for copy in copies:
            copy.wait()

    up, down = buf[0], buf[1]
    u = mm(n_ref[...], up) + bias_ref[...]
    cdf = 0.5 * (1.0 + lax.erf(u * ROOT_HALF))
    g = (u * cdf).astype(BF16)
    slope = cdf + u * (jnp.exp(-0.5 * u * u) * DENSITY)
    for at, tile in enumerate((0, 2, 1, 3)):
        g_ref[:, at * tn : (at + 1) * tn] = g[:, tile * tn : (tile + 1) * tn]
    du = (mm(dy_ref[...], down) * slope).astype(BF16)
    du_ref[...] = du
    add_up(bsum_ref, i == 0, col_sum(du.astype(F32)))
    low = mm_nt(g, down)
    lift = mm_nt(du, up)
    if not final:
        rest[3][...] = low.astype(BF16)
        rest[4][...] = lift.astype(BF16)
        return
    mine_ref, theirs_ref, lift_ref = rest[3:6]
    held = rest[8]
    lift_ref[...] = (lift + before[1][...].astype(F32)).astype(BF16)
    held[...] = low + before[0][...].astype(F32)
    width = D // 4
    core = place_ref[0]
    for far in range(2):
        here = pl.multiple_of((2 * far + core) * width, width)
        other = pl.multiple_of((2 * far + 1 - core) * width, width)
        mine_ref[:, far * width : (far + 1) * width] = held[:, pl.ds(here, width)]
        theirs_ref[:, far * width : (far + 1) * width] = held[:, pl.ds(other, width)].astype(BF16)


def mlp(place, n2, dy, bias, packs, before=()):
    split = len(packs) == 5
    packs = packs if split else (*packs, packs[-1])
    rows = n2.shape[0]
    hid = 2 * packs[0].shape[1]
    part = 1 if before else 0

    def block(cols):
        return pl.BlockSpec((PAD, cols), lambda i, *_: (i, 0))

    out_specs = [block(hid), block(hid), fixed((1, hid))]
    out_shape = [like((rows, hid), BF16), like((rows, hid), BF16), like((1, hid), F32)]
    scratch = [pltpu.VMEM((2, D, hid), BF16), pltpu.SemaphoreType.DMA((2, 4))]
    if before:
        out_specs += [block(D // 2), block(D // 2), block(D)]
        out_shape += [like((rows, D // 2), F32), like((rows, D // 2), BF16), like((rows, D), BF16)]
        scratch += [pltpu.VMEM((PAD, D), F32)]
    else:
        out_specs += [block(D), block(D)]
        out_shape += [like((rows, D), BF16)] * 2
    return pl.pallas_call(
        functools.partial(mlp_kernel, bool(before), split),
        name="mlp_second" if before else "mlp_first",
        grid_spec=pltpu.PrefetchScalarGridSpec(
            num_scalar_prefetch=1,
            grid=(rows // PAD,),
            in_specs=[block(D), block(D), pl.BlockSpec((1, hid), lambda i, *_: (0, part))]
            + [pl.BlockSpec(memory_space=pl.ANY)] * 5
            + [block(D)] * len(before),
            out_specs=out_specs,
            scratch_shapes=scratch,
        ),
        out_shape=out_shape,
        compiler_params=params(1),
        cost_estimate=cost(8 * rows * D * hid, 20 * rows * D, 2 * rows * hid),
    )(place, n2, dy, bias, *packs, *before)


def turn_kernel(
    place_ref, h_ref, dy_ref, a_ref, b_ref, low_ref, other_ref, gain_ref, bias_ref, w_ref,
    dh_ref, da_ref, do_ref, sums_ref, mine_ref, theirs_ref,
):
    h = h_ref[...]
    core, side = place_ref[0], place_ref[1]
    width = D // 4
    low = low_ref[...] + other_ref[...].astype(F32)
    for far in range(2):
        at = pl.ds(pl.multiple_of((2 * far + core) * width, width), width)
        out = h_ref[:, at] + bias_ref[:, at] + low[:, far * width : (far + 1) * width]
        out = out.astype(BF16)

        @pl.when(side == far)
        def _(out=out):
            mine_ref[...] = out

        @pl.when(side != far)
        def _(out=out):
            theirs_ref[...] = out

    middle, scaled = stats(h)
    c = (h - middle) * scaled
    dn = a_ref[...].astype(F32) + b_ref[...].astype(F32)
    dy = dy_ref[...].astype(F32)
    e = dn * gain_ref[...]
    dh = dy + scaled * (e - row_mean(e) - c * row_mean(e * c))
    dh_ref[...] = dh
    da = dh.astype(BF16)
    da_ref[...] = da
    do_ref[...] = mm(da, w_ref[...]).astype(BF16)
    part = jnp.concatenate(
        [col_sum(da.astype(F32)), col_sum(dy), col_sum(dn * c), col_sum(dn)], axis=0
    )
    add_up(sums_ref, pl.program_id(0) == 0, part)


def turn(place, h, dy, a, b, low_mine, low_other, gain, bias, weights):
    rows = h.shape[0]
    wide = weights.shape[1] // 4
    width = D // 4
    return pl.pallas_call(
        turn_kernel,
        name="turn",
        grid_spec=pltpu.PrefetchScalarGridSpec(
            num_scalar_prefetch=1,
            grid=(rows // TM,),
            in_specs=[row_spec(D)] * 4
            + [row_spec(D // 2)] * 2
            + [gain[1], bias[1]]
            + [pl.BlockSpec((D, wide), lambda i, *_: (0, 3), pipeline_mode=pl.Buffered(1))],
            out_specs=[
                row_spec(D),
                row_spec(D),
                row_spec(wide),
                fixed((4, D)),
                row_spec(width),
                row_spec(width),
            ],
        ),
        out_shape=[
            like((rows, D), F32),
            like((rows, D), BF16),
            like((rows, wide), BF16),
            like((4, D), F32),
            like((rows, width), BF16),
            like((rows, width), BF16),
        ],
        compiler_params=params(1),
        cost_estimate=cost(2 * rows * D * wide, 20 * rows * D),
    )(place, h, dy, a, b, low_mine, low_other, gain[0], bias[0], weights)


def last_kernel(
    place_ref, x_ref, dh_ref, a_ref, b_ref, gain_ref, mine_ref, theirs_ref, sum_mine, sum_theirs, held, sums
):
    x = x_ref[...].astype(F32)
    middle, scaled = stats(x)
    c = (x - middle) * scaled
    dn = a_ref[...].astype(F32) + b_ref[...].astype(F32)
    e = dn * gain_ref[...]
    held[...] = dh_ref[...] + scaled * (e - row_mean(e) - c * row_mean(e * c))
    width = D // 4
    core, side = place_ref[0], place_ref[1]
    here = pl.ds(pl.multiple_of((2 * side + core) * width, width), width)
    there = pl.ds(pl.multiple_of((2 * (1 - side) + core) * width, width), width)
    mine_ref[...] = held[:, here]
    theirs_ref[...] = held[:, there].astype(BF16)
    i = pl.program_id(0)
    add_up(sums, i == 0, jnp.concatenate([col_sum(dn * c), col_sum(dn)], axis=0))

    @pl.when(i == pl.num_programs(0) - 1)
    def _():
        sum_mine[...] = sums[:, here]
        sum_theirs[...] = sums[:, there]


def last(place, x, dh, a, b, gain):
    rows = x.shape[0]
    width = D // 4
    return pl.pallas_call(
        last_kernel,
        name="last",
        grid_spec=pltpu.PrefetchScalarGridSpec(
            num_scalar_prefetch=1,
            grid=(rows // TM,),
            in_specs=[row_spec(D)] * 4 + [gain[1]],
            out_specs=[row_spec(width), row_spec(width), fixed((2, width)), fixed((2, width))],
            scratch_shapes=[pltpu.VMEM((TM, D), F32), pltpu.VMEM((2, D), F32)],
        ),
        out_shape=[
            like((rows, width), F32),
            like((rows, width), BF16),
            like((2, width), F32),
            like((2, width), F32),
        ],
        compiler_params=params(1),
        cost_estimate=cost(20 * rows * D, 12 * rows * D),
    )(place, x, dh, a, b, gain[0])


def join_kernel(*refs):
    out_ref = refs[-1]
    start = 0
    for mine, got in zip(refs[:-1:2], refs[1:-1:2]):
        width = got.shape[1]
        total = mine[...].astype(F32) + got[...].astype(F32)
        out_ref[:, start : start + width] = total.astype(BF16)
        start += width


def join(*parts):
    rows = parts[0].shape[0]
    tm = rows // 4
    widths = [item.shape[1] for item in parts[1::2]]
    return pl.pallas_call(
        join_kernel,
        grid=(4,),
        name="join",
        in_specs=[
            pl.BlockSpec((tm, width), lambda i: (i, 0)) for width in widths for _ in range(2)
        ],
        out_specs=pl.BlockSpec((tm, sum(widths)), lambda i: (i, 0)),
        out_shape=like((rows, sum(widths)), BF16),
        compiler_params=params(1),
        cost_estimate=cost(rows * sum(widths), 6 * rows * sum(widths)),
    )(*parts)


def pack_kernel(*refs):
    out_ref = refs[-1]
    width = refs[0].shape[0]
    for at, ref in enumerate(refs[:-2]):
        out_ref[at, :] = ref[...]
    for at in range(4):
        out_ref[len(refs) - 2 + at, :] = refs[-2][width * at : width * (at + 1)]


def pack(vectors, long_vector):
    width = vectors[0].shape[0]
    return pl.pallas_call(
        pack_kernel,
        name="pack",
        out_shape=like((len(vectors) + 4, width), F32),
    )(*vectors, long_vector)


def unpack_kernel(place_ref, own, far, own_other, far_other, vec_ref, qkv_ref, tile_ref):
    core, side, half = place_ref[0], place_ref[1], place_ref[2]
    width = own.shape[1]
    one = width // 2

    def put(ref, at_side, at_core):
        at = pl.multiple_of((2 * at_side + at_core) * width, width)
        for k in range(6):
            vec_ref[k, :, pl.ds(at, width)] = ref[k : k + 1, :]

    put(own, side, core)
    put(far, 1 - side, core)
    put(own_other, side, 1 - core)
    put(far_other, 1 - side, 1 - core)
    qkv_ref[...] = jnp.zeros_like(qkv_ref)
    blocks = ((own, half), (far, half), (own, 1 - half), (far, 1 - half))
    for at, (ref, which) in enumerate(blocks):
        cut = pl.ds(pl.multiple_of(which * one, one), one)
        qkv_ref[:, 3 * one * at : 3 * one * at + one] = ref[6:7, cut]
        qkv_ref[:, 3 * one * at + 2 * one : 3 * one * (at + 1)] = ref[7:8, cut]
    order = (0, 1, 2, 3), (0, 2, 1, 3)
    for part in range(2):
        for at, index in enumerate(order[part]):
            ref, which = blocks[index]
            start = width * (4 * part + at)
            tile_ref[:, start : start + width] = ref[pl.ds(8 + 2 * which + part, 1), :]


def unpack(place, own, far, own_other, far_other):
    width = own.shape[1]
    return pl.pallas_call(
        unpack_kernel,
        name="unpack",
        in_specs=[pl.BlockSpec(memory_space=pltpu.SMEM)]
        + [pl.BlockSpec(memory_space=pltpu.VMEM)] * 4,
        out_shape=[like((6, 1, D), F32), like((1, 6 * width), F32), like((1, 8 * width), F32)],
    )(place, own, far, own_other, far_other)


def collect_kernel(
    place_ref, turn_ref, qkv_ref, up_a_ref, up_b_ref, a_ref, b_ref, mine_ref, theirs_ref
):
    core, side, half = place_ref[0], place_ref[1], place_ref[2]
    width = mine_ref.shape[1]
    one = width // 2
    for ref, at_side in ((mine_ref, side), (theirs_ref, 1 - side)):
        at = pl.ds(pl.multiple_of((2 * at_side + core) * width, width), width)
        ref[2:6, :] = turn_ref[:, at]
    mine_ref[10:12, :] = a_ref[...]
    theirs_ref[10:12, :] = b_ref[...]
    for at in range(4):
        ref = (mine_ref, theirs_ref)[at % 2]
        which = half if at < 2 else 1 - half
        cut = pl.ds(pl.multiple_of(which * one, one), one)
        ref[0:1, cut] = qkv_ref[:, 3 * one * at : 3 * one * at + one]
        ref[1:2, cut] = qkv_ref[:, 3 * one * at + 2 * one : 3 * one * (at + 1)]
    order = (0, 1, 2, 3), (0, 2, 1, 3)
    for part in range(2):
        for at, index in enumerate(order[part]):
            ref = (mine_ref, theirs_ref)[index % 2]
            which = half if index < 2 else 1 - half
            up_ref = (up_a_ref, up_b_ref)[part]
            ref[pl.ds(6 + 2 * which + part, 1), :] = up_ref[:, width * at : width * (at + 1)]


def collect(place, *sums):
    width = D // 4
    return pl.pallas_call(
        collect_kernel,
        name="collect",
        in_specs=[pl.BlockSpec(memory_space=pltpu.SMEM)]
        + [pl.BlockSpec(memory_space=pltpu.VMEM)] * 6,
        out_shape=[like((12, width), F32)] * 2,
    )(place, *sums)


def hand_out_kernel(a_ref, b_ref, *outs):
    sums = a_ref[...] + b_ref[...]
    width = a_ref.shape[1]
    for at in range(6):
        outs[at][...] = sums[at, :]
    for at in range(4):
        outs[6][width * at : width * (at + 1)] = sums[6 + at, :]
    for at in range(2):
        outs[7 + at][...] = sums[10 + at, :]


def hand_out(mine, got):
    width = mine.shape[1]
    one = like((width,), F32)
    return pl.pallas_call(
        hand_out_kernel,
        name="hand_out",
        out_shape=[one] * 6 + [like((4 * width,), F32)] + [one] * 2,
    )(mine, got)


def place_mlp_kernel(swapped, place_ref, mine_ref, other_ref, a_ref, b_ref, up_ref, down_ref, out_ref):
    half = place_ref[2]
    width = up_ref.shape[1] // 2
    quarter = width // 2
    heads = out_ref.shape[0] // 2
    for ref, at in ((mine_ref, half), (other_ref, 1 - half)):
        up_ref[:, pl.ds(pl.multiple_of(at * width, width), width)] = ref[:, :width].astype(F32)
        down_ref[pl.ds(pl.multiple_of(at * width + quarter, quarter), quarter), :] = (
            ref[:, width : width + quarter].astype(F32).T
        )
        out_ref[pl.ds(pl.multiple_of(at * heads, heads), heads), :] = (
            ref[:, width + quarter :].astype(F32).T
        )
    for part, at in ((0, half), (1, 1 - half)):
        from_b = 1 - part if swapped else part
        total = a_ref[:, part * quarter : (part + 1) * quarter].astype(F32)
        total = total + b_ref[:, from_b * quarter : (from_b + 1) * quarter].astype(F32)
        down_ref[pl.ds(pl.multiple_of(at * width, width), quarter), :] = total.T


def place_mlp(place, mine, other, a, b, swapped):
    strip, cols = mine.shape
    quarter = a.shape[1] // 2
    heads = cols - 3 * quarter
    return pl.pallas_call(
        functools.partial(place_mlp_kernel, swapped),
        name="place_mlp",
        in_specs=[pl.BlockSpec(memory_space=pltpu.SMEM)]
        + [pl.BlockSpec(memory_space=pltpu.VMEM)] * 4,
        out_shape=[
            like((strip, 4 * quarter), F32),
            like((4 * quarter, strip), F32),
            like((2 * heads, strip), F32),
        ],
    )(place, mine, other, a, b)


def place_qkv_kernel(place_ref, mine_ref, other_ref, *outs):
    half = place_ref[2]
    heads = outs[0].shape[1] // 2
    for ref, at in ((mine_ref, half), (other_ref, 1 - half)):
        here = pl.ds(pl.multiple_of(at * heads, heads), heads)
        for w in range(3):
            outs[w][:, here] = ref[:, heads * w : heads * (w + 1)].astype(F32)


def place_qkv(place, mine, other):
    strip, cols = mine.shape
    return pl.pallas_call(
        place_qkv_kernel,
        name="place_qkv",
        in_specs=[pl.BlockSpec(memory_space=pltpu.SMEM)]
        + [pl.BlockSpec(memory_space=pltpu.VMEM)] * 2,
        out_shape=[like((strip, cols // 3 * 2), F32)] * 3,
    )(place, mine, other)


def local(
    sizes,
    inputs,
    query_weight,
    key_weight,
    value_weight,
    query_bias,
    value_bias,
    out_weight,
    out_bias,
    up_weight,
    up_bias,
    down_weight,
    down_bias,
    first_gain,
    first_shift,
    second_gain,
    second_shift,
    cotangent,
):
    n_dp, n_row, n_xa, n_core = sizes
    my_x = lax.axis_index("xa")
    my_core = lax.axis_index("core")
    my_row = lax.axis_index("row")
    my_half = lax.axis_index("dp") % 2
    place = jnp.stack([my_core, my_x, my_half, my_row]).astype(jnp.int32)
    tokens_here, width = inputs.shape
    images = tokens_here // SEQ
    held = images // n_xa
    rows = held * PAD
    half = up_weight.shape[1] // 2
    quarter = half // 2
    heads_half = width // 2
    three = 3 * heads_half

    def swap(value, axis, size, bit=1):
        return lax.ppermute(value, axis, [(at, at ^ bit) for at in range(size)])

    def shifted(value, shift):
        return lax.ppermute(value, "row", [(at, (at + shift) % n_row) for at in range(n_row)])

    def across(value):
        return swap(value, "xa", n_xa)

    def beside(value):
        return swap(value, "core", n_core)

    def over(value):
        return swap(value, "dp", n_dp)

    def pick(value, at, axis):
        return lax.dynamic_index_in_dim(value, at, axis, keepdims=False)

    def in_order(mine, other, at):
        return jnp.where(at == 0, mine, other), jnp.where(at == 0, other, mine)

    def after(value, *others):
        return lax.optimization_barrier((value, *others))[0]

    def halves(value, axis):
        cut = value.shape[axis] // 2
        both = value.reshape(value.shape[:axis] + (2, cut) + value.shape[axis + 1 :])
        return pick(both, my_half, axis), pick(both, my_half ^ 1, axis)

    count = held * SEQ

    def send_tokens(value):
        return lax.dynamic_slice_in_dim(value, (my_x ^ 1) * count, count, 0)

    def wide_tokens(value, got):
        mine = lax.dynamic_slice_in_dim(value, my_x * count, count, 0)
        pair = jnp.concatenate([mine, got], axis=1).reshape(held, SEQ, 2 * width)
        pair = jnp.pad(pair, ((0, 0), (0, PAD - SEQ), (0, 0))).reshape(rows, 2 * width)
        other = beside(pair)
        left, right = in_order(pair, other, my_core)
        first_left, second_left = in_order(left[:, :width], left[:, width:], my_x)
        first_right, second_right = in_order(right[:, :width], right[:, width:], my_x)
        return jnp.concatenate([first_left, first_right, second_left, second_right], axis=1)

    attn_shard = jnp.concatenate(
        [halves(item, 1)[0] for item in (query_weight, key_weight, value_weight)]
        + [halves(out_weight, 0)[0].T],
        axis=1,
    )
    input_leaves = send_tokens(inputs)
    attn_shard = after(attn_shard, input_leaves)
    input_got = across(input_leaves)
    pieces = [attn_shard] + [shifted(attn_shard, shift) for shift in range(1, n_row)]
    small = pack(
        (
            out_bias,
            down_bias,
            first_gain,
            first_shift,
            second_gain,
            second_shift,
            query_bias,
            value_bias,
        ),
        up_bias,
    )
    fars = [across(piece) for piece in pieces]
    oths = [over(piece) for piece in pieces]
    small_far = across(small)
    vectors, qkv_bias, tile_bias = unpack(
        place, small, after(small_far, pieces[-1]), beside(small), beside(small_far)
    )
    out_bias_all, down_bias_all, gain_one, shift_one, gain_two, shift_two = (
        (vectors, pl.BlockSpec((None, 1, D), lambda i, *_, at=at: (at, 0, 0))) for at in range(6)
    )
    wide_input = wide_tokens(inputs, after(input_got, pieces[-1]))
    far_oths = [
        across(after(oths[at], wide_input, qkv_bias))
        if at % 2
        else over(fars[at])
        for at in range(n_row)
    ]

    def gather(part):
        up_part = halves(up_weight, 1)[0][:, quarter * part : quarter * (part + 1)]
        down_part = halves(down_weight, 0)[0][quarter * part : quarter * (part + 1)].T
        shard = after(jnp.concatenate([up_part, down_part], axis=1), *pieces)
        return lax.all_gather(shard, "row", axis=0, tiled=True)

    own_a, own_b = gather(0), gather(1)
    grad_got = across(after(send_tokens(cotangent), wide_input))

    wide_one, qkv, attn_weights = norm_qkv(
        place, wide_input, gain_one, shift_one, qkv_bias, (*pieces, *fars, *oths, *far_oths)
    )
    oth_a, far_a = over(own_a), across(own_a)
    oth_b, far_b = over(own_b), across(own_b)
    first_heads = attend(qkv)
    attended, probs = attend(qkv, first_heads)
    mixed = mm_nt(attended, attn_weights[:, 4 * three :]).astype(BF16)
    mixed_other = beside(mixed)
    wide_grad = wide_tokens(cotangent, after(grad_got, mixed))
    far_oth_a = over(far_a)
    middle_sum, wide_two = middle(wide_input, mixed, mixed_other, out_bias_all, gain_two, shift_two)
    up_far_oth_b = over(far_b[:, :quarter])
    down_far_oth_b = across(oth_b[:, quarter:])

    def tiles(value, first, end):
        return value[:, quarter * first : quarter * end]

    gate_a, pre_a, up_sums_a, low_a, lift_a = mlp(
        place, wide_two, wide_grad, tile_bias, (own_a, far_a, oth_a, far_oth_a)
    )
    up_over = mm_tn(wide_two, tiles(pre_a, 2, 4)).astype(BF16)
    down_a = mm_tn(wide_grad, gate_a).astype(BF16)
    up_over_got = over(up_over)
    down_piece = lax.psum_scatter(down_a, "row", scatter_dimension=0, tiled=True)
    gate_b, pre_b, up_sums_b, low_mine, low_theirs, lifted_two = mlp(
        place,
        after(wide_two, up_over, down_a),
        wide_grad,
        tile_bias,
        (own_b, oth_b, far_b, up_far_oth_b, down_far_oth_b),
        (low_a, lift_a),
    )

    def wide_add(mine, got):
        return (mine.astype(F32) + got.astype(F32)).astype(BF16)

    def same_half(value):
        if n_dp == 2:
            return value
        groups = [[at + bit for at in range(0, n_dp, 2)] for bit in range(2)]
        return lax.psum(value.astype(F32), "dp", axis_index_groups=groups).astype(BF16)

    def scatter(value):
        return lax.psum_scatter(value, "row", scatter_dimension=0, tiled=True)

    lifted_other = beside(lifted_two)
    low_other = beside(low_theirs)
    up_across = mm_tn(wide_two, tiles(pre_b, 2, 4)).astype(BF16)
    down_over = mm_tn(wide_grad, tiles(gate_b, 2, 4)).astype(BF16)
    up_across_got, down_over_got = across(up_across), over(down_over)

    middle_grad, attn_grad, head_grad, turn_sums, out_mine, out_theirs = turn(
        place,
        middle_sum,
        wide_grad,
        lifted_two,
        after(lifted_other, up_across, down_over),
        low_mine,
        low_other,
        gain_two,
        down_bias_all,
        attn_weights,
    )
    out_all = mm_tn(attn_grad, attended).astype(BF16)
    out_over_got = over(out_all[:, 2 * heads_half :])
    down_x_got = across(after(down_piece, attn_grad)[:, half:])
    up_over_got, up_across_got, down_over_got, _ = lax.optimization_barrier(
        (up_over_got, up_across_got, down_over_got, out_all)
    )
    up_a = wide_add(mm_tn(wide_two, tiles(pre_a, 0, 2)), up_over_got)
    up_b = wide_add(mm_tn(wide_two, tiles(pre_b, 0, 2)), up_across_got)
    down_b = wide_add(mm_tn(wide_grad, tiles(gate_b, 0, 2)), down_over_got)
    up_a_got, up_b_got = across(up_a[:, quarter:]), over(up_b[:, quarter:])
    out_own = wide_add(out_all[:, : 2 * heads_half], after(out_over_got, down_b))
    out_far_got = across(out_own[:, heads_half:])
    down_x = wide_add(down_piece[:, :half], after(down_x_got, down_b))
    down_y_got = over(down_x)
    down_b_got = across(down_b[:, quarter:])
    out_got = across(after(out_theirs, down_b))
    dqkv, qkv_sums = attend_back(qkv, probs, after(head_grad, up_a, up_b, out_own, down_x))

    def to_feature_blocks(mine, got, dtype):
        first, second = in_order(mine.astype(dtype), got.astype(dtype), my_x)
        both = jnp.concatenate([first, second]).reshape(images, PAD, width)
        return both[:, :SEQ].reshape(tokens_here, width)

    cut = 2 * heads_half
    split = 3 * three + cut
    far_oth_qk = mm_tn(wide_one, dqkv[:, 3 * three : split]).astype(BF16)
    far_oth_v = mm_tn(after(wide_one, far_oth_qk), dqkv[:, split:]).astype(BF16)
    qk_got, v_got = over(far_oth_qk), across(far_oth_v)
    up_sum = join(
        up_a, up_a_got, up_b, up_b_got, down_b, down_b_got, out_own, after(out_far_got, far_oth_v)
    )
    up_piece = same_half(scatter(up_sum))
    near_oth = wide_add(
        mm_tn(wide_one, dqkv[:, 2 * three : 3 * three]),
        jnp.pad(after(v_got, up_sum), ((0, 0), (cut, 0))),
    )
    near_oth_got = over(near_oth)
    far_own = wide_add(
        mm_tn(wide_one, dqkv[:, three : 2 * three]),
        jnp.pad(after(qk_got, near_oth), ((0, 0), (0, three - cut))),
    )
    far_own_got = across(far_own)
    lifted_one = mm_nt(
        after(dqkv, far_own), attn_weights[:, : 4 * three]
    ).astype(BF16)
    lifted_one_other = beside(lifted_one)

    near_own = mm_tn(after(wide_one, lifted_one), dqkv[:, :three])
    input_mine, input_theirs, late_mine, late_theirs = last(
        place, wide_input, middle_grad, lifted_one, after(lifted_one_other, near_own), gain_one
    )
    mine_sums, theirs_sums = collect(
        place, turn_sums, qkv_sums, up_sums_a, up_sums_b, late_mine, late_theirs
    )

    near_sum = (near_own + near_oth_got.astype(F32) + after(far_own_got, mine_sums).astype(F32)).astype(
        BF16
    )
    strip = D // n_row

    def rows_of(value, shift):
        return lax.dynamic_slice_in_dim(value, (my_row + shift) % n_row * strip, strip, 0)

    gots = [shifted(rows_of(near_sum, shift), shift) for shift in range(1, n_row)]
    input_got = across(after(input_theirs, near_sum))
    sums = mine_sums + across(after(theirs_sums, near_sum))
    steps = [("row", n_row, 1 << bit) for bit in range(n_row.bit_length() - 1)]
    steps += [("dp", n_dp, 1 << bit) for bit in range(n_dp.bit_length() - 1)]
    for step in steps[:-1]:
        sums = sums + swap(sums, *step)
    sums_got = swap(sums, *steps[-1])
    outputs = to_feature_blocks(out_mine, after(out_got, near_sum), BF16)

    qkv_total = rows_of(near_sum, 0).astype(F32)
    for got in gots:
        qkv_total = qkv_total + got.astype(F32)
    qkv_piece = same_half(qkv_total.astype(BF16))
    qkv_other = over(qkv_piece)
    input_grad = to_feature_blocks(input_mine, input_got, F32)
    up_other = over(up_piece)

    if n_dp > 2:
        down_total = down_x.astype(F32) + jnp.concatenate(
            [down_y_got[:, quarter:], down_y_got[:, :quarter]], axis=1
        ).astype(F32)
        groups = [[at + bit for at in range(0, n_dp, 2)] for bit in range(2)]
        down_total = lax.psum(down_total, "dp", axis_index_groups=groups)
        parts = (down_total, jnp.zeros_like(down_total))
    else:
        parts = (down_x, down_y_got)
    up_grad, down_grad, out_grad = place_mlp(place, up_piece, up_other, *parts, n_dp == 2)
    sums = hand_out(sums, after(sums_got, up_grad, input_grad))
    query_grad, key_grad, value_grad = place_qkv(
        place, qkv_piece, after(qkv_other, up_grad, input_grad)
    )

    return (
        outputs,
        input_grad,
        query_grad,
        key_grad,
        value_grad,
        sums[0],
        sums[1],
        out_grad,
        sums[2],
        up_grad,
        sums[6],
        down_grad,
        sums[3],
        sums[7],
        sums[8],
        sums[4],
        sums[5],
    )


def solution(mesh):
    n_dp, n_row, n_col = (mesh.shape[name] for name in ("dp", "row", "col"))
    sizes = (n_dp, n_row, n_col // 2, 2)
    split = Mesh(mesh.devices.reshape(sizes), ("dp", "row", "xa", "core"))
    col = ("xa", "core")
    tokens, rows, cols, vec = P(("dp", "row"), col), P("row", col), P(col, "row"), P(col)
    in_specs = (
        (tokens, rows, rows, rows, vec, vec, cols, vec, rows, vec, cols)
        + (vec,) * 5
        + (tokens,)
    )
    out_specs = (
        (tokens, tokens, rows, rows, rows, vec, vec, cols, vec, rows, vec, cols) + (vec,) * 5
    )

    def body(*args):
        return local(sizes, *args)

    return jax.shard_map(
        body, mesh=split, in_specs=in_specs, out_specs=out_specs, check_vma=False
    )
```
